32 devices in a mesh: section: 2 (over core), dp: 4 (over z), seq: 4 (over y, x).
Axes of the slice: x: 2, y: 2, z: 4, core: 2. Of those that a mesh axis runs over, the one named last changes fastest.
Arguments:
- signal: bfloat16 [8, 1024, 1024], P('dp', 'seq'), may hold values from -6 to 6
- frame_segment_index: int32 [8, 1024], P('dp'), may hold values from 0 to 3, as said below
- conv_weight: float32 [8192, 1024], P(('section', 'dp', 'seq')), may hold values from -0.25 to 0.25
- conv_bias: float32 [1024], P(('section', 'dp', 'seq')), may hold values from -3 to 3
- norm1_gain: float32 [2, 1024], P('section', ('dp', 'seq')), may hold values from 0.1 to 1.9
- qkv_weight: float32 [2, 1024, 3072], P('section', ('dp', 'seq')), may hold values from -0.1875 to 0.1875
- out_weight: float32 [2, 1024, 1024], P('section', ('dp', 'seq')), may hold values from -2 to 2
- norm2_gain: float32 [2, 1024], P('section', ('dp', 'seq')), may hold values from 0.1 to 1.9
- up_weight: float32 [2, 1024, 4096], P('section', ('dp', 'seq')), may hold values from -0.1875 to 0.1875
- down_weight: float32 [2, 4096, 1024], P('section', ('dp', 'seq')), may hold values from -0.09375 to 0.09375
- cotangent: bfloat16 [8, 1024, 1024], P('dp', 'seq'), may hold values from -6 to 6
Outputs:
- ends: float32 [2, 8, 1024, 1024], P('section', 'dp', 'seq')
- conv_weight_grad: float32 [8192, 1024], P(('section', 'dp', 'seq'))
- conv_bias_grad: float32 [1024], P(('section', 'dp', 'seq'))
- norm1_gain_grad: float32 [2, 1024], P('section', ('dp', 'seq'))
- qkv_weight_grad: float32 [2, 1024, 3072], P('section', ('dp', 'seq'))
- out_weight_grad: float32 [2, 1024, 1024], P('section', ('dp', 'seq'))
- norm2_gain_grad: float32 [2, 1024], P('section', ('dp', 'seq'))
- up_weight_grad: float32 [2, 1024, 4096], P('section', ('dp', 'seq'))
- down_weight_grad: float32 [2, 4096, 1024], P('section', ('dp', 'seq'))
The draws below stay inside these ranges and needn't reach their ends.
Inputs may be any that keep to these rules, and one draw needn't show every extreme that they name: `frame_segment_index`: in each row the segment ids start at 0 and never fall, each segment covering consecutive frames. In each aligned block of 2 rows (the rows of one index of dp) one row, drawn from the seed, is a single segment; every other row has exactly 4 segments.
All inputs are finite; a program needn't handle non-finite values.
Results may differ from the reference program's by a relative error of at most 0.018.
Values may be sent and summed in bfloat16 or wider, within the bound.
A program may use at most 832 MiB of HBM per device.

```python
import math
import jax
import jax.numpy as jnp
from jax import lax

MODEL_WIDTH = 1024
HEAD_DIM = 64
FF = 4096
GROUPS = 16
TAPS = 128
ROW_SEGMENTS = 4
MB = 2
PACKED_ROW_FRAMES = 1024
PACKED_ROWS = 8
N_SECTION = 2


def draw_frame_segment_index(key, part):
    cut_key = jax.random.fold_in(key, 11)
    pick_key = jax.random.fold_in(key, 12)
    row_keys = jax.random.split(cut_key, PACKED_ROWS)
    shuffled = jax.vmap(lambda row_key: jax.random.permutation(row_key, PACKED_ROW_FRAMES - 1))(row_keys) + 1
    cuts = jnp.sort(shuffled[:, :ROW_SEGMENTS - 1], axis=1)
    positions = jnp.arange(PACKED_ROW_FRAMES, dtype=jnp.int32)
    several = jnp.sum((positions[None, :, None] >= cuts[:, None, :]).astype(jnp.int32), axis=2)
    chosen = jax.random.randint(pick_key, (PACKED_ROWS // MB,), 0, MB)
    row_ids = jnp.arange(PACKED_ROWS, dtype=jnp.int32)
    single = row_ids % MB == chosen[row_ids // MB]
    return jnp.where(single[:, None], 0, several).astype(jnp.int32)


def block_scale(own_key, dims, cuts, least, top_value):
    def one(position, shards_of):
        steps = jax.random.uniform(jax.random.fold_in(jax.random.fold_in(own_key, 6), position), (shards_of,), jnp.float32, least / len(cuts), top_value / len(cuts))
        return jnp.repeat(jnp.exp(steps), dims[position] // shards_of).reshape((-1,) + (1,) * (len(dims) - position - 1))

    level = one(*cuts[0])
    for cut in cuts[1:]:
        level = level * one(*cut)
    return level


def gaussian(key, shape, scale, reach, shards=(), held_as=jnp.bfloat16):
    array = scale * jax.random.normal(key, shape, jnp.float32)
    if shards:
        array = array * block_scale(key, shape, shards, -0.22, 0.18)
    return jnp.clip(array, -reach, reach).astype(held_as)


def setup_inputs(seed: int = 0) -> dict:
    key_list = jax.random.split(jax.random.key(seed), 12)
    signal = gaussian(key_list[0], (PACKED_ROWS, PACKED_ROW_FRAMES, MODEL_WIDTH), 1.0, 6.0, ((0, 4), (1, 4)))
    frame_segment_index = draw_frame_segment_index(jax.random.fold_in(key_list[11], 71), 0)
    conv_weight = gaussian(key_list[2], (TAPS * (MODEL_WIDTH // GROUPS), MODEL_WIDTH), (TAPS * MODEL_WIDTH // GROUPS // 16) ** -0.5, 0.25, ((0, 32),), jnp.float32)
    conv_bias = gaussian(key_list[3], (MODEL_WIDTH,), 0.5, 3.0, ((0, 32),), jnp.float32)
    norm1_gain = jnp.clip(1.0 + 0.18 * jax.random.normal(key_list[4], (N_SECTION, MODEL_WIDTH), jnp.float32), 0.1, 1.9)
    qkv_weight = gaussian(key_list[5], (N_SECTION, MODEL_WIDTH, 3 * MODEL_WIDTH), MODEL_WIDTH ** -0.5, 0.1875, ((0, 2), (1, 16)), jnp.float32)
    out_weight = gaussian(key_list[6], (N_SECTION, MODEL_WIDTH, MODEL_WIDTH), 8 ** -0.5, 2.0, ((0, 2), (1, 16)), jnp.float32)
    norm2_gain = jnp.clip(1.0 + 0.18 * jax.random.normal(key_list[7], (N_SECTION, MODEL_WIDTH), jnp.float32), 0.1, 1.9)
    up_weight = gaussian(key_list[8], (N_SECTION, MODEL_WIDTH, FF), MODEL_WIDTH ** -0.5, 0.1875, ((0, 2), (1, 16)), jnp.float32)
    down_weight = gaussian(key_list[9], (N_SECTION, FF, MODEL_WIDTH), FF ** -0.5, 0.09375, ((0, 2), (1, 16)), jnp.float32)
    cotangent = gaussian(key_list[10], (PACKED_ROWS, PACKED_ROW_FRAMES, MODEL_WIDTH), 1.0, 6.0, ((0, 4), (1, 4)))
    return dict(signal=signal, frame_segment_index=frame_segment_index, conv_weight=conv_weight, conv_bias=conv_bias, norm1_gain=norm1_gain, qkv_weight=qkv_weight, out_weight=out_weight, norm2_gain=norm2_gain, up_weight=up_weight, down_weight=down_weight, cotangent=cotangent)


@jax.custom_vjp
def low(v):
    return lax.optimization_barrier(v.astype(jnp.bfloat16)).astype(jnp.float32)

@jax.custom_vjp
def low_back(v):
    return v

def low_keep(v):
    return (low(v), None)

def low_pass(kept, grad):
    return (grad,)

def back_keep(v):
    return (v, None)

def back_low(kept, grad):
    return (low(grad),)
low.defvjp(low_keep, low_pass)
low_back.defvjp(back_keep, back_low)
EPS = 1e-05
NEG = -1e+30
HIGH = lax.Precision.HIGHEST

def normalize(values, gain):
    average = lax.optimization_barrier(jnp.mean(values, axis=-1, keepdims=True))
    centred = values - average
    spread = lax.optimization_barrier(jnp.mean(centred * centred, axis=-1, keepdims=True))
    return centred * lax.rsqrt(spread + EPS) * gain

def smooth(values):
    return jax.nn.gelu(values, approximate=False)

def matmul(left, right_edge):
    return jnp.dot(left, right_edge, precision=HIGH, preferred_element_type=jnp.float32)

def position_conv(frames, kernel):
    per_group = MODEL_WIDTH // GROUPS
    weight_view = jnp.transpose(kernel.reshape(TAPS, per_group, MODEL_WIDTH), (2, 1, 0))
    result = lax.conv_general_dilated(frames.T[None], weight_view, (1,), [(TAPS // 2, TAPS // 2 - 1)], feature_group_count=GROUPS, precision=HIGH, preferred_element_type=jnp.float32)
    return result[0].T

def attention(queries, keys, values, segments):
    length = queries.shape[0]
    head_count = MODEL_WIDTH // HEAD_DIM
    block_rows = math.gcd(length, 512)
    query_heads = queries.reshape(length // block_rows, block_rows, head_count, HEAD_DIM)
    query_segs = segments.reshape(length // block_rows, block_rows)
    key_heads = keys.reshape(length, head_count, HEAD_DIM)
    value_heads = values.reshape(length, head_count, HEAD_DIM)
    factor = 1.0 / math.sqrt(HEAD_DIM)

    def one_block(row_pair):
        query_block, seg_block = row_pair
        scores = low_back(jnp.einsum('qhd,khd->hqk', query_block, key_heads, precision=HIGH) * factor)
        allowed = seg_block[:, None] == segments[None, :]
        masked = jnp.where(allowed[None], scores, NEG)
        row_top = lax.optimization_barrier(jnp.max(masked, axis=-1, keepdims=True))
        raised = jnp.exp(masked - row_top)
        chances = low(raised / lax.optimization_barrier(jnp.sum(raised, axis=-1, keepdims=True)))
        mixture = jnp.einsum('hqk,khd->qhd', chances, value_heads, precision=HIGH)
        return mixture.reshape(block_rows, MODEL_WIDTH)
    return lax.map(jax.checkpoint(one_block), (query_heads, query_segs)).reshape(length, MODEL_WIDTH)

def block(frames, segments, layer_weights, conv_weights, with_conv):
    gain_one, w_qkv, w_out, gain_two, w_up, w_down = layer_weights
    if with_conv:
        conv_pre = low_back(position_conv(frames, conv_weights[0]) + conv_weights[1])
        frames = frames + smooth(conv_pre)
    normed_one = low(normalize(frames, gain_one))
    packed = low_back(low(matmul(normed_one, w_qkv)))
    attended = low_back(low(attention(packed[:, :MODEL_WIDTH], packed[:, MODEL_WIDTH:2 * MODEL_WIDTH], packed[:, 2 * MODEL_WIDTH:], segments)))
    resid_two = frames + low_back(matmul(attended, w_out))
    normed_two = low(normalize(resid_two, gain_two))
    hidden = low(smooth(low_back(matmul(normed_two, w_up))))
    return resid_two + low_back(matmul(hidden, w_down))

def reference(signal, frame_segment_index, conv_weight, conv_bias, norm1_gain, qkv_weight, out_weight, norm2_gain, up_weight, down_weight, cotangent):
    frames_all = signal.astype(jnp.float32)

    def forward(frames_in, conv_w, conv_b, gain_a, w_qkv, w_out, gain_b, w_up, w_down):
        conv_weights = (low(conv_w), low(conv_b))
        stacks = [low(member) for member in (gain_a, w_qkv, w_out, gain_b, w_up, w_down)]
        layer_zero = tuple((member[0] for member in stacks))
        layer_one = tuple((member[1] for member in stacks))

        def one_row(row_pair):
            frames, segments = row_pair
            middle = low_back(low(block(frames, segments, layer_zero, conv_weights, True)))
            return block(middle, segments, layer_one, conv_weights, False)
        return lax.map(one_row, (frames_in, frame_segment_index))
    output, pullback = jax.vjp(forward, frames_all, conv_weight, conv_bias, norm1_gain, qkv_weight, out_weight, norm2_gain, up_weight, down_weight)
    grads = pullback(cotangent.astype(jnp.float32))
    ends = jnp.stack([grads[0], output])
    return (ends, grads[1], grads[2], grads[3], grads[4], grads[5], grads[6], grads[7], grads[8])
```

```python
import functools
import math

import jax
import jax.numpy as jnp
from jax import lax
from jax.experimental import pallas as pl
from jax.experimental.pallas import tpu as pltpu
from jax.sharding import PartitionSpec as P

HEAD_DIM = 64
GROUPS = 16
TAPS = 128


EPS = 1e-05
NEG = -1e30


def padded_2(block, sides, width):
    for axis, dim in sides:
        count = lax.axis_size(axis)
        forward = [(i, i + 1) for i in range(count - 1)]
        backward = [(target, source) for source, target in forward]
        low = lax.ppermute(
            lax.slice_in_dim(block, block.shape[dim] - width, None, axis=dim), axis, forward
        )
        high = lax.ppermute(lax.slice_in_dim(block, 0, width, axis=dim), axis, backward)
        block = jnp.concatenate([low, block, high], axis=dim)
    return block


def from_behind(value, axis, steps):
    count = lax.axis_size(axis)
    first, last = (max(0, -steps), min(count, count - steps))
    return lax.ppermute(value, axis, [(source, source + steps) for source in range(first, last)])


def normalize(values, gain):
    average = jnp.mean(values, axis=-1, keepdims=True)
    centred = values - average
    spread = jnp.mean(centred * centred, axis=-1, keepdims=True)
    return centred * lax.rsqrt(spread + EPS) * gain


def smooth(values):
    return jax.nn.gelu(values, approximate=False)


def conv_taps(padded, kernel, frames):
    width_all = padded.shape[1]
    per_group = width_all // GROUPS
    tap_step = math.gcd(TAPS, 16)
    weight_view = kernel.reshape(TAPS, per_group, GROUPS, per_group)
    running = jnp.zeros((frames, GROUPS, per_group), jnp.float32)
    for first_tap in range(0, TAPS, tap_step):
        windows = jnp.stack(
            [padded[first_tap + offset : first_tap + offset + frames] for offset in range(tap_step)]
        )
        windows = windows.reshape(tap_step, frames, GROUPS, per_group)
        running = running + jnp.einsum(
            "jtgc,jcgo->tgo",
            windows,
            weight_view[first_tap : first_tap + tap_step],
            preferred_element_type=jnp.float32,
        )
    return running.reshape(frames, width_all)


def conv_input_grad(grad_pad, kernel, frames):
    width_all = grad_pad.shape[1]
    per_group = width_all // GROUPS
    tap_step = math.gcd(TAPS, 16)
    weight_view = kernel.reshape(TAPS, per_group, GROUPS, per_group)
    running = jnp.zeros((frames, GROUPS, per_group), jnp.float32)
    for first_tap in range(0, TAPS, tap_step):
        back_windows = jnp.stack(
            [
                grad_pad[TAPS - first_tap - offset : TAPS - first_tap - offset + frames]
                for offset in range(tap_step)
            ]
        )
        back_windows = back_windows.reshape(tap_step, frames, GROUPS, per_group)
        running = running + jnp.einsum(
            "jtgo,jcgo->tgc",
            back_windows,
            weight_view[first_tap : first_tap + tap_step],
            preferred_element_type=jnp.float32,
        )
    return running.reshape(frames, width_all)


def conv_kernel_grad(padded_all, grad_all):
    step_count, frames, width_all = grad_all.shape
    per_group = width_all // GROUPS
    tap_step = math.gcd(TAPS, 16)
    grad_view = grad_all.reshape(step_count * frames, GROUPS, per_group)
    kernel_parts = []
    for first_tap in range(0, TAPS, tap_step):
        windows = jnp.stack(
            [
                padded_all[:, first_tap + offset : first_tap + offset + frames]
                for offset in range(tap_step)
            ]
        )
        windows = windows.reshape(tap_step, step_count * frames, GROUPS, per_group)
        kernel_parts.append(
            jnp.einsum("jtgc,tgo->jcgo", windows, grad_view, preferred_element_type=jnp.float32)
        )
    return jnp.concatenate(kernel_parts, axis=0).reshape(TAPS * per_group, width_all)


def score_block(query_heads, key_block, query_segs, key_segs, factor):
    scores = (
        jnp.einsum("qhd,khd->hqk", query_heads, key_block, preferred_element_type=jnp.float32)
        * factor
    )
    allowed = (query_segs[:, None] == key_segs[None, :])[None]
    return (scores, allowed)


def front(layer_in, weights, kernel, conv_shift, first_section):
    frames, width_all = layer_in.shape
    padded = padded_2(layer_in, (("seq", 0),), TAPS // 2)
    conv_pre = lax.cond(
        first_section,
        lambda: conv_taps(padded, kernel, frames) + conv_shift.astype(jnp.float32),
        lambda: jnp.zeros((frames, width_all), jnp.float32),
    )
    conv_val, conv_pull = jax.vjp(smooth, conv_pre)
    resid_one = layer_in.astype(jnp.float32) + conv_val
    normed_val, norm_pull = jax.vjp(normalize, resid_one, weights[0].astype(jnp.float32))
    normed_one = normed_val.astype(jnp.bfloat16)
    packed = jnp.dot(normed_one, weights[1], preferred_element_type=jnp.float32).astype(
        jnp.bfloat16
    )
    return (padded, conv_pull, resid_one, norm_pull, normed_one, packed)


def tail(resid_one, attn_low, weights):
    resid_two = resid_one + jnp.dot(attn_low, weights[2], preferred_element_type=jnp.float32)
    normed_val, norm_pull = jax.vjp(normalize, resid_two, weights[3].astype(jnp.float32))
    normed_two = normed_val.astype(jnp.bfloat16)
    hidden_pre = jnp.dot(normed_two, weights[4], preferred_element_type=jnp.float32)
    hidden_val, gelu_pull = jax.vjp(smooth, hidden_pre)
    hidden_low = hidden_val.astype(jnp.bfloat16)
    result = resid_two + jnp.dot(hidden_low, weights[5], preferred_element_type=jnp.float32)
    return (result, norm_pull, normed_two, gelu_pull, hidden_low)


def key_loop(keys_all, values_all, segment_row, head_count, visit, initial):
    total_rows = keys_all.shape[0]
    block_rows = math.gcd(total_rows, 512)

    def one_block(block_index, running):
        offset = block_index * block_rows
        key_block = lax.dynamic_slice_in_dim(keys_all, offset, block_rows, 0).reshape(
            block_rows, head_count, HEAD_DIM
        )
        value_block = lax.dynamic_slice_in_dim(values_all, offset, block_rows, 0).reshape(
            block_rows, head_count, HEAD_DIM
        )
        key_segs = lax.dynamic_slice_in_dim(segment_row, offset, block_rows, 0)
        return visit(running, key_block, value_block, key_segs)

    return lax.fori_loop(0, total_rows // block_rows, one_block, initial)


def layer_forward(
    layer_in, segment_row, weights, kernel, conv_shift, first_section, my_start, factor
):
    frames, width_all = layer_in.shape
    head_count = width_all // HEAD_DIM
    padded, conv_pull, resid_one, norm_pull, normed_one, packed = front(
        layer_in, weights, kernel, conv_shift, first_section
    )
    query_heads = packed[:, :width_all].reshape(frames, head_count, HEAD_DIM)
    query_segs = lax.dynamic_slice_in_dim(segment_row, my_start, frames, 0)
    initial = (
        jnp.full((head_count, frames), NEG, jnp.float32),
        jnp.zeros((head_count, frames), jnp.float32),
        jnp.zeros((head_count, frames, HEAD_DIM), jnp.float32),
    )
    key_piece = lax.all_gather(packed[:, width_all : 2 * width_all], "seq", axis=0, tiled=True)
    value_piece = lax.all_gather(packed[:, 2 * width_all :], "seq", axis=0, tiled=True)
    piece_rows = key_piece.shape[0]
    block_rows = math.gcd(piece_rows, 512)

    def one_block(block_index, running):
        run_max, run_sum, run_acc = running
        offset = block_index * block_rows
        key_block = lax.dynamic_slice_in_dim(key_piece, offset, block_rows, 0).reshape(
            block_rows, head_count, HEAD_DIM
        )
        value_block = lax.dynamic_slice_in_dim(value_piece, offset, block_rows, 0).reshape(
            block_rows, head_count, HEAD_DIM
        )
        key_segs = lax.dynamic_slice_in_dim(segment_row, offset, block_rows, 0)
        scores, allowed = score_block(query_heads, key_block, query_segs, key_segs, factor)
        masked = jnp.where(allowed, scores, NEG)
        new_max = jnp.maximum(run_max, jnp.max(masked, axis=-1))
        weights_now = jnp.where(allowed, jnp.exp(masked - new_max[..., None]), 0.0)
        rescale = jnp.exp(run_max - new_max)
        run_sum = run_sum * rescale + jnp.sum(weights_now, axis=-1)
        run_acc = run_acc * rescale[..., None] + jnp.einsum(
            "hqk,khd->hqd",
            weights_now.astype(jnp.bfloat16),
            value_block,
            preferred_element_type=jnp.float32,
        )
        return (new_max, run_sum, run_acc)

    run_max, run_sum, run_acc = lax.fori_loop(0, piece_rows // block_rows, one_block, initial)
    log_total = run_max + jnp.log(run_sum)
    mixture = run_acc / run_sum[..., None]
    attn_low = jnp.transpose(mixture, (1, 0, 2)).reshape(frames, width_all).astype(jnp.bfloat16)
    result, norm_two_pull, normed_two, gelu_pull, hidden_low = tail(resid_one, attn_low, weights)
    kept = (
        padded,
        conv_pull,
        norm_pull,
        normed_one,
        packed,
        log_total,
        mixture,
        attn_low,
        norm_two_pull,
        normed_two,
        gelu_pull,
        hidden_low,
        segment_row,
    )
    return (result, kept)


def layer_backward(kept, grad_out, weights, kernel, first_section, my_start, factor):
    (
        padded,
        conv_pull,
        norm_one_pull,
        normed_one,
        packed,
        log_total,
        mixture,
        attn_low,
        norm_two_pull,
        normed_two,
        gelu_pull,
        hidden_low,
        segment_row,
    ) = kept
    frames, width_all = normed_one.shape
    head_count = width_all // HEAD_DIM
    query_heads = packed[:, :width_all].reshape(frames, head_count, HEAD_DIM)
    key_local = packed[:, width_all : 2 * width_all]
    value_local = packed[:, 2 * width_all :]
    query_segs = lax.dynamic_slice_in_dim(segment_row, my_start, frames, 0)
    keys_all, values_all = (
        lax.all_gather(key_local, "seq", axis=0, tiled=True),
        lax.all_gather(value_local, "seq", axis=0, tiled=True),
    )

    def chances_for(key_block, key_segs):
        scores, allowed = score_block(query_heads, key_block, query_segs, key_segs, factor)
        return jnp.where(
            allowed, jnp.exp(jnp.where(allowed, scores, NEG) - log_total[..., None]), 0.0
        )

    branch_grad = grad_out.astype(jnp.bfloat16)
    hidden_grad = jnp.einsum(
        "to,io->ti", branch_grad, weights[5], preferred_element_type=jnp.float32
    )
    pre_grad = gelu_pull(hidden_grad)[0].astype(jnp.bfloat16)
    normed_two_grad = jnp.einsum(
        "tf,if->ti", pre_grad, weights[4], preferred_element_type=jnp.float32
    )
    resid_two_grad, grad_gain_two = norm_two_pull(normed_two_grad)
    resid_two_grad = resid_two_grad + grad_out
    attn_branch_grad = resid_two_grad.astype(jnp.bfloat16)
    attended_grad = jnp.einsum(
        "to,io->ti", attn_branch_grad, weights[2], preferred_element_type=jnp.float32
    ).astype(jnp.bfloat16)
    dout_heads = attended_grad.reshape(frames, head_count, HEAD_DIM)
    delta_rows = jnp.einsum("qhd,hqd->hq", dout_heads.astype(jnp.float32), mixture)

    def visit_query(running, key_block, value_block, key_segs):
        chances = chances_for(key_block, key_segs)
        prob_grad = jnp.einsum(
            "qhd,khd->hqk", dout_heads, value_block, preferred_element_type=jnp.float32
        )
        score_grad = (chances * (prob_grad - delta_rows[..., None])).astype(jnp.bfloat16)
        return running + jnp.einsum(
            "hqk,khd->qhd", score_grad, key_block, preferred_element_type=jnp.float32
        )

    grad_query = (
        key_loop(
            keys_all,
            values_all,
            segment_row,
            head_count,
            visit_query,
            jnp.zeros((frames, head_count, HEAD_DIM), jnp.float32),
        )
        * factor
    )
    row_stats = (
        lax.all_gather(log_total, "seq", axis=1, tiled=True),
        lax.all_gather(delta_rows, "seq", axis=1, tiled=True),
    )
    key_heads = key_local.reshape(frames, head_count, HEAD_DIM)
    value_heads = value_local.reshape(frames, head_count, HEAD_DIM)
    start_acc = (
        jnp.zeros((frames, head_count, HEAD_DIM), jnp.float32),
        jnp.zeros((frames, head_count, HEAD_DIM), jnp.float32),
    )
    query_piece = lax.all_gather(packed[:, :width_all], "seq", axis=0, tiled=True)
    dout_piece = lax.all_gather(attended_grad, "seq", axis=0, tiled=True)
    piece_rows = query_piece.shape[0]
    block_rows = math.gcd(piece_rows, 512)

    def one_block(block_index, running):
        key_acc, value_acc = running
        offset = block_index * block_rows
        query_block = lax.dynamic_slice_in_dim(query_piece, offset, block_rows, 0).reshape(
            block_rows, head_count, HEAD_DIM
        )
        dout_block = lax.dynamic_slice_in_dim(dout_piece, offset, block_rows, 0).reshape(
            block_rows, head_count, HEAD_DIM
        )
        seg_block = lax.dynamic_slice_in_dim(segment_row, offset, block_rows, 0)
        total_block = lax.dynamic_slice_in_dim(row_stats[0], offset, block_rows, 1)
        delta_block = lax.dynamic_slice_in_dim(row_stats[1], offset, block_rows, 1)
        scores, allowed = score_block(query_block, key_heads, seg_block, query_segs, factor)
        chances = jnp.where(
            allowed, jnp.exp(jnp.where(allowed, scores, NEG) - total_block[..., None]), 0.0
        )
        prob_grad = jnp.einsum(
            "qhd,khd->hqk", dout_block, value_heads, preferred_element_type=jnp.float32
        )
        score_grad = (chances * (prob_grad - delta_block[..., None])).astype(jnp.bfloat16)
        key_acc = (
            key_acc
            + jnp.einsum(
                "hqk,qhd->khd", score_grad, query_block, preferred_element_type=jnp.float32
            )
            * factor
        )
        value_acc = value_acc + jnp.einsum(
            "hqk,qhd->khd",
            chances.astype(jnp.bfloat16),
            dout_block,
            preferred_element_type=jnp.float32,
        )
        return (key_acc, value_acc)

    key_acc, value_acc = lax.fori_loop(0, piece_rows // block_rows, one_block, start_acc)
    grad_key = key_acc.reshape(frames, width_all)
    grad_value = value_acc.reshape(frames, width_all)
    packed_grad = jnp.concatenate(
        [grad_query.reshape(frames, width_all), grad_key, grad_value], axis=1
    ).astype(jnp.bfloat16)
    normed_one_grad = jnp.einsum(
        "tj,ij->ti", packed_grad, weights[1], preferred_element_type=jnp.float32
    )
    resid_one_grad, grad_gain_one = norm_one_pull(normed_one_grad)
    resid_one_grad = resid_one_grad + resid_two_grad
    conv_grad = jnp.where(first_section, conv_pull(resid_one_grad)[0], 0.0).astype(jnp.bfloat16)
    grad_pad = padded_2(conv_grad, (("seq", 0),), TAPS // 2)
    back_sum = lax.cond(
        first_section,
        lambda: conv_input_grad(grad_pad, kernel, frames),
        lambda: jnp.zeros((frames, width_all), jnp.float32),
    )
    grad_in = resid_one_grad + back_sum
    products = (
        normed_one,
        packed_grad,
        attn_low,
        attn_branch_grad,
        normed_two,
        pre_grad,
        hidden_low,
        branch_grad,
        padded,
        conv_grad,
    )
    return (grad_in, (grad_gain_one, grad_gain_two), products)


def per_device(
    signal,
    frame_segment_index,
    conv_weight,
    conv_bias,
    norm1_gain,
    qkv_weight,
    out_weight,
    norm2_gain,
    up_weight,
    down_weight,
    cotangent,
):
    micro_count, frames, width_all = signal.shape
    factor = 1.0 / math.sqrt(HEAD_DIM)
    first_section = lax.axis_index("section") == 0
    my_start = lax.axis_index("seq") * frames
    gathered = (
        lax.all_gather(norm1_gain.astype(jnp.bfloat16), ("dp", "seq"), axis=1, tiled=True),
        lax.all_gather(qkv_weight.astype(jnp.bfloat16), ("dp", "seq"), axis=1, tiled=True),
        lax.all_gather(out_weight.astype(jnp.bfloat16), ("dp", "seq"), axis=1, tiled=True),
        lax.all_gather(norm2_gain.astype(jnp.bfloat16), ("dp", "seq"), axis=1, tiled=True),
        lax.all_gather(up_weight.astype(jnp.bfloat16), ("dp", "seq"), axis=1, tiled=True),
        lax.all_gather(down_weight.astype(jnp.bfloat16), ("dp", "seq"), axis=1, tiled=True),
    )
    weights = tuple((member[0] for member in gathered))
    kernel, conv_shift = (
        lax.all_gather(
            conv_weight.astype(jnp.bfloat16), ("section", "dp", "seq"), axis=0, tiled=True
        ),
        lax.all_gather(
            conv_bias.astype(jnp.bfloat16), ("section", "dp", "seq"), axis=0, tiled=True
        ),
    )
    received = jnp.zeros((frames, width_all), jnp.bfloat16)
    saved = []
    forward_outs = []
    for step_index in range(micro_count + 1):
        own_index = min(step_index, micro_count - 1)
        prior_index = max(step_index - 1, 0)
        layer_in = jnp.where(first_section, signal[own_index], received)
        segment_row = jnp.where(
            first_section, frame_segment_index[own_index], frame_segment_index[prior_index]
        )
        result, kept = layer_forward(
            layer_in, segment_row, weights, kernel, conv_shift, first_section, my_start, factor
        )
        saved.append(kept)
        forward_outs.append(result)
        if step_index < micro_count:
            received = from_behind(result.astype(jnp.bfloat16), "section", 1)
    received_back = jnp.zeros((frames, width_all), jnp.bfloat16)
    input_grads = []
    gain_totals = None
    product_list = []
    for step_index in range(micro_count + 1):
        kept = saved[micro_count - step_index]
        if step_index < micro_count:
            top_grad = cotangent[micro_count - 1 - step_index].astype(jnp.float32)
        else:
            top_grad = jnp.zeros((frames, width_all), jnp.float32)
        incoming = jnp.where(first_section, received_back.astype(jnp.float32), top_grad)
        grad_in, gain_grads, products = layer_backward(
            kept, incoming, weights, kernel, first_section, my_start, factor
        )
        input_grads.append(grad_in)
        product_list.append(products)
        if gain_totals is None:
            gain_totals = gain_grads
        else:
            gain_totals = (gain_totals[0] + gain_grads[0], gain_totals[1] + gain_grads[1])
        if step_index < micro_count:
            received_back = from_behind(grad_in.astype(jnp.bfloat16), "section", -1)

    def joined(position):
        return jnp.concatenate([member[position] for member in product_list], axis=0)

    grad_qkv = jnp.einsum("ti,tj->ij", joined(0), joined(1), preferred_element_type=jnp.float32)
    grad_out_weight = jnp.einsum(
        "ti,to->io", joined(2), joined(3), preferred_element_type=jnp.float32
    )
    grad_up = jnp.einsum("ti,tf->if", joined(4), joined(5), preferred_element_type=jnp.float32)
    grad_down = jnp.einsum("ti,to->io", joined(6), joined(7), preferred_element_type=jnp.float32)
    padded_all = jnp.stack([member[8] for member in product_list])
    conv_grad_all = jnp.stack([member[9] for member in product_list])
    kernel_grad = conv_kernel_grad(padded_all, conv_grad_all)
    bias_grad = jnp.sum(joined(9).astype(jnp.float32), axis=0)
    ends = jnp.stack(
        [
            jnp.where(
                first_section, input_grads[micro_count - mb_index], forward_outs[mb_index + 1]
            )
            for mb_index in range(micro_count)
        ]
    )[None]
    layer_sums = (
        lax.psum_scatter(gain_totals[0][None], ("dp", "seq"), scatter_dimension=1, tiled=True),
        lax.psum_scatter(grad_qkv[None], ("dp", "seq"), scatter_dimension=1, tiled=True),
        lax.psum_scatter(grad_out_weight[None], ("dp", "seq"), scatter_dimension=1, tiled=True),
        lax.psum_scatter(gain_totals[1][None], ("dp", "seq"), scatter_dimension=1, tiled=True),
        lax.psum_scatter(grad_up[None], ("dp", "seq"), scatter_dimension=1, tiled=True),
        lax.psum_scatter(grad_down[None], ("dp", "seq"), scatter_dimension=1, tiled=True),
    )
    conv_sums = (
        lax.psum_scatter(kernel_grad, ("section", "dp", "seq"), scatter_dimension=0, tiled=True),
        lax.psum_scatter(bias_grad, ("section", "dp", "seq"), scatter_dimension=0, tiled=True),
    )
    return (
        ends,
        conv_sums[0],
        conv_sums[1],
        layer_sums[0],
        layer_sums[1],
        layer_sums[2],
        layer_sums[3],
        layer_sums[4],
        layer_sums[5],
    )


def swap_section(value):
    return lax.ppermute(value, "section", [(0, 1), (1, 0)])


def swap_x(value):
    return lax.ppermute(value, "seq", [(q, q ^ 1) for q in range(4)])


def pair_sum(value):
    low = value.astype(jnp.bfloat16)
    return low.astype(jnp.float32) + swap_x(low).astype(jnp.float32)


def choose(flag, first, second):
    return jnp.where(flag, first, second), jnp.where(flag, second, first)


def y_groups():
    return [[d * 4 + y * 2 + x for d in range(lax.axis_size("dp")) for y in range(2)] for x in range(2)]


def gather_yz(value):
    return lax.all_gather(value, ("dp", "seq"), axis=0, tiled=False, axis_index_groups=y_groups())


def scatter_yz(value):
    return lax.psum_scatter(
        value, ("dp", "seq"), scatter_dimension=0, tiled=False, axis_index_groups=y_groups()
    )


def norm_stats(values):
    average = jnp.mean(values, axis=-1, keepdims=True)
    centred = values - average
    spread = jnp.mean(centred * centred, axis=-1, keepdims=True)
    return centred, lax.rsqrt(spread + EPS)


def norm_back(values, gain, grad):
    centred, inv = norm_stats(values)
    unit = centred * inv
    gain_grad = jnp.sum(grad * unit, axis=0)
    f = grad * gain
    mean_f = jnp.mean(f, axis=-1, keepdims=True)
    mean_fu = jnp.mean(f * unit, axis=-1, keepdims=True)
    return (f - mean_f - unit * mean_fu) * inv, gain_grad


def gelu_slope(values):
    cdf = 0.5 * (1.0 + lax.erf(values * (1.0 / math.sqrt(2.0))))
    pdf = jnp.exp(-0.5 * values * values) * (1.0 / math.sqrt(2.0 * math.pi))
    return cdf + values * pdf


def attention_forward_kernel(factor, q_ref, k_ref, v_ref, qs_ref, ks_ref, o_ref, lse_ref):
    queries = q_ref[...]
    lane = lax.broadcasted_iota(jnp.int32, queries.shape, 1)
    allowed = qs_ref[...] == ks_ref[...]
    keys = k_ref[...]
    values = v_ref[...]
    outs = []
    for head in range(2):
        mine = (lane < HEAD_DIM) if head == 0 else (lane >= HEAD_DIM)
        own = jnp.where(mine, queries, jnp.zeros_like(queries))
        scores = lax.dot_general(
            own, keys, (((1,), (1,)), ((), ())), preferred_element_type=jnp.float32
        ) * factor
        scores = jnp.where(allowed, scores, NEG)
        top = jnp.max(scores, axis=-1, keepdims=True)
        raised = jnp.exp(scores - top)
        total = jnp.sum(raised, axis=-1, keepdims=True)
        chances = (raised * (1.0 / total)).astype(jnp.bfloat16)
        outs.append(jnp.dot(chances, values, preferred_element_type=jnp.float32))
        lse_ref[0, head] = top + jnp.log(total)
    o_ref[...] = jnp.where(lane < HEAD_DIM, outs[0], outs[1]).astype(o_ref.dtype)


def attention_forward(packed, kv_all, query_segs, key_segs, factor):
    frames = packed.shape[0]
    keys = kv_all.shape[0]
    width = packed.shape[1] // 3
    pairs = width // 128
    rows = math.gcd(frames, 256)
    return pl.pallas_call(
        functools.partial(attention_forward_kernel, factor),
        grid=(pairs, frames // rows),
        in_specs=[
            pl.BlockSpec((rows, 128), lambda h, i: (i, h)),
            pl.BlockSpec((keys, 128), lambda h, i: (0, h)),
            pl.BlockSpec((keys, 128), lambda h, i: (0, pairs + h)),
            pl.BlockSpec((rows, 1), lambda h, i: (i, 0)),
            pl.BlockSpec((1, keys), lambda h, i: (0, 0)),
        ],
        out_specs=[
            pl.BlockSpec((rows, 128), lambda h, i: (i, h)),
            pl.BlockSpec((1, 2, rows, 1), lambda h, i: (h, 0, i, 0)),
        ],
        out_shape=[
            jax.ShapeDtypeStruct((frames, width), jnp.bfloat16),
            jax.ShapeDtypeStruct((pairs, 2, frames, 1), jnp.float32),
        ],
        compiler_params=pltpu.CompilerParams(vmem_limit_bytes=40 * 1024 * 1024),
        cost_estimate=pl.CostEstimate(
            flops=4 * frames * keys * width * 2,
            bytes_accessed=2 * (frames * width * 2 + keys * width * 2),
            transcendentals=frames * keys * (width // HEAD_DIM),
        ),
        name="attention_forward",
    )(packed, kv_all, kv_all, query_segs[:, None], key_segs[None, :])


def attention_backward_kernel(
    factor, q_ref, k_ref, v_ref, g_ref, o_ref, lse_ref, qs_ref, ks_ref, dq_ref, dk_ref, dv_ref
):
    step = pl.program_id(1)

    @pl.when(step == 0)
    def _():
        dk_ref[...] = jnp.zeros_like(dk_ref)
        dv_ref[...] = jnp.zeros_like(dv_ref)

    queries = q_ref[...]
    grads = g_ref[...]
    keys = k_ref[...]
    values = v_ref[...]
    lane = lax.broadcasted_iota(jnp.int32, queries.shape, 1)
    key_lane = lax.broadcasted_iota(jnp.int32, keys.shape, 1)
    allowed = qs_ref[...] == ks_ref[...]
    product = grads.astype(jnp.float32) * o_ref[...].astype(jnp.float32)
    dq = None
    for head in range(2):
        mine = (lane < HEAD_DIM) if head == 0 else (lane >= HEAD_DIM)
        key_mine = (key_lane < HEAD_DIM) if head == 0 else (key_lane >= HEAD_DIM)
        own_q = jnp.where(mine, queries, jnp.zeros_like(queries))
        own_g = jnp.where(mine, grads, jnp.zeros_like(grads))
        own_k = jnp.where(key_mine, keys, jnp.zeros_like(keys))
        delta = jnp.sum(jnp.where(mine, product, 0.0), axis=-1, keepdims=True)
        scores = lax.dot_general(
            own_q, keys, (((1,), (1,)), ((), ())), preferred_element_type=jnp.float32
        ) * factor
        chances = jnp.exp(jnp.where(allowed, scores, NEG) - lse_ref[0, head])
        prob_grad = lax.dot_general(
            own_g, values, (((1,), (1,)), ((), ())), preferred_element_type=jnp.float32
        )
        score_grad = (chances * (prob_grad - delta)).astype(jnp.bfloat16)
        part = jnp.dot(score_grad, own_k, preferred_element_type=jnp.float32)
        dq = part if dq is None else dq + part
        dk_ref[...] += lax.dot_general(
            score_grad, own_q, (((0,), (0,)), ((), ())), preferred_element_type=jnp.float32
        ) * factor
        dv_ref[...] += lax.dot_general(
            chances.astype(jnp.bfloat16), own_g, (((0,), (0,)), ((), ())),
            preferred_element_type=jnp.float32,
        )
    dq_ref[...] = (dq * factor).astype(dq_ref.dtype)


def attention_backward(packed, kv_all, grads, attended, lse, query_segs, key_segs, factor):
    frames = packed.shape[0]
    keys = kv_all.shape[0]
    width = packed.shape[1] // 3
    pairs = width // 128
    rows = math.gcd(frames, 256)
    return pl.pallas_call(
        functools.partial(attention_backward_kernel, factor),
        grid=(pairs, frames // rows),
        in_specs=[
            pl.BlockSpec((rows, 128), lambda h, i: (i, h)),
            pl.BlockSpec((keys, 128), lambda h, i: (0, h)),
            pl.BlockSpec((keys, 128), lambda h, i: (0, pairs + h)),
            pl.BlockSpec((rows, 128), lambda h, i: (i, h)),
            pl.BlockSpec((rows, 128), lambda h, i: (i, h)),
            pl.BlockSpec((1, 2, rows, 1), lambda h, i: (h, 0, i, 0)),
            pl.BlockSpec((rows, 1), lambda h, i: (i, 0)),
            pl.BlockSpec((1, keys), lambda h, i: (0, 0)),
        ],
        out_specs=[
            pl.BlockSpec((rows, 128), lambda h, i: (i, h)),
            pl.BlockSpec((keys, 128), lambda h, i: (0, h)),
            pl.BlockSpec((keys, 128), lambda h, i: (0, h)),
        ],
        out_shape=[
            jax.ShapeDtypeStruct((frames, width), jnp.bfloat16),
            jax.ShapeDtypeStruct((keys, width), jnp.float32),
            jax.ShapeDtypeStruct((keys, width), jnp.float32),
        ],
        compiler_params=pltpu.CompilerParams(vmem_limit_bytes=48 * 1024 * 1024),
        cost_estimate=pl.CostEstimate(
            flops=10 * frames * keys * width * 2,
            bytes_accessed=4 * (frames * width * 2 + keys * width * 2),
            transcendentals=frames * keys * (width // HEAD_DIM),
        ),
        name="attention_backward",
    )(packed, kv_all, kv_all, grads, attended, lse, query_segs[:, None], key_segs[None, :])


CONV_STEP = 4


def conv_bands(kernel, per_group):
    groups = kernel.shape[1] // per_group
    steps = TAPS // CONV_STEP + 1
    bands = []
    for group in range(groups):
        own = kernel[:, group * per_group : (group + 1) * per_group]
        shifted = [
            jnp.pad(own, ((shift * per_group, (CONV_STEP - shift) * per_group), (0, 0)))
            for shift in range(CONV_STEP)
        ]
        band = jnp.concatenate(shifted, axis=1)
        bands.append(band.reshape(steps, CONV_STEP * per_group, CONV_STEP * per_group))
    return bands


def group_view(values, per_group):
    rows, frames, width = values.shape
    return [
        values[:, :, g * per_group : (g + 1) * per_group].reshape(
            rows, frames // CONV_STEP, CONV_STEP * per_group
        )
        for g in range(width // per_group)
    ]


def ungroup(parts, per_group):
    rows, blocks, _ = parts[0].shape
    return jnp.concatenate(
        [part.reshape(rows, blocks * CONV_STEP, per_group) for part in parts], axis=2
    )


CONV_DIMS = ("NWC", "WIO", "NWC")


def conv_forward(views, bands):
    half = TAPS // 2 // CONV_STEP
    return [
        lax.conv_general_dilated(
            view, band, (1,), [(half, half)], dimension_numbers=CONV_DIMS,
            preferred_element_type=jnp.float32,
        )
        for view, band in zip(views, bands)
    ]


def conv_back(grad_views, bands):
    half = TAPS // 2 // CONV_STEP
    return [
        lax.conv_general_dilated(
            view, jnp.transpose(band[::-1], (0, 2, 1)), (1,), [(half, half)],
            dimension_numbers=CONV_DIMS, preferred_element_type=jnp.float32,
        )
        for view, band in zip(grad_views, bands)
    ]


def conv_taps_grad(views, grad_views, per_group):
    half = TAPS // 2 // CONV_STEP
    results = []
    for view, grad in zip(views, grad_views):
        band = lax.conv_general_dilated(
            view, grad, (1,), [(half, half)],
            dimension_numbers=("CWN", "IWO", "WNC"),
            preferred_element_type=jnp.float32,
        )
        flat = band.reshape(-1, CONV_STEP, per_group)
        total = None
        for shift in range(CONV_STEP):
            part = flat[shift * per_group : (shift + TAPS) * per_group, shift]
            total = part if total is None else total + part
        results.append(total)
    return jnp.concatenate(results, axis=1)


def to_column(vector, width):
    return jnp.pad(vector[:, None], ((0, 0), (0, width - 1)))


def per_device_pairs(
    signal, frame_segment_index, conv_weight, conv_bias, norm1_gain, qkv_weight, out_weight,
    norm2_gain, up_weight, down_weight, cotangent,
):
    micro_count, frames, width = signal.shape
    bf16, f32 = jnp.bfloat16, jnp.float32
    per_group = width // GROUPS
    dp_count = lax.axis_size("dp")
    factor = 1.0 / math.sqrt(HEAD_DIM)
    sec = lax.axis_index("section")
    dp = lax.axis_index("dp")
    seq = lax.axis_index("seq")
    x, y = seq % 2, seq // 2
    sec0, x0 = sec == 0, x == 0
    row_frames = 4 * frames
    half_frames = 2 * frames
    both = ("section", "seq")

    block_width = width // 8
    rows_here = conv_weight.shape[0]
    conv_low = conv_weight.astype(bf16).reshape(rows_here, 8, block_width)
    bias_low = jnp.pad(conv_bias.astype(bf16), (0, block_width - conv_bias.shape[0]))
    bias_rows = jnp.pad(
        jnp.broadcast_to(bias_low[None, None, :], (1, 8, block_width)), ((0, 15), (0, 0), (0, 0))
    )
    conv_send = jnp.transpose(jnp.concatenate([conv_low, bias_rows], axis=0), (1, 0, 2))
    conv_got = lax.all_to_all(conv_send, both, 0, 0, tiled=True)

    own_half = jnp.where(sec0, signal[:, :, : width // 2], signal[:, :, width // 2 :])
    sig_send = jnp.transpose(own_half.reshape(micro_count, frames, 4, block_width), (2, 0, 1, 3))
    sig_got = lax.all_to_all(sig_send, "seq", 0, 0, tiled=True)
    sig_all = jnp.transpose(sig_got, (1, 0, 2, 3)).reshape(micro_count, row_frames, block_width)

    up_chain = [(i, i + 1) for i in range(dp_count - 1)]
    down_chain = [(i + 1, i) for i in range(dp_count - 1)]
    from_low, from_high = conv_got, conv_got
    pieces = [conv_got]
    lows, highs = [], []
    for _ in range(dp_count - 1):
        from_low = lax.ppermute(from_low, "dp", up_chain)
        from_high = lax.ppermute(from_high, "dp", down_chain)
        lows.append(from_low)
        highs.append(from_high)
    ordered = []
    for source in range(dp_count):
        value = conv_got
        for distance in range(1, dp_count):
            if source - distance >= 0 or source + distance < dp_count:
                if source + distance < dp_count:
                    value = jnp.where(dp == source + distance, lows[distance - 1], value)
                if source - distance >= 0:
                    value = jnp.where(dp == source - distance, highs[distance - 1], value)
        ordered.append(value)
    conv_all = jnp.stack(ordered)
    conv_all = conv_all.reshape(dp_count, 2, 4, rows_here + 16, block_width)
    conv_all = jnp.transpose(conv_all, (1, 0, 2, 3, 4))
    bias_all = conv_all[:, :, :, rows_here, : conv_bias.shape[0]].reshape(width)
    bias_own = lax.dynamic_slice_in_dim(bias_all, (sec * 4 + seq) * block_width, block_width, 0)
    kernel_own = conv_all[:, :, :, :rows_here].reshape(TAPS * per_group, block_width)
    bands = conv_bands(kernel_own, per_group)

    def exchange_columns(weight, gain, unit):
        rows, columns = weight.shape
        view = weight.astype(bf16).reshape(rows, columns // (2 * unit), 2, unit)
        keep, send = choose(x0, view[:, :, 0], view[:, :, 1])
        gain_part = to_column(gain.astype(bf16), 128)
        keep = jnp.concatenate([keep.reshape(rows, columns // 2), gain_part], axis=1)
        send = jnp.concatenate([send.reshape(rows, columns // 2), gain_part], axis=1)
        got = swap_x(send)
        return choose(x0, keep, got)

    qkv_halves = exchange_columns(qkv_weight[0], norm1_gain[0], HEAD_DIM)
    up_halves = exchange_columns(up_weight[0], norm2_gain[0], down_weight.shape[1])
    out_rows = out_weight.shape[1] // 2
    out_low = out_weight[0].astype(bf16)
    down_rows = down_weight.shape[1] // 2
    down_low = down_weight[0].astype(bf16)
    halves = (
        qkv_halves,
        (out_low[:out_rows], out_low[out_rows:]),
        up_halves,
        (down_low[:down_rows], down_low[down_rows:]),
    )
    own_parts = []
    for first, second in halves:
        keep, send = choose(sec0, first, second)
        got = swap_section(send)
        own_parts.append(choose(sec0, keep, got))
    layer_weights = []
    for layer in range(2):
        full = []
        for part in own_parts:
            mine = gather_yz(part[layer])
            other = swap_section(mine)
            first, second = choose(sec0, mine, other)
            joined = jnp.stack([first, second], axis=1)
            full.append(joined.reshape(-1, joined.shape[-1]))
        w_qkv, w_out, w_up, w_down = full
        gain_one = w_qkv[:, -128].astype(f32)[None, :]
        gain_two = w_up[:, -128].astype(f32)[None, :]
        layer_weights.append((gain_one, w_qkv[:, :-128], w_out, gain_two, w_up[:, :-128], w_down))

    picked = jnp.where(sec0, cotangent[0], cotangent[1])
    across = [(s * 4 + 2 * yy + xx, yy * 4 + 2 * s + xx) for s in range(2) for yy in range(2) for xx in range(2)]
    cot_own = lax.ppermute(picked, both, across)
    cot_other = swap_x(cot_own)
    cot_pair = choose(x0, cot_own, cot_other)
    top_grad = jnp.concatenate(cot_pair, axis=0).astype(f32)

    segment_row = jnp.where(y == 0, frame_segment_index[0], frame_segment_index[1])
    seg_pair = choose(sec0, segment_row[:half_frames], segment_row[half_frames:])
    query_segs = seg_pair[0]
    key_segs = jnp.concatenate(seg_pair)

    sig_views = group_view(sig_all, per_group)
    conv_pre = ungroup(conv_forward(sig_views, bands), per_group) + bias_own.astype(f32)
    stream = (sig_all.astype(f32) + smooth(conv_pre)).astype(bf16)
    slope = gelu_slope(conv_pre).astype(bf16)
    stream_send = stream.reshape(2, 2, half_frames, block_width)
    stream_send = jnp.transpose(stream_send, (1, 0, 2, 3))
    stream_send = jnp.repeat(stream_send.reshape(4, half_frames, block_width), 2, axis=0)
    stream_got = lax.all_to_all(stream_send, both, 0, 0, tiled=True)
    layer_in = jnp.transpose(stream_got, (1, 0, 2)).reshape(half_frames, width).astype(f32)

    kept = []
    for layer in range(2):
        gain_one, w_qkv, w_out, gain_two, w_up, w_down = layer_weights[layer]
        centred, inv = norm_stats(layer_in)
        normed_one = (centred * inv * gain_one).astype(bf16)
        packed = jnp.dot(normed_one, w_qkv, preferred_element_type=f32).astype(bf16)
        kv_own = packed[:, width // 2 :]
        kv_all = jnp.concatenate([kv_own, swap_section(kv_own)], axis=0)
        attended, lse = attention_forward(packed, kv_all, query_segs, key_segs, factor)
        resid_two = layer_in + pair_sum(jnp.dot(attended, w_out, preferred_element_type=f32))
        centred, inv = norm_stats(resid_two)
        normed_two = (centred * inv * gain_two).astype(bf16)
        hidden_pre = jnp.dot(normed_two, w_up, preferred_element_type=f32)
        hidden = smooth(hidden_pre).astype(bf16)
        hidden_slope = gelu_slope(hidden_pre).astype(bf16)
        result = resid_two + pair_sum(jnp.dot(hidden, w_down, preferred_element_type=f32))
        kept.append(
            (layer_in, normed_one, packed, kv_all, attended, lse, resid_two, normed_two, hidden, hidden_slope)
        )
        layer_in = result.astype(bf16).astype(f32)
    output = result

    grad_out = top_grad
    reduced = [None, None]
    for layer in (1, 0):
        gain_one, w_qkv, w_out, gain_two, w_up, w_down = layer_weights[layer]
        (layer_in, normed_one, packed, kv_all, attended, lse, resid_two, normed_two, hidden, hidden_slope) = kept[layer]
        branch = grad_out.astype(bf16)
        hidden_grad = lax.dot_general(
            branch, w_down, (((1,), (1,)), ((), ())), preferred_element_type=f32
        )
        pre_grad = (hidden_grad * hidden_slope.astype(f32)).astype(bf16)
        part = lax.dot_general(
            pre_grad, w_up, (((1,), (1,)), ((), ())), preferred_element_type=f32
        )
        normed_grad = pair_sum(part)
        grad_down = lax.dot_general(
            hidden, branch, (((0,), (0,)), ((), ())), preferred_element_type=f32
        ).astype(bf16)
        grad_up = lax.dot_general(
            normed_two, pre_grad, (((0,), (0,)), ((), ())), preferred_element_type=f32
        ).astype(bf16)
        resid_grad, gain_two_grad = norm_back(resid_two, gain_two, normed_grad)
        resid_grad = resid_grad + grad_out
        attn_branch = resid_grad.astype(bf16)
        attended_grad = lax.dot_general(
            attn_branch, w_out, (((1,), (1,)), ((), ())), preferred_element_type=f32
        ).astype(bf16)
        dq, dk, dv = attention_backward(
            packed, kv_all, attended_grad, attended, lse, query_segs, key_segs, factor
        )
        dkv = jnp.concatenate([dk, dv], axis=1)
        other_dkv = swap_section(dkv[half_frames:].astype(bf16))
        dkv_own = (dkv[:half_frames] + other_dkv.astype(f32)).astype(bf16)
        packed_grad = jnp.concatenate([dq, dkv_own], axis=1)
        part = lax.dot_general(
            packed_grad, w_qkv, (((1,), (1,)), ((), ())), preferred_element_type=f32
        )
        normed_grad = pair_sum(part)
        grad_out_weight = lax.dot_general(
            attended, attn_branch, (((0,), (0,)), ((), ())), preferred_element_type=f32
        ).astype(bf16)
        grad_qkv = lax.dot_general(
            normed_one, packed_grad, (((0,), (0,)), ((), ())), preferred_element_type=f32
        ).astype(bf16)
        in_grad, gain_one_grad = norm_back(layer_in, gain_one, normed_grad)
        grad_in = resid_grad + in_grad
        grad_up = jnp.concatenate([grad_up, to_column(gain_two_grad.astype(bf16), 128)], axis=1)
        grad_qkv = jnp.concatenate([grad_qkv, to_column(gain_one_grad.astype(bf16), 128)], axis=1)
        sums = []
        for member in (grad_qkv, grad_out_weight, grad_up, grad_down):
            blocks = member.reshape(2 * dp_count, 2, -1, member.shape[-1])
            keep, send = choose(sec0, blocks[:, 0], blocks[:, 1])
            total = (keep.astype(f32) + swap_section(send).astype(f32)).astype(bf16)
            sums.append(scatter_yz(total))
        reduced[layer] = sums
        grad_out = grad_in.astype(bf16).astype(f32)
    grad_in_low = grad_in.astype(bf16)

    lig_send = jnp.transpose(grad_in_low.reshape(half_frames, 8, block_width), (1, 0, 2))
    lig_got = lax.all_to_all(lig_send, both, 0, 0, tiled=True).reshape(2, 2, 2, half_frames, block_width)
    lig = jnp.transpose(lig_got[:, :, 0], (1, 0, 2, 3)).reshape(micro_count, row_frames, block_width)
    conv_grad = (lig.astype(f32) * slope.astype(f32)).astype(bf16)
    grad_views = group_view(conv_grad, per_group)
    back = ungroup(conv_back(grad_views, bands), per_group)
    grad_signal = (lig.astype(f32) + back).astype(bf16)
    gs_send = jnp.transpose(
        grad_signal.reshape(micro_count, 4, frames, block_width), (1, 0, 2, 3)
    )
    gs_send = jnp.concatenate([gs_send, gs_send], axis=0)
    gs_got = lax.all_to_all(gs_send, both, 0, 0, tiled=True)
    gs_rows = jnp.transpose(gs_got, (1, 2, 0, 3)).reshape(micro_count, frames, width).astype(f32)

    taps_grad = conv_taps_grad(sig_views, grad_views, per_group)
    bias_grad = jnp.sum(conv_grad.astype(f32), axis=(0, 1))
    taps_view = jnp.transpose(
        taps_grad.reshape(2, dp_count, 4, rows_here, block_width), (1, 0, 2, 3, 4)
    ).astype(bf16)
    bias_view = jnp.pad(
        jnp.broadcast_to(bias_grad.astype(bf16), (dp_count, 2, 4, 1, block_width)),
        ((0, 0), (0, 0), (0, 0), (0, 15), (0, 0)),
    )
    taps_send = jnp.concatenate([taps_view, bias_view], axis=3)
    taps_sum = lax.psum_scatter(taps_send, "dp", scatter_dimension=0, tiled=False)
    taps_got = lax.all_to_all(
        taps_sum.reshape(8, rows_here + 16, block_width), both, 0, 0, tiled=True
    )
    conv_weight_grad = jnp.transpose(taps_got[:, :rows_here], (1, 0, 2)).reshape(rows_here, width).astype(f32)
    bias_count = conv_bias.shape[0]
    conv_bias_grad = lax.dynamic_slice_in_dim(
        taps_got[:, rows_here].reshape(width),
        ((sec * dp_count + dp) * 4 + seq) * bias_count,
        bias_count,
        0,
    ).astype(f32)

    own_block = jnp.where(x0, output[:frames], output[frames:])
    row_block = lax.ppermute(own_block, both, across)
    other_row = swap_section(row_block)
    output_rows = jnp.stack(choose(sec0, row_block, other_row))
    ends = jnp.where(sec0, gs_rows, output_rows)[None]

    own_layer = []
    for first, second in zip(reduced[0], reduced[1]):
        keep, send = choose(sec0, first, second)
        got = swap_section(send)
        own_layer.append(choose(sec0, keep, got))

    def finish_columns(pair, unit):
        keep, send = choose(x0, pair[0], pair[1])
        rows = keep.shape[0]
        columns = keep.shape[1] - 128
        gain_grad = keep[:, columns].astype(f32)
        got = swap_x(send)
        shape = (rows, columns // unit, unit)
        parity = choose(x0, keep[:, :columns].reshape(shape), got[:, :columns].reshape(shape))
        joined = jnp.stack(parity, axis=2).reshape(rows, 2 * columns)
        return joined.astype(f32)[None], gain_grad[None]

    qkv_grad, norm1_grad = finish_columns(own_layer[0], HEAD_DIM)
    up_grad, norm2_grad = finish_columns(own_layer[2], down_weight.shape[1])
    out_grad = jnp.concatenate(own_layer[1], axis=0).astype(f32)[None]
    down_grad = jnp.concatenate(own_layer[3], axis=0).astype(f32)[None]
    return (ends, conv_weight_grad, conv_bias_grad, norm1_grad, qkv_grad, out_grad, norm2_grad, up_grad, down_grad)


def solution(mesh):
    placed = (
        P("dp", "seq", None),
        P("dp", None),
        P(("section", "dp", "seq"), None),
        P(("section", "dp", "seq")),
        P("section", ("dp", "seq")),
        P("section", ("dp", "seq"), None),
        P("section", ("dp", "seq"), None),
        P("section", ("dp", "seq")),
        P("section", ("dp", "seq"), None),
        P("section", ("dp", "seq"), None),
        P("dp", "seq", None),
    )

    def step(*arrays):
        pairs = mesh.shape["seq"] == 4 and mesh.shape["section"] == 2 and arrays[0].shape[0] == 2
        return (per_device_pairs if pairs else per_device)(*arrays)

    return jax.shard_map(
        step,
        mesh=mesh,
        in_specs=placed,
        out_specs=(
            P("section", "dp", "seq", None),
            P(("section", "dp", "seq"), None),
            P(("section", "dp", "seq")),
            P("section", ("dp", "seq")),
            P("section", ("dp", "seq"), None),
            P("section", ("dp", "seq"), None),
            P("section", ("dp", "seq")),
            P("section", ("dp", "seq"), None),
            P("section", ("dp", "seq"), None),
        ),
        check_vma=False,
    )
```

```python
import functools
import math

import jax
import jax.numpy as jnp
from jax import lax
from jax.experimental import pallas as pl
from jax.experimental.pallas import tpu as pltpu
from jax.sharding import PartitionSpec as P

HEAD_DIM = 64
GROUPS = 16
TAPS = 128


EPS = 1e-05
NEG = -1e30


def padded_2(block, sides, width):
    for axis, dim in sides:
        count = lax.axis_size(axis)
        forward = [(i, i + 1) for i in range(count - 1)]
        backward = [(target, source) for source, target in forward]
        low = lax.ppermute(
            lax.slice_in_dim(block, block.shape[dim] - width, None, axis=dim), axis, forward
        )
        high = lax.ppermute(lax.slice_in_dim(block, 0, width, axis=dim), axis, backward)
        block = jnp.concatenate([low, block, high], axis=dim)
    return block


def from_behind(value, axis, steps):
    count = lax.axis_size(axis)
    first, last = (max(0, -steps), min(count, count - steps))
    return lax.ppermute(value, axis, [(source, source + steps) for source in range(first, last)])


def normalize(values, gain):
    average = jnp.mean(values, axis=-1, keepdims=True)
    centred = values - average
    spread = jnp.mean(centred * centred, axis=-1, keepdims=True)
    return centred * lax.rsqrt(spread + EPS) * gain


def smooth(values):
    return jax.nn.gelu(values, approximate=False)


def conv_taps(padded, kernel, frames):
    width_all = padded.shape[1]
    per_group = width_all // GROUPS
    tap_step = math.gcd(TAPS, 16)
    weight_view = kernel.reshape(TAPS, per_group, GROUPS, per_group)
    running = jnp.zeros((frames, GROUPS, per_group), jnp.float32)
    for first_tap in range(0, TAPS, tap_step):
        windows = jnp.stack(
            [padded[first_tap + offset : first_tap + offset + frames] for offset in range(tap_step)]
        )
        windows = windows.reshape(tap_step, frames, GROUPS, per_group)
        running = running + jnp.einsum(
            "jtgc,jcgo->tgo",
            windows,
            weight_view[first_tap : first_tap + tap_step],
            preferred_element_type=jnp.float32,
        )
    return running.reshape(frames, width_all)


def conv_input_grad(grad_pad, kernel, frames):
    width_all = grad_pad.shape[1]
    per_group = width_all // GROUPS
    tap_step = math.gcd(TAPS, 16)
    weight_view = kernel.reshape(TAPS, per_group, GROUPS, per_group)
    running = jnp.zeros((frames, GROUPS, per_group), jnp.float32)
    for first_tap in range(0, TAPS, tap_step):
        back_windows = jnp.stack(
            [
                grad_pad[TAPS - first_tap - offset : TAPS - first_tap - offset + frames]
                for offset in range(tap_step)
            ]
        )
        back_windows = back_windows.reshape(tap_step, frames, GROUPS, per_group)
        running = running + jnp.einsum(
            "jtgo,jcgo->tgc",
            back_windows,
            weight_view[first_tap : first_tap + tap_step],
            preferred_element_type=jnp.float32,
        )
    return running.reshape(frames, width_all)


def conv_kernel_grad(padded_all, grad_all):
    step_count, frames, width_all = grad_all.shape
    per_group = width_all // GROUPS
    tap_step = math.gcd(TAPS, 16)
    grad_view = grad_all.reshape(step_count * frames, GROUPS, per_group)
    kernel_parts = []
    for first_tap in range(0, TAPS, tap_step):
        windows = jnp.stack(
            [
                padded_all[:, first_tap + offset : first_tap + offset + frames]
                for offset in range(tap_step)
            ]
        )
        windows = windows.reshape(tap_step, step_count * frames, GROUPS, per_group)
        kernel_parts.append(
            jnp.einsum("jtgc,tgo->jcgo", windows, grad_view, preferred_element_type=jnp.float32)
        )
    return jnp.concatenate(kernel_parts, axis=0).reshape(TAPS * per_group, width_all)


def score_block(query_heads, key_block, query_segs, key_segs, factor):
    scores = (
        jnp.einsum("qhd,khd->hqk", query_heads, key_block, preferred_element_type=jnp.float32)
        * factor
    )
    allowed = (query_segs[:, None] == key_segs[None, :])[None]
    return (scores, allowed)


def front(layer_in, weights, kernel, conv_shift, first_section):
    frames, width_all = layer_in.shape
    padded = padded_2(layer_in, (("seq", 0),), TAPS // 2)
    conv_pre = lax.cond(
        first_section,
        lambda: conv_taps(padded, kernel, frames) + conv_shift.astype(jnp.float32),
        lambda: jnp.zeros((frames, width_all), jnp.float32),
    )
    conv_val, conv_pull = jax.vjp(smooth, conv_pre)
    resid_one = layer_in.astype(jnp.float32) + conv_val
    normed_val, norm_pull = jax.vjp(normalize, resid_one, weights[0].astype(jnp.float32))
    normed_one = normed_val.astype(jnp.bfloat16)
    packed = jnp.dot(normed_one, weights[1], preferred_element_type=jnp.float32).astype(
        jnp.bfloat16
    )
    return (padded, conv_pull, resid_one, norm_pull, normed_one, packed)


def tail(resid_one, attn_low, weights):
    resid_two = resid_one + jnp.dot(attn_low, weights[2], preferred_element_type=jnp.float32)
    normed_val, norm_pull = jax.vjp(normalize, resid_two, weights[3].astype(jnp.float32))
    normed_two = normed_val.astype(jnp.bfloat16)
    hidden_pre = jnp.dot(normed_two, weights[4], preferred_element_type=jnp.float32)
    hidden_val, gelu_pull = jax.vjp(smooth, hidden_pre)
    hidden_low = hidden_val.astype(jnp.bfloat16)
    result = resid_two + jnp.dot(hidden_low, weights[5], preferred_element_type=jnp.float32)
    return (result, norm_pull, normed_two, gelu_pull, hidden_low)


def key_loop(keys_all, values_all, segment_row, head_count, visit, initial):
    total_rows = keys_all.shape[0]
    block_rows = math.gcd(total_rows, 512)

    def one_block(block_index, running):
        offset = block_index * block_rows
        key_block = lax.dynamic_slice_in_dim(keys_all, offset, block_rows, 0).reshape(
            block_rows, head_count, HEAD_DIM
        )
        value_block = lax.dynamic_slice_in_dim(values_all, offset, block_rows, 0).reshape(
            block_rows, head_count, HEAD_DIM
        )
        key_segs = lax.dynamic_slice_in_dim(segment_row, offset, block_rows, 0)
        return visit(running, key_block, value_block, key_segs)

    return lax.fori_loop(0, total_rows // block_rows, one_block, initial)


def layer_forward(
    layer_in, segment_row, weights, kernel, conv_shift, first_section, my_start, factor
):
    frames, width_all = layer_in.shape
    head_count = width_all // HEAD_DIM
    padded, conv_pull, resid_one, norm_pull, normed_one, packed = front(
        layer_in, weights, kernel, conv_shift, first_section
    )
    query_heads = packed[:, :width_all].reshape(frames, head_count, HEAD_DIM)
    query_segs = lax.dynamic_slice_in_dim(segment_row, my_start, frames, 0)
    initial = (
        jnp.full((head_count, frames), NEG, jnp.float32),
        jnp.zeros((head_count, frames), jnp.float32),
        jnp.zeros((head_count, frames, HEAD_DIM), jnp.float32),
    )
    key_piece = lax.all_gather(packed[:, width_all : 2 * width_all], "seq", axis=0, tiled=True)
    value_piece = lax.all_gather(packed[:, 2 * width_all :], "seq", axis=0, tiled=True)
    piece_rows = key_piece.shape[0]
    block_rows = math.gcd(piece_rows, 512)

    def one_block(block_index, running):
        run_max, run_sum, run_acc = running
        offset = block_index * block_rows
        key_block = lax.dynamic_slice_in_dim(key_piece, offset, block_rows, 0).reshape(
            block_rows, head_count, HEAD_DIM
        )
        value_block = lax.dynamic_slice_in_dim(value_piece, offset, block_rows, 0).reshape(
            block_rows, head_count, HEAD_DIM
        )
        key_segs = lax.dynamic_slice_in_dim(segment_row, offset, block_rows, 0)
        scores, allowed = score_block(query_heads, key_block, query_segs, key_segs, factor)
        masked = jnp.where(allowed, scores, NEG)
        new_max = jnp.maximum(run_max, jnp.max(masked, axis=-1))
        weights_now = jnp.where(allowed, jnp.exp(masked - new_max[..., None]), 0.0)
        rescale = jnp.exp(run_max - new_max)
        run_sum = run_sum * rescale + jnp.sum(weights_now, axis=-1)
        run_acc = run_acc * rescale[..., None] + jnp.einsum(
            "hqk,khd->hqd",
            weights_now.astype(jnp.bfloat16),
            value_block,
            preferred_element_type=jnp.float32,
        )
        return (new_max, run_sum, run_acc)

    run_max, run_sum, run_acc = lax.fori_loop(0, piece_rows // block_rows, one_block, initial)
    log_total = run_max + jnp.log(run_sum)
    mixture = run_acc / run_sum[..., None]
    attn_low = jnp.transpose(mixture, (1, 0, 2)).reshape(frames, width_all).astype(jnp.bfloat16)
    result, norm_two_pull, normed_two, gelu_pull, hidden_low = tail(resid_one, attn_low, weights)
    kept = (
        padded,
        conv_pull,
        norm_pull,
        normed_one,
        packed,
        log_total,
        mixture,
        attn_low,
        norm_two_pull,
        normed_two,
        gelu_pull,
        hidden_low,
        segment_row,
    )
    return (result, kept)


def layer_backward(kept, grad_out, weights, kernel, first_section, my_start, factor):
    (
        padded,
        conv_pull,
        norm_one_pull,
        normed_one,
        packed,
        log_total,
        mixture,
        attn_low,
        norm_two_pull,
        normed_two,
        gelu_pull,
        hidden_low,
        segment_row,
    ) = kept
    frames, width_all = normed_one.shape
    head_count = width_all // HEAD_DIM
    query_heads = packed[:, :width_all].reshape(frames, head_count, HEAD_DIM)
    key_local = packed[:, width_all : 2 * width_all]
    value_local = packed[:, 2 * width_all :]
    query_segs = lax.dynamic_slice_in_dim(segment_row, my_start, frames, 0)
    keys_all, values_all = (
        lax.all_gather(key_local, "seq", axis=0, tiled=True),
        lax.all_gather(value_local, "seq", axis=0, tiled=True),
    )

    def chances_for(key_block, key_segs):
        scores, allowed = score_block(query_heads, key_block, query_segs, key_segs, factor)
        return jnp.where(
            allowed, jnp.exp(jnp.where(allowed, scores, NEG) - log_total[..., None]), 0.0
        )

    branch_grad = grad_out.astype(jnp.bfloat16)
    hidden_grad = jnp.einsum(
        "to,io->ti", branch_grad, weights[5], preferred_element_type=jnp.float32
    )
    pre_grad = gelu_pull(hidden_grad)[0].astype(jnp.bfloat16)
    normed_two_grad = jnp.einsum(
        "tf,if->ti", pre_grad, weights[4], preferred_element_type=jnp.float32
    )
    resid_two_grad, grad_gain_two = norm_two_pull(normed_two_grad)
    resid_two_grad = resid_two_grad + grad_out
    attn_branch_grad = resid_two_grad.astype(jnp.bfloat16)
    attended_grad = jnp.einsum(
        "to,io->ti", attn_branch_grad, weights[2], preferred_element_type=jnp.float32
    ).astype(jnp.bfloat16)
    dout_heads = attended_grad.reshape(frames, head_count, HEAD_DIM)
    delta_rows = jnp.einsum("qhd,hqd->hq", dout_heads.astype(jnp.float32), mixture)

    def visit_query(running, key_block, value_block, key_segs):
        chances = chances_for(key_block, key_segs)
        prob_grad = jnp.einsum(
            "qhd,khd->hqk", dout_heads, value_block, preferred_element_type=jnp.float32
        )
        score_grad = (chances * (prob_grad - delta_rows[..., None])).astype(jnp.bfloat16)
        return running + jnp.einsum(
            "hqk,khd->qhd", score_grad, key_block, preferred_element_type=jnp.float32
        )

    grad_query = (
        key_loop(
            keys_all,
            values_all,
            segment_row,
            head_count,
            visit_query,
            jnp.zeros((frames, head_count, HEAD_DIM), jnp.float32),
        )
        * factor
    )
    row_stats = (
        lax.all_gather(log_total, "seq", axis=1, tiled=True),
        lax.all_gather(delta_rows, "seq", axis=1, tiled=True),
    )
    key_heads = key_local.reshape(frames, head_count, HEAD_DIM)
    value_heads = value_local.reshape(frames, head_count, HEAD_DIM)
    start_acc = (
        jnp.zeros((frames, head_count, HEAD_DIM), jnp.float32),
        jnp.zeros((frames, head_count, HEAD_DIM), jnp.float32),
    )
    query_piece = lax.all_gather(packed[:, :width_all], "seq", axis=0, tiled=True)
    dout_piece = lax.all_gather(attended_grad, "seq", axis=0, tiled=True)
    piece_rows = query_piece.shape[0]
    block_rows = math.gcd(piece_rows, 512)

    def one_block(block_index, running):
        key_acc, value_acc = running
        offset = block_index * block_rows
        query_block = lax.dynamic_slice_in_dim(query_piece, offset, block_rows, 0).reshape(
            block_rows, head_count, HEAD_DIM
        )
        dout_block = lax.dynamic_slice_in_dim(dout_piece, offset, block_rows, 0).reshape(
            block_rows, head_count, HEAD_DIM
        )
        seg_block = lax.dynamic_slice_in_dim(segment_row, offset, block_rows, 0)
        total_block = lax.dynamic_slice_in_dim(row_stats[0], offset, block_rows, 1)
        delta_block = lax.dynamic_slice_in_dim(row_stats[1], offset, block_rows, 1)
        scores, allowed = score_block(query_block, key_heads, seg_block, query_segs, factor)
        chances = jnp.where(
            allowed, jnp.exp(jnp.where(allowed, scores, NEG) - total_block[..., None]), 0.0
        )
        prob_grad = jnp.einsum(
            "qhd,khd->hqk", dout_block, value_heads, preferred_element_type=jnp.float32
        )
        score_grad = (chances * (prob_grad - delta_block[..., None])).astype(jnp.bfloat16)
        key_acc = (
            key_acc
            + jnp.einsum(
                "hqk,qhd->khd", score_grad, query_block, preferred_element_type=jnp.float32
            )
            * factor
        )
        value_acc = value_acc + jnp.einsum(
            "hqk,qhd->khd",
            chances.astype(jnp.bfloat16),
            dout_block,
            preferred_element_type=jnp.float32,
        )
        return (key_acc, value_acc)

    key_acc, value_acc = lax.fori_loop(0, piece_rows // block_rows, one_block, start_acc)
    grad_key = key_acc.reshape(frames, width_all)
    grad_value = value_acc.reshape(frames, width_all)
    packed_grad = jnp.concatenate(
        [grad_query.reshape(frames, width_all), grad_key, grad_value], axis=1
    ).astype(jnp.bfloat16)
    normed_one_grad = jnp.einsum(
        "tj,ij->ti", packed_grad, weights[1], preferred_element_type=jnp.float32
    )
    resid_one_grad, grad_gain_one = norm_one_pull(normed_one_grad)
    resid_one_grad = resid_one_grad + resid_two_grad
    conv_grad = jnp.where(first_section, conv_pull(resid_one_grad)[0], 0.0).astype(jnp.bfloat16)
    grad_pad = padded_2(conv_grad, (("seq", 0),), TAPS // 2)
    back_sum = lax.cond(
        first_section,
        lambda: conv_input_grad(grad_pad, kernel, frames),
        lambda: jnp.zeros((frames, width_all), jnp.float32),
    )
    grad_in = resid_one_grad + back_sum
    products = (
        normed_one,
        packed_grad,
        attn_low,
        attn_branch_grad,
        normed_two,
        pre_grad,
        hidden_low,
        branch_grad,
        padded,
        conv_grad,
    )
    return (grad_in, (grad_gain_one, grad_gain_two), products)


def per_device(
    signal,
    frame_segment_index,
    conv_weight,
    conv_bias,
    norm1_gain,
    qkv_weight,
    out_weight,
    norm2_gain,
    up_weight,
    down_weight,
    cotangent,
):
    micro_count, frames, width_all = signal.shape
    factor = 1.0 / math.sqrt(HEAD_DIM)
    first_section = lax.axis_index("section") == 0
    my_start = lax.axis_index("seq") * frames
    gathered = (
        lax.all_gather(norm1_gain.astype(jnp.bfloat16), ("dp", "seq"), axis=1, tiled=True),
        lax.all_gather(qkv_weight.astype(jnp.bfloat16), ("dp", "seq"), axis=1, tiled=True),
        lax.all_gather(out_weight.astype(jnp.bfloat16), ("dp", "seq"), axis=1, tiled=True),
        lax.all_gather(norm2_gain.astype(jnp.bfloat16), ("dp", "seq"), axis=1, tiled=True),
        lax.all_gather(up_weight.astype(jnp.bfloat16), ("dp", "seq"), axis=1, tiled=True),
        lax.all_gather(down_weight.astype(jnp.bfloat16), ("dp", "seq"), axis=1, tiled=True),
    )
    weights = tuple((member[0] for member in gathered))
    kernel, conv_shift = (
        lax.all_gather(
            conv_weight.astype(jnp.bfloat16), ("section", "dp", "seq"), axis=0, tiled=True
        ),
        lax.all_gather(
            conv_bias.astype(jnp.bfloat16), ("section", "dp", "seq"), axis=0, tiled=True
        ),
    )
    received = jnp.zeros((frames, width_all), jnp.bfloat16)
    saved = []
    forward_outs = []
    for step_index in range(micro_count + 1):
        own_index = min(step_index, micro_count - 1)
        prior_index = max(step_index - 1, 0)
        layer_in = jnp.where(first_section, signal[own_index], received)
        segment_row = jnp.where(
            first_section, frame_segment_index[own_index], frame_segment_index[prior_index]
        )
        result, kept = layer_forward(
            layer_in, segment_row, weights, kernel, conv_shift, first_section, my_start, factor
        )
        saved.append(kept)
        forward_outs.append(result)
        if step_index < micro_count:
            received = from_behind(result.astype(jnp.bfloat16), "section", 1)
    received_back = jnp.zeros((frames, width_all), jnp.bfloat16)
    input_grads = []
    gain_totals = None
    product_list = []
    for step_index in range(micro_count + 1):
        kept = saved[micro_count - step_index]
        if step_index < micro_count:
            top_grad = cotangent[micro_count - 1 - step_index].astype(jnp.float32)
        else:
            top_grad = jnp.zeros((frames, width_all), jnp.float32)
        incoming = jnp.where(first_section, received_back.astype(jnp.float32), top_grad)
        grad_in, gain_grads, products = layer_backward(
            kept, incoming, weights, kernel, first_section, my_start, factor
        )
        input_grads.append(grad_in)
        product_list.append(products)
        if gain_totals is None:
            gain_totals = gain_grads
        else:
            gain_totals = (gain_totals[0] + gain_grads[0], gain_totals[1] + gain_grads[1])
        if step_index < micro_count:
            received_back = from_behind(grad_in.astype(jnp.bfloat16), "section", -1)

    def joined(position):
        return jnp.concatenate([member[position] for member in product_list], axis=0)

    grad_qkv = jnp.einsum("ti,tj->ij", joined(0), joined(1), preferred_element_type=jnp.float32)
    grad_out_weight = jnp.einsum(
        "ti,to->io", joined(2), joined(3), preferred_element_type=jnp.float32
    )
    grad_up = jnp.einsum("ti,tf->if", joined(4), joined(5), preferred_element_type=jnp.float32)
    grad_down = jnp.einsum("ti,to->io", joined(6), joined(7), preferred_element_type=jnp.float32)
    padded_all = jnp.stack([member[8] for member in product_list])
    conv_grad_all = jnp.stack([member[9] for member in product_list])
    kernel_grad = conv_kernel_grad(padded_all, conv_grad_all)
    bias_grad = jnp.sum(joined(9).astype(jnp.float32), axis=0)
    ends = jnp.stack(
        [
            jnp.where(
                first_section, input_grads[micro_count - mb_index], forward_outs[mb_index + 1]
            )
            for mb_index in range(micro_count)
        ]
    )[None]
    layer_sums = (
        lax.psum_scatter(gain_totals[0][None], ("dp", "seq"), scatter_dimension=1, tiled=True),
        lax.psum_scatter(grad_qkv[None], ("dp", "seq"), scatter_dimension=1, tiled=True),
        lax.psum_scatter(grad_out_weight[None], ("dp", "seq"), scatter_dimension=1, tiled=True),
        lax.psum_scatter(gain_totals[1][None], ("dp", "seq"), scatter_dimension=1, tiled=True),
        lax.psum_scatter(grad_up[None], ("dp", "seq"), scatter_dimension=1, tiled=True),
        lax.psum_scatter(grad_down[None], ("dp", "seq"), scatter_dimension=1, tiled=True),
    )
    conv_sums = (
        lax.psum_scatter(kernel_grad, ("section", "dp", "seq"), scatter_dimension=0, tiled=True),
        lax.psum_scatter(bias_grad, ("section", "dp", "seq"), scatter_dimension=0, tiled=True),
    )
    return (
        ends,
        conv_sums[0],
        conv_sums[1],
        layer_sums[0],
        layer_sums[1],
        layer_sums[2],
        layer_sums[3],
        layer_sums[4],
        layer_sums[5],
    )


def swap_section(value):
    return lax.ppermute(value, "section", [(0, 1), (1, 0)])


def swap_x(value):
    return lax.ppermute(value, "seq", [(q, q ^ 1) for q in range(4)])


def pair_sum(value):
    low = value.astype(jnp.bfloat16)
    return low.astype(jnp.float32) + swap_x(low).astype(jnp.float32)


def choose(flag, first, second):
    return jnp.where(flag, first, second), jnp.where(flag, second, first)


def chain_steps(value):
    count = lax.axis_size("dp")
    upward = [(i, i + 1) for i in range(count - 1)]
    downward = [(i + 1, i) for i in range(count - 1)]
    low, high = value, value
    lows, highs = [], []
    for _ in range(count - 1):
        low = lax.ppermute(low, "dp", upward)
        high = lax.ppermute(high, "dp", downward)
        lows.append(low)
        highs.append(high)
    return lows, highs


def place_dp(value, dp):
    count = lax.axis_size("dp")
    lows, highs = chain_steps(value)
    whole = jnp.zeros((count, *value.shape), value.dtype)
    whole = lax.dynamic_update_index_in_dim(whole, value, dp, 0)
    for turn in range(1, count):
        piece = jnp.where(dp + turn < count, highs[turn - 1], lows[count - turn - 1])
        whole = lax.dynamic_update_index_in_dim(whole, piece, (dp + turn) % count, 0)
    return whole


def sum_dp(blocks, dp):
    count = lax.axis_size("dp")
    f32, bf16 = jnp.float32, jnp.bfloat16

    def block(index):
        return lax.dynamic_index_in_dim(blocks, jnp.clip(index, 0, count - 1), 0, keepdims=False)

    total = block(dp).astype(f32)
    for sign in (1, -1):
        pairs = [(i, i + sign) for i in range(count) if 0 <= i + sign < count]
        running = None
        for distance in range(count - 1, 0, -1):
            own = block(dp + sign * distance)
            if running is not None:
                own = (own.astype(f32) + running.astype(f32)).astype(bf16)
            live = [(a, b) for a, b in pairs if 0 <= a + sign * distance < count]
            running = lax.ppermute(own, "dp", live)
        total = total + running.astype(f32)
    return total.astype(bf16)


def line_groups():
    count = lax.axis_size("dp")
    return [
        [(s * count + d) * 4 + 2 * y + x for d in range(count) for y in range(2) for s in range(2)]
        for x in range(2)
    ]


def gather_rows(piece):
    return lax.all_gather(
        piece, ("section", "dp", "seq"), axis=0, tiled=True, axis_index_groups=line_groups()
    )


def scatter_rows(partial):
    return lax.psum_scatter(
        partial, ("section", "dp", "seq"), scatter_dimension=0, tiled=True,
        axis_index_groups=line_groups(),
    )


def norm_stats(values):
    average = jnp.mean(values, axis=-1, keepdims=True)
    centred = values - average
    spread = jnp.mean(centred * centred, axis=-1, keepdims=True)
    return centred, lax.rsqrt(spread + EPS)


def norm_back(values, gain, grad):
    centred, inv = norm_stats(values)
    unit = centred * inv
    gain_grad = jnp.sum(grad * unit, axis=0)
    f = grad * gain
    mean_f = jnp.mean(f, axis=-1, keepdims=True)
    mean_fu = jnp.mean(f * unit, axis=-1, keepdims=True)
    return (f - mean_f - unit * mean_fu) * inv, gain_grad


def gelu_slope(values):
    cdf = 0.5 * (1.0 + lax.erf(values * (1.0 / math.sqrt(2.0))))
    pdf = jnp.exp(-0.5 * values * values) * (1.0 / math.sqrt(2.0 * math.pi))
    return cdf + values * pdf


def attention_forward_kernel(factor, q_ref, k_ref, v_ref, qs_ref, ks_ref, o_ref, lse_ref):
    queries = q_ref[...]
    lane = lax.broadcasted_iota(jnp.int32, queries.shape, 1)
    allowed = qs_ref[...] == ks_ref[...]
    keys = k_ref[...]
    values = v_ref[...]
    outs = []
    for head in range(2):
        mine = (lane < HEAD_DIM) if head == 0 else (lane >= HEAD_DIM)
        own = jnp.where(mine, queries, jnp.zeros_like(queries))
        scores = lax.dot_general(
            own, keys, (((1,), (1,)), ((), ())), preferred_element_type=jnp.float32
        ) * factor
        scores = jnp.where(allowed, scores, NEG)
        top = jnp.max(scores, axis=-1, keepdims=True)
        raised = jnp.exp(scores - top)
        total = jnp.sum(raised, axis=-1, keepdims=True)
        chances = (raised * (1.0 / total)).astype(jnp.bfloat16)
        outs.append(jnp.dot(chances, values, preferred_element_type=jnp.float32))
        lse_ref[0, head] = top + jnp.log(total)
    o_ref[...] = jnp.where(lane < HEAD_DIM, outs[0], outs[1]).astype(o_ref.dtype)


def attention_forward(packed, kv_all, query_segs, key_segs, factor):
    frames = packed.shape[0]
    keys = kv_all.shape[0]
    width = packed.shape[1] // 3
    pairs = width // 128
    rows = math.gcd(frames, 256)
    return pl.pallas_call(
        functools.partial(attention_forward_kernel, factor),
        grid=(pairs, frames // rows),
        in_specs=[
            pl.BlockSpec((rows, 128), lambda h, i: (i, h)),
            pl.BlockSpec((keys, 128), lambda h, i: (0, h)),
            pl.BlockSpec((keys, 128), lambda h, i: (0, pairs + h)),
            pl.BlockSpec((rows, 1), lambda h, i: (i, 0)),
            pl.BlockSpec((1, keys), lambda h, i: (0, 0)),
        ],
        out_specs=[
            pl.BlockSpec((rows, 128), lambda h, i: (i, h)),
            pl.BlockSpec((1, 2, rows, 1), lambda h, i: (h, 0, i, 0)),
        ],
        out_shape=[
            jax.ShapeDtypeStruct((frames, width), jnp.bfloat16),
            jax.ShapeDtypeStruct((pairs, 2, frames, 1), jnp.float32),
        ],
        compiler_params=pltpu.CompilerParams(vmem_limit_bytes=40 * 1024 * 1024),
        cost_estimate=pl.CostEstimate(
            flops=4 * frames * keys * width * 2,
            bytes_accessed=2 * (frames * width * 2 + keys * width * 2),
            transcendentals=frames * keys * (width // HEAD_DIM),
        ),
        name="attention_forward",
    )(packed, kv_all, kv_all, query_segs[:, None], key_segs[None, :])


def attention_backward_kernel(
    factor, q_ref, k_ref, v_ref, g_ref, o_ref, lse_ref, qs_ref, ks_ref, dq_ref, dk_ref, dv_ref
):
    step = pl.program_id(1)

    @pl.when(step == 0)
    def _():
        dk_ref[...] = jnp.zeros_like(dk_ref)
        dv_ref[...] = jnp.zeros_like(dv_ref)

    queries = q_ref[...]
    grads = g_ref[...]
    keys = k_ref[...]
    values = v_ref[...]
    lane = lax.broadcasted_iota(jnp.int32, queries.shape, 1)
    key_lane = lax.broadcasted_iota(jnp.int32, keys.shape, 1)
    allowed = qs_ref[...] == ks_ref[...]
    product = grads.astype(jnp.float32) * o_ref[...].astype(jnp.float32)
    dq = None
    for head in range(2):
        mine = (lane < HEAD_DIM) if head == 0 else (lane >= HEAD_DIM)
        key_mine = (key_lane < HEAD_DIM) if head == 0 else (key_lane >= HEAD_DIM)
        own_q = jnp.where(mine, queries, jnp.zeros_like(queries))
        own_g = jnp.where(mine, grads, jnp.zeros_like(grads))
        own_k = jnp.where(key_mine, keys, jnp.zeros_like(keys))
        delta = jnp.sum(jnp.where(mine, product, 0.0), axis=-1, keepdims=True)
        scores = lax.dot_general(
            own_q, keys, (((1,), (1,)), ((), ())), preferred_element_type=jnp.float32
        ) * factor
        chances = jnp.exp(jnp.where(allowed, scores, NEG) - lse_ref[0, head])
        prob_grad = lax.dot_general(
            own_g, values, (((1,), (1,)), ((), ())), preferred_element_type=jnp.float32
        )
        score_grad = (chances * (prob_grad - delta)).astype(jnp.bfloat16)
        part = jnp.dot(score_grad, own_k, preferred_element_type=jnp.float32)
        dq = part if dq is None else dq + part
        dk_ref[...] += lax.dot_general(
            score_grad, own_q, (((0,), (0,)), ((), ())), preferred_element_type=jnp.float32
        ) * factor
        dv_ref[...] += lax.dot_general(
            chances.astype(jnp.bfloat16), own_g, (((0,), (0,)), ((), ())),
            preferred_element_type=jnp.float32,
        )
    dq_ref[...] = (dq * factor).astype(dq_ref.dtype)


def attention_backward(packed, kv_all, grads, attended, lse, query_segs, key_segs, factor):
    frames = packed.shape[0]
    keys = kv_all.shape[0]
    width = packed.shape[1] // 3
    pairs = width // 128
    rows = math.gcd(frames, 256)
    return pl.pallas_call(
        functools.partial(attention_backward_kernel, factor),
        grid=(pairs, frames // rows),
        in_specs=[
            pl.BlockSpec((rows, 128), lambda h, i: (i, h)),
            pl.BlockSpec((keys, 128), lambda h, i: (0, h)),
            pl.BlockSpec((keys, 128), lambda h, i: (0, pairs + h)),
            pl.BlockSpec((rows, 128), lambda h, i: (i, h)),
            pl.BlockSpec((rows, 128), lambda h, i: (i, h)),
            pl.BlockSpec((1, 2, rows, 1), lambda h, i: (h, 0, i, 0)),
            pl.BlockSpec((rows, 1), lambda h, i: (i, 0)),
            pl.BlockSpec((1, keys), lambda h, i: (0, 0)),
        ],
        out_specs=[
            pl.BlockSpec((rows, 128), lambda h, i: (i, h)),
            pl.BlockSpec((keys, 128), lambda h, i: (0, h)),
            pl.BlockSpec((keys, 128), lambda h, i: (0, h)),
        ],
        out_shape=[
            jax.ShapeDtypeStruct((frames, width), jnp.bfloat16),
            jax.ShapeDtypeStruct((keys, width), jnp.float32),
            jax.ShapeDtypeStruct((keys, width), jnp.float32),
        ],
        compiler_params=pltpu.CompilerParams(vmem_limit_bytes=48 * 1024 * 1024),
        cost_estimate=pl.CostEstimate(
            flops=10 * frames * keys * width * 2,
            bytes_accessed=4 * (frames * width * 2 + keys * width * 2),
            transcendentals=frames * keys * (width // HEAD_DIM),
        ),
        name="attention_backward",
    )(packed, kv_all, kv_all, grads, attended, lse, query_segs[:, None], key_segs[None, :])


CONV_STEP = 4


def conv_bands(kernel, per_group):
    groups = kernel.shape[1] // per_group
    steps = TAPS // CONV_STEP + 1
    bands = []
    for group in range(groups):
        own = kernel[:, group * per_group : (group + 1) * per_group]
        shifted = [
            jnp.pad(own, ((shift * per_group, (CONV_STEP - shift) * per_group), (0, 0)))
            for shift in range(CONV_STEP)
        ]
        band = jnp.concatenate(shifted, axis=1)
        bands.append(band.reshape(steps, CONV_STEP * per_group, CONV_STEP * per_group))
    return bands


def group_view(values, per_group):
    rows, frames, width = values.shape
    return [
        values[:, :, g * per_group : (g + 1) * per_group].reshape(
            rows, frames // CONV_STEP, CONV_STEP * per_group
        )
        for g in range(width // per_group)
    ]


def ungroup(parts, per_group):
    rows, blocks, _ = parts[0].shape
    return jnp.concatenate(
        [part.reshape(rows, blocks * CONV_STEP, per_group) for part in parts], axis=2
    )


CONV_DIMS = ("NWC", "WIO", "NWC")


def conv_forward(views, bands):
    half = TAPS // 2 // CONV_STEP
    return [
        lax.conv_general_dilated(
            view, band, (1,), [(half, half)], dimension_numbers=CONV_DIMS,
            preferred_element_type=jnp.float32,
        )
        for view, band in zip(views, bands)
    ]


def conv_back(grad_views, bands):
    half = TAPS // 2 // CONV_STEP
    return [
        lax.conv_general_dilated(
            view, jnp.transpose(band[::-1], (0, 2, 1)), (1,), [(half, half)],
            dimension_numbers=CONV_DIMS, preferred_element_type=jnp.float32,
        )
        for view, band in zip(grad_views, bands)
    ]


def conv_taps_grad(views, grad_views, per_group):
    half = TAPS // 2 // CONV_STEP
    results = []
    for view, grad in zip(views, grad_views):
        band = lax.conv_general_dilated(
            view, grad, (1,), [(half, half)],
            dimension_numbers=("CWN", "IWO", "WNC"),
            preferred_element_type=jnp.float32,
        )
        flat = band.reshape(-1, CONV_STEP * per_group)
        total = None
        for shift in range(CONV_STEP):
            part = flat[
                shift * per_group : (shift + TAPS) * per_group,
                shift * per_group : (shift + 1) * per_group,
            ]
            total = part if total is None else total + part
        results.append(total)
    return jnp.concatenate(results, axis=1)


def to_column(vector, width):
    return jnp.pad(vector[:, None], ((0, 0), (0, width - 1)))


def per_device_pairs(
    signal, frame_segment_index, conv_weight, conv_bias, norm1_gain, qkv_weight, out_weight,
    norm2_gain, up_weight, down_weight, cotangent,
):
    micro_count, frames, width = signal.shape
    bf16, f32 = jnp.bfloat16, jnp.float32
    per_group = width // GROUPS
    dp_count = lax.axis_size("dp")
    factor = 1.0 / math.sqrt(HEAD_DIM)
    sec = lax.axis_index("section")
    dp = lax.axis_index("dp")
    seq = lax.axis_index("seq")
    x, y = seq % 2, seq // 2
    sec0, x0 = sec == 0, x == 0
    row_frames = 4 * frames
    half_frames = 2 * frames
    both = ("section", "seq")

    block_width = width // 8
    rows_here = conv_weight.shape[0]
    conv_low = conv_weight.astype(bf16).reshape(rows_here, 8, block_width)
    bias_low = jnp.pad(conv_bias.astype(bf16), (0, block_width - conv_bias.shape[0]))
    bias_rows = jnp.pad(
        jnp.broadcast_to(bias_low[None, None, :], (1, 8, block_width)), ((0, 15), (0, 0), (0, 0))
    )
    conv_send = jnp.transpose(jnp.concatenate([conv_low, bias_rows], axis=0), (1, 0, 2))
    conv_got = lax.all_to_all(conv_send, both, 0, 0, tiled=True)

    own_half = jnp.where(sec0, signal[:, :, : width // 2], signal[:, :, width // 2 :])
    sig_send = jnp.transpose(own_half.reshape(micro_count, frames, 4, block_width), (2, 0, 1, 3))
    sig_got = lax.all_to_all(sig_send, "seq", 0, 0, tiled=True)
    sig_all = jnp.transpose(sig_got, (1, 0, 2, 3)).reshape(micro_count, row_frames, block_width)

    conv_all = place_dp(conv_got, dp)
    conv_all = conv_all.reshape(dp_count, 2, 4, rows_here + 16, block_width)
    conv_all = jnp.transpose(conv_all, (1, 0, 2, 3, 4))
    bias_all = conv_all[:, :, :, rows_here, : conv_bias.shape[0]].reshape(width)
    bias_own = lax.dynamic_slice_in_dim(bias_all, (sec * 4 + seq) * block_width, block_width, 0)
    kernel_own = conv_all[:, :, :, :rows_here].reshape(TAPS * per_group, block_width)
    bands = conv_bands(kernel_own, per_group)

    in_rows = qkv_weight.shape[1]
    unit = down_weight.shape[1] // 4
    qkv_view = qkv_weight[0].astype(bf16).reshape(in_rows, -1, 2, HEAD_DIM)
    qkv_parity = [qkv_view[:, :, p].reshape(in_rows, -1) for p in range(2)]
    up_view = up_weight[0].astype(bf16).reshape(in_rows, -1, 2, 2, 2, unit)
    up_parity = [
        jnp.transpose(up_view[:, :, p], (0, 3, 1, 2, 4)).reshape(in_rows, -1) for p in range(2)
    ]
    qkv_cols, up_cols = qkv_parity[0].shape[1], up_parity[0].shape[1]
    col_one = to_column(norm1_gain[0].astype(bf16), 128)
    col_two = to_column(norm2_gain[0].astype(bf16), 128)
    cut = qkv_cols + 128
    keep_cols, send_cols = [
        jnp.concatenate([a, col_one, b, col_two], axis=1)
        for a, b in zip(choose(x0, *qkv_parity), choose(x0, *up_parity))
    ]
    row_sets = choose(x0, keep_cols, swap_x(send_cols))
    out_low = out_weight[0].astype(bf16)
    down_low = down_weight[0].astype(bf16).reshape(2, 2, unit, width)
    out_at, up_at = cut, cut + width // 2
    two_at = up_at + up_cols
    down_at = two_at + 128
    row_parts = [
        jnp.concatenate(
            [
                row_sets[h][:, :cut],
                out_low[:, h * width // 2 : (h + 1) * width // 2],
                row_sets[h][:, cut:],
                down_low[h, 0],
                down_low[h, 1],
            ],
            axis=1,
        )
        for h in range(2)
    ]
    keep, send = choose(sec0, *row_parts)
    layer_pieces = choose(sec0, keep, swap_section(send))
    layer_weights = []
    for layer in range(2):
        whole = gather_rows(layer_pieces[layer])
        w_out = jnp.transpose(
            whole[:, out_at:up_at].reshape(-1, 2, in_rows, width // 2), (0, 2, 1, 3)
        ).reshape(-1, width)
        gain_one = whole[:, qkv_cols].astype(f32)[None, :]
        gain_two = whole[:, two_at].astype(f32)[None, :]
        w_up = [whole[:, up_at + part * width : up_at + (part + 1) * width] for part in range(2)]
        w_down = [whole[:, down_at + part * width : down_at + (part + 1) * width] for part in range(2)]
        layer_weights.append((gain_one, whole[:, :qkv_cols], w_out, gain_two, w_up, w_down))

    picked = jnp.where(sec0, cotangent[0], cotangent[1])
    across = [(s * 4 + 2 * yy + xx, yy * 4 + 2 * s + xx) for s in range(2) for yy in range(2) for xx in range(2)]
    cot_own = lax.ppermute(picked, both, across)
    cot_other = swap_x(cot_own)
    cot_pair = choose(x0, cot_own, cot_other)
    top_grad = jnp.concatenate(cot_pair, axis=0).astype(f32)

    segment_row = jnp.where(y == 0, frame_segment_index[0], frame_segment_index[1])
    seg_pair = choose(sec0, segment_row[:half_frames], segment_row[half_frames:])
    query_segs = seg_pair[0]
    key_segs = jnp.concatenate(seg_pair)

    sig_views = group_view(sig_all, per_group)
    conv_pre = ungroup(conv_forward(sig_views, bands), per_group) + bias_own.astype(f32)
    stream = (sig_all.astype(f32) + smooth(conv_pre)).astype(bf16)
    slope = gelu_slope(conv_pre).astype(bf16)
    stream_send = stream.reshape(2, 2, half_frames, block_width)
    stream_send = jnp.transpose(stream_send, (1, 0, 2, 3))
    stream_send = jnp.repeat(stream_send.reshape(4, half_frames, block_width), 2, axis=0)
    stream_got = lax.all_to_all(stream_send, both, 0, 0, tiled=True)
    layer_in = jnp.transpose(stream_got, (1, 0, 2)).reshape(half_frames, width).astype(f32)

    kept = []
    for layer in range(2):
        gain_one, w_qkv, w_out, gain_two, w_up, w_down = layer_weights[layer]
        centred, inv = norm_stats(layer_in)
        normed_one = (centred * inv * gain_one).astype(bf16)
        packed = jnp.dot(normed_one, w_qkv, preferred_element_type=f32).astype(bf16)
        kv_own = packed[:, width // 2 :]
        kv_all = jnp.concatenate([kv_own, swap_section(kv_own)], axis=0)
        attended, lse = attention_forward(packed, kv_all, query_segs, key_segs, factor)
        resid_two = layer_in + pair_sum(jnp.dot(attended, w_out, preferred_element_type=f32))
        centred, inv = norm_stats(resid_two)
        normed_two = (centred * inv * gain_two).astype(bf16)
        hidden, hidden_slope, down_sum = [], [], None
        for part in range(2):
            hidden_pre = jnp.dot(normed_two, w_up[part], preferred_element_type=f32)
            hidden.append(smooth(hidden_pre).astype(bf16))
            hidden_slope.append(gelu_slope(hidden_pre).astype(bf16))
        for part in range(2):
            term = jnp.dot(hidden[part], w_down[part], preferred_element_type=f32)
            down_sum = term if down_sum is None else down_sum + term
        result = resid_two + pair_sum(down_sum)
        kept.append(
            (layer_in, normed_one, packed, kv_all, attended, lse, resid_two, normed_two, hidden, hidden_slope)
        )
        layer_in = result.astype(bf16).astype(f32)
    output = result

    grad_out = top_grad
    reduced = [None, None]
    for layer in (1, 0):
        gain_one, w_qkv, w_out, gain_two, w_up, w_down = layer_weights[layer]
        (layer_in, normed_one, packed, kv_all, attended, lse, resid_two, normed_two, hidden, hidden_slope) = kept[layer]
        branch = grad_out.astype(bf16)
        pre_grad, part_sum = [], None
        for part in range(2):
            hidden_grad = lax.dot_general(
                branch, w_down[part], (((1,), (1,)), ((), ())), preferred_element_type=f32
            )
            pre_grad.append((hidden_grad * hidden_slope[part].astype(f32)).astype(bf16))
        for part in range(2):
            term = lax.dot_general(
                pre_grad[part], w_up[part], (((1,), (1,)), ((), ())), preferred_element_type=f32
            )
            part_sum = term if part_sum is None else part_sum + term
        normed_grad = pair_sum(part_sum)
        resid_grad, gain_two_grad = norm_back(resid_two, gain_two, normed_grad)
        resid_grad = resid_grad + grad_out
        attn_branch = resid_grad.astype(bf16)
        attended_grad = lax.dot_general(
            attn_branch, w_out, (((1,), (1,)), ((), ())), preferred_element_type=f32
        ).astype(bf16)
        dq, dk, dv = attention_backward(
            packed, kv_all, attended_grad, attended, lse, query_segs, key_segs, factor
        )
        dkv = jnp.concatenate([dk, dv], axis=1)
        other_dkv = swap_section(dkv[half_frames:].astype(bf16))
        dkv_own = (dkv[:half_frames] + other_dkv.astype(f32)).astype(bf16)
        packed_grad = jnp.concatenate([dq, dkv_own], axis=1)
        part = lax.dot_general(
            packed_grad, w_qkv, (((1,), (1,)), ((), ())), preferred_element_type=f32
        )
        normed_grad = pair_sum(part)
        in_grad, gain_one_grad = norm_back(layer_in, gain_one, normed_grad)
        grad_in = resid_grad + in_grad
        def outer(left, right):
            return lax.dot_general(
                left, right, (((0,), (0,)), ((), ())), preferred_element_type=f32
            ).astype(bf16)

        grad_out_weight = jnp.transpose(
            outer(attended, attn_branch).reshape(-1, in_rows, 2, width // 2), (0, 2, 1, 3)
        ).reshape(-1, width // 2)
        partial = jnp.concatenate(
            [
                outer(normed_one, packed_grad),
                to_column(gain_one_grad.astype(bf16), 128),
                grad_out_weight,
                outer(normed_two, pre_grad[0]),
                outer(normed_two, pre_grad[1]),
                to_column(gain_two_grad.astype(bf16), 128),
                outer(hidden[0], branch),
                outer(hidden[1], branch),
            ],
            axis=1,
        )
        reduced[layer] = scatter_rows(partial)
        grad_out = grad_in.astype(bf16).astype(f32)
    grad_in_low = grad_in.astype(bf16)

    lig_send = jnp.transpose(grad_in_low.reshape(half_frames, 8, block_width), (1, 0, 2))
    lig_got = lax.all_to_all(lig_send, both, 0, 0, tiled=True).reshape(2, 2, 2, half_frames, block_width)
    lig = jnp.transpose(lig_got[:, :, 0], (1, 0, 2, 3)).reshape(micro_count, row_frames, block_width)
    conv_grad = (lig.astype(f32) * slope.astype(f32)).astype(bf16)
    grad_views = group_view(conv_grad, per_group)
    back = ungroup(conv_back(grad_views, bands), per_group)
    grad_signal = (lig.astype(f32) + back).astype(bf16)
    gs_send = jnp.transpose(
        grad_signal.reshape(micro_count, 4, frames, block_width), (1, 0, 2, 3)
    )
    gs_send = jnp.concatenate([gs_send, gs_send], axis=0)
    gs_got = lax.all_to_all(gs_send, both, 0, 0, tiled=True)
    gs_rows = jnp.transpose(gs_got, (1, 2, 0, 3)).reshape(micro_count, frames, width).astype(f32)

    taps_grad = conv_taps_grad(sig_views, grad_views, per_group)
    bias_grad = jnp.sum(conv_grad.astype(f32), axis=(0, 1))
    taps_view = jnp.transpose(
        taps_grad.reshape(2, dp_count, 4, rows_here, block_width), (1, 0, 2, 3, 4)
    ).astype(bf16)
    bias_view = jnp.pad(
        jnp.broadcast_to(bias_grad.astype(bf16), (dp_count, 2, 4, 1, block_width)),
        ((0, 0), (0, 0), (0, 0), (0, 15), (0, 0)),
    )
    taps_send = jnp.concatenate([taps_view, bias_view], axis=3)
    taps_sum = sum_dp(taps_send, dp)
    taps_got = lax.all_to_all(
        taps_sum.reshape(8, rows_here + 16, block_width), both, 0, 0, tiled=True
    )
    conv_weight_grad = jnp.transpose(taps_got[:, :rows_here], (1, 0, 2)).reshape(rows_here, width).astype(f32)
    bias_count = conv_bias.shape[0]
    conv_bias_grad = lax.dynamic_slice_in_dim(
        taps_got[:, rows_here].reshape(width),
        ((sec * dp_count + dp) * 4 + seq) * bias_count,
        bias_count,
        0,
    ).astype(f32)

    own_block = jnp.where(x0, output[:frames], output[frames:])
    row_block = lax.ppermute(own_block, both, across)
    other_row = swap_section(row_block)
    output_rows = jnp.stack(choose(sec0, row_block, other_row))
    ends = jnp.where(sec0, gs_rows, output_rows)[None]

    keep, send = choose(sec0, reduced[0], reduced[1])
    half_sets = choose(sec0, keep, swap_section(send))
    out_grad = jnp.concatenate([member[:, out_at:up_at] for member in half_sets], axis=1).astype(f32)[None]
    down_grad = jnp.concatenate(
        [member[:, at : at + width] for member in half_sets for at in (down_at, down_at + width)],
        axis=0,
    ).astype(f32)[None]
    col_first, col_second = [
        jnp.concatenate([member[:, :cut], member[:, up_at:down_at]], axis=1) for member in half_sets
    ]
    keep, send = choose(x0, col_first, col_second)
    norm1_grad = keep[:, qkv_cols].astype(f32)[None]
    norm2_grad = keep[:, cut + up_cols].astype(f32)[None]
    first, second = choose(x0, keep, swap_x(send))
    qkv_grad = jnp.stack(
        [member[:, :qkv_cols].reshape(in_rows, -1, HEAD_DIM) for member in (first, second)], axis=2
    ).reshape(in_rows, -1).astype(f32)[None]
    up_grad = jnp.stack(
        [
            jnp.transpose(
                member[:, cut : cut + up_cols].reshape(in_rows, 2, -1, 2, unit), (0, 2, 3, 1, 4)
            )
            for member in (first, second)
        ],
        axis=2,
    ).reshape(in_rows, -1).astype(f32)[None]
    return (ends, conv_weight_grad, conv_bias_grad, norm1_grad, qkv_grad, out_grad, norm2_grad, up_grad, down_grad)


def solution(mesh):
    placed = (
        P("dp", "seq", None),
        P("dp", None),
        P(("section", "dp", "seq"), None),
        P(("section", "dp", "seq")),
        P("section", ("dp", "seq")),
        P("section", ("dp", "seq"), None),
        P("section", ("dp", "seq"), None),
        P("section", ("dp", "seq")),
        P("section", ("dp", "seq"), None),
        P("section", ("dp", "seq"), None),
        P("dp", "seq", None),
    )

    def step(*arrays):
        pairs = mesh.shape["seq"] == 4 and mesh.shape["section"] == 2 and arrays[0].shape[0] == 2
        return (per_device_pairs if pairs else per_device)(*arrays)

    return jax.shard_map(
        step,
        mesh=mesh,
        in_specs=placed,
        out_specs=(
            P("section", "dp", "seq", None),
            P(("section", "dp", "seq"), None),
            P(("section", "dp", "seq")),
            P("section", ("dp", "seq")),
            P("section", ("dp", "seq"), None),
            P("section", ("dp", "seq"), None),
            P("section", ("dp", "seq")),
            P("section", ("dp", "seq"), None),
            P("section", ("dp", "seq"), None),
        ),
        check_vma=False,
    )
```

```python
import functools
import math

import jax
import jax.numpy as jnp
from jax import lax
from jax.experimental import pallas as pl
from jax.experimental.pallas import tpu as pltpu
from jax.sharding import PartitionSpec as P

HEAD_DIM = 64
GROUPS = 16
TAPS = 128


EPS = 1e-05
NEG = -1e30


def padded_2(block, sides, width):
    for axis, dim in sides:
        count = lax.axis_size(axis)
        forward = [(i, i + 1) for i in range(count - 1)]
        backward = [(target, source) for source, target in forward]
        low = lax.ppermute(
            lax.slice_in_dim(block, block.shape[dim] - width, None, axis=dim), axis, forward
        )
        high = lax.ppermute(lax.slice_in_dim(block, 0, width, axis=dim), axis, backward)
        block = jnp.concatenate([low, block, high], axis=dim)
    return block


def from_behind(value, axis, steps):
    count = lax.axis_size(axis)
    first, last = (max(0, -steps), min(count, count - steps))
    return lax.ppermute(value, axis, [(source, source + steps) for source in range(first, last)])


def normalize(values, gain):
    average = jnp.mean(values, axis=-1, keepdims=True)
    centred = values - average
    spread = jnp.mean(centred * centred, axis=-1, keepdims=True)
    return centred * lax.rsqrt(spread + EPS) * gain


def smooth(values):
    return jax.nn.gelu(values, approximate=False)


def conv_taps(padded, kernel, frames):
    width_all = padded.shape[1]
    per_group = width_all // GROUPS
    tap_step = math.gcd(TAPS, 16)
    weight_view = kernel.reshape(TAPS, per_group, GROUPS, per_group)
    running = jnp.zeros((frames, GROUPS, per_group), jnp.float32)
    for first_tap in range(0, TAPS, tap_step):
        windows = jnp.stack(
            [padded[first_tap + offset : first_tap + offset + frames] for offset in range(tap_step)]
        )
        windows = windows.reshape(tap_step, frames, GROUPS, per_group)
        running = running + jnp.einsum(
            "jtgc,jcgo->tgo",
            windows,
            weight_view[first_tap : first_tap + tap_step],
            preferred_element_type=jnp.float32,
        )
    return running.reshape(frames, width_all)


def conv_input_grad(grad_pad, kernel, frames):
    width_all = grad_pad.shape[1]
    per_group = width_all // GROUPS
    tap_step = math.gcd(TAPS, 16)
    weight_view = kernel.reshape(TAPS, per_group, GROUPS, per_group)
    running = jnp.zeros((frames, GROUPS, per_group), jnp.float32)
    for first_tap in range(0, TAPS, tap_step):
        back_windows = jnp.stack(
            [
                grad_pad[TAPS - first_tap - offset : TAPS - first_tap - offset + frames]
                for offset in range(tap_step)
            ]
        )
        back_windows = back_windows.reshape(tap_step, frames, GROUPS, per_group)
        running = running + jnp.einsum(
            "jtgo,jcgo->tgc",
            back_windows,
            weight_view[first_tap : first_tap + tap_step],
            preferred_element_type=jnp.float32,
        )
    return running.reshape(frames, width_all)


def conv_kernel_grad(padded_all, grad_all):
    step_count, frames, width_all = grad_all.shape
    per_group = width_all // GROUPS
    tap_step = math.gcd(TAPS, 16)
    grad_view = grad_all.reshape(step_count * frames, GROUPS, per_group)
    kernel_parts = []
    for first_tap in range(0, TAPS, tap_step):
        windows = jnp.stack(
            [
                padded_all[:, first_tap + offset : first_tap + offset + frames]
                for offset in range(tap_step)
            ]
        )
        windows = windows.reshape(tap_step, step_count * frames, GROUPS, per_group)
        kernel_parts.append(
            jnp.einsum("jtgc,tgo->jcgo", windows, grad_view, preferred_element_type=jnp.float32)
        )
    return jnp.concatenate(kernel_parts, axis=0).reshape(TAPS * per_group, width_all)


def score_block(query_heads, key_block, query_segs, key_segs, factor):
    scores = (
        jnp.einsum("qhd,khd->hqk", query_heads, key_block, preferred_element_type=jnp.float32)
        * factor
    )
    allowed = (query_segs[:, None] == key_segs[None, :])[None]
    return (scores, allowed)


def front(layer_in, weights, kernel, conv_shift, first_section):
    frames, width_all = layer_in.shape
    padded = padded_2(layer_in, (("seq", 0),), TAPS // 2)
    conv_pre = lax.cond(
        first_section,
        lambda: conv_taps(padded, kernel, frames) + conv_shift.astype(jnp.float32),
        lambda: jnp.zeros((frames, width_all), jnp.float32),
    )
    conv_val, conv_pull = jax.vjp(smooth, conv_pre)
    resid_one = layer_in.astype(jnp.float32) + conv_val
    normed_val, norm_pull = jax.vjp(normalize, resid_one, weights[0].astype(jnp.float32))
    normed_one = normed_val.astype(jnp.bfloat16)
    packed = jnp.dot(normed_one, weights[1], preferred_element_type=jnp.float32).astype(
        jnp.bfloat16
    )
    return (padded, conv_pull, resid_one, norm_pull, normed_one, packed)


def tail(resid_one, attn_low, weights):
    resid_two = resid_one + jnp.dot(attn_low, weights[2], preferred_element_type=jnp.float32)
    normed_val, norm_pull = jax.vjp(normalize, resid_two, weights[3].astype(jnp.float32))
    normed_two = normed_val.astype(jnp.bfloat16)
    hidden_pre = jnp.dot(normed_two, weights[4], preferred_element_type=jnp.float32)
    hidden_val, gelu_pull = jax.vjp(smooth, hidden_pre)
    hidden_low = hidden_val.astype(jnp.bfloat16)
    result = resid_two + jnp.dot(hidden_low, weights[5], preferred_element_type=jnp.float32)
    return (result, norm_pull, normed_two, gelu_pull, hidden_low)


def key_loop(keys_all, values_all, segment_row, head_count, visit, initial):
    total_rows = keys_all.shape[0]
    block_rows = math.gcd(total_rows, 512)

    def one_block(block_index, running):
        offset = block_index * block_rows
        key_block = lax.dynamic_slice_in_dim(keys_all, offset, block_rows, 0).reshape(
            block_rows, head_count, HEAD_DIM
        )
        value_block = lax.dynamic_slice_in_dim(values_all, offset, block_rows, 0).reshape(
            block_rows, head_count, HEAD_DIM
        )
        key_segs = lax.dynamic_slice_in_dim(segment_row, offset, block_rows, 0)
        return visit(running, key_block, value_block, key_segs)

    return lax.fori_loop(0, total_rows // block_rows, one_block, initial)


def layer_forward(
    layer_in, segment_row, weights, kernel, conv_shift, first_section, my_start, factor
):
    frames, width_all = layer_in.shape
    head_count = width_all // HEAD_DIM
    padded, conv_pull, resid_one, norm_pull, normed_one, packed = front(
        layer_in, weights, kernel, conv_shift, first_section
    )
    query_heads = packed[:, :width_all].reshape(frames, head_count, HEAD_DIM)
    query_segs = lax.dynamic_slice_in_dim(segment_row, my_start, frames, 0)
    initial = (
        jnp.full((head_count, frames), NEG, jnp.float32),
        jnp.zeros((head_count, frames), jnp.float32),
        jnp.zeros((head_count, frames, HEAD_DIM), jnp.float32),
    )
    key_piece = lax.all_gather(packed[:, width_all : 2 * width_all], "seq", axis=0, tiled=True)
    value_piece = lax.all_gather(packed[:, 2 * width_all :], "seq", axis=0, tiled=True)
    piece_rows = key_piece.shape[0]
    block_rows = math.gcd(piece_rows, 512)

    def one_block(block_index, running):
        run_max, run_sum, run_acc = running
        offset = block_index * block_rows
        key_block = lax.dynamic_slice_in_dim(key_piece, offset, block_rows, 0).reshape(
            block_rows, head_count, HEAD_DIM
        )
        value_block = lax.dynamic_slice_in_dim(value_piece, offset, block_rows, 0).reshape(
            block_rows, head_count, HEAD_DIM
        )
        key_segs = lax.dynamic_slice_in_dim(segment_row, offset, block_rows, 0)
        scores, allowed = score_block(query_heads, key_block, query_segs, key_segs, factor)
        masked = jnp.where(allowed, scores, NEG)
        new_max = jnp.maximum(run_max, jnp.max(masked, axis=-1))
        weights_now = jnp.where(allowed, jnp.exp(masked - new_max[..., None]), 0.0)
        rescale = jnp.exp(run_max - new_max)
        run_sum = run_sum * rescale + jnp.sum(weights_now, axis=-1)
        run_acc = run_acc * rescale[..., None] + jnp.einsum(
            "hqk,khd->hqd",
            weights_now.astype(jnp.bfloat16),
            value_block,
            preferred_element_type=jnp.float32,
        )
        return (new_max, run_sum, run_acc)

    run_max, run_sum, run_acc = lax.fori_loop(0, piece_rows // block_rows, one_block, initial)
    log_total = run_max + jnp.log(run_sum)
    mixture = run_acc / run_sum[..., None]
    attn_low = jnp.transpose(mixture, (1, 0, 2)).reshape(frames, width_all).astype(jnp.bfloat16)
    result, norm_two_pull, normed_two, gelu_pull, hidden_low = tail(resid_one, attn_low, weights)
    kept = (
        padded,
        conv_pull,
        norm_pull,
        normed_one,
        packed,
        log_total,
        mixture,
        attn_low,
        norm_two_pull,
        normed_two,
        gelu_pull,
        hidden_low,
        segment_row,
    )
    return (result, kept)


def layer_backward(kept, grad_out, weights, kernel, first_section, my_start, factor):
    (
        padded,
        conv_pull,
        norm_one_pull,
        normed_one,
        packed,
        log_total,
        mixture,
        attn_low,
        norm_two_pull,
        normed_two,
        gelu_pull,
        hidden_low,
        segment_row,
    ) = kept
    frames, width_all = normed_one.shape
    head_count = width_all // HEAD_DIM
    query_heads = packed[:, :width_all].reshape(frames, head_count, HEAD_DIM)
    key_local = packed[:, width_all : 2 * width_all]
    value_local = packed[:, 2 * width_all :]
    query_segs = lax.dynamic_slice_in_dim(segment_row, my_start, frames, 0)
    keys_all, values_all = (
        lax.all_gather(key_local, "seq", axis=0, tiled=True),
        lax.all_gather(value_local, "seq", axis=0, tiled=True),
    )

    def chances_for(key_block, key_segs):
        scores, allowed = score_block(query_heads, key_block, query_segs, key_segs, factor)
        return jnp.where(
            allowed, jnp.exp(jnp.where(allowed, scores, NEG) - log_total[..., None]), 0.0
        )

    branch_grad = grad_out.astype(jnp.bfloat16)
    hidden_grad = jnp.einsum(
        "to,io->ti", branch_grad, weights[5], preferred_element_type=jnp.float32
    )
    pre_grad = gelu_pull(hidden_grad)[0].astype(jnp.bfloat16)
    normed_two_grad = jnp.einsum(
        "tf,if->ti", pre_grad, weights[4], preferred_element_type=jnp.float32
    )
    resid_two_grad, grad_gain_two = norm_two_pull(normed_two_grad)
    resid_two_grad = resid_two_grad + grad_out
    attn_branch_grad = resid_two_grad.astype(jnp.bfloat16)
    attended_grad = jnp.einsum(
        "to,io->ti", attn_branch_grad, weights[2], preferred_element_type=jnp.float32
    ).astype(jnp.bfloat16)
    dout_heads = attended_grad.reshape(frames, head_count, HEAD_DIM)
    delta_rows = jnp.einsum("qhd,hqd->hq", dout_heads.astype(jnp.float32), mixture)

    def visit_query(running, key_block, value_block, key_segs):
        chances = chances_for(key_block, key_segs)
        prob_grad = jnp.einsum(
            "qhd,khd->hqk", dout_heads, value_block, preferred_element_type=jnp.float32
        )
        score_grad = (chances * (prob_grad - delta_rows[..., None])).astype(jnp.bfloat16)
        return running + jnp.einsum(
            "hqk,khd->qhd", score_grad, key_block, preferred_element_type=jnp.float32
        )

    grad_query = (
        key_loop(
            keys_all,
            values_all,
            segment_row,
            head_count,
            visit_query,
            jnp.zeros((frames, head_count, HEAD_DIM), jnp.float32),
        )
        * factor
    )
    row_stats = (
        lax.all_gather(log_total, "seq", axis=1, tiled=True),
        lax.all_gather(delta_rows, "seq", axis=1, tiled=True),
    )
    key_heads = key_local.reshape(frames, head_count, HEAD_DIM)
    value_heads = value_local.reshape(frames, head_count, HEAD_DIM)
    start_acc = (
        jnp.zeros((frames, head_count, HEAD_DIM), jnp.float32),
        jnp.zeros((frames, head_count, HEAD_DIM), jnp.float32),
    )
    query_piece = lax.all_gather(packed[:, :width_all], "seq", axis=0, tiled=True)
    dout_piece = lax.all_gather(attended_grad, "seq", axis=0, tiled=True)
    piece_rows = query_piece.shape[0]
    block_rows = math.gcd(piece_rows, 512)

    def one_block(block_index, running):
        key_acc, value_acc = running
        offset = block_index * block_rows
        query_block = lax.dynamic_slice_in_dim(query_piece, offset, block_rows, 0).reshape(
            block_rows, head_count, HEAD_DIM
        )
        dout_block = lax.dynamic_slice_in_dim(dout_piece, offset, block_rows, 0).reshape(
            block_rows, head_count, HEAD_DIM
        )
        seg_block = lax.dynamic_slice_in_dim(segment_row, offset, block_rows, 0)
        total_block = lax.dynamic_slice_in_dim(row_stats[0], offset, block_rows, 1)
        delta_block = lax.dynamic_slice_in_dim(row_stats[1], offset, block_rows, 1)
        scores, allowed = score_block(query_block, key_heads, seg_block, query_segs, factor)
        chances = jnp.where(
            allowed, jnp.exp(jnp.where(allowed, scores, NEG) - total_block[..., None]), 0.0
        )
        prob_grad = jnp.einsum(
            "qhd,khd->hqk", dout_block, value_heads, preferred_element_type=jnp.float32
        )
        score_grad = (chances * (prob_grad - delta_block[..., None])).astype(jnp.bfloat16)
        key_acc = (
            key_acc
            + jnp.einsum(
                "hqk,qhd->khd", score_grad, query_block, preferred_element_type=jnp.float32
            )
            * factor
        )
        value_acc = value_acc + jnp.einsum(
            "hqk,qhd->khd",
            chances.astype(jnp.bfloat16),
            dout_block,
            preferred_element_type=jnp.float32,
        )
        return (key_acc, value_acc)

    key_acc, value_acc = lax.fori_loop(0, piece_rows // block_rows, one_block, start_acc)
    grad_key = key_acc.reshape(frames, width_all)
    grad_value = value_acc.reshape(frames, width_all)
    packed_grad = jnp.concatenate(
        [grad_query.reshape(frames, width_all), grad_key, grad_value], axis=1
    ).astype(jnp.bfloat16)
    normed_one_grad = jnp.einsum(
        "tj,ij->ti", packed_grad, weights[1], preferred_element_type=jnp.float32
    )
    resid_one_grad, grad_gain_one = norm_one_pull(normed_one_grad)
    resid_one_grad = resid_one_grad + resid_two_grad
    conv_grad = jnp.where(first_section, conv_pull(resid_one_grad)[0], 0.0).astype(jnp.bfloat16)
    grad_pad = padded_2(conv_grad, (("seq", 0),), TAPS // 2)
    back_sum = lax.cond(
        first_section,
        lambda: conv_input_grad(grad_pad, kernel, frames),
        lambda: jnp.zeros((frames, width_all), jnp.float32),
    )
    grad_in = resid_one_grad + back_sum
    products = (
        normed_one,
        packed_grad,
        attn_low,
        attn_branch_grad,
        normed_two,
        pre_grad,
        hidden_low,
        branch_grad,
        padded,
        conv_grad,
    )
    return (grad_in, (grad_gain_one, grad_gain_two), products)


def per_device(
    signal,
    frame_segment_index,
    conv_weight,
    conv_bias,
    norm1_gain,
    qkv_weight,
    out_weight,
    norm2_gain,
    up_weight,
    down_weight,
    cotangent,
):
    micro_count, frames, width_all = signal.shape
    factor = 1.0 / math.sqrt(HEAD_DIM)
    first_section = lax.axis_index("section") == 0
    my_start = lax.axis_index("seq") * frames
    gathered = (
        lax.all_gather(norm1_gain.astype(jnp.bfloat16), ("dp", "seq"), axis=1, tiled=True),
        lax.all_gather(qkv_weight.astype(jnp.bfloat16), ("dp", "seq"), axis=1, tiled=True),
        lax.all_gather(out_weight.astype(jnp.bfloat16), ("dp", "seq"), axis=1, tiled=True),
        lax.all_gather(norm2_gain.astype(jnp.bfloat16), ("dp", "seq"), axis=1, tiled=True),
        lax.all_gather(up_weight.astype(jnp.bfloat16), ("dp", "seq"), axis=1, tiled=True),
        lax.all_gather(down_weight.astype(jnp.bfloat16), ("dp", "seq"), axis=1, tiled=True),
    )
    weights = tuple((member[0] for member in gathered))
    kernel, conv_shift = (
        lax.all_gather(
            conv_weight.astype(jnp.bfloat16), ("section", "dp", "seq"), axis=0, tiled=True
        ),
        lax.all_gather(
            conv_bias.astype(jnp.bfloat16), ("section", "dp", "seq"), axis=0, tiled=True
        ),
    )
    received = jnp.zeros((frames, width_all), jnp.bfloat16)
    saved = []
    forward_outs = []
    for step_index in range(micro_count + 1):
        own_index = min(step_index, micro_count - 1)
        prior_index = max(step_index - 1, 0)
        layer_in = jnp.where(first_section, signal[own_index], received)
        segment_row = jnp.where(
            first_section, frame_segment_index[own_index], frame_segment_index[prior_index]
        )
        result, kept = layer_forward(
            layer_in, segment_row, weights, kernel, conv_shift, first_section, my_start, factor
        )
        saved.append(kept)
        forward_outs.append(result)
        if step_index < micro_count:
            received = from_behind(result.astype(jnp.bfloat16), "section", 1)
    received_back = jnp.zeros((frames, width_all), jnp.bfloat16)
    input_grads = []
    gain_totals = None
    product_list = []
    for step_index in range(micro_count + 1):
        kept = saved[micro_count - step_index]
        if step_index < micro_count:
            top_grad = cotangent[micro_count - 1 - step_index].astype(jnp.float32)
        else:
            top_grad = jnp.zeros((frames, width_all), jnp.float32)
        incoming = jnp.where(first_section, received_back.astype(jnp.float32), top_grad)
        grad_in, gain_grads, products = layer_backward(
            kept, incoming, weights, kernel, first_section, my_start, factor
        )
        input_grads.append(grad_in)
        product_list.append(products)
        if gain_totals is None:
            gain_totals = gain_grads
        else:
            gain_totals = (gain_totals[0] + gain_grads[0], gain_totals[1] + gain_grads[1])
        if step_index < micro_count:
            received_back = from_behind(grad_in.astype(jnp.bfloat16), "section", -1)

    def joined(position):
        return jnp.concatenate([member[position] for member in product_list], axis=0)

    grad_qkv = jnp.einsum("ti,tj->ij", joined(0), joined(1), preferred_element_type=jnp.float32)
    grad_out_weight = jnp.einsum(
        "ti,to->io", joined(2), joined(3), preferred_element_type=jnp.float32
    )
    grad_up = jnp.einsum("ti,tf->if", joined(4), joined(5), preferred_element_type=jnp.float32)
    grad_down = jnp.einsum("ti,to->io", joined(6), joined(7), preferred_element_type=jnp.float32)
    padded_all = jnp.stack([member[8] for member in product_list])
    conv_grad_all = jnp.stack([member[9] for member in product_list])
    kernel_grad = conv_kernel_grad(padded_all, conv_grad_all)
    bias_grad = jnp.sum(joined(9).astype(jnp.float32), axis=0)
    ends = jnp.stack(
        [
            jnp.where(
                first_section, input_grads[micro_count - mb_index], forward_outs[mb_index + 1]
            )
            for mb_index in range(micro_count)
        ]
    )[None]
    layer_sums = (
        lax.psum_scatter(gain_totals[0][None], ("dp", "seq"), scatter_dimension=1, tiled=True),
        lax.psum_scatter(grad_qkv[None], ("dp", "seq"), scatter_dimension=1, tiled=True),
        lax.psum_scatter(grad_out_weight[None], ("dp", "seq"), scatter_dimension=1, tiled=True),
        lax.psum_scatter(gain_totals[1][None], ("dp", "seq"), scatter_dimension=1, tiled=True),
        lax.psum_scatter(grad_up[None], ("dp", "seq"), scatter_dimension=1, tiled=True),
        lax.psum_scatter(grad_down[None], ("dp", "seq"), scatter_dimension=1, tiled=True),
    )
    conv_sums = (
        lax.psum_scatter(kernel_grad, ("section", "dp", "seq"), scatter_dimension=0, tiled=True),
        lax.psum_scatter(bias_grad, ("section", "dp", "seq"), scatter_dimension=0, tiled=True),
    )
    return (
        ends,
        conv_sums[0],
        conv_sums[1],
        layer_sums[0],
        layer_sums[1],
        layer_sums[2],
        layer_sums[3],
        layer_sums[4],
        layer_sums[5],
    )


def swap_section(value):
    return lax.ppermute(value, "section", [(0, 1), (1, 0)])


def swap_x(value):
    return lax.ppermute(value, "seq", [(q, q ^ 1) for q in range(4)])


def pair_sum(low):
    return low.astype(jnp.float32) + swap_x(low).astype(jnp.float32)


def after(first, second):
    return lax.optimization_barrier((first, second))


def choose(flag, first, second):
    return jnp.where(flag, first, second), jnp.where(flag, second, first)


def chain_steps(value):
    count = lax.axis_size("dp")
    upward = [(i, i + 1) for i in range(count - 1)]
    downward = [(i + 1, i) for i in range(count - 1)]
    low, high = value, value
    lows, highs = [], []
    for _ in range(count - 1):
        low = lax.ppermute(low, "dp", upward)
        high = lax.ppermute(high, "dp", downward)
        lows.append(low)
        highs.append(high)
    return lows, highs


def place_dp(value, dp):
    count = lax.axis_size("dp")
    lows, highs = chain_steps(value)
    whole = jnp.zeros((count, *value.shape), value.dtype)
    whole = lax.dynamic_update_index_in_dim(whole, value, dp, 0)
    for turn in range(1, count):
        piece = jnp.where(dp + turn < count, highs[turn - 1], lows[count - turn - 1])
        whole = lax.dynamic_update_index_in_dim(whole, piece, (dp + turn) % count, 0)
    return whole


def sum_dp(blocks, dp):
    count = lax.axis_size("dp")
    f32, bf16 = jnp.float32, jnp.bfloat16

    def block(index):
        return lax.dynamic_index_in_dim(blocks, jnp.clip(index, 0, count - 1), 0, keepdims=False)

    total = block(dp).astype(f32)
    for sign in (1, -1):
        pairs = [(i, i + sign) for i in range(count) if 0 <= i + sign < count]
        running = None
        for distance in range(count - 1, 0, -1):
            own = block(dp + sign * distance)
            if running is not None:
                own = (own.astype(f32) + running.astype(f32)).astype(bf16)
            live = [(a, b) for a, b in pairs if 0 <= a + sign * distance < count]
            running = lax.ppermute(own, "dp", live)
        total = total + running.astype(f32)
    return total.astype(bf16)


def line_groups():
    count = lax.axis_size("dp")
    return [
        [(s * count + d) * 4 + 2 * y + x for d in range(count) for y in range(2) for s in range(2)]
        for x in range(2)
    ]


def gather_rows(piece):
    return lax.all_gather(
        piece, ("section", "dp", "seq"), axis=0, tiled=True, axis_index_groups=line_groups()
    )


def scatter_rows(partial):
    return lax.psum_scatter(
        partial, ("section", "dp", "seq"), scatter_dimension=0, tiled=True,
        axis_index_groups=line_groups(),
    )


def norm_stats(values):
    average = jnp.mean(values, axis=-1, keepdims=True)
    centred = values - average
    spread = jnp.mean(centred * centred, axis=-1, keepdims=True)
    return centred, lax.rsqrt(spread + EPS)


def norm_back(values, gain, grad):
    centred, inv = norm_stats(values)
    unit = centred * inv
    gain_grad = jnp.sum(grad * unit, axis=0)
    f = grad * gain
    mean_f = jnp.mean(f, axis=-1, keepdims=True)
    mean_fu = jnp.mean(f * unit, axis=-1, keepdims=True)
    return (f - mean_f - unit * mean_fu) * inv, gain_grad


def gelu_slope(values):
    cdf = 0.5 * (1.0 + lax.erf(values * (1.0 / math.sqrt(2.0))))
    pdf = jnp.exp(-0.5 * values * values) * (1.0 / math.sqrt(2.0 * math.pi))
    return cdf + values * pdf


def attention_forward_kernel(factor, q_ref, k_ref, v_ref, qs_ref, ks_ref, o_ref, lse_ref):
    queries = q_ref[...]
    lane = lax.broadcasted_iota(jnp.int32, queries.shape, 1)
    allowed = qs_ref[...] == ks_ref[...]
    keys = k_ref[...]
    values = v_ref[...]
    outs = []
    for head in range(2):
        mine = (lane < HEAD_DIM) if head == 0 else (lane >= HEAD_DIM)
        own = jnp.where(mine, queries, jnp.zeros_like(queries))
        scores = lax.dot_general(
            own, keys, (((1,), (1,)), ((), ())), preferred_element_type=jnp.float32
        ) * factor
        scores = jnp.where(allowed, scores, NEG)
        top = jnp.max(scores, axis=-1, keepdims=True)
        raised = jnp.exp(scores - top)
        total = jnp.sum(raised, axis=-1, keepdims=True)
        chances = (raised * (1.0 / total)).astype(jnp.bfloat16)
        outs.append(jnp.dot(chances, values, preferred_element_type=jnp.float32))
        lse_ref[0, head] = top + jnp.log(total)
    o_ref[...] = jnp.where(lane < HEAD_DIM, outs[0], outs[1]).astype(o_ref.dtype)


def attention_forward(packed, kv_all, query_segs, key_segs, factor):
    frames = packed.shape[0]
    keys = kv_all.shape[0]
    width = packed.shape[1] // 3
    pairs = width // 128
    rows = math.gcd(frames, 256)
    return pl.pallas_call(
        functools.partial(attention_forward_kernel, factor),
        grid=(pairs, frames // rows),
        in_specs=[
            pl.BlockSpec((rows, 128), lambda h, i: (i, h)),
            pl.BlockSpec((keys, 128), lambda h, i: (0, h)),
            pl.BlockSpec((keys, 128), lambda h, i: (0, pairs + h)),
            pl.BlockSpec((rows, 1), lambda h, i: (i, 0)),
            pl.BlockSpec((1, keys), lambda h, i: (0, 0)),
        ],
        out_specs=[
            pl.BlockSpec((rows, 128), lambda h, i: (i, h)),
            pl.BlockSpec((1, 2, rows, 1), lambda h, i: (h, 0, i, 0)),
        ],
        out_shape=[
            jax.ShapeDtypeStruct((frames, width), jnp.bfloat16),
            jax.ShapeDtypeStruct((pairs, 2, frames, 1), jnp.float32),
        ],
        compiler_params=pltpu.CompilerParams(vmem_limit_bytes=40 * 1024 * 1024),
        cost_estimate=pl.CostEstimate(
            flops=4 * frames * keys * width * 2,
            bytes_accessed=2 * (frames * width * 2 + keys * width * 2),
            transcendentals=frames * keys * (width // HEAD_DIM),
        ),
        name="attention_forward",
    )(packed, kv_all, kv_all, query_segs[:, None], key_segs[None, :])


def attention_backward_kernel(
    factor, q_ref, k_ref, v_ref, g_ref, o_ref, lse_ref, qs_ref, ks_ref, *rest
):
    *begin, dq_ref, dk_ref, dv_ref = rest
    step = pl.program_id(1)

    @pl.when(step == 0)
    def _():
        for index, total_ref in enumerate((dk_ref, dv_ref)):
            total_ref[...] = begin[index][...] if begin else jnp.zeros_like(total_ref)

    queries = q_ref[...]
    grads = g_ref[...]
    keys = k_ref[...]
    values = v_ref[...]
    lane = lax.broadcasted_iota(jnp.int32, queries.shape, 1)
    key_lane = lax.broadcasted_iota(jnp.int32, keys.shape, 1)
    allowed = qs_ref[...] == ks_ref[...]
    product = grads.astype(jnp.float32) * o_ref[...].astype(jnp.float32)
    dq = None
    for head in range(2):
        mine = (lane < HEAD_DIM) if head == 0 else (lane >= HEAD_DIM)
        key_mine = (key_lane < HEAD_DIM) if head == 0 else (key_lane >= HEAD_DIM)
        own_q = jnp.where(mine, queries, jnp.zeros_like(queries))
        own_g = jnp.where(mine, grads, jnp.zeros_like(grads))
        own_k = jnp.where(key_mine, keys, jnp.zeros_like(keys))
        delta = jnp.sum(jnp.where(mine, product, 0.0), axis=-1, keepdims=True)
        scores = lax.dot_general(
            own_q, keys, (((1,), (1,)), ((), ())), preferred_element_type=jnp.float32
        ) * factor
        chances = jnp.exp(jnp.where(allowed, scores, NEG) - lse_ref[0, head])
        prob_grad = lax.dot_general(
            own_g, values, (((1,), (1,)), ((), ())), preferred_element_type=jnp.float32
        )
        score_grad = (chances * (prob_grad - delta)).astype(jnp.bfloat16)
        part = jnp.dot(score_grad, own_k, preferred_element_type=jnp.float32)
        dq = part if dq is None else dq + part
        dk_ref[...] += lax.dot_general(
            score_grad, own_q, (((0,), (0,)), ((), ())), preferred_element_type=jnp.float32
        ) * factor
        dv_ref[...] += lax.dot_general(
            chances.astype(jnp.bfloat16), own_g, (((0,), (0,)), ((), ())),
            preferred_element_type=jnp.float32,
        )
    dq_ref[...] = (dq * factor).astype(dq_ref.dtype)


def attention_backward(packed, kv_all, grads, attended, lse, query_segs, key_segs, factor, begin=None):
    frames = packed.shape[0]
    keys = kv_all.shape[0]
    width = packed.shape[1] // 3
    pairs = width // 128
    rows = math.gcd(frames, 256)
    return pl.pallas_call(
        functools.partial(attention_backward_kernel, factor),
        grid=(pairs, frames // rows),
        in_specs=[
            pl.BlockSpec((rows, 128), lambda h, i: (i, h)),
            pl.BlockSpec((keys, 128), lambda h, i: (0, h)),
            pl.BlockSpec((keys, 128), lambda h, i: (0, pairs + h)),
            pl.BlockSpec((rows, 128), lambda h, i: (i, h)),
            pl.BlockSpec((rows, 128), lambda h, i: (i, h)),
            pl.BlockSpec((1, 2, rows, 1), lambda h, i: (h, 0, i, 0)),
            pl.BlockSpec((rows, 1), lambda h, i: (i, 0)),
            pl.BlockSpec((1, keys), lambda h, i: (0, 0)),
        ]
        + [pl.BlockSpec((keys, 128), lambda h, i: (0, h))] * (2 if begin else 0),
        out_specs=[
            pl.BlockSpec((rows, 128), lambda h, i: (i, h)),
            pl.BlockSpec((keys, 128), lambda h, i: (0, h)),
            pl.BlockSpec((keys, 128), lambda h, i: (0, h)),
        ],
        out_shape=[
            jax.ShapeDtypeStruct((frames, width), jnp.bfloat16),
            jax.ShapeDtypeStruct((keys, width), jnp.float32),
            jax.ShapeDtypeStruct((keys, width), jnp.float32),
        ],
        compiler_params=pltpu.CompilerParams(vmem_limit_bytes=48 * 1024 * 1024),
        cost_estimate=pl.CostEstimate(
            flops=10 * frames * keys * width * 2,
            bytes_accessed=4 * (frames * width * 2 + keys * width * 2),
            transcendentals=frames * keys * (width // HEAD_DIM),
        ),
        name="attention_backward",
    )(packed, kv_all, kv_all, grads, attended, lse, query_segs[:, None], key_segs[None, :], *(begin or ()))


CONV_STEP = 4


def conv_bands(kernel, per_group):
    groups = kernel.shape[1] // per_group
    steps = TAPS // CONV_STEP + 1
    bands = []
    for group in range(groups):
        own = kernel[:, group * per_group : (group + 1) * per_group]
        shifted = [
            jnp.pad(own, ((shift * per_group, (CONV_STEP - shift) * per_group), (0, 0)))
            for shift in range(CONV_STEP)
        ]
        band = jnp.concatenate(shifted, axis=1)
        bands.append(band.reshape(steps, CONV_STEP * per_group, CONV_STEP * per_group))
    return bands


def group_view(values, per_group):
    rows, frames, width = values.shape
    return [
        values[:, :, g * per_group : (g + 1) * per_group].reshape(
            rows, frames // CONV_STEP, CONV_STEP * per_group
        )
        for g in range(width // per_group)
    ]


def ungroup(parts, per_group):
    rows, blocks, _ = parts[0].shape
    return jnp.concatenate(
        [part.reshape(rows, blocks * CONV_STEP, per_group) for part in parts], axis=2
    )


CONV_DIMS = ("NWC", "WIO", "NWC")


def conv_forward(views, bands):
    half = TAPS // 2 // CONV_STEP
    return [
        lax.conv_general_dilated(
            view, band, (1,), [(half, half)], dimension_numbers=CONV_DIMS,
            preferred_element_type=jnp.float32,
        )
        for view, band in zip(views, bands)
    ]


def conv_back(grad_views, bands):
    half = TAPS // 2 // CONV_STEP
    return [
        lax.conv_general_dilated(
            view, jnp.transpose(band[::-1], (0, 2, 1)), (1,), [(half, half)],
            dimension_numbers=CONV_DIMS, preferred_element_type=jnp.float32,
        )
        for view, band in zip(grad_views, bands)
    ]


def conv_taps_grad(views, grad_views, per_group):
    half = TAPS // 2 // CONV_STEP
    results = []
    for view, grad in zip(views, grad_views):
        band = lax.conv_general_dilated(
            view, grad, (1,), [(half, half)],
            dimension_numbers=("CWN", "IWO", "WNC"),
            preferred_element_type=jnp.float32,
        )
        flat = band.reshape(-1, CONV_STEP * per_group)
        total = None
        for shift in range(CONV_STEP):
            part = flat[
                shift * per_group : (shift + TAPS) * per_group,
                shift * per_group : (shift + 1) * per_group,
            ]
            total = part if total is None else total + part
        results.append(total)
    return jnp.concatenate(results, axis=1)


def to_column(vector, width):
    return jnp.pad(vector[:, None], ((0, 0), (0, width - 1)))


def per_device_pairs(
    signal, frame_segment_index, conv_weight, conv_bias, norm1_gain, qkv_weight, out_weight,
    norm2_gain, up_weight, down_weight, cotangent,
):
    micro_count, frames, width = signal.shape
    bf16, f32 = jnp.bfloat16, jnp.float32
    per_group = width // GROUPS
    dp_count = lax.axis_size("dp")
    factor = 1.0 / math.sqrt(HEAD_DIM)
    sec = lax.axis_index("section")
    dp = lax.axis_index("dp")
    seq = lax.axis_index("seq")
    x, y = seq % 2, seq // 2
    sec0, x0 = sec == 0, x == 0
    row_frames = 4 * frames
    half_frames = 2 * frames
    both = ("section", "seq")

    block_width = width // 8
    rows_here = conv_weight.shape[0]
    conv_low = conv_weight.astype(bf16).reshape(rows_here, 8, block_width)
    bias_low = jnp.pad(conv_bias.astype(bf16), (0, block_width - conv_bias.shape[0]))
    bias_rows = jnp.pad(
        jnp.broadcast_to(bias_low[None, None, :], (1, 8, block_width)), ((0, 15), (0, 0), (0, 0))
    )
    conv_send = jnp.transpose(jnp.concatenate([conv_low, bias_rows], axis=0), (1, 0, 2))
    conv_got = lax.all_to_all(conv_send, both, 0, 0, tiled=True)

    own_half = jnp.where(sec0, signal[:, :, : width // 2], signal[:, :, width // 2 :])
    sig_send = jnp.transpose(own_half.reshape(micro_count, frames, 4, block_width), (2, 0, 1, 3))
    sig_got = lax.all_to_all(sig_send, "seq", 0, 0, tiled=True)
    sig_all = jnp.transpose(sig_got, (1, 0, 2, 3)).reshape(micro_count, row_frames, block_width)

    conv_all = place_dp(conv_got, dp)
    conv_all = conv_all.reshape(dp_count, 2, 4, rows_here + 16, block_width)
    conv_all = jnp.transpose(conv_all, (1, 0, 2, 3, 4))
    bias_all = conv_all[:, :, :, rows_here, : conv_bias.shape[0]].reshape(width)
    bias_own = lax.dynamic_slice_in_dim(bias_all, (sec * 4 + seq) * block_width, block_width, 0)
    kernel_own = conv_all[:, :, :, :rows_here].reshape(TAPS * per_group, block_width)
    bands = conv_bands(kernel_own, per_group)

    in_rows = qkv_weight.shape[1]
    unit = down_weight.shape[1] // 4
    qkv_view = qkv_weight[0].astype(bf16).reshape(in_rows, -1, 2, HEAD_DIM)
    qkv_parity = [qkv_view[:, :, p].reshape(in_rows, -1) for p in range(2)]
    up_view = up_weight[0].astype(bf16).reshape(in_rows, -1, 2, 2, 2, unit)
    up_parity = [
        jnp.transpose(up_view[:, :, p], (0, 3, 1, 2, 4)).reshape(in_rows, -1) for p in range(2)
    ]
    qkv_cols, up_cols = qkv_parity[0].shape[1], up_parity[0].shape[1]
    col_one = to_column(norm1_gain[0].astype(bf16), 128)
    col_two = to_column(norm2_gain[0].astype(bf16), 128)
    cut = qkv_cols + 128
    keep_cols, send_cols = [
        jnp.concatenate([a, col_one, b, col_two], axis=1)
        for a, b in zip(choose(x0, *qkv_parity), choose(x0, *up_parity))
    ]
    row_sets = choose(x0, keep_cols, swap_x(send_cols))
    out_low = out_weight[0].astype(bf16)
    down_low = down_weight[0].astype(bf16).reshape(2, 2, unit, width)
    out_at, up_at = cut, cut + width // 2
    two_at = up_at + up_cols
    down_at = two_at + 128
    row_parts = [
        jnp.concatenate(
            [
                row_sets[h][:, :cut],
                out_low[:, h * width // 2 : (h + 1) * width // 2],
                row_sets[h][:, cut:],
                down_low[h, 0],
                down_low[h, 1],
            ],
            axis=1,
        )
        for h in range(2)
    ]
    keep, send = choose(sec0, *row_parts)
    layer_pieces = choose(sec0, keep, swap_section(send))
    gathered = [gather_rows(layer_pieces[layer]) for layer in range(2)]

    def views(whole):
        w_out = jnp.transpose(
            whole[:, out_at:up_at].reshape(-1, 2, in_rows, width // 2), (0, 2, 1, 3)
        ).reshape(-1, width)
        gain_one = whole[:, qkv_cols].astype(f32)[None, :]
        gain_two = whole[:, two_at].astype(f32)[None, :]
        w_up = [whole[:, up_at + part * width : up_at + (part + 1) * width] for part in range(2)]
        w_down = [whole[:, down_at + part * width : down_at + (part + 1) * width] for part in range(2)]
        return gain_one, whole[:, :qkv_cols], w_out, gain_two, w_up, w_down

    layer_weights = []

    picked = jnp.where(sec0, cotangent[0], cotangent[1])
    across = [(s * 4 + 2 * yy + xx, yy * 4 + 2 * s + xx) for s in range(2) for yy in range(2) for xx in range(2)]
    cot_own = lax.ppermute(picked, both, across)
    cot_other = swap_x(cot_own)
    cot_pair = choose(x0, cot_own, cot_other)
    top_grad = jnp.concatenate(cot_pair, axis=0).astype(f32)

    segment_row = jnp.where(y == 0, frame_segment_index[0], frame_segment_index[1])
    seg_pair = choose(sec0, segment_row[:half_frames], segment_row[half_frames:])
    query_segs = seg_pair[0]
    key_segs = jnp.concatenate(seg_pair)

    sig_views = group_view(sig_all, per_group)
    conv_pre = ungroup(conv_forward(sig_views, bands), per_group) + bias_own.astype(f32)
    stream = (sig_all.astype(f32) + smooth(conv_pre)).astype(bf16)
    slope = gelu_slope(conv_pre).astype(bf16)
    stream_send = stream.reshape(2, 2, half_frames, block_width)
    stream_send = jnp.transpose(stream_send, (1, 0, 2, 3))
    stream_send = jnp.repeat(stream_send.reshape(4, half_frames, block_width), 2, axis=0)
    stream_got = lax.all_to_all(stream_send, both, 0, 0, tiled=True)
    layer_in = jnp.transpose(stream_got, (1, 0, 2)).reshape(half_frames, width).astype(f32)

    chunks = 2
    rows = half_frames // chunks
    layer_in = [layer_in[c * rows : (c + 1) * rows] for c in range(chunks)]
    chunk_segs = [query_segs[c * rows : (c + 1) * rows] for c in range(chunks)]
    kept = []
    for layer in range(2):
        layer_in, whole = after(layer_in, gathered[layer])
        layer_weights.append(views(whole))
        gain_one, w_qkv, w_out, gain_two, w_up, w_down = layer_weights[layer]
        normed_one, packed, kv_own, kv_other = [], [], [], []
        for c in range(chunks):
            centred, inv = norm_stats(layer_in[c])
            normed_one.append((centred * inv * gain_one).astype(bf16))
            packed.append(jnp.dot(normed_one[c], w_qkv, preferred_element_type=f32).astype(bf16))
            kv_own.append(packed[c][:, width // 2 :])
            kv_other.append(swap_section(kv_own[c]))
        kv_all = jnp.concatenate(kv_own + kv_other, axis=0)
        attended, lse, resid_two, normed_two, hidden, hidden_slope, result = [], [], [], [], [], [], []
        low = None
        for c in range(chunks):
            own = packed[c]
            if low is not None:
                low, own = after(low, own)
                resid_two.append(layer_in[c - 1] + pair_sum(low))
            mixed, log_total = attention_forward(own, kv_all, chunk_segs[c], key_segs, factor)
            attended.append(mixed)
            lse.append(log_total)
            low = jnp.dot(mixed, w_out, preferred_element_type=f32).astype(bf16)
        resid_two.append(layer_in[-1] + pair_sum(low))
        low, lows = None, []
        for c in range(chunks):
            values = resid_two[c]
            if low is not None:
                low, values = after(low, values)
                lows.append(low)
            centred, inv = norm_stats(values)
            normed_two.append((centred * inv * gain_two).astype(bf16))
            down_sum, own_hidden, own_slope = None, [], []
            for part in range(2):
                hidden_pre = jnp.dot(normed_two[c], w_up[part], preferred_element_type=f32)
                own_hidden.append(smooth(hidden_pre).astype(bf16))
                own_slope.append(gelu_slope(hidden_pre).astype(bf16))
            for part in range(2):
                term = jnp.dot(own_hidden[part], w_down[part], preferred_element_type=f32)
                down_sum = term if down_sum is None else down_sum + term
            hidden.append(own_hidden)
            hidden_slope.append(own_slope)
            low = down_sum.astype(bf16)
        lows.append(low)

        def joined(members):
            return jnp.concatenate(members, axis=0)

        resid_two_last = resid_two
        kept.append((layer_in, normed_one, packed, kv_all, attended, lse, resid_two, normed_two, hidden, hidden_slope))
        if layer == 0:
            result = [member + pair_sum(low) for member, low in zip(resid_two, lows)]
            layer_in = [member.astype(bf16).astype(f32) for member in result]

    def outer(left, right):
        return lax.dot_general(
            left, right, (((0,), (0,)), ((), ())), preferred_element_type=f32
        ).astype(bf16)

    def back(left, right):
        return lax.dot_general(left, right, (((1,), (1,)), ((), ())), preferred_element_type=f32)

    grad_out = [top_grad[c * rows : (c + 1) * rows] for c in range(chunks)]
    attn_members, scattered = [], []
    for layer in (1, 0):
        gain_one, w_qkv, w_out, gain_two, w_up, w_down = layer_weights[layer]
        (layer_in, normed_one, packed, kv_all, attended, lse, resid_two, normed_two, hidden, hidden_slope) = kept[layer]
        branch = [member.astype(bf16) for member in grad_out]
        pre_grad, sums, low = [], [], None
        for c in range(chunks):
            own = branch[c]
            if low is not None:
                low, own = after(low, own)
                sums.append(pair_sum(low))
            own_pre, part_sum = [], None
            for part in range(2):
                own_pre.append((back(own, w_down[part]) * hidden_slope[c][part].astype(f32)).astype(bf16))
            for part in range(2):
                term = back(own_pre[part], w_up[part])
                part_sum = term if part_sum is None else part_sum + term
            pre_grad.append(own_pre)
            low = part_sum.astype(bf16)
        sums.append(pair_sum(low))
        whole_pre = [jnp.concatenate([pre_grad[c][p] for c in range(chunks)]) for p in range(2)]
        whole_hidden = [jnp.concatenate([hidden[c][p] for c in range(chunks)]) for p in range(2)]
        whole_branch, whole_two = jnp.concatenate(branch), jnp.concatenate(normed_two)
        ff_members = [
            outer(whole_two, whole_pre[0]), outer(whole_two, whole_pre[1]),
            outer(whole_hidden[0], whole_branch), outer(whole_hidden[1], whole_branch),
        ]
        if layer == 1:
            ff_members.append(jnp.zeros((width, 128), bf16))
        partial = jnp.concatenate(attn_members + ff_members, axis=1)
        if layer == 0:
            sums, partial = after(sums, partial)
        scattered.append(scatter_rows(partial))
        resid_grad, attn_branch, dq, gain_two_grad = [], [], [], None
        dkv = None
        for c in range(chunks):
            in_part, gain_part = norm_back(resid_two[c], gain_two, sums[c])
            gain_two_grad = gain_part if gain_two_grad is None else gain_two_grad + gain_part
            resid_grad.append(in_part + grad_out[c])
            attn_branch.append(resid_grad[c].astype(bf16))
            attended_grad = back(attn_branch[c], w_out).astype(bf16)
            own_dq, *dkv = attention_backward(
                packed[c], kv_all, attended_grad, attended[c], lse[c], chunk_segs[c], key_segs, factor,
                None if c == 0 else dkv,
            )
            dq.append(own_dq)
        if layer == 0:
            dkv, scattered[0] = after(dkv, scattered[0])
        dkv = jnp.concatenate(dkv, axis=1)
        other_dkv = swap_section(dkv[half_frames:].astype(bf16))
        dkv_own = (dkv[:half_frames] + other_dkv.astype(f32)).astype(bf16)
        packed_grad, sums, low = [], [], None
        for c in range(chunks):
            packed_grad.append(jnp.concatenate([dq[c], dkv_own[c * rows : (c + 1) * rows]], axis=1))
            own = packed_grad[c]
            if low is not None:
                low, own = after(low, own)
                sums.append(pair_sum(low))
            low = back(own, w_qkv).astype(bf16)
        sums.append(pair_sum(low))
        next_grad, gain_one_grad = [], None
        for c in range(chunks):
            in_part, gain_part = norm_back(layer_in[c], gain_one, sums[c])
            gain_one_grad = gain_part if gain_one_grad is None else gain_one_grad + gain_part
            next_grad.append((resid_grad[c] + in_part).astype(bf16))
        whole_one, whole_pg, whole_att, whole_ab = [
            jnp.concatenate(m) for m in (normed_one, packed_grad, attended, attn_branch)
        ]
        grad_out_weight = jnp.transpose(
            outer(whole_att, whole_ab).reshape(-1, in_rows, 2, width // 2), (0, 2, 1, 3)
        ).reshape(-1, width // 2)
        gain_grads = jnp.stack([gain_one_grad, gain_two_grad], axis=1).astype(bf16)
        gain_grads = jnp.pad(gain_grads, ((0, 0), (0, 126)))
        attn_members = [outer(whole_one, whole_pg), gain_grads, grad_out_weight]
        grad_out = [member.astype(f32) for member in next_grad]
    grad_in_low = jnp.concatenate(next_grad)
    scattered.append(scatter_rows(jnp.concatenate(attn_members, axis=1)))
    grad_in_low, lows = after(grad_in_low, lows)
    output = jnp.concatenate([member + pair_sum(low) for member, low in zip(resid_two_last, lows)])

    lig_send = jnp.transpose(grad_in_low.reshape(half_frames, 8, block_width), (1, 0, 2))
    lig_got = lax.all_to_all(lig_send, both, 0, 0, tiled=True).reshape(2, 2, 2, half_frames, block_width)
    lig = jnp.transpose(lig_got[:, :, 0], (1, 0, 2, 3)).reshape(micro_count, row_frames, block_width)
    conv_grad = (lig.astype(f32) * slope.astype(f32)).astype(bf16)
    grad_views = group_view(conv_grad, per_group)
    back = ungroup(conv_back(grad_views, bands), per_group)
    grad_signal = (lig.astype(f32) + back).astype(bf16)
    gs_send = jnp.transpose(
        grad_signal.reshape(micro_count, 4, frames, block_width), (1, 0, 2, 3)
    )
    gs_send = jnp.concatenate([gs_send, gs_send], axis=0)
    gs_got = lax.all_to_all(gs_send, both, 0, 0, tiled=True)
    gs_rows = jnp.transpose(gs_got, (1, 2, 0, 3)).reshape(micro_count, frames, width).astype(f32)

    taps_grad = conv_taps_grad(sig_views, grad_views, per_group)
    bias_grad = jnp.sum(conv_grad.astype(f32), axis=(0, 1))
    taps_view = jnp.transpose(
        taps_grad.reshape(2, dp_count, 4, rows_here, block_width), (1, 0, 2, 3, 4)
    ).astype(bf16)
    bias_view = jnp.pad(
        jnp.broadcast_to(bias_grad.astype(bf16), (dp_count, 2, 4, 1, block_width)),
        ((0, 0), (0, 0), (0, 0), (0, 15), (0, 0)),
    )
    taps_send = jnp.concatenate([taps_view, bias_view], axis=3)
    taps_send, scattered[1] = after(taps_send, scattered[1])
    taps_sum = sum_dp(taps_send, dp)
    taps_got = lax.all_to_all(
        taps_sum.reshape(8, rows_here + 16, block_width), both, 0, 0, tiled=True
    )
    conv_weight_grad = jnp.transpose(taps_got[:, :rows_here], (1, 0, 2)).reshape(rows_here, width).astype(f32)
    bias_count = conv_bias.shape[0]
    conv_bias_grad = lax.dynamic_slice_in_dim(
        taps_got[:, rows_here].reshape(width),
        ((sec * dp_count + dp) * 4 + seq) * bias_count,
        bias_count,
        0,
    ).astype(f32)

    own_block = jnp.where(x0, output[:frames], output[frames:])
    row_block = lax.ppermute(own_block, both, across)
    other_row = swap_section(row_block)
    output_rows = jnp.stack(choose(sec0, row_block, other_row))
    ends = jnp.where(sec0, gs_rows, output_rows)[None]

    attn_cols = up_at
    attn_sums = (scattered[2], scattered[1][:, :attn_cols])
    ff_sums = (scattered[1][:, attn_cols:], scattered[0][:, :-128])
    half_sets = []
    for sums in (attn_sums, ff_sums):
        keep, send = choose(sec0, *sums)
        half_sets.append(choose(sec0, keep, swap_section(send)))
    attn_sets, ff_sets = half_sets
    out_grad = jnp.concatenate([member[:, out_at:up_at] for member in attn_sets], axis=1).astype(f32)[None]
    down_grad = jnp.concatenate(
        [member[:, up_cols + at : up_cols + at + width] for member in ff_sets for at in (0, width)],
        axis=0,
    ).astype(f32)[None]

    def finish_columns(first, second, gains):
        keep, send = choose(x0, first, second)
        return keep[:, : keep.shape[1] - gains], keep[:, keep.shape[1] - gains :], choose(x0, keep, swap_x(send))

    qkv_own, gain_own, qkv_sets = finish_columns(attn_sets[0][:, :cut], attn_sets[1][:, :cut], 128)
    _, _, up_sets = finish_columns(ff_sets[0][:, :up_cols], ff_sets[1][:, :up_cols], 0)
    norm1_grad = gain_own[:, 0].astype(f32)[None]
    norm2_grad = gain_own[:, 1].astype(f32)[None]
    qkv_grad = jnp.stack(
        [member[:, :qkv_cols].reshape(in_rows, -1, HEAD_DIM) for member in qkv_sets], axis=2
    ).reshape(in_rows, -1).astype(f32)[None]
    up_grad = jnp.stack(
        [
            jnp.transpose(member.reshape(in_rows, 2, -1, 2, unit), (0, 2, 3, 1, 4))
            for member in up_sets
        ],
        axis=2,
    ).reshape(in_rows, -1).astype(f32)[None]
    return (ends, conv_weight_grad, conv_bias_grad, norm1_grad, qkv_grad, out_grad, norm2_grad, up_grad, down_grad)


def solution(mesh):
    placed = (
        P("dp", "seq", None),
        P("dp", None),
        P(("section", "dp", "seq"), None),
        P(("section", "dp", "seq")),
        P("section", ("dp", "seq")),
        P("section", ("dp", "seq"), None),
        P("section", ("dp", "seq"), None),
        P("section", ("dp", "seq")),
        P("section", ("dp", "seq"), None),
        P("section", ("dp", "seq"), None),
        P("dp", "seq", None),
    )

    def step(*arrays):
        pairs = mesh.shape["seq"] == 4 and mesh.shape["section"] == 2 and arrays[0].shape[0] == 2
        return (per_device_pairs if pairs else per_device)(*arrays)

    return jax.shard_map(
        step,
        mesh=mesh,
        in_specs=placed,
        out_specs=(
            P("section", "dp", "seq", None),
            P(("section", "dp", "seq"), None),
            P(("section", "dp", "seq")),
            P("section", ("dp", "seq")),
            P("section", ("dp", "seq"), None),
            P("section", ("dp", "seq"), None),
            P("section", ("dp", "seq")),
            P("section", ("dp", "seq"), None),
            P("section", ("dp", "seq"), None),
        ),
        check_vma=False,
    )
```

```python
import functools
import math

import jax
import jax.numpy as jnp
from jax import lax
from jax.experimental import pallas as pl
from jax.experimental.pallas import tpu as pltpu
from jax.sharding import PartitionSpec as P

HEAD_DIM = 64
GROUPS = 16
TAPS = 128


EPS = 1e-05
NEG = -1e30


def padded_2(block, sides, width):
    for axis, dim in sides:
        count = lax.axis_size(axis)
        forward = [(i, i + 1) for i in range(count - 1)]
        backward = [(target, source) for source, target in forward]
        low = lax.ppermute(
            lax.slice_in_dim(block, block.shape[dim] - width, None, axis=dim), axis, forward
        )
        high = lax.ppermute(lax.slice_in_dim(block, 0, width, axis=dim), axis, backward)
        block = jnp.concatenate([low, block, high], axis=dim)
    return block


def from_behind(value, axis, steps):
    count = lax.axis_size(axis)
    first, last = (max(0, -steps), min(count, count - steps))
    return lax.ppermute(value, axis, [(source, source + steps) for source in range(first, last)])


def normalize(values, gain):
    average = jnp.mean(values, axis=-1, keepdims=True)
    centred = values - average
    spread = jnp.mean(centred * centred, axis=-1, keepdims=True)
    return centred * lax.rsqrt(spread + EPS) * gain


def smooth(values):
    return jax.nn.gelu(values, approximate=False)


def conv_taps(padded, kernel, frames):
    width_all = padded.shape[1]
    per_group = width_all // GROUPS
    tap_step = math.gcd(TAPS, 16)
    weight_view = kernel.reshape(TAPS, per_group, GROUPS, per_group)
    running = jnp.zeros((frames, GROUPS, per_group), jnp.float32)
    for first_tap in range(0, TAPS, tap_step):
        windows = jnp.stack(
            [padded[first_tap + offset : first_tap + offset + frames] for offset in range(tap_step)]
        )
        windows = windows.reshape(tap_step, frames, GROUPS, per_group)
        running = running + jnp.einsum(
            "jtgc,jcgo->tgo",
            windows,
            weight_view[first_tap : first_tap + tap_step],
            preferred_element_type=jnp.float32,
        )
    return running.reshape(frames, width_all)


def conv_input_grad(grad_pad, kernel, frames):
    width_all = grad_pad.shape[1]
    per_group = width_all // GROUPS
    tap_step = math.gcd(TAPS, 16)
    weight_view = kernel.reshape(TAPS, per_group, GROUPS, per_group)
    running = jnp.zeros((frames, GROUPS, per_group), jnp.float32)
    for first_tap in range(0, TAPS, tap_step):
        back_windows = jnp.stack(
            [
                grad_pad[TAPS - first_tap - offset : TAPS - first_tap - offset + frames]
                for offset in range(tap_step)
            ]
        )
        back_windows = back_windows.reshape(tap_step, frames, GROUPS, per_group)
        running = running + jnp.einsum(
            "jtgo,jcgo->tgc",
            back_windows,
            weight_view[first_tap : first_tap + tap_step],
            preferred_element_type=jnp.float32,
        )
    return running.reshape(frames, width_all)


def conv_kernel_grad(padded_all, grad_all):
    step_count, frames, width_all = grad_all.shape
    per_group = width_all // GROUPS
    tap_step = math.gcd(TAPS, 16)
    grad_view = grad_all.reshape(step_count * frames, GROUPS, per_group)
    kernel_parts = []
    for first_tap in range(0, TAPS, tap_step):
        windows = jnp.stack(
            [
                padded_all[:, first_tap + offset : first_tap + offset + frames]
                for offset in range(tap_step)
            ]
        )
        windows = windows.reshape(tap_step, step_count * frames, GROUPS, per_group)
        kernel_parts.append(
            jnp.einsum("jtgc,tgo->jcgo", windows, grad_view, preferred_element_type=jnp.float32)
        )
    return jnp.concatenate(kernel_parts, axis=0).reshape(TAPS * per_group, width_all)


def score_block(query_heads, key_block, query_segs, key_segs, factor):
    scores = (
        jnp.einsum("qhd,khd->hqk", query_heads, key_block, preferred_element_type=jnp.float32)
        * factor
    )
    allowed = (query_segs[:, None] == key_segs[None, :])[None]
    return (scores, allowed)


def front(layer_in, weights, kernel, conv_shift, first_section):
    frames, width_all = layer_in.shape
    padded = padded_2(layer_in, (("seq", 0),), TAPS // 2)
    conv_pre = lax.cond(
        first_section,
        lambda: conv_taps(padded, kernel, frames) + conv_shift.astype(jnp.float32),
        lambda: jnp.zeros((frames, width_all), jnp.float32),
    )
    conv_val, conv_pull = jax.vjp(smooth, conv_pre)
    resid_one = layer_in.astype(jnp.float32) + conv_val
    normed_val, norm_pull = jax.vjp(normalize, resid_one, weights[0].astype(jnp.float32))
    normed_one = normed_val.astype(jnp.bfloat16)
    packed = jnp.dot(normed_one, weights[1], preferred_element_type=jnp.float32).astype(
        jnp.bfloat16
    )
    return (padded, conv_pull, resid_one, norm_pull, normed_one, packed)


def tail(resid_one, attn_low, weights):
    resid_two = resid_one + jnp.dot(attn_low, weights[2], preferred_element_type=jnp.float32)
    normed_val, norm_pull = jax.vjp(normalize, resid_two, weights[3].astype(jnp.float32))
    normed_two = normed_val.astype(jnp.bfloat16)
    hidden_pre = jnp.dot(normed_two, weights[4], preferred_element_type=jnp.float32)
    hidden_val, gelu_pull = jax.vjp(smooth, hidden_pre)
    hidden_low = hidden_val.astype(jnp.bfloat16)
    result = resid_two + jnp.dot(hidden_low, weights[5], preferred_element_type=jnp.float32)
    return (result, norm_pull, normed_two, gelu_pull, hidden_low)


def key_loop(keys_all, values_all, segment_row, head_count, visit, initial):
    total_rows = keys_all.shape[0]
    block_rows = math.gcd(total_rows, 512)

    def one_block(block_index, running):
        offset = block_index * block_rows
        key_block = lax.dynamic_slice_in_dim(keys_all, offset, block_rows, 0).reshape(
            block_rows, head_count, HEAD_DIM
        )
        value_block = lax.dynamic_slice_in_dim(values_all, offset, block_rows, 0).reshape(
            block_rows, head_count, HEAD_DIM
        )
        key_segs = lax.dynamic_slice_in_dim(segment_row, offset, block_rows, 0)
        return visit(running, key_block, value_block, key_segs)

    return lax.fori_loop(0, total_rows // block_rows, one_block, initial)


def layer_forward(
    layer_in, segment_row, weights, kernel, conv_shift, first_section, my_start, factor
):
    frames, width_all = layer_in.shape
    head_count = width_all // HEAD_DIM
    padded, conv_pull, resid_one, norm_pull, normed_one, packed = front(
        layer_in, weights, kernel, conv_shift, first_section
    )
    query_heads = packed[:, :width_all].reshape(frames, head_count, HEAD_DIM)
    query_segs = lax.dynamic_slice_in_dim(segment_row, my_start, frames, 0)
    initial = (
        jnp.full((head_count, frames), NEG, jnp.float32),
        jnp.zeros((head_count, frames), jnp.float32),
        jnp.zeros((head_count, frames, HEAD_DIM), jnp.float32),
    )
    key_piece = lax.all_gather(packed[:, width_all : 2 * width_all], "seq", axis=0, tiled=True)
    value_piece = lax.all_gather(packed[:, 2 * width_all :], "seq", axis=0, tiled=True)
    piece_rows = key_piece.shape[0]
    block_rows = math.gcd(piece_rows, 512)

    def one_block(block_index, running):
        run_max, run_sum, run_acc = running
        offset = block_index * block_rows
        key_block = lax.dynamic_slice_in_dim(key_piece, offset, block_rows, 0).reshape(
            block_rows, head_count, HEAD_DIM
        )
        value_block = lax.dynamic_slice_in_dim(value_piece, offset, block_rows, 0).reshape(
            block_rows, head_count, HEAD_DIM
        )
        key_segs = lax.dynamic_slice_in_dim(segment_row, offset, block_rows, 0)
        scores, allowed = score_block(query_heads, key_block, query_segs, key_segs, factor)
        masked = jnp.where(allowed, scores, NEG)
        new_max = jnp.maximum(run_max, jnp.max(masked, axis=-1))
        weights_now = jnp.where(allowed, jnp.exp(masked - new_max[..., None]), 0.0)
        rescale = jnp.exp(run_max - new_max)
        run_sum = run_sum * rescale + jnp.sum(weights_now, axis=-1)
        run_acc = run_acc * rescale[..., None] + jnp.einsum(
            "hqk,khd->hqd",
            weights_now.astype(jnp.bfloat16),
            value_block,
            preferred_element_type=jnp.float32,
        )
        return (new_max, run_sum, run_acc)

    run_max, run_sum, run_acc = lax.fori_loop(0, piece_rows // block_rows, one_block, initial)
    log_total = run_max + jnp.log(run_sum)
    mixture = run_acc / run_sum[..., None]
    attn_low = jnp.transpose(mixture, (1, 0, 2)).reshape(frames, width_all).astype(jnp.bfloat16)
    result, norm_two_pull, normed_two, gelu_pull, hidden_low = tail(resid_one, attn_low, weights)
    kept = (
        padded,
        conv_pull,
        norm_pull,
        normed_one,
        packed,
        log_total,
        mixture,
        attn_low,
        norm_two_pull,
        normed_two,
        gelu_pull,
        hidden_low,
        segment_row,
    )
    return (result, kept)


def layer_backward(kept, grad_out, weights, kernel, first_section, my_start, factor):
    (
        padded,
        conv_pull,
        norm_one_pull,
        normed_one,
        packed,
        log_total,
        mixture,
        attn_low,
        norm_two_pull,
        normed_two,
        gelu_pull,
        hidden_low,
        segment_row,
    ) = kept
    frames, width_all = normed_one.shape
    head_count = width_all // HEAD_DIM
    query_heads = packed[:, :width_all].reshape(frames, head_count, HEAD_DIM)
    key_local = packed[:, width_all : 2 * width_all]
    value_local = packed[:, 2 * width_all :]
    query_segs = lax.dynamic_slice_in_dim(segment_row, my_start, frames, 0)
    keys_all, values_all = (
        lax.all_gather(key_local, "seq", axis=0, tiled=True),
        lax.all_gather(value_local, "seq", axis=0, tiled=True),
    )

    def chances_for(key_block, key_segs):
        scores, allowed = score_block(query_heads, key_block, query_segs, key_segs, factor)
        return jnp.where(
            allowed, jnp.exp(jnp.where(allowed, scores, NEG) - log_total[..., None]), 0.0
        )

    branch_grad = grad_out.astype(jnp.bfloat16)
    hidden_grad = jnp.einsum(
        "to,io->ti", branch_grad, weights[5], preferred_element_type=jnp.float32
    )
    pre_grad = gelu_pull(hidden_grad)[0].astype(jnp.bfloat16)
    normed_two_grad = jnp.einsum(
        "tf,if->ti", pre_grad, weights[4], preferred_element_type=jnp.float32
    )
    resid_two_grad, grad_gain_two = norm_two_pull(normed_two_grad)
    resid_two_grad = resid_two_grad + grad_out
    attn_branch_grad = resid_two_grad.astype(jnp.bfloat16)
    attended_grad = jnp.einsum(
        "to,io->ti", attn_branch_grad, weights[2], preferred_element_type=jnp.float32
    ).astype(jnp.bfloat16)
    dout_heads = attended_grad.reshape(frames, head_count, HEAD_DIM)
    delta_rows = jnp.einsum("qhd,hqd->hq", dout_heads.astype(jnp.float32), mixture)

    def visit_query(running, key_block, value_block, key_segs):
        chances = chances_for(key_block, key_segs)
        prob_grad = jnp.einsum(
            "qhd,khd->hqk", dout_heads, value_block, preferred_element_type=jnp.float32
        )
        score_grad = (chances * (prob_grad - delta_rows[..., None])).astype(jnp.bfloat16)
        return running + jnp.einsum(
            "hqk,khd->qhd", score_grad, key_block, preferred_element_type=jnp.float32
        )

    grad_query = (
        key_loop(
            keys_all,
            values_all,
            segment_row,
            head_count,
            visit_query,
            jnp.zeros((frames, head_count, HEAD_DIM), jnp.float32),
        )
        * factor
    )
    row_stats = (
        lax.all_gather(log_total, "seq", axis=1, tiled=True),
        lax.all_gather(delta_rows, "seq", axis=1, tiled=True),
    )
    key_heads = key_local.reshape(frames, head_count, HEAD_DIM)
    value_heads = value_local.reshape(frames, head_count, HEAD_DIM)
    start_acc = (
        jnp.zeros((frames, head_count, HEAD_DIM), jnp.float32),
        jnp.zeros((frames, head_count, HEAD_DIM), jnp.float32),
    )
    query_piece = lax.all_gather(packed[:, :width_all], "seq", axis=0, tiled=True)
    dout_piece = lax.all_gather(attended_grad, "seq", axis=0, tiled=True)
    piece_rows = query_piece.shape[0]
    block_rows = math.gcd(piece_rows, 512)

    def one_block(block_index, running):
        key_acc, value_acc = running
        offset = block_index * block_rows
        query_block = lax.dynamic_slice_in_dim(query_piece, offset, block_rows, 0).reshape(
            block_rows, head_count, HEAD_DIM
        )
        dout_block = lax.dynamic_slice_in_dim(dout_piece, offset, block_rows, 0).reshape(
            block_rows, head_count, HEAD_DIM
        )
        seg_block = lax.dynamic_slice_in_dim(segment_row, offset, block_rows, 0)
        total_block = lax.dynamic_slice_in_dim(row_stats[0], offset, block_rows, 1)
        delta_block = lax.dynamic_slice_in_dim(row_stats[1], offset, block_rows, 1)
        scores, allowed = score_block(query_block, key_heads, seg_block, query_segs, factor)
        chances = jnp.where(
            allowed, jnp.exp(jnp.where(allowed, scores, NEG) - total_block[..., None]), 0.0
        )
        prob_grad = jnp.einsum(
            "qhd,khd->hqk", dout_block, value_heads, preferred_element_type=jnp.float32
        )
        score_grad = (chances * (prob_grad - delta_block[..., None])).astype(jnp.bfloat16)
        key_acc = (
            key_acc
            + jnp.einsum(
                "hqk,qhd->khd", score_grad, query_block, preferred_element_type=jnp.float32
            )
            * factor
        )
        value_acc = value_acc + jnp.einsum(
            "hqk,qhd->khd",
            chances.astype(jnp.bfloat16),
            dout_block,
            preferred_element_type=jnp.float32,
        )
        return (key_acc, value_acc)

    key_acc, value_acc = lax.fori_loop(0, piece_rows // block_rows, one_block, start_acc)
    grad_key = key_acc.reshape(frames, width_all)
    grad_value = value_acc.reshape(frames, width_all)
    packed_grad = jnp.concatenate(
        [grad_query.reshape(frames, width_all), grad_key, grad_value], axis=1
    ).astype(jnp.bfloat16)
    normed_one_grad = jnp.einsum(
        "tj,ij->ti", packed_grad, weights[1], preferred_element_type=jnp.float32
    )
    resid_one_grad, grad_gain_one = norm_one_pull(normed_one_grad)
    resid_one_grad = resid_one_grad + resid_two_grad
    conv_grad = jnp.where(first_section, conv_pull(resid_one_grad)[0], 0.0).astype(jnp.bfloat16)
    grad_pad = padded_2(conv_grad, (("seq", 0),), TAPS // 2)
    back_sum = lax.cond(
        first_section,
        lambda: conv_input_grad(grad_pad, kernel, frames),
        lambda: jnp.zeros((frames, width_all), jnp.float32),
    )
    grad_in = resid_one_grad + back_sum
    products = (
        normed_one,
        packed_grad,
        attn_low,
        attn_branch_grad,
        normed_two,
        pre_grad,
        hidden_low,
        branch_grad,
        padded,
        conv_grad,
    )
    return (grad_in, (grad_gain_one, grad_gain_two), products)


def per_device(
    signal,
    frame_segment_index,
    conv_weight,
    conv_bias,
    norm1_gain,
    qkv_weight,
    out_weight,
    norm2_gain,
    up_weight,
    down_weight,
    cotangent,
):
    micro_count, frames, width_all = signal.shape
    factor = 1.0 / math.sqrt(HEAD_DIM)
    first_section = lax.axis_index("section") == 0
    my_start = lax.axis_index("seq") * frames
    gathered = (
        lax.all_gather(norm1_gain.astype(jnp.bfloat16), ("dp", "seq"), axis=1, tiled=True),
        lax.all_gather(qkv_weight.astype(jnp.bfloat16), ("dp", "seq"), axis=1, tiled=True),
        lax.all_gather(out_weight.astype(jnp.bfloat16), ("dp", "seq"), axis=1, tiled=True),
        lax.all_gather(norm2_gain.astype(jnp.bfloat16), ("dp", "seq"), axis=1, tiled=True),
        lax.all_gather(up_weight.astype(jnp.bfloat16), ("dp", "seq"), axis=1, tiled=True),
        lax.all_gather(down_weight.astype(jnp.bfloat16), ("dp", "seq"), axis=1, tiled=True),
    )
    weights = tuple((member[0] for member in gathered))
    kernel, conv_shift = (
        lax.all_gather(
            conv_weight.astype(jnp.bfloat16), ("section", "dp", "seq"), axis=0, tiled=True
        ),
        lax.all_gather(
            conv_bias.astype(jnp.bfloat16), ("section", "dp", "seq"), axis=0, tiled=True
        ),
    )
    received = jnp.zeros((frames, width_all), jnp.bfloat16)
    saved = []
    forward_outs = []
    for step_index in range(micro_count + 1):
        own_index = min(step_index, micro_count - 1)
        prior_index = max(step_index - 1, 0)
        layer_in = jnp.where(first_section, signal[own_index], received)
        segment_row = jnp.where(
            first_section, frame_segment_index[own_index], frame_segment_index[prior_index]
        )
        result, kept = layer_forward(
            layer_in, segment_row, weights, kernel, conv_shift, first_section, my_start, factor
        )
        saved.append(kept)
        forward_outs.append(result)
        if step_index < micro_count:
            received = from_behind(result.astype(jnp.bfloat16), "section", 1)
    received_back = jnp.zeros((frames, width_all), jnp.bfloat16)
    input_grads = []
    gain_totals = None
    product_list = []
    for step_index in range(micro_count + 1):
        kept = saved[micro_count - step_index]
        if step_index < micro_count:
            top_grad = cotangent[micro_count - 1 - step_index].astype(jnp.float32)
        else:
            top_grad = jnp.zeros((frames, width_all), jnp.float32)
        incoming = jnp.where(first_section, received_back.astype(jnp.float32), top_grad)
        grad_in, gain_grads, products = layer_backward(
            kept, incoming, weights, kernel, first_section, my_start, factor
        )
        input_grads.append(grad_in)
        product_list.append(products)
        if gain_totals is None:
            gain_totals = gain_grads
        else:
            gain_totals = (gain_totals[0] + gain_grads[0], gain_totals[1] + gain_grads[1])
        if step_index < micro_count:
            received_back = from_behind(grad_in.astype(jnp.bfloat16), "section", -1)

    def joined(position):
        return jnp.concatenate([member[position] for member in product_list], axis=0)

    grad_qkv = jnp.einsum("ti,tj->ij", joined(0), joined(1), preferred_element_type=jnp.float32)
    grad_out_weight = jnp.einsum(
        "ti,to->io", joined(2), joined(3), preferred_element_type=jnp.float32
    )
    grad_up = jnp.einsum("ti,tf->if", joined(4), joined(5), preferred_element_type=jnp.float32)
    grad_down = jnp.einsum("ti,to->io", joined(6), joined(7), preferred_element_type=jnp.float32)
    padded_all = jnp.stack([member[8] for member in product_list])
    conv_grad_all = jnp.stack([member[9] for member in product_list])
    kernel_grad = conv_kernel_grad(padded_all, conv_grad_all)
    bias_grad = jnp.sum(joined(9).astype(jnp.float32), axis=0)
    ends = jnp.stack(
        [
            jnp.where(
                first_section, input_grads[micro_count - mb_index], forward_outs[mb_index + 1]
            )
            for mb_index in range(micro_count)
        ]
    )[None]
    layer_sums = (
        lax.psum_scatter(gain_totals[0][None], ("dp", "seq"), scatter_dimension=1, tiled=True),
        lax.psum_scatter(grad_qkv[None], ("dp", "seq"), scatter_dimension=1, tiled=True),
        lax.psum_scatter(grad_out_weight[None], ("dp", "seq"), scatter_dimension=1, tiled=True),
        lax.psum_scatter(gain_totals[1][None], ("dp", "seq"), scatter_dimension=1, tiled=True),
        lax.psum_scatter(grad_up[None], ("dp", "seq"), scatter_dimension=1, tiled=True),
        lax.psum_scatter(grad_down[None], ("dp", "seq"), scatter_dimension=1, tiled=True),
    )
    conv_sums = (
        lax.psum_scatter(kernel_grad, ("section", "dp", "seq"), scatter_dimension=0, tiled=True),
        lax.psum_scatter(bias_grad, ("section", "dp", "seq"), scatter_dimension=0, tiled=True),
    )
    return (
        ends,
        conv_sums[0],
        conv_sums[1],
        layer_sums[0],
        layer_sums[1],
        layer_sums[2],
        layer_sums[3],
        layer_sums[4],
        layer_sums[5],
    )


def swap_section(value):
    return lax.ppermute(value, "section", [(0, 1), (1, 0)])


def swap_x(value):
    return lax.ppermute(value, "seq", [(q, q ^ 1) for q in range(4)])


def pair_sum(low, behind=None):
    other = swap_x(low)
    if behind is not None:
        other, _ = lax.optimization_barrier((other, behind))
    return low.astype(jnp.float32) + other.astype(jnp.float32)


def after(first, second):
    return lax.optimization_barrier((first, second))


def choose(flag, first, second):
    return jnp.where(flag, first, second), jnp.where(flag, second, first)


def sum_dp(blocks, dp):
    count = lax.axis_size("dp")
    f32, bf16 = jnp.float32, jnp.bfloat16

    def block(index):
        return lax.dynamic_index_in_dim(blocks, jnp.clip(index, 0, count - 1), 0, keepdims=False)

    total = block(dp).astype(f32)
    for sign in (1, -1):
        pairs = [(i, i + sign) for i in range(count) if 0 <= i + sign < count]
        running = None
        for distance in range(count - 1, 0, -1):
            own = block(dp + sign * distance)
            if running is not None:
                own = (own.astype(f32) + running.astype(f32)).astype(bf16)
            live = [(a, b) for a, b in pairs if 0 <= a + sign * distance < count]
            running = lax.ppermute(own, "dp", live)
        total = total + running.astype(f32)
    return total.astype(bf16)


def line_groups():
    count = lax.axis_size("dp")
    return [
        [(s * count + d) * 4 + 2 * y + x for d in range(count) for y in range(2) for s in range(2)]
        for x in range(2)
    ]


def gather_rows(piece):
    return lax.all_gather(
        piece, ("section", "dp", "seq"), axis=0, tiled=True, axis_index_groups=line_groups()
    )


def scatter_rows(partial):
    return lax.psum_scatter(
        partial, ("section", "dp", "seq"), scatter_dimension=0, tiled=True,
        axis_index_groups=line_groups(),
    )


MESH = pl.DeviceIdType.MESH


def opening_kernel(
    dp_count, parts, conv_ref, signal_ref, keep_ref, send_ref, rest_ref, conv_out, signal_out, whole_out,
    local_sem, a2a_send, a2a_recv, sig_send, sig_recv, line_send, line_recv, own_send, own_recv,
    up_send, up_recv, y_send, y_recv, core_send, core_recv,
):
    sec, dp, seq = (lax.axis_index(name) for name in ("section", "dp", "seq"))
    me = sec * 4 + seq
    x, y = seq % 2, seq // 2
    partner_x = (seq + 1 - 2 * x) % 4
    partner_y = {"seq": (seq + 2) % 4}
    sibling = {"section": 1 - sec}
    has_up, has_down = dp < dp_count - 1, dp > 0
    split = keep_ref.shape[1]
    rows = keep_ref.shape[0] // parts

    barrier = pltpu.get_barrier_semaphore()
    for turn in range(1, 8):
        other = (me + turn) % 8
        pl.semaphore_signal(
            barrier, inc=1, device_id={"section": other // 4, "seq": other % 4}, device_id_type=MESH
        )
    for there, step in ((has_up, 1), (has_down, -1)):

        @pl.when(there)
        def _(step=step):
            pl.semaphore_signal(barrier, inc=1, device_id={"dp": dp + step}, device_id_type=MESH)

    pl.semaphore_wait(barrier, 7 + jnp.where(has_up, 1, 0) + jnp.where(has_down, 1, 0))

    def remote(source, target, send, recv, device):
        return pltpu.make_async_remote_copy(
            src_ref=source, dst_ref=target, send_sem=send, recv_sem=recv,
            device_id=device, device_id_type=MESH,
        )

    def a2a(target, source):
        return remote(
            conv_ref.at[target], conv_out.at[dp, source], a2a_send.at[target], a2a_recv.at[source],
            {"section": target // 4, "seq": target % 4},
        )

    def sig(target, source):
        return remote(
            signal_ref.at[target], signal_out.at[source], sig_send.at[target], sig_recv.at[source],
            {"seq": target},
        )

    for turn in range(1, 8):
        a2a((me + turn) % 8, me).start()
    conv_local = pltpu.make_async_copy(conv_ref.at[me], conv_out.at[dp, me], local_sem.at[0])
    signal_local = pltpu.make_async_copy(signal_ref.at[seq], signal_out.at[seq], local_sem.at[1])
    conv_local.start()
    signal_local.start()

    def columns(half):
        return whole_out.at[dp, y, half, :, pl.ds(0, split)]

    def others(half):
        return whole_out.at[dp, y, half, :, pl.ds(split, rest_ref.shape[2])]

    keep_local = pltpu.make_async_copy(keep_ref, columns(0), local_sem.at[2])
    rest_local = pltpu.make_async_copy(rest_ref.at[0], others(0), local_sem.at[3])
    keep_far = remote(keep_ref, columns(1), own_send.at[0], own_recv.at[0], {"section": 1})
    send_same = remote(send_ref, columns(0), own_send.at[1], own_recv.at[0], {"seq": partner_x})
    send_cross = remote(
        send_ref, columns(1), own_send.at[1], own_recv.at[0], {"section": 1, "seq": partner_x}
    )
    rest_far = remote(rest_ref.at[1], others(1), own_send.at[2], own_recv.at[1], {"section": 1})
    first, second = sec == 0, sec == 1

    @pl.when(first & (x == 0))
    def _():
        send_same.start()
        keep_local.start()

    @pl.when(first & (x == 1))
    def _():
        send_cross.start()
        keep_far.start()

    @pl.when(first)
    def _():
        rest_far.start()
        rest_local.start()

    for turn in range(1, 4):
        sig((seq + turn) % 4, seq).start()

    def line(slot, direction):
        index = (direction + 1) // 2
        return remote(
            conv_out.at[slot], conv_out.at[slot], line_send.at[index, slot], line_recv.at[slot],
            {"dp": dp + direction},
        )

    def place(slot, row, half, part):
        return whole_out.at[slot, row, half, pl.ds(part * rows, rows)]

    def along(slot, direction, part):
        index = (direction + 1) // 2
        ref = place(slot, y, sec, part)
        return remote(
            ref, ref, up_send.at[index, slot, part], up_recv.at[slot, part], {"dp": dp + direction}
        )

    def across(slot, row, part):
        ref = place(slot, row, sec, part)
        return remote(ref, ref, y_send.at[slot, part], y_recv.at[slot, part], partner_y)

    def to_core(slot, row, half, part):
        ref = place(slot, row, half, part)
        return remote(
            ref, ref, core_send.at[slot, row, part], core_recv.at[slot, row, part], sibling
        )

    for turn in range(1, 8):
        a2a((me + turn) % 8, (me + turn) % 8).wait_recv()
    conv_local.wait()
    for there, direction in ((has_up, 1), (has_down, -1)):

        @pl.when(there)
        def _(direction=direction):
            line(dp, direction).start()

    @pl.when(first & (x == 0))
    def _():
        keep_local.wait()

    @pl.when(first & (x == 1))
    def _():
        send_same.wait_recv()

    @pl.when(first)
    def _():
        rest_local.wait()

    @pl.when(second & (x == 0))
    def _():
        send_cross.wait_recv()

    @pl.when(second & (x == 1))
    def _():
        keep_far.wait_recv()

    @pl.when(second)
    def _():
        rest_far.wait_recv()

    for part in range(parts):
        for there, direction in ((has_up, 1), (has_down, -1)):

            @pl.when(there)
            def _(direction=direction, part=part):
                along(dp, direction, part).start()

        across(dp, y, part).start()
        to_core(dp, y, sec, part).start()

    def stage(distance):
        arrivals = []
        for direction in (1, -1):
            slot = dp - direction * distance
            arrives = (slot >= 0) & (slot < dp_count)
            goes_on = arrives & (has_up if direction == 1 else has_down)
            arrivals.append((direction, slot, arrives, goes_on))

            @pl.when(arrives)
            def _(slot=slot, direction=direction):
                line(slot, direction).wait_recv()

            @pl.when(goes_on)
            def _(slot=slot, direction=direction):
                line(slot, direction).start()

        for part in range(parts):
            for direction, slot, arrives, goes_on in arrivals:

                @pl.when(arrives)
                def _(slot=slot, direction=direction, part=part):
                    along(slot, direction, part).wait_recv()

                @pl.when(goes_on)
                def _(slot=slot, direction=direction, part=part):
                    along(slot, direction, part).start()

                @pl.when(arrives)
                def _(slot=slot, part=part):
                    across(slot, y, part).start()
                    to_core(slot, y, sec, part).start()

    def pass_crossed(distance):
        for part in range(parts):
            for sign in (1, -1) if distance else (1,):
                slot = dp - sign * distance

                @pl.when((slot >= 0) & (slot < dp_count))
                def _(slot=slot, part=part):
                    across(slot, 1 - y, part).wait_recv()
                    to_core(slot, 1 - y, sec, part).start()

    for distance in range(1, dp_count):
        stage(distance)
        pass_crossed(distance - 1)
    pass_crossed(dp_count - 1)

    for slot in range(dp_count):
        for part in range(parts):
            for row in range(2):
                to_core(slot, row, 1 - sec, part).wait_recv()
                to_core(slot, row, sec, part).wait_send()
            across(slot, y, part).wait_send()
        for direction in (1, -1):
            sent = (slot <= dp if direction == 1 else slot >= dp) & (has_up if direction == 1 else has_down)

            @pl.when(sent)
            def _(slot=slot, direction=direction):
                line(slot, direction).wait_send()
                for part in range(parts):
                    along(slot, direction, part).wait_send()

    @pl.when(first & (x == 0))
    def _():
        send_same.wait_send()

    @pl.when(first & (x == 1))
    def _():
        send_cross.wait_send()
        keep_far.wait_send()

    @pl.when(first)
    def _():
        rest_far.wait_send()

    for turn in range(1, 8):
        a2a((me + turn) % 8, me).wait_send()
    for turn in range(1, 4):
        sig((seq + turn) % 4, (seq + turn) % 4).wait_recv()
        sig((seq + turn) % 4, seq).wait_send()
    signal_local.wait()


def opening(conv_send, signal_send, keep, send, rest):
    count = lax.axis_size("dp")
    parts = 2
    rows, columns = keep.shape[0], keep.shape[1] + rest.shape[2]
    anywhere = pl.BlockSpec(memory_space=pl.ANY)
    dma = pltpu.SemaphoreType.DMA
    conv_all, signal_all, whole = pl.pallas_call(
        functools.partial(opening_kernel, count, parts),
        in_specs=[anywhere] * 5,
        out_specs=[anywhere] * 3,
        out_shape=[
            jax.ShapeDtypeStruct((count, *conv_send.shape), conv_send.dtype),
            jax.ShapeDtypeStruct(signal_send.shape, signal_send.dtype),
            jax.ShapeDtypeStruct((count, 2, 2, rows, columns), keep.dtype),
        ],
        scratch_shapes=[
            dma((4,)), dma((8,)), dma((8,)), dma((4,)), dma((4,)), dma((2, count)), dma((count,)),
            dma((3,)), dma((2,)), dma((2, count, parts)), dma((count, parts)), dma((count, parts)),
            dma((count, parts)), dma((count, 2, parts)), dma((count, 2, parts)),
        ],
        compiler_params=pltpu.CompilerParams(
            collective_id=0, has_side_effects=True, vmem_limit_bytes=4 * 1024 * 1024
        ),
        name="opening",
    )(conv_send, signal_send, keep, send, rest)
    return conv_all, signal_all, whole.reshape(-1, columns)


def norm_stats(values):
    average = jnp.mean(values, axis=-1, keepdims=True)
    centred = values - average
    spread = jnp.mean(centred * centred, axis=-1, keepdims=True)
    return centred, lax.rsqrt(spread + EPS)


def norm_back(values, gain, grad):
    centred, inv = norm_stats(values)
    unit = centred * inv
    gain_grad = jnp.sum(grad * unit, axis=0)
    f = grad * gain
    mean_f = jnp.mean(f, axis=-1, keepdims=True)
    mean_fu = jnp.mean(f * unit, axis=-1, keepdims=True)
    return (f - mean_f - unit * mean_fu) * inv, gain_grad


def gelu_slope(values):
    cdf = 0.5 * (1.0 + lax.erf(values * (1.0 / math.sqrt(2.0))))
    pdf = jnp.exp(-0.5 * values * values) * (1.0 / math.sqrt(2.0 * math.pi))
    return cdf + values * pdf


def attention_forward_kernel(factor, q_ref, k_ref, v_ref, qs_ref, ks_ref, o_ref, lse_ref):
    queries = q_ref[...]
    lane = lax.broadcasted_iota(jnp.int32, queries.shape, 1)
    allowed = qs_ref[...] == ks_ref[...]
    keys = k_ref[...]
    values = v_ref[...]
    outs = []
    for head in range(2):
        mine = (lane < HEAD_DIM) if head == 0 else (lane >= HEAD_DIM)
        own = jnp.where(mine, queries, jnp.zeros_like(queries))
        scores = lax.dot_general(
            own, keys, (((1,), (1,)), ((), ())), preferred_element_type=jnp.float32
        ) * factor
        scores = jnp.where(allowed, scores, NEG)
        top = jnp.max(scores, axis=-1, keepdims=True)
        raised = jnp.exp(scores - top)
        total = jnp.sum(raised, axis=-1, keepdims=True)
        chances = (raised * (1.0 / total)).astype(jnp.bfloat16)
        outs.append(jnp.dot(chances, values, preferred_element_type=jnp.float32))
        lse_ref[0, head] = top + jnp.log(total)
    o_ref[...] = jnp.where(lane < HEAD_DIM, outs[0], outs[1]).astype(o_ref.dtype)


def attention_forward(packed, kv_all, query_segs, key_segs, factor):
    frames = packed.shape[0]
    keys = kv_all.shape[0]
    width = packed.shape[1] // 3
    pairs = width // 128
    rows = math.gcd(frames, 256)
    return pl.pallas_call(
        functools.partial(attention_forward_kernel, factor),
        grid=(pairs, frames // rows),
        in_specs=[
            pl.BlockSpec((rows, 128), lambda h, i: (i, h)),
            pl.BlockSpec((keys, 128), lambda h, i: (0, h)),
            pl.BlockSpec((keys, 128), lambda h, i: (0, pairs + h)),
            pl.BlockSpec((rows, 1), lambda h, i: (i, 0)),
            pl.BlockSpec((1, keys), lambda h, i: (0, 0)),
        ],
        out_specs=[
            pl.BlockSpec((rows, 128), lambda h, i: (i, h)),
            pl.BlockSpec((1, 2, rows, 1), lambda h, i: (h, 0, i, 0)),
        ],
        out_shape=[
            jax.ShapeDtypeStruct((frames, width), jnp.bfloat16),
            jax.ShapeDtypeStruct((pairs, 2, frames, 1), jnp.float32),
        ],
        compiler_params=pltpu.CompilerParams(vmem_limit_bytes=40 * 1024 * 1024),
        cost_estimate=pl.CostEstimate(
            flops=4 * frames * keys * width * 2,
            bytes_accessed=2 * (frames * width * 2 + keys * width * 2),
            transcendentals=frames * keys * (width // HEAD_DIM),
        ),
        name="attention_forward",
    )(packed, kv_all, kv_all, query_segs[:, None], key_segs[None, :])


def attention_backward_kernel(
    factor, q_ref, k_ref, v_ref, g_ref, o_ref, lse_ref, qs_ref, ks_ref, *rest
):
    *begin, dq_ref, dk_ref, dv_ref = rest
    step = pl.program_id(1)

    @pl.when(step == 0)
    def _():
        for index, total_ref in enumerate((dk_ref, dv_ref)):
            total_ref[...] = begin[index][...] if begin else jnp.zeros_like(total_ref)

    queries = q_ref[...]
    grads = g_ref[...]
    keys = k_ref[...]
    values = v_ref[...]
    lane = lax.broadcasted_iota(jnp.int32, queries.shape, 1)
    key_lane = lax.broadcasted_iota(jnp.int32, keys.shape, 1)
    allowed = qs_ref[...] == ks_ref[...]
    product = grads.astype(jnp.float32) * o_ref[...].astype(jnp.float32)
    dq = None
    for head in range(2):
        mine = (lane < HEAD_DIM) if head == 0 else (lane >= HEAD_DIM)
        key_mine = (key_lane < HEAD_DIM) if head == 0 else (key_lane >= HEAD_DIM)
        own_q = jnp.where(mine, queries, jnp.zeros_like(queries))
        own_g = jnp.where(mine, grads, jnp.zeros_like(grads))
        own_k = jnp.where(key_mine, keys, jnp.zeros_like(keys))
        delta = jnp.sum(jnp.where(mine, product, 0.0), axis=-1, keepdims=True)
        scores = lax.dot_general(
            own_q, keys, (((1,), (1,)), ((), ())), preferred_element_type=jnp.float32
        ) * factor
        chances = jnp.exp(jnp.where(allowed, scores, NEG) - lse_ref[0, head])
        prob_grad = lax.dot_general(
            own_g, values, (((1,), (1,)), ((), ())), preferred_element_type=jnp.float32
        )
        score_grad = (chances * (prob_grad - delta)).astype(jnp.bfloat16)
        part = jnp.dot(score_grad, own_k, preferred_element_type=jnp.float32)
        dq = part if dq is None else dq + part
        dk_ref[...] += lax.dot_general(
            score_grad, own_q, (((0,), (0,)), ((), ())), preferred_element_type=jnp.float32
        ) * factor
        dv_ref[...] += lax.dot_general(
            chances.astype(jnp.bfloat16), own_g, (((0,), (0,)), ((), ())),
            preferred_element_type=jnp.float32,
        )
    dq_ref[...] = (dq * factor).astype(dq_ref.dtype)


def attention_backward(packed, kv_all, grads, attended, lse, query_segs, key_segs, factor, begin=None):
    frames = packed.shape[0]
    keys = kv_all.shape[0]
    width = packed.shape[1] // 3
    pairs = width // 128
    rows = math.gcd(frames, 256)
    return pl.pallas_call(
        functools.partial(attention_backward_kernel, factor),
        grid=(pairs, frames // rows),
        in_specs=[
            pl.BlockSpec((rows, 128), lambda h, i: (i, h)),
            pl.BlockSpec((keys, 128), lambda h, i: (0, h)),
            pl.BlockSpec((keys, 128), lambda h, i: (0, pairs + h)),
            pl.BlockSpec((rows, 128), lambda h, i: (i, h)),
            pl.BlockSpec((rows, 128), lambda h, i: (i, h)),
            pl.BlockSpec((1, 2, rows, 1), lambda h, i: (h, 0, i, 0)),
            pl.BlockSpec((rows, 1), lambda h, i: (i, 0)),
            pl.BlockSpec((1, keys), lambda h, i: (0, 0)),
        ]
        + [pl.BlockSpec((keys, 128), lambda h, i: (0, h))] * (2 if begin else 0),
        out_specs=[
            pl.BlockSpec((rows, 128), lambda h, i: (i, h)),
            pl.BlockSpec((keys, 128), lambda h, i: (0, h)),
            pl.BlockSpec((keys, 128), lambda h, i: (0, h)),
        ],
        out_shape=[
            jax.ShapeDtypeStruct((frames, width), jnp.bfloat16),
            jax.ShapeDtypeStruct((keys, width), jnp.float32),
            jax.ShapeDtypeStruct((keys, width), jnp.float32),
        ],
        compiler_params=pltpu.CompilerParams(vmem_limit_bytes=48 * 1024 * 1024),
        cost_estimate=pl.CostEstimate(
            flops=10 * frames * keys * width * 2,
            bytes_accessed=4 * (frames * width * 2 + keys * width * 2),
            transcendentals=frames * keys * (width // HEAD_DIM),
        ),
        name="attention_backward",
    )(packed, kv_all, kv_all, grads, attended, lse, query_segs[:, None], key_segs[None, :], *(begin or ()))


CONV_STEP = 4


def conv_bands(kernel, per_group):
    groups = kernel.shape[1] // per_group
    steps = TAPS // CONV_STEP + 1
    bands = []
    for group in range(groups):
        own = kernel[:, group * per_group : (group + 1) * per_group]
        shifted = [
            jnp.pad(own, ((shift * per_group, (CONV_STEP - shift) * per_group), (0, 0)))
            for shift in range(CONV_STEP)
        ]
        band = jnp.concatenate(shifted, axis=1)
        bands.append(band.reshape(steps, CONV_STEP * per_group, CONV_STEP * per_group))
    return bands


def group_view(values, per_group):
    rows, frames, width = values.shape
    return [
        values[:, :, g * per_group : (g + 1) * per_group].reshape(
            rows, frames // CONV_STEP, CONV_STEP * per_group
        )
        for g in range(width // per_group)
    ]


def ungroup(parts, per_group):
    rows, blocks, _ = parts[0].shape
    return jnp.concatenate(
        [part.reshape(rows, blocks * CONV_STEP, per_group) for part in parts], axis=2
    )


CONV_DIMS = ("NWC", "WIO", "NWC")


def conv_forward(views, bands):
    half = TAPS // 2 // CONV_STEP
    return [
        lax.conv_general_dilated(
            view, band, (1,), [(half, half)], dimension_numbers=CONV_DIMS,
            preferred_element_type=jnp.float32,
        )
        for view, band in zip(views, bands)
    ]


def conv_back(grad_views, bands):
    half = TAPS // 2 // CONV_STEP
    return [
        lax.conv_general_dilated(
            view, jnp.transpose(band[::-1], (0, 2, 1)), (1,), [(half, half)],
            dimension_numbers=CONV_DIMS, preferred_element_type=jnp.float32,
        )
        for view, band in zip(grad_views, bands)
    ]


def conv_taps_grad(views, grad_views, per_group):
    half = TAPS // 2 // CONV_STEP
    results = []
    for view, grad in zip(views, grad_views):
        band = lax.conv_general_dilated(
            view, grad, (1,), [(half, half)],
            dimension_numbers=("CWN", "IWO", "WNC"),
            preferred_element_type=jnp.float32,
        )
        flat = band.reshape(-1, CONV_STEP * per_group)
        total = None
        for shift in range(CONV_STEP):
            part = flat[
                shift * per_group : (shift + TAPS) * per_group,
                shift * per_group : (shift + 1) * per_group,
            ]
            total = part if total is None else total + part
        results.append(total)
    return jnp.concatenate(results, axis=1)


def to_column(vector, width):
    return jnp.pad(vector[:, None], ((0, 0), (0, width - 1)))


def per_device_pairs(
    signal, frame_segment_index, conv_weight, conv_bias, norm1_gain, qkv_weight, out_weight,
    norm2_gain, up_weight, down_weight, cotangent,
):
    micro_count, frames, width = signal.shape
    bf16, f32 = jnp.bfloat16, jnp.float32
    per_group = width // GROUPS
    dp_count = lax.axis_size("dp")
    factor = 1.0 / math.sqrt(HEAD_DIM)
    sec = lax.axis_index("section")
    dp = lax.axis_index("dp")
    seq = lax.axis_index("seq")
    x, y = seq % 2, seq // 2
    sec0, x0 = sec == 0, x == 0
    row_frames = 4 * frames
    half_frames = 2 * frames
    both = ("section", "seq")

    block_width = width // 8
    rows_here = conv_weight.shape[0]
    conv_low = conv_weight.astype(bf16).reshape(rows_here, 8, block_width)
    bias_low = jnp.pad(conv_bias.astype(bf16), (0, block_width - conv_bias.shape[0]))
    bias_rows = jnp.pad(
        jnp.broadcast_to(bias_low[None, None, :], (1, 8, block_width)), ((0, 15), (0, 0), (0, 0))
    )
    conv_send = jnp.transpose(jnp.concatenate([conv_low, bias_rows], axis=0), (1, 0, 2))

    own_half = jnp.where(sec0, signal[:, :, : width // 2], signal[:, :, width // 2 :])
    sig_send = jnp.transpose(own_half.reshape(micro_count, frames, 4, block_width), (2, 0, 1, 3))
    in_rows = qkv_weight.shape[1]
    unit = down_weight.shape[1] // 4
    qkv_view = qkv_weight[0].astype(bf16).reshape(in_rows, -1, 2, HEAD_DIM)
    qkv_parity = [qkv_view[:, :, p].reshape(in_rows, -1) for p in range(2)]
    up_view = up_weight[0].astype(bf16).reshape(in_rows, -1, 2, 2, 2, unit)
    up_parity = [
        jnp.transpose(up_view[:, :, p], (0, 3, 1, 2, 4)).reshape(in_rows, -1) for p in range(2)
    ]
    qkv_cols, up_cols = qkv_parity[0].shape[1], up_parity[0].shape[1]
    col_one = to_column(norm1_gain[0].astype(bf16), 128)
    col_two = to_column(norm2_gain[0].astype(bf16), 128)
    cut = qkv_cols + 128
    keep_cols, send_cols = [
        jnp.concatenate([a, col_one, b, col_two], axis=1)
        for a, b in zip(choose(x0, *qkv_parity), choose(x0, *up_parity))
    ]
    out_low = out_weight[0].astype(bf16)
    down_low = down_weight[0].astype(bf16).reshape(2, 2, unit, width)
    rest = jnp.stack(
        [
            jnp.concatenate(
                [out_low[:, h * width // 2 : (h + 1) * width // 2], down_low[h, 0], down_low[h, 1]], axis=1
            )
            for h in range(2)
        ]
    )
    up_at = cut
    two_at = up_at + up_cols
    out_at = two_at + 128
    down_at = out_at + width // 2
    conv_all, sig_got, whole = opening(conv_send, sig_send, keep_cols, send_cols, rest)
    whole, (keep_cols, send_cols) = after(whole, (keep_cols, send_cols))
    row_sets = choose(x0, keep_cols, swap_x(send_cols))
    row_parts = [jnp.concatenate([row_sets[h], rest[h]], axis=1) for h in range(2)]
    keep, send = choose(sec0, *row_parts)
    _, second_piece = choose(sec0, keep, swap_section(send))
    gathered = [whole, gather_rows(second_piece)]
    sig_all = jnp.transpose(sig_got, (1, 0, 2, 3)).reshape(micro_count, row_frames, block_width)
    conv_all = conv_all.reshape(dp_count, 2, 4, rows_here + 16, block_width)
    conv_all = jnp.transpose(conv_all, (1, 0, 2, 3, 4))
    bias_all = conv_all[:, :, :, rows_here, : conv_bias.shape[0]].reshape(width)
    bias_own = lax.dynamic_slice_in_dim(bias_all, (sec * 4 + seq) * block_width, block_width, 0)
    kernel_own = conv_all[:, :, :, :rows_here].reshape(TAPS * per_group, block_width)
    bands = conv_bands(kernel_own, per_group)


    def views(whole):
        w_out = jnp.transpose(
            whole[:, out_at:down_at].reshape(-1, 2, in_rows, width // 2), (0, 2, 1, 3)
        ).reshape(-1, width)
        gain_one = whole[:, qkv_cols].astype(f32)[None, :]
        gain_two = whole[:, two_at].astype(f32)[None, :]
        w_up = [whole[:, up_at + part * width : up_at + (part + 1) * width] for part in range(2)]
        w_down = [whole[:, down_at + part * width : down_at + (part + 1) * width] for part in range(2)]
        return gain_one, whole[:, :qkv_cols], w_out, gain_two, w_up, w_down

    layer_weights = []

    picked = jnp.where(sec0, cotangent[0], cotangent[1])
    across = [(s * 4 + 2 * yy + xx, yy * 4 + 2 * s + xx) for s in range(2) for yy in range(2) for xx in range(2)]
    cot_own = lax.ppermute(picked, both, across)
    cot_other = swap_x(cot_own)
    cot_pair = choose(x0, cot_own, cot_other)
    top_grad = jnp.concatenate(cot_pair, axis=0).astype(f32)

    segment_row = jnp.where(y == 0, frame_segment_index[0], frame_segment_index[1])
    seg_pair = choose(sec0, segment_row[:half_frames], segment_row[half_frames:])
    query_segs = seg_pair[0]
    key_segs = jnp.concatenate(seg_pair)

    sig_views = group_view(sig_all, per_group)
    conv_pre = ungroup(conv_forward(sig_views, bands), per_group) + bias_own.astype(f32)
    stream = (sig_all.astype(f32) + smooth(conv_pre)).astype(bf16)
    slope = gelu_slope(conv_pre).astype(bf16)
    stream_send = stream.reshape(2, 2, half_frames, block_width)
    stream_send = jnp.transpose(stream_send, (1, 0, 2, 3))
    stream_send = jnp.repeat(stream_send.reshape(4, half_frames, block_width), 2, axis=0)
    stream_got = lax.all_to_all(stream_send, both, 0, 0, tiled=True)
    layer_in = jnp.transpose(stream_got, (1, 0, 2)).reshape(half_frames, width).astype(f32)

    chunks = 2
    rows = half_frames // chunks
    layer_in = [layer_in[c * rows : (c + 1) * rows] for c in range(chunks)]
    chunk_segs = [query_segs[c * rows : (c + 1) * rows] for c in range(chunks)]
    kept = []
    for layer in range(2):
        whole = gathered[layer]
        if layer:
            layer_in = []
            previous_lows[0], whole = after(previous_lows[0], whole)
        layer_weights.append(views(whole))
        gain_one, w_qkv, w_out, gain_two, w_up, w_down = layer_weights[layer]
        normed_one, packed, kv_own, kv_other = [], [], [], []
        for c in range(chunks):
            if layer:
                total = previous[c] + pair_sum(previous_lows[c], packed[-1] if c else None)
                layer_in.append(total.astype(bf16).astype(f32))
            centred, inv = norm_stats(layer_in[c])
            normed_one.append((centred * inv * gain_one).astype(bf16))
            packed.append(jnp.dot(normed_one[c], w_qkv, preferred_element_type=f32).astype(bf16))
            kv_own.append(packed[c][:, width // 2 :])
            kv_other.append(swap_section(kv_own[c]))
        kv_all = jnp.concatenate(kv_own + kv_other, axis=0)
        attended, lse, resid_two, normed_two, hidden, hidden_slope = [], [], [], [], [], []
        attn_lows, lows = [], []
        for c in range(chunks):
            own = packed[c]
            if c:
                attn_lows[-1], own = after(attn_lows[-1], own)
            mixed, log_total = attention_forward(own, kv_all, chunk_segs[c], key_segs, factor)
            attended.append(mixed)
            lse.append(log_total)
            attn_lows.append(jnp.dot(mixed, w_out, preferred_element_type=f32).astype(bf16))
        for c in range(chunks):
            resid_two.append(layer_in[c] + pair_sum(attn_lows[c], lows[-1] if c else None))
            centred, inv = norm_stats(resid_two[c])
            normed_two.append((centred * inv * gain_two).astype(bf16))
            down_sum, own_hidden, own_slope = None, [], []
            for part in range(2):
                hidden_pre = jnp.dot(normed_two[c], w_up[part], preferred_element_type=f32)
                own_hidden.append(smooth(hidden_pre).astype(bf16))
                own_slope.append(gelu_slope(hidden_pre).astype(bf16))
            for part in range(2):
                term = jnp.dot(own_hidden[part], w_down[part], preferred_element_type=f32)
                down_sum = term if down_sum is None else down_sum + term
            hidden.append(own_hidden)
            hidden_slope.append(own_slope)
            lows.append(down_sum.astype(bf16))

        resid_two_last = resid_two
        kept.append((layer_in, normed_one, packed, kv_all, attended, lse, resid_two, normed_two, hidden, hidden_slope))
        previous, previous_lows = resid_two, lows

    def outer(left, right):
        return lax.dot_general(
            left, right, (((0,), (0,)), ((), ())), preferred_element_type=f32
        ).astype(bf16)

    def back(left, right):
        return lax.dot_general(left, right, (((1,), (1,)), ((), ())), preferred_element_type=f32)

    grad_out = [top_grad[c * rows : (c + 1) * rows] for c in range(chunks)]
    attn_members, scattered = [], []
    for layer in (1, 0):
        gain_one, w_qkv, w_out, gain_two, w_up, w_down = layer_weights[layer]
        (layer_in, normed_one, packed, kv_all, attended, lse, resid_two, normed_two, hidden, hidden_slope) = kept[layer]
        branch = [member.astype(bf16) for member in grad_out]
        pre_grad, sums, low = [], [], None
        for c in range(chunks):
            own = branch[c]
            if low is not None:
                low, own = after(low, own)
                sums.append(pair_sum(low))
            own_pre, part_sum = [], None
            for part in range(2):
                own_pre.append((back(own, w_down[part]) * hidden_slope[c][part].astype(f32)).astype(bf16))
            for part in range(2):
                term = back(own_pre[part], w_up[part])
                part_sum = term if part_sum is None else part_sum + term
            pre_grad.append(own_pre)
            low = part_sum.astype(bf16)
        sums.append(pair_sum(low))
        whole_pre = [jnp.concatenate([pre_grad[c][p] for c in range(chunks)]) for p in range(2)]
        whole_hidden = [jnp.concatenate([hidden[c][p] for c in range(chunks)]) for p in range(2)]
        whole_branch, whole_two = jnp.concatenate(branch), jnp.concatenate(normed_two)
        ff_members = [
            outer(whole_two, whole_pre[0]), outer(whole_two, whole_pre[1]),
            outer(whole_hidden[0], whole_branch), outer(whole_hidden[1], whole_branch),
        ]
        if layer == 1:
            ff_members.append(jnp.zeros((width, 128), bf16))
        partial = jnp.concatenate(attn_members + ff_members, axis=1)
        if layer == 0:
            sums, partial = after(sums, partial)
        scattered.append(scatter_rows(partial))
        resid_grad, attn_branch, dq, gain_two_grad = [], [], [], None
        dkv = None
        for c in range(chunks):
            in_part, gain_part = norm_back(resid_two[c], gain_two, sums[c])
            gain_two_grad = gain_part if gain_two_grad is None else gain_two_grad + gain_part
            resid_grad.append(in_part + grad_out[c])
            attn_branch.append(resid_grad[c].astype(bf16))
            attended_grad = back(attn_branch[c], w_out).astype(bf16)
            if layer == 1 and c == 0:
                attended_grad, lows = after(attended_grad, lows)
                output = [member + pair_sum(low) for member, low in zip(resid_two_last, lows)]
            own_dq, *dkv = attention_backward(
                packed[c], kv_all, attended_grad, attended[c], lse[c], chunk_segs[c], key_segs, factor,
                None if c == 0 else dkv,
            )
            dq.append(own_dq)
        if layer == 0:
            dkv, scattered[0] = after(dkv, scattered[0])
        else:
            dkv, output = after(dkv, output)
        dkv = jnp.concatenate(dkv, axis=1)
        other_dkv = swap_section(dkv[half_frames:].astype(bf16))
        dkv_own = (dkv[:half_frames] + other_dkv.astype(f32)).astype(bf16)
        packed_grad, sums, low = [], [], None
        for c in range(chunks):
            packed_grad.append(jnp.concatenate([dq[c], dkv_own[c * rows : (c + 1) * rows]], axis=1))
            own = packed_grad[c]
            if low is not None:
                low, own = after(low, own)
                sums.append(pair_sum(low))
            low = back(own, w_qkv).astype(bf16)
        sums.append(pair_sum(low))
        next_grad, gain_one_grad = [], None
        for c in range(chunks):
            in_part, gain_part = norm_back(layer_in[c], gain_one, sums[c])
            gain_one_grad = gain_part if gain_one_grad is None else gain_one_grad + gain_part
            next_grad.append((resid_grad[c] + in_part).astype(bf16))
        whole_one, whole_pg, whole_att, whole_ab = [
            jnp.concatenate(m) for m in (normed_one, packed_grad, attended, attn_branch)
        ]
        grad_out_weight = jnp.transpose(
            outer(whole_att, whole_ab).reshape(-1, in_rows, 2, width // 2), (0, 2, 1, 3)
        ).reshape(-1, width // 2)
        gain_grads = jnp.stack([gain_one_grad, gain_two_grad], axis=1).astype(bf16)
        gain_grads = jnp.pad(gain_grads, ((0, 0), (0, 126)))
        attn_members = [outer(whole_one, whole_pg), gain_grads, grad_out_weight]
        grad_out = [member.astype(f32) for member in next_grad]
    grad_in_low = jnp.concatenate(next_grad)
    scattered.append(scatter_rows(jnp.concatenate(attn_members, axis=1)))
    output = jnp.concatenate(output)

    lig_send = jnp.transpose(grad_in_low.reshape(half_frames, 8, block_width), (1, 0, 2))
    lig_got = lax.all_to_all(lig_send, both, 0, 0, tiled=True).reshape(2, 2, 2, half_frames, block_width)
    lig = jnp.transpose(lig_got[:, :, 0], (1, 0, 2, 3)).reshape(micro_count, row_frames, block_width)
    conv_grad = (lig.astype(f32) * slope.astype(f32)).astype(bf16)
    grad_views = group_view(conv_grad, per_group)
    back = ungroup(conv_back(grad_views, bands), per_group)
    grad_signal = (lig.astype(f32) + back).astype(bf16)
    gs_send = jnp.transpose(
        grad_signal.reshape(micro_count, 4, frames, block_width), (1, 0, 2, 3)
    )
    gs_send = jnp.concatenate([gs_send, gs_send], axis=0)
    gs_got = lax.all_to_all(gs_send, both, 0, 0, tiled=True)
    gs_got, scattered[1] = after(gs_got, scattered[1])
    gs_rows = jnp.transpose(gs_got, (1, 2, 0, 3)).reshape(micro_count, frames, width).astype(f32)

    taps_grad = conv_taps_grad(sig_views, grad_views, per_group)
    bias_grad = jnp.sum(conv_grad.astype(f32), axis=(0, 1))
    taps_view = jnp.transpose(
        taps_grad.reshape(2, dp_count, 4, rows_here, block_width), (1, 0, 2, 3, 4)
    ).astype(bf16)
    bias_view = jnp.pad(
        jnp.broadcast_to(bias_grad.astype(bf16), (dp_count, 2, 4, 1, block_width)),
        ((0, 0), (0, 0), (0, 0), (0, 15), (0, 0)),
    )
    taps_send = jnp.concatenate([taps_view, bias_view], axis=3)
    taps_sum = sum_dp(taps_send, dp)
    taps_got = lax.all_to_all(
        taps_sum.reshape(8, rows_here + 16, block_width), both, 0, 0, tiled=True
    )
    conv_weight_grad = jnp.transpose(taps_got[:, :rows_here], (1, 0, 2)).reshape(rows_here, width).astype(f32)
    bias_count = conv_bias.shape[0]
    conv_bias_grad = lax.dynamic_slice_in_dim(
        taps_got[:, rows_here].reshape(width),
        ((sec * dp_count + dp) * 4 + seq) * bias_count,
        bias_count,
        0,
    ).astype(f32)

    own_block = jnp.where(x0, output[:frames], output[frames:])
    row_block = lax.ppermute(own_block, both, across)
    other_row = swap_section(row_block)
    output_rows = jnp.stack(choose(sec0, row_block, other_row))
    ends = jnp.where(sec0, gs_rows, output_rows)[None]

    attn_cols = cut + width // 2
    attn_sums = (scattered[2], scattered[1][:, :attn_cols])
    ff_sums = (scattered[1][:, attn_cols:], scattered[0][:, :-128])
    half_sets = []
    for sums in (attn_sums, ff_sums):
        keep, send = choose(sec0, *sums)
        half_sets.append(choose(sec0, keep, swap_section(send)))
    attn_sets, ff_sets = half_sets
    out_grad = jnp.concatenate([member[:, cut:attn_cols] for member in attn_sets], axis=1).astype(f32)[None]
    down_grad = jnp.concatenate(
        [member[:, up_cols + at : up_cols + at + width] for member in ff_sets for at in (0, width)],
        axis=0,
    ).astype(f32)[None]

    def finish_columns(first, second, gains):
        keep, send = choose(x0, first, second)
        return keep[:, : keep.shape[1] - gains], keep[:, keep.shape[1] - gains :], choose(x0, keep, swap_x(send))

    qkv_own, gain_own, qkv_sets = finish_columns(attn_sets[0][:, :cut], attn_sets[1][:, :cut], 128)
    _, _, up_sets = finish_columns(ff_sets[0][:, :up_cols], ff_sets[1][:, :up_cols], 0)
    norm1_grad = gain_own[:, 0].astype(f32)[None]
    norm2_grad = gain_own[:, 1].astype(f32)[None]
    qkv_grad = jnp.stack(
        [member[:, :qkv_cols].reshape(in_rows, -1, HEAD_DIM) for member in qkv_sets], axis=2
    ).reshape(in_rows, -1).astype(f32)[None]
    up_grad = jnp.stack(
        [
            jnp.transpose(member.reshape(in_rows, 2, -1, 2, unit), (0, 2, 3, 1, 4))
            for member in up_sets
        ],
        axis=2,
    ).reshape(in_rows, -1).astype(f32)[None]
    return (ends, conv_weight_grad, conv_bias_grad, norm1_grad, qkv_grad, out_grad, norm2_grad, up_grad, down_grad)


def solution(mesh):
    placed = (
        P("dp", "seq", None),
        P("dp", None),
        P(("section", "dp", "seq"), None),
        P(("section", "dp", "seq")),
        P("section", ("dp", "seq")),
        P("section", ("dp", "seq"), None),
        P("section", ("dp", "seq"), None),
        P("section", ("dp", "seq")),
        P("section", ("dp", "seq"), None),
        P("section", ("dp", "seq"), None),
        P("dp", "seq", None),
    )

    def step(*arrays):
        pairs = mesh.shape["seq"] == 4 and mesh.shape["section"] == 2 and arrays[0].shape[0] == 2
        return (per_device_pairs if pairs else per_device)(*arrays)

    return jax.shard_map(
        step,
        mesh=mesh,
        in_specs=placed,
        out_specs=(
            P("section", "dp", "seq", None),
            P(("section", "dp", "seq"), None),
            P(("section", "dp", "seq")),
            P("section", ("dp", "seq")),
            P("section", ("dp", "seq"), None),
            P("section", ("dp", "seq"), None),
            P("section", ("dp", "seq")),
            P("section", ("dp", "seq"), None),
            P("section", ("dp", "seq"), None),
        ),
        check_vma=False,
    )
```

```python
import functools
import math

import jax
import jax.numpy as jnp
from jax import lax
from jax.experimental import pallas as pl
from jax.experimental.pallas import tpu as pltpu
from jax.sharding import PartitionSpec as P

HEAD_DIM = 64
GROUPS = 16
TAPS = 128


EPS = 1e-05
NEG = -1e30


def padded_2(block, sides, width):
    for axis, dim in sides:
        count = lax.axis_size(axis)
        forward = [(i, i + 1) for i in range(count - 1)]
        backward = [(target, source) for source, target in forward]
        low = lax.ppermute(
            lax.slice_in_dim(block, block.shape[dim] - width, None, axis=dim), axis, forward
        )
        high = lax.ppermute(lax.slice_in_dim(block, 0, width, axis=dim), axis, backward)
        block = jnp.concatenate([low, block, high], axis=dim)
    return block


def from_behind(value, axis, steps):
    count = lax.axis_size(axis)
    first, last = (max(0, -steps), min(count, count - steps))
    return lax.ppermute(value, axis, [(source, source + steps) for source in range(first, last)])


def normalize(values, gain):
    average = jnp.mean(values, axis=-1, keepdims=True)
    centred = values - average
    spread = jnp.mean(centred * centred, axis=-1, keepdims=True)
    return centred * lax.rsqrt(spread + EPS) * gain


def smooth(values):
    return jax.nn.gelu(values, approximate=False)


def conv_taps(padded, kernel, frames):
    width_all = padded.shape[1]
    per_group = width_all // GROUPS
    tap_step = math.gcd(TAPS, 16)
    weight_view = kernel.reshape(TAPS, per_group, GROUPS, per_group)
    running = jnp.zeros((frames, GROUPS, per_group), jnp.float32)
    for first_tap in range(0, TAPS, tap_step):
        windows = jnp.stack(
            [padded[first_tap + offset : first_tap + offset + frames] for offset in range(tap_step)]
        )
        windows = windows.reshape(tap_step, frames, GROUPS, per_group)
        running = running + jnp.einsum(
            "jtgc,jcgo->tgo",
            windows,
            weight_view[first_tap : first_tap + tap_step],
            preferred_element_type=jnp.float32,
        )
    return running.reshape(frames, width_all)


def conv_input_grad(grad_pad, kernel, frames):
    width_all = grad_pad.shape[1]
    per_group = width_all // GROUPS
    tap_step = math.gcd(TAPS, 16)
    weight_view = kernel.reshape(TAPS, per_group, GROUPS, per_group)
    running = jnp.zeros((frames, GROUPS, per_group), jnp.float32)
    for first_tap in range(0, TAPS, tap_step):
        back_windows = jnp.stack(
            [
                grad_pad[TAPS - first_tap - offset : TAPS - first_tap - offset + frames]
                for offset in range(tap_step)
            ]
        )
        back_windows = back_windows.reshape(tap_step, frames, GROUPS, per_group)
        running = running + jnp.einsum(
            "jtgo,jcgo->tgc",
            back_windows,
            weight_view[first_tap : first_tap + tap_step],
            preferred_element_type=jnp.float32,
        )
    return running.reshape(frames, width_all)


def conv_kernel_grad(padded_all, grad_all):
    step_count, frames, width_all = grad_all.shape
    per_group = width_all // GROUPS
    tap_step = math.gcd(TAPS, 16)
    grad_view = grad_all.reshape(step_count * frames, GROUPS, per_group)
    kernel_parts = []
    for first_tap in range(0, TAPS, tap_step):
        windows = jnp.stack(
            [
                padded_all[:, first_tap + offset : first_tap + offset + frames]
                for offset in range(tap_step)
            ]
        )
        windows = windows.reshape(tap_step, step_count * frames, GROUPS, per_group)
        kernel_parts.append(
            jnp.einsum("jtgc,tgo->jcgo", windows, grad_view, preferred_element_type=jnp.float32)
        )
    return jnp.concatenate(kernel_parts, axis=0).reshape(TAPS * per_group, width_all)


def score_block(query_heads, key_block, query_segs, key_segs, factor):
    scores = (
        jnp.einsum("qhd,khd->hqk", query_heads, key_block, preferred_element_type=jnp.float32)
        * factor
    )
    allowed = (query_segs[:, None] == key_segs[None, :])[None]
    return (scores, allowed)


def front(layer_in, weights, kernel, conv_shift, first_section):
    frames, width_all = layer_in.shape
    padded = padded_2(layer_in, (("seq", 0),), TAPS // 2)
    conv_pre = lax.cond(
        first_section,
        lambda: conv_taps(padded, kernel, frames) + conv_shift.astype(jnp.float32),
        lambda: jnp.zeros((frames, width_all), jnp.float32),
    )
    conv_val, conv_pull = jax.vjp(smooth, conv_pre)
    resid_one = layer_in.astype(jnp.float32) + conv_val
    normed_val, norm_pull = jax.vjp(normalize, resid_one, weights[0].astype(jnp.float32))
    normed_one = normed_val.astype(jnp.bfloat16)
    packed = jnp.dot(normed_one, weights[1], preferred_element_type=jnp.float32).astype(
        jnp.bfloat16
    )
    return (padded, conv_pull, resid_one, norm_pull, normed_one, packed)


def tail(resid_one, attn_low, weights):
    resid_two = resid_one + jnp.dot(attn_low, weights[2], preferred_element_type=jnp.float32)
    normed_val, norm_pull = jax.vjp(normalize, resid_two, weights[3].astype(jnp.float32))
    normed_two = normed_val.astype(jnp.bfloat16)
    hidden_pre = jnp.dot(normed_two, weights[4], preferred_element_type=jnp.float32)
    hidden_val, gelu_pull = jax.vjp(smooth, hidden_pre)
    hidden_low = hidden_val.astype(jnp.bfloat16)
    result = resid_two + jnp.dot(hidden_low, weights[5], preferred_element_type=jnp.float32)
    return (result, norm_pull, normed_two, gelu_pull, hidden_low)


def key_loop(keys_all, values_all, segment_row, head_count, visit, initial):
    total_rows = keys_all.shape[0]
    block_rows = math.gcd(total_rows, 512)

    def one_block(block_index, running):
        offset = block_index * block_rows
        key_block = lax.dynamic_slice_in_dim(keys_all, offset, block_rows, 0).reshape(
            block_rows, head_count, HEAD_DIM
        )
        value_block = lax.dynamic_slice_in_dim(values_all, offset, block_rows, 0).reshape(
            block_rows, head_count, HEAD_DIM
        )
        key_segs = lax.dynamic_slice_in_dim(segment_row, offset, block_rows, 0)
        return visit(running, key_block, value_block, key_segs)

    return lax.fori_loop(0, total_rows // block_rows, one_block, initial)


def layer_forward(
    layer_in, segment_row, weights, kernel, conv_shift, first_section, my_start, factor
):
    frames, width_all = layer_in.shape
    head_count = width_all // HEAD_DIM
    padded, conv_pull, resid_one, norm_pull, normed_one, packed = front(
        layer_in, weights, kernel, conv_shift, first_section
    )
    query_heads = packed[:, :width_all].reshape(frames, head_count, HEAD_DIM)
    query_segs = lax.dynamic_slice_in_dim(segment_row, my_start, frames, 0)
    initial = (
        jnp.full((head_count, frames), NEG, jnp.float32),
        jnp.zeros((head_count, frames), jnp.float32),
        jnp.zeros((head_count, frames, HEAD_DIM), jnp.float32),
    )
    key_piece = lax.all_gather(packed[:, width_all : 2 * width_all], "seq", axis=0, tiled=True)
    value_piece = lax.all_gather(packed[:, 2 * width_all :], "seq", axis=0, tiled=True)
    piece_rows = key_piece.shape[0]
    block_rows = math.gcd(piece_rows, 512)

    def one_block(block_index, running):
        run_max, run_sum, run_acc = running
        offset = block_index * block_rows
        key_block = lax.dynamic_slice_in_dim(key_piece, offset, block_rows, 0).reshape(
            block_rows, head_count, HEAD_DIM
        )
        value_block = lax.dynamic_slice_in_dim(value_piece, offset, block_rows, 0).reshape(
            block_rows, head_count, HEAD_DIM
        )
        key_segs = lax.dynamic_slice_in_dim(segment_row, offset, block_rows, 0)
        scores, allowed = score_block(query_heads, key_block, query_segs, key_segs, factor)
        masked = jnp.where(allowed, scores, NEG)
        new_max = jnp.maximum(run_max, jnp.max(masked, axis=-1))
        weights_now = jnp.where(allowed, jnp.exp(masked - new_max[..., None]), 0.0)
        rescale = jnp.exp(run_max - new_max)
        run_sum = run_sum * rescale + jnp.sum(weights_now, axis=-1)
        run_acc = run_acc * rescale[..., None] + jnp.einsum(
            "hqk,khd->hqd",
            weights_now.astype(jnp.bfloat16),
            value_block,
            preferred_element_type=jnp.float32,
        )
        return (new_max, run_sum, run_acc)

    run_max, run_sum, run_acc = lax.fori_loop(0, piece_rows // block_rows, one_block, initial)
    log_total = run_max + jnp.log(run_sum)
    mixture = run_acc / run_sum[..., None]
    attn_low = jnp.transpose(mixture, (1, 0, 2)).reshape(frames, width_all).astype(jnp.bfloat16)
    result, norm_two_pull, normed_two, gelu_pull, hidden_low = tail(resid_one, attn_low, weights)
    kept = (
        padded,
        conv_pull,
        norm_pull,
        normed_one,
        packed,
        log_total,
        mixture,
        attn_low,
        norm_two_pull,
        normed_two,
        gelu_pull,
        hidden_low,
        segment_row,
    )
    return (result, kept)


def layer_backward(kept, grad_out, weights, kernel, first_section, my_start, factor):
    (
        padded,
        conv_pull,
        norm_one_pull,
        normed_one,
        packed,
        log_total,
        mixture,
        attn_low,
        norm_two_pull,
        normed_two,
        gelu_pull,
        hidden_low,
        segment_row,
    ) = kept
    frames, width_all = normed_one.shape
    head_count = width_all // HEAD_DIM
    query_heads = packed[:, :width_all].reshape(frames, head_count, HEAD_DIM)
    key_local = packed[:, width_all : 2 * width_all]
    value_local = packed[:, 2 * width_all :]
    query_segs = lax.dynamic_slice_in_dim(segment_row, my_start, frames, 0)
    keys_all, values_all = (
        lax.all_gather(key_local, "seq", axis=0, tiled=True),
        lax.all_gather(value_local, "seq", axis=0, tiled=True),
    )

    def chances_for(key_block, key_segs):
        scores, allowed = score_block(query_heads, key_block, query_segs, key_segs, factor)
        return jnp.where(
            allowed, jnp.exp(jnp.where(allowed, scores, NEG) - log_total[..., None]), 0.0
        )

    branch_grad = grad_out.astype(jnp.bfloat16)
    hidden_grad = jnp.einsum(
        "to,io->ti", branch_grad, weights[5], preferred_element_type=jnp.float32
    )
    pre_grad = gelu_pull(hidden_grad)[0].astype(jnp.bfloat16)
    normed_two_grad = jnp.einsum(
        "tf,if->ti", pre_grad, weights[4], preferred_element_type=jnp.float32
    )
    resid_two_grad, grad_gain_two = norm_two_pull(normed_two_grad)
    resid_two_grad = resid_two_grad + grad_out
    attn_branch_grad = resid_two_grad.astype(jnp.bfloat16)
    attended_grad = jnp.einsum(
        "to,io->ti", attn_branch_grad, weights[2], preferred_element_type=jnp.float32
    ).astype(jnp.bfloat16)
    dout_heads = attended_grad.reshape(frames, head_count, HEAD_DIM)
    delta_rows = jnp.einsum("qhd,hqd->hq", dout_heads.astype(jnp.float32), mixture)

    def visit_query(running, key_block, value_block, key_segs):
        chances = chances_for(key_block, key_segs)
        prob_grad = jnp.einsum(
            "qhd,khd->hqk", dout_heads, value_block, preferred_element_type=jnp.float32
        )
        score_grad = (chances * (prob_grad - delta_rows[..., None])).astype(jnp.bfloat16)
        return running + jnp.einsum(
            "hqk,khd->qhd", score_grad, key_block, preferred_element_type=jnp.float32
        )

    grad_query = (
        key_loop(
            keys_all,
            values_all,
            segment_row,
            head_count,
            visit_query,
            jnp.zeros((frames, head_count, HEAD_DIM), jnp.float32),
        )
        * factor
    )
    row_stats = (
        lax.all_gather(log_total, "seq", axis=1, tiled=True),
        lax.all_gather(delta_rows, "seq", axis=1, tiled=True),
    )
    key_heads = key_local.reshape(frames, head_count, HEAD_DIM)
    value_heads = value_local.reshape(frames, head_count, HEAD_DIM)
    start_acc = (
        jnp.zeros((frames, head_count, HEAD_DIM), jnp.float32),
        jnp.zeros((frames, head_count, HEAD_DIM), jnp.float32),
    )
    query_piece = lax.all_gather(packed[:, :width_all], "seq", axis=0, tiled=True)
    dout_piece = lax.all_gather(attended_grad, "seq", axis=0, tiled=True)
    piece_rows = query_piece.shape[0]
    block_rows = math.gcd(piece_rows, 512)

    def one_block(block_index, running):
        key_acc, value_acc = running
        offset = block_index * block_rows
        query_block = lax.dynamic_slice_in_dim(query_piece, offset, block_rows, 0).reshape(
            block_rows, head_count, HEAD_DIM
        )
        dout_block = lax.dynamic_slice_in_dim(dout_piece, offset, block_rows, 0).reshape(
            block_rows, head_count, HEAD_DIM
        )
        seg_block = lax.dynamic_slice_in_dim(segment_row, offset, block_rows, 0)
        total_block = lax.dynamic_slice_in_dim(row_stats[0], offset, block_rows, 1)
        delta_block = lax.dynamic_slice_in_dim(row_stats[1], offset, block_rows, 1)
        scores, allowed = score_block(query_block, key_heads, seg_block, query_segs, factor)
        chances = jnp.where(
            allowed, jnp.exp(jnp.where(allowed, scores, NEG) - total_block[..., None]), 0.0
        )
        prob_grad = jnp.einsum(
            "qhd,khd->hqk", dout_block, value_heads, preferred_element_type=jnp.float32
        )
        score_grad = (chances * (prob_grad - delta_block[..., None])).astype(jnp.bfloat16)
        key_acc = (
            key_acc
            + jnp.einsum(
                "hqk,qhd->khd", score_grad, query_block, preferred_element_type=jnp.float32
            )
            * factor
        )
        value_acc = value_acc + jnp.einsum(
            "hqk,qhd->khd",
            chances.astype(jnp.bfloat16),
            dout_block,
            preferred_element_type=jnp.float32,
        )
        return (key_acc, value_acc)

    key_acc, value_acc = lax.fori_loop(0, piece_rows // block_rows, one_block, start_acc)
    grad_key = key_acc.reshape(frames, width_all)
    grad_value = value_acc.reshape(frames, width_all)
    packed_grad = jnp.concatenate(
        [grad_query.reshape(frames, width_all), grad_key, grad_value], axis=1
    ).astype(jnp.bfloat16)
    normed_one_grad = jnp.einsum(
        "tj,ij->ti", packed_grad, weights[1], preferred_element_type=jnp.float32
    )
    resid_one_grad, grad_gain_one = norm_one_pull(normed_one_grad)
    resid_one_grad = resid_one_grad + resid_two_grad
    conv_grad = jnp.where(first_section, conv_pull(resid_one_grad)[0], 0.0).astype(jnp.bfloat16)
    grad_pad = padded_2(conv_grad, (("seq", 0),), TAPS // 2)
    back_sum = lax.cond(
        first_section,
        lambda: conv_input_grad(grad_pad, kernel, frames),
        lambda: jnp.zeros((frames, width_all), jnp.float32),
    )
    grad_in = resid_one_grad + back_sum
    products = (
        normed_one,
        packed_grad,
        attn_low,
        attn_branch_grad,
        normed_two,
        pre_grad,
        hidden_low,
        branch_grad,
        padded,
        conv_grad,
    )
    return (grad_in, (grad_gain_one, grad_gain_two), products)


def per_device(
    signal,
    frame_segment_index,
    conv_weight,
    conv_bias,
    norm1_gain,
    qkv_weight,
    out_weight,
    norm2_gain,
    up_weight,
    down_weight,
    cotangent,
):
    micro_count, frames, width_all = signal.shape
    factor = 1.0 / math.sqrt(HEAD_DIM)
    first_section = lax.axis_index("section") == 0
    my_start = lax.axis_index("seq") * frames
    gathered = (
        lax.all_gather(norm1_gain.astype(jnp.bfloat16), ("dp", "seq"), axis=1, tiled=True),
        lax.all_gather(qkv_weight.astype(jnp.bfloat16), ("dp", "seq"), axis=1, tiled=True),
        lax.all_gather(out_weight.astype(jnp.bfloat16), ("dp", "seq"), axis=1, tiled=True),
        lax.all_gather(norm2_gain.astype(jnp.bfloat16), ("dp", "seq"), axis=1, tiled=True),
        lax.all_gather(up_weight.astype(jnp.bfloat16), ("dp", "seq"), axis=1, tiled=True),
        lax.all_gather(down_weight.astype(jnp.bfloat16), ("dp", "seq"), axis=1, tiled=True),
    )
    weights = tuple((member[0] for member in gathered))
    kernel, conv_shift = (
        lax.all_gather(
            conv_weight.astype(jnp.bfloat16), ("section", "dp", "seq"), axis=0, tiled=True
        ),
        lax.all_gather(
            conv_bias.astype(jnp.bfloat16), ("section", "dp", "seq"), axis=0, tiled=True
        ),
    )
    received = jnp.zeros((frames, width_all), jnp.bfloat16)
    saved = []
    forward_outs = []
    for step_index in range(micro_count + 1):
        own_index = min(step_index, micro_count - 1)
        prior_index = max(step_index - 1, 0)
        layer_in = jnp.where(first_section, signal[own_index], received)
        segment_row = jnp.where(
            first_section, frame_segment_index[own_index], frame_segment_index[prior_index]
        )
        result, kept = layer_forward(
            layer_in, segment_row, weights, kernel, conv_shift, first_section, my_start, factor
        )
        saved.append(kept)
        forward_outs.append(result)
        if step_index < micro_count:
            received = from_behind(result.astype(jnp.bfloat16), "section", 1)
    received_back = jnp.zeros((frames, width_all), jnp.bfloat16)
    input_grads = []
    gain_totals = None
    product_list = []
    for step_index in range(micro_count + 1):
        kept = saved[micro_count - step_index]
        if step_index < micro_count:
            top_grad = cotangent[micro_count - 1 - step_index].astype(jnp.float32)
        else:
            top_grad = jnp.zeros((frames, width_all), jnp.float32)
        incoming = jnp.where(first_section, received_back.astype(jnp.float32), top_grad)
        grad_in, gain_grads, products = layer_backward(
            kept, incoming, weights, kernel, first_section, my_start, factor
        )
        input_grads.append(grad_in)
        product_list.append(products)
        if gain_totals is None:
            gain_totals = gain_grads
        else:
            gain_totals = (gain_totals[0] + gain_grads[0], gain_totals[1] + gain_grads[1])
        if step_index < micro_count:
            received_back = from_behind(grad_in.astype(jnp.bfloat16), "section", -1)

    def joined(position):
        return jnp.concatenate([member[position] for member in product_list], axis=0)

    grad_qkv = jnp.einsum("ti,tj->ij", joined(0), joined(1), preferred_element_type=jnp.float32)
    grad_out_weight = jnp.einsum(
        "ti,to->io", joined(2), joined(3), preferred_element_type=jnp.float32
    )
    grad_up = jnp.einsum("ti,tf->if", joined(4), joined(5), preferred_element_type=jnp.float32)
    grad_down = jnp.einsum("ti,to->io", joined(6), joined(7), preferred_element_type=jnp.float32)
    padded_all = jnp.stack([member[8] for member in product_list])
    conv_grad_all = jnp.stack([member[9] for member in product_list])
    kernel_grad = conv_kernel_grad(padded_all, conv_grad_all)
    bias_grad = jnp.sum(joined(9).astype(jnp.float32), axis=0)
    ends = jnp.stack(
        [
            jnp.where(
                first_section, input_grads[micro_count - mb_index], forward_outs[mb_index + 1]
            )
            for mb_index in range(micro_count)
        ]
    )[None]
    layer_sums = (
        lax.psum_scatter(gain_totals[0][None], ("dp", "seq"), scatter_dimension=1, tiled=True),
        lax.psum_scatter(grad_qkv[None], ("dp", "seq"), scatter_dimension=1, tiled=True),
        lax.psum_scatter(grad_out_weight[None], ("dp", "seq"), scatter_dimension=1, tiled=True),
        lax.psum_scatter(gain_totals[1][None], ("dp", "seq"), scatter_dimension=1, tiled=True),
        lax.psum_scatter(grad_up[None], ("dp", "seq"), scatter_dimension=1, tiled=True),
        lax.psum_scatter(grad_down[None], ("dp", "seq"), scatter_dimension=1, tiled=True),
    )
    conv_sums = (
        lax.psum_scatter(kernel_grad, ("section", "dp", "seq"), scatter_dimension=0, tiled=True),
        lax.psum_scatter(bias_grad, ("section", "dp", "seq"), scatter_dimension=0, tiled=True),
    )
    return (
        ends,
        conv_sums[0],
        conv_sums[1],
        layer_sums[0],
        layer_sums[1],
        layer_sums[2],
        layer_sums[3],
        layer_sums[4],
        layer_sums[5],
    )


def swap_section(value):
    return lax.ppermute(value, "section", [(0, 1), (1, 0)])


def swap_x(value):
    return lax.ppermute(value, "seq", [(q, q ^ 1) for q in range(4)])


def pair_sum(low, behind=None):
    other = swap_x(low)
    if behind is not None:
        other, _ = lax.optimization_barrier((other, behind))
    return low.astype(jnp.float32) + other.astype(jnp.float32)


def after(first, second):
    return lax.optimization_barrier((first, second))


def choose(flag, first, second):
    return jnp.where(flag, first, second), jnp.where(flag, second, first)


def sum_dp(blocks, dp, meanwhile):
    count = lax.axis_size("dp")
    f32, bf16 = jnp.float32, jnp.bfloat16
    meanwhile = list(meanwhile)

    def block(index):
        return lax.dynamic_index_in_dim(blocks, jnp.clip(index, 0, count - 1), 0, keepdims=False)

    running = [None, None]
    for turn, distance in enumerate(range(count - 1, 0, -1)):
        for way, sign in enumerate((1, -1)):
            own = block(dp + sign * distance)
            if running[way] is not None:
                own = (own.astype(f32) + running[way].astype(f32)).astype(bf16)
            live = [(i, i + sign) for i in range(count) if 0 <= i + sign < count and 0 <= i + sign * distance < count]
            running[way] = lax.ppermute(own, "dp", live)
        if turn < len(meanwhile):
            running, meanwhile[turn] = after(running, meanwhile[turn])
            running = list(running)
    total = block(dp).astype(f32) + running[0].astype(f32) + running[1].astype(f32)
    return total.astype(bf16), meanwhile


def line_groups():
    count = lax.axis_size("dp")
    return [
        [(s * count + d) * 4 + 2 * y + x for d in range(count) for y in range(2) for s in range(2)]
        for x in range(2)
    ]


def gather_rows(piece):
    return lax.all_gather(
        piece, ("section", "dp", "seq"), axis=0, tiled=True, axis_index_groups=line_groups()
    )


def scatter_rows(partial):
    return lax.psum_scatter(
        partial, ("section", "dp", "seq"), scatter_dimension=0, tiled=True,
        axis_index_groups=line_groups(),
    )


MESH = pl.DeviceIdType.MESH


def opening_kernel(
    dp_count, parts, conv_ref, signal_ref, keep_ref, send_ref, rest_ref,
    conv_out, signal_out, whole_out, second_out,
    local_sem, a2a_send, a2a_recv, sig_send, sig_recv, line_send, line_recv, own_send, column_recv, rest_recv,
    up_send, up_recv, y_send, y_recv, core_send, core_recv,
):
    sec, dp, seq = (lax.axis_index(name) for name in ("section", "dp", "seq"))
    me = sec * 4 + seq
    x, y = seq % 2, seq // 2
    partner_x = (seq + 1 - 2 * x) % 4
    partner_y = {"seq": (seq + 2) % 4}
    sibling = {"section": 1 - sec}
    has_up, has_down = dp < dp_count - 1, dp > 0
    split = keep_ref.shape[1]
    rows = keep_ref.shape[0] // parts

    barrier = pltpu.get_barrier_semaphore()
    for turn in range(1, 8):
        other = (me + turn) % 8
        pl.semaphore_signal(
            barrier, inc=1, device_id={"section": other // 4, "seq": other % 4}, device_id_type=MESH
        )
    for there, step in ((has_up, 1), (has_down, -1)):

        @pl.when(there)
        def _(step=step):
            pl.semaphore_signal(barrier, inc=1, device_id={"dp": dp + step}, device_id_type=MESH)

    pl.semaphore_wait(barrier, 7 + jnp.where(has_up, 1, 0) + jnp.where(has_down, 1, 0))

    def remote(source, target, send, recv, device):
        return pltpu.make_async_remote_copy(
            src_ref=source, dst_ref=target, send_sem=send, recv_sem=recv,
            device_id=device, device_id_type=MESH,
        )

    def a2a(target, source):
        return remote(
            conv_ref.at[target], conv_out.at[dp, source], a2a_send.at[target], a2a_recv.at[source],
            {"section": target // 4, "seq": target % 4},
        )

    def sig(target, source):
        return remote(
            signal_ref.at[target], signal_out.at[source], sig_send.at[target], sig_recv.at[source],
            {"seq": target},
        )

    for turn in range(1, 8):
        a2a((me + turn) % 8, me).start()
    conv_local = pltpu.make_async_copy(conv_ref.at[me], conv_out.at[dp, me], local_sem.at[0])
    signal_local = pltpu.make_async_copy(signal_ref.at[seq], signal_out.at[seq], local_sem.at[1])
    conv_local.start()
    signal_local.start()

    def columns(layer, half):
        return (second_out if layer else whole_out.at[dp, y, half]).at[:, pl.ds(0, split)]

    def others(layer, half):
        return (second_out if layer else whole_out.at[dp, y, half]).at[:, pl.ds(split, rest_ref.shape[2])]

    class Layer:
        def __init__(self, layer):
            far = {"section": 1 - layer}
            self.mine = sec == layer
            self.even = x == layer
            received = column_recv.at[layer]
            self.keep_local = pltpu.make_async_copy(keep_ref, columns(layer, layer), local_sem.at[2])
            self.rest_local = pltpu.make_async_copy(rest_ref.at[layer], others(layer, layer), local_sem.at[3])
            self.keep_far = remote(keep_ref, columns(layer, 1 - layer), own_send.at[0], received, far)
            self.send_same = remote(
                send_ref, columns(layer, layer), own_send.at[1], received, {"seq": partner_x}
            )
            self.send_cross = remote(
                send_ref, columns(layer, 1 - layer), own_send.at[1], received, {**far, "seq": partner_x}
            )
            self.rest_far = remote(
                rest_ref.at[1 - layer], others(layer, 1 - layer), own_send.at[2], rest_recv.at[layer], far
            )

        def start(self):
            @pl.when(self.mine & self.even)
            def _():
                self.send_same.start()
                self.keep_local.start()

            @pl.when(self.mine & jnp.logical_not(self.even))
            def _():
                self.send_cross.start()
                self.keep_far.start()

            @pl.when(self.mine)
            def _():
                self.rest_far.start()
                self.rest_local.start()

        def wait(self):
            other = jnp.logical_not(self.mine)
            odd = jnp.logical_not(self.even)

            @pl.when(self.mine & self.even)
            def _():
                self.keep_local.wait()

            @pl.when(self.mine & odd)
            def _():
                self.send_same.wait_recv()

            @pl.when(self.mine)
            def _():
                self.rest_local.wait()

            @pl.when(other & self.even)
            def _():
                self.send_cross.wait_recv()

            @pl.when(other & odd)
            def _():
                self.keep_far.wait_recv()

            @pl.when(other)
            def _():
                self.rest_far.wait_recv()

        def finish(self):
            @pl.when(self.mine & self.even)
            def _():
                self.send_same.wait_send()

            @pl.when(self.mine & jnp.logical_not(self.even))
            def _():
                self.send_cross.wait_send()
                self.keep_far.wait_send()

            @pl.when(self.mine)
            def _():
                self.rest_far.wait_send()

    layers = [Layer(0), Layer(1)]
    for layer in layers:
        layer.start()
    for turn in range(1, 4):
        sig((seq + turn) % 4, seq).start()

    def line(slot, direction):
        index = (direction + 1) // 2
        return remote(
            conv_out.at[slot], conv_out.at[slot], line_send.at[index, slot], line_recv.at[slot],
            {"dp": dp + direction},
        )

    def place(slot, row, half, part):
        return whole_out.at[slot, row, half, pl.ds(part * rows, rows)]

    def along(slot, direction, part):
        index = (direction + 1) // 2
        ref = place(slot, y, sec, part)
        return remote(
            ref, ref, up_send.at[index, slot, part], up_recv.at[slot, part], {"dp": dp + direction}
        )

    def across(slot, row, part):
        ref = place(slot, row, sec, part)
        return remote(ref, ref, y_send.at[slot, part], y_recv.at[slot, part], partner_y)

    def to_core(slot, row, half, part):
        ref = place(slot, row, half, part)
        return remote(
            ref, ref, core_send.at[slot, row, part], core_recv.at[slot, row, part], sibling
        )

    for turn in range(1, 8):
        a2a((me + turn) % 8, (me + turn) % 8).wait_recv()
    conv_local.wait()
    for there, direction in ((has_up, 1), (has_down, -1)):

        @pl.when(there)
        def _(direction=direction):
            line(dp, direction).start()

    layers[0].wait()
    for part in range(parts):
        for there, direction in ((has_up, 1), (has_down, -1)):

            @pl.when(there)
            def _(direction=direction, part=part):
                along(dp, direction, part).start()

        across(dp, y, part).start()
        to_core(dp, y, sec, part).start()

    def stage(distance):
        arrivals = []
        for direction in (1, -1):
            slot = dp - direction * distance
            arrives = (slot >= 0) & (slot < dp_count)
            goes_on = arrives & (has_up if direction == 1 else has_down)
            arrivals.append((direction, slot, arrives, goes_on))

            @pl.when(arrives)
            def _(slot=slot, direction=direction):
                line(slot, direction).wait_recv()

            @pl.when(goes_on)
            def _(slot=slot, direction=direction):
                line(slot, direction).start()

        for part in range(parts):
            for direction, slot, arrives, goes_on in arrivals:

                @pl.when(arrives)
                def _(slot=slot, direction=direction, part=part):
                    along(slot, direction, part).wait_recv()

                @pl.when(goes_on)
                def _(slot=slot, direction=direction, part=part):
                    along(slot, direction, part).start()

                @pl.when(arrives)
                def _(slot=slot, part=part):
                    across(slot, y, part).start()
                    to_core(slot, y, sec, part).start()

    def pass_crossed(distance):
        for part in range(parts):
            for sign in (1, -1) if distance else (1,):
                slot = dp - sign * distance

                @pl.when((slot >= 0) & (slot < dp_count))
                def _(slot=slot, part=part):
                    across(slot, 1 - y, part).wait_recv()
                    to_core(slot, 1 - y, sec, part).start()

    for distance in range(1, dp_count):
        stage(distance)
        pass_crossed(distance - 1)
    pass_crossed(dp_count - 1)

    for slot in range(dp_count):
        for part in range(parts):
            for row in range(2):
                to_core(slot, row, 1 - sec, part).wait_recv()
                to_core(slot, row, sec, part).wait_send()
            across(slot, y, part).wait_send()
        for direction in (1, -1):
            sent = (slot <= dp if direction == 1 else slot >= dp) & (has_up if direction == 1 else has_down)

            @pl.when(sent)
            def _(slot=slot, direction=direction):
                line(slot, direction).wait_send()
                for part in range(parts):
                    along(slot, direction, part).wait_send()

    layers[1].wait()
    for layer in layers:
        layer.finish()
    for turn in range(1, 8):
        a2a((me + turn) % 8, me).wait_send()
    for turn in range(1, 4):
        sig((seq + turn) % 4, (seq + turn) % 4).wait_recv()
        sig((seq + turn) % 4, seq).wait_send()
    signal_local.wait()


def opening(conv_send, signal_send, keep, send, rest):
    count = lax.axis_size("dp")
    parts = 2
    rows, columns = keep.shape[0], keep.shape[1] + rest.shape[2]
    anywhere = pl.BlockSpec(memory_space=pl.ANY)
    dma = pltpu.SemaphoreType.DMA
    conv_all, signal_all, whole, second = pl.pallas_call(
        functools.partial(opening_kernel, count, parts),
        in_specs=[anywhere] * 5,
        out_specs=[anywhere] * 4,
        out_shape=[
            jax.ShapeDtypeStruct((count, *conv_send.shape), conv_send.dtype),
            jax.ShapeDtypeStruct(signal_send.shape, signal_send.dtype),
            jax.ShapeDtypeStruct((count, 2, 2, rows, columns), keep.dtype),
            jax.ShapeDtypeStruct((rows, columns), keep.dtype),
        ],
        scratch_shapes=[
            dma((4,)), dma((8,)), dma((8,)), dma((4,)), dma((4,)), dma((2, count)), dma((count,)),
            dma((3,)), dma((2,)), dma((2,)), dma((2, count, parts)), dma((count, parts)), dma((count, parts)),
            dma((count, parts)), dma((count, 2, parts)), dma((count, 2, parts)),
        ],
        compiler_params=pltpu.CompilerParams(
            collective_id=0, has_side_effects=True, vmem_limit_bytes=4 * 1024 * 1024
        ),
        name="opening",
    )(conv_send, signal_send, keep, send, rest)
    return conv_all, signal_all, whole.reshape(-1, columns), second


def norm_stats(values):
    average = jnp.mean(values, axis=-1, keepdims=True)
    centred = values - average
    spread = jnp.mean(centred * centred, axis=-1, keepdims=True)
    return centred, lax.rsqrt(spread + EPS)


def norm_back(values, gain, grad):
    centred, inv = norm_stats(values)
    unit = centred * inv
    gain_grad = jnp.sum(grad * unit, axis=0)
    f = grad * gain
    mean_f = jnp.mean(f, axis=-1, keepdims=True)
    mean_fu = jnp.mean(f * unit, axis=-1, keepdims=True)
    return (f - mean_f - unit * mean_fu) * inv, gain_grad


def gelu_slope(values):
    cdf = 0.5 * (1.0 + lax.erf(values * (1.0 / math.sqrt(2.0))))
    pdf = jnp.exp(-0.5 * values * values) * (1.0 / math.sqrt(2.0 * math.pi))
    return cdf + values * pdf


def attention_forward_kernel(factor, q_ref, k_ref, v_ref, qs_ref, ks_ref, o_ref, lse_ref):
    queries = q_ref[...]
    lane = lax.broadcasted_iota(jnp.int32, queries.shape, 1)
    allowed = qs_ref[...] == ks_ref[...]
    keys = k_ref[...]
    values = v_ref[...]
    outs = []
    for head in range(2):
        mine = (lane < HEAD_DIM) if head == 0 else (lane >= HEAD_DIM)
        own = jnp.where(mine, queries, jnp.zeros_like(queries))
        scores = lax.dot_general(
            own, keys, (((1,), (1,)), ((), ())), preferred_element_type=jnp.float32
        ) * factor
        scores = jnp.where(allowed, scores, NEG)
        top = jnp.max(scores, axis=-1, keepdims=True)
        raised = jnp.exp(scores - top)
        total = jnp.sum(raised, axis=-1, keepdims=True)
        chances = (raised * (1.0 / total)).astype(jnp.bfloat16)
        outs.append(jnp.dot(chances, values, preferred_element_type=jnp.float32))
        lse_ref[0, head] = top + jnp.log(total)
    o_ref[...] = jnp.where(lane < HEAD_DIM, outs[0], outs[1]).astype(o_ref.dtype)


def attention_forward(packed, kv_all, query_segs, key_segs, factor):
    frames = packed.shape[0]
    keys = kv_all.shape[0]
    width = packed.shape[1] // 3
    pairs = width // 128
    rows = math.gcd(frames, 256)
    return pl.pallas_call(
        functools.partial(attention_forward_kernel, factor),
        grid=(pairs, frames // rows),
        in_specs=[
            pl.BlockSpec((rows, 128), lambda h, i: (i, h)),
            pl.BlockSpec((keys, 128), lambda h, i: (0, h)),
            pl.BlockSpec((keys, 128), lambda h, i: (0, pairs + h)),
            pl.BlockSpec((rows, 1), lambda h, i: (i, 0)),
            pl.BlockSpec((1, keys), lambda h, i: (0, 0)),
        ],
        out_specs=[
            pl.BlockSpec((rows, 128), lambda h, i: (i, h)),
            pl.BlockSpec((1, 2, rows, 1), lambda h, i: (h, 0, i, 0)),
        ],
        out_shape=[
            jax.ShapeDtypeStruct((frames, width), jnp.bfloat16),
            jax.ShapeDtypeStruct((pairs, 2, frames, 1), jnp.float32),
        ],
        compiler_params=pltpu.CompilerParams(vmem_limit_bytes=40 * 1024 * 1024),
        cost_estimate=pl.CostEstimate(
            flops=4 * frames * keys * width * 2,
            bytes_accessed=2 * (frames * width * 2 + keys * width * 2),
            transcendentals=frames * keys * (width // HEAD_DIM),
        ),
        name="attention_forward",
    )(packed, kv_all, kv_all, query_segs[:, None], key_segs[None, :])


def attention_backward_kernel(
    factor, q_ref, k_ref, v_ref, g_ref, o_ref, lse_ref, qs_ref, ks_ref, *rest
):
    *begin, dq_ref, dk_ref, dv_ref = rest
    step = pl.program_id(1)

    @pl.when(step == 0)
    def _():
        for index, total_ref in enumerate((dk_ref, dv_ref)):
            total_ref[...] = begin[index][...] if begin else jnp.zeros_like(total_ref)

    queries = q_ref[...]
    grads = g_ref[...]
    keys = k_ref[...]
    values = v_ref[...]
    lane = lax.broadcasted_iota(jnp.int32, queries.shape, 1)
    key_lane = lax.broadcasted_iota(jnp.int32, keys.shape, 1)
    allowed = qs_ref[...] == ks_ref[...]
    product = grads.astype(jnp.float32) * o_ref[...].astype(jnp.float32)
    dq = None
    for head in range(2):
        mine = (lane < HEAD_DIM) if head == 0 else (lane >= HEAD_DIM)
        key_mine = (key_lane < HEAD_DIM) if head == 0 else (key_lane >= HEAD_DIM)
        own_q = jnp.where(mine, queries, jnp.zeros_like(queries))
        own_g = jnp.where(mine, grads, jnp.zeros_like(grads))
        own_k = jnp.where(key_mine, keys, jnp.zeros_like(keys))
        delta = jnp.sum(jnp.where(mine, product, 0.0), axis=-1, keepdims=True)
        scores = lax.dot_general(
            own_q, keys, (((1,), (1,)), ((), ())), preferred_element_type=jnp.float32
        ) * factor
        chances = jnp.exp(jnp.where(allowed, scores, NEG) - lse_ref[0, head])
        prob_grad = lax.dot_general(
            own_g, values, (((1,), (1,)), ((), ())), preferred_element_type=jnp.float32
        )
        score_grad = (chances * (prob_grad - delta)).astype(jnp.bfloat16)
        part = jnp.dot(score_grad, own_k, preferred_element_type=jnp.float32)
        dq = part if dq is None else dq + part
        dk_ref[...] += lax.dot_general(
            score_grad, own_q, (((0,), (0,)), ((), ())), preferred_element_type=jnp.float32
        ) * factor
        dv_ref[...] += lax.dot_general(
            chances.astype(jnp.bfloat16), own_g, (((0,), (0,)), ((), ())),
            preferred_element_type=jnp.float32,
        )
    dq_ref[...] = (dq * factor).astype(dq_ref.dtype)


def attention_backward(packed, kv_all, grads, attended, lse, query_segs, key_segs, factor, begin=None):
    frames = packed.shape[0]
    keys = kv_all.shape[0]
    width = packed.shape[1] // 3
    pairs = width // 128
    rows = math.gcd(frames, 256)
    return pl.pallas_call(
        functools.partial(attention_backward_kernel, factor),
        grid=(pairs, frames // rows),
        in_specs=[
            pl.BlockSpec((rows, 128), lambda h, i: (i, h)),
            pl.BlockSpec((keys, 128), lambda h, i: (0, h)),
            pl.BlockSpec((keys, 128), lambda h, i: (0, pairs + h)),
            pl.BlockSpec((rows, 128), lambda h, i: (i, h)),
            pl.BlockSpec((rows, 128), lambda h, i: (i, h)),
            pl.BlockSpec((1, 2, rows, 1), lambda h, i: (h, 0, i, 0)),
            pl.BlockSpec((rows, 1), lambda h, i: (i, 0)),
            pl.BlockSpec((1, keys), lambda h, i: (0, 0)),
        ]
        + [pl.BlockSpec((keys, 128), lambda h, i: (0, h))] * (2 if begin else 0),
        out_specs=[
            pl.BlockSpec((rows, 128), lambda h, i: (i, h)),
            pl.BlockSpec((keys, 128), lambda h, i: (0, h)),
            pl.BlockSpec((keys, 128), lambda h, i: (0, h)),
        ],
        out_shape=[
            jax.ShapeDtypeStruct((frames, width), jnp.bfloat16),
            jax.ShapeDtypeStruct((keys, width), jnp.float32),
            jax.ShapeDtypeStruct((keys, width), jnp.float32),
        ],
        compiler_params=pltpu.CompilerParams(vmem_limit_bytes=48 * 1024 * 1024),
        cost_estimate=pl.CostEstimate(
            flops=10 * frames * keys * width * 2,
            bytes_accessed=4 * (frames * width * 2 + keys * width * 2),
            transcendentals=frames * keys * (width // HEAD_DIM),
        ),
        name="attention_backward",
    )(packed, kv_all, kv_all, grads, attended, lse, query_segs[:, None], key_segs[None, :], *(begin or ()))


CONV_STEP = 4


def conv_bands(kernel, per_group):
    groups = kernel.shape[1] // per_group
    steps = TAPS // CONV_STEP + 1
    bands = []
    for group in range(groups):
        own = kernel[:, group * per_group : (group + 1) * per_group]
        shifted = [
            jnp.pad(own, ((shift * per_group, (CONV_STEP - shift) * per_group), (0, 0)))
            for shift in range(CONV_STEP)
        ]
        band = jnp.concatenate(shifted, axis=1)
        bands.append(band.reshape(steps, CONV_STEP * per_group, CONV_STEP * per_group))
    return bands


def group_view(values, per_group):
    rows, frames, width = values.shape
    return [
        values[:, :, g * per_group : (g + 1) * per_group].reshape(
            rows, frames // CONV_STEP, CONV_STEP * per_group
        )
        for g in range(width // per_group)
    ]


def ungroup(parts, per_group):
    rows, blocks, _ = parts[0].shape
    return jnp.concatenate(
        [part.reshape(rows, blocks * CONV_STEP, per_group) for part in parts], axis=2
    )


CONV_DIMS = ("NWC", "WIO", "NWC")


def conv_forward(views, bands):
    half = TAPS // 2 // CONV_STEP
    return [
        lax.conv_general_dilated(
            view, band, (1,), [(half, half)], dimension_numbers=CONV_DIMS,
            preferred_element_type=jnp.float32,
        )
        for view, band in zip(views, bands)
    ]


def conv_back(grad_views, bands):
    half = TAPS // 2 // CONV_STEP
    return [
        lax.conv_general_dilated(
            view, jnp.transpose(band[::-1], (0, 2, 1)), (1,), [(half, half)],
            dimension_numbers=CONV_DIMS, preferred_element_type=jnp.float32,
        )
        for view, band in zip(grad_views, bands)
    ]


def conv_taps_grad(views, grad_views, per_group):
    half = TAPS // 2 // CONV_STEP
    results = []
    for view, grad in zip(views, grad_views):
        band = lax.conv_general_dilated(
            view, grad, (1,), [(half, half)],
            dimension_numbers=("CWN", "IWO", "WNC"),
            preferred_element_type=jnp.float32,
        )
        flat = band.reshape(-1, CONV_STEP * per_group)
        total = None
        for shift in range(CONV_STEP):
            part = flat[
                shift * per_group : (shift + TAPS) * per_group,
                shift * per_group : (shift + 1) * per_group,
            ]
            total = part if total is None else total + part
        results.append(total)
    return jnp.concatenate(results, axis=1)


def to_column(vector, width):
    return jnp.pad(vector[:, None], ((0, 0), (0, width - 1)))


def per_device_pairs(
    signal, frame_segment_index, conv_weight, conv_bias, norm1_gain, qkv_weight, out_weight,
    norm2_gain, up_weight, down_weight, cotangent,
):
    micro_count, frames, width = signal.shape
    bf16, f32 = jnp.bfloat16, jnp.float32
    per_group = width // GROUPS
    dp_count = lax.axis_size("dp")
    factor = 1.0 / math.sqrt(HEAD_DIM)
    sec = lax.axis_index("section")
    dp = lax.axis_index("dp")
    seq = lax.axis_index("seq")
    x, y = seq % 2, seq // 2
    sec0, x0 = sec == 0, x == 0
    row_frames = 4 * frames
    half_frames = 2 * frames
    both = ("section", "seq")

    block_width = width // 8
    rows_here = conv_weight.shape[0]
    conv_low = conv_weight.astype(bf16).reshape(rows_here, 8, block_width)
    bias_low = jnp.pad(conv_bias.astype(bf16), (0, block_width - conv_bias.shape[0]))
    bias_rows = jnp.pad(
        jnp.broadcast_to(bias_low[None, None, :], (1, 8, block_width)), ((0, 15), (0, 0), (0, 0))
    )
    conv_send = jnp.transpose(jnp.concatenate([conv_low, bias_rows], axis=0), (1, 0, 2))

    own_half = jnp.where(sec0, signal[:, :, : width // 2], signal[:, :, width // 2 :])
    sig_send = jnp.transpose(own_half.reshape(micro_count, frames, 4, block_width), (2, 0, 1, 3))
    in_rows = qkv_weight.shape[1]
    unit = down_weight.shape[1] // 4
    qkv_view = qkv_weight[0].astype(bf16).reshape(in_rows, -1, 2, HEAD_DIM)
    qkv_parity = [qkv_view[:, :, p].reshape(in_rows, -1) for p in range(2)]
    up_view = up_weight[0].astype(bf16).reshape(in_rows, -1, 2, 2, 2, unit)
    up_parity = [
        jnp.transpose(up_view[:, :, p], (0, 3, 1, 2, 4)).reshape(in_rows, -1) for p in range(2)
    ]
    qkv_cols, up_cols = qkv_parity[0].shape[1], up_parity[0].shape[1]
    col_one = to_column(norm1_gain[0].astype(bf16), 128)
    col_two = to_column(norm2_gain[0].astype(bf16), 128)
    cut = qkv_cols + 128
    keep_cols, send_cols = [
        jnp.concatenate([a, col_one, b, col_two], axis=1)
        for a, b in zip(choose(x0, *qkv_parity), choose(x0, *up_parity))
    ]
    out_low = out_weight[0].astype(bf16)
    down_low = down_weight[0].astype(bf16).reshape(2, 2, unit, width)
    rest = jnp.stack(
        [
            jnp.concatenate(
                [out_low[:, h * width // 2 : (h + 1) * width // 2], down_low[h, 0], down_low[h, 1]], axis=1
            )
            for h in range(2)
        ]
    )
    up_at = cut
    two_at = up_at + up_cols
    out_at = two_at + 128
    down_at = out_at + width // 2
    conv_all, sig_got, whole, second_piece = opening(conv_send, sig_send, keep_cols, send_cols, rest)
    gathered = [whole, gather_rows(second_piece)]
    sig_all = jnp.transpose(sig_got, (1, 0, 2, 3)).reshape(micro_count, row_frames, block_width)
    conv_all = conv_all.reshape(dp_count, 2, 4, rows_here + 16, block_width)
    conv_all = jnp.transpose(conv_all, (1, 0, 2, 3, 4))
    bias_all = conv_all[:, :, :, rows_here, : conv_bias.shape[0]].reshape(width)
    bias_own = lax.dynamic_slice_in_dim(bias_all, (sec * 4 + seq) * block_width, block_width, 0)
    kernel_own = conv_all[:, :, :, :rows_here].reshape(TAPS * per_group, block_width)
    bands = conv_bands(kernel_own, per_group)


    def views(whole):
        w_out = jnp.transpose(
            whole[:, out_at:down_at].reshape(-1, 2, in_rows, width // 2), (0, 2, 1, 3)
        ).reshape(-1, width)
        gain_one = whole[:, qkv_cols].astype(f32)[None, :]
        gain_two = whole[:, two_at].astype(f32)[None, :]
        w_up = [whole[:, up_at + part * width : up_at + (part + 1) * width] for part in range(2)]
        w_down = [whole[:, down_at + part * width : down_at + (part + 1) * width] for part in range(2)]
        return gain_one, whole[:, :qkv_cols], w_out, gain_two, w_up, w_down

    layer_weights = []

    picked = jnp.where(sec0, cotangent[0], cotangent[1])
    across = [(s * 4 + 2 * yy + xx, yy * 4 + 2 * s + xx) for s in range(2) for yy in range(2) for xx in range(2)]
    cot_own = lax.ppermute(picked, both, across)
    cot_other = swap_x(cot_own)
    cot_pair = choose(x0, cot_own, cot_other)
    top_grad = jnp.concatenate(cot_pair, axis=0).astype(f32)

    segment_row = jnp.where(y == 0, frame_segment_index[0], frame_segment_index[1])
    seg_pair = choose(sec0, segment_row[:half_frames], segment_row[half_frames:])
    query_segs = seg_pair[0]
    key_segs = jnp.concatenate(seg_pair)

    sig_views = group_view(sig_all, per_group)
    conv_pre = ungroup(conv_forward(sig_views, bands), per_group) + bias_own.astype(f32)
    stream = (sig_all.astype(f32) + smooth(conv_pre)).astype(bf16)
    slope = gelu_slope(conv_pre).astype(bf16)
    stream_send = stream.reshape(2, 2, half_frames, block_width)
    stream_send = jnp.transpose(stream_send, (1, 0, 2, 3))
    stream_send = jnp.repeat(stream_send.reshape(4, half_frames, block_width), 2, axis=0)
    stream_got = lax.all_to_all(stream_send, both, 0, 0, tiled=True)
    layer_in = jnp.transpose(stream_got, (1, 0, 2)).reshape(half_frames, width).astype(f32)

    chunks = 2
    rows = half_frames // chunks
    layer_in = [layer_in[c * rows : (c + 1) * rows] for c in range(chunks)]
    chunk_segs = [query_segs[c * rows : (c + 1) * rows] for c in range(chunks)]
    kept = []
    for layer in range(2):
        whole = gathered[layer]
        if layer:
            layer_in = []
            previous_lows[0], whole = after(previous_lows[0], whole)
        layer_weights.append(views(whole))
        gain_one, w_qkv, w_out, gain_two, w_up, w_down = layer_weights[layer]
        normed_one, packed, kv_own, kv_other = [], [], [], []
        for c in range(chunks):
            if layer:
                total = previous[c] + pair_sum(previous_lows[c], packed[-1] if c else None)
                layer_in.append(total.astype(bf16).astype(f32))
            centred, inv = norm_stats(layer_in[c])
            normed_one.append((centred * inv * gain_one).astype(bf16))
            packed.append(jnp.dot(normed_one[c], w_qkv, preferred_element_type=f32).astype(bf16))
            kv_own.append(packed[c][:, width // 2 :])
            kv_other.append(swap_section(kv_own[c]))
        kv_all = jnp.concatenate(kv_own + kv_other, axis=0)
        attended, lse, resid_two, normed_two, hidden, hidden_slope = [], [], [], [], [], []
        attn_lows, lows = [], []
        for c in range(chunks):
            own = packed[c]
            if c:
                attn_lows[-1], own = after(attn_lows[-1], own)
            mixed, log_total = attention_forward(own, kv_all, chunk_segs[c], key_segs, factor)
            attended.append(mixed)
            lse.append(log_total)
            attn_lows.append(jnp.dot(mixed, w_out, preferred_element_type=f32).astype(bf16))
        for c in range(chunks):
            resid_two.append(layer_in[c] + pair_sum(attn_lows[c], lows[-1] if c else None))
            centred, inv = norm_stats(resid_two[c])
            normed_two.append((centred * inv * gain_two).astype(bf16))
            down_sum, own_hidden, own_slope = None, [], []
            for part in range(2):
                hidden_pre = jnp.dot(normed_two[c], w_up[part], preferred_element_type=f32)
                own_hidden.append(smooth(hidden_pre).astype(bf16))
                own_slope.append(gelu_slope(hidden_pre).astype(bf16))
            for part in range(2):
                term = jnp.dot(own_hidden[part], w_down[part], preferred_element_type=f32)
                down_sum = term if down_sum is None else down_sum + term
            hidden.append(own_hidden)
            hidden_slope.append(own_slope)
            lows.append(down_sum.astype(bf16))

        resid_two_last = resid_two
        kept.append((layer_in, normed_one, packed, kv_all, attended, lse, resid_two, normed_two, hidden, hidden_slope))
        previous, previous_lows = resid_two, lows

    def outer(left, right):
        return lax.dot_general(
            left, right, (((0,), (0,)), ((), ())), preferred_element_type=f32
        ).astype(bf16)

    def back(left, right):
        return lax.dot_general(left, right, (((1,), (1,)), ((), ())), preferred_element_type=f32)

    grad_out = [top_grad[c * rows : (c + 1) * rows] for c in range(chunks)]
    attn_members, scattered = [], []
    for layer in (1, 0):
        gain_one, w_qkv, w_out, gain_two, w_up, w_down = layer_weights[layer]
        (layer_in, normed_one, packed, kv_all, attended, lse, resid_two, normed_two, hidden, hidden_slope) = kept[layer]
        branch = [member.astype(bf16) for member in grad_out]
        pre_grad, sums, low = [], [], None
        for c in range(chunks):
            own = branch[c]
            if low is not None:
                low, own = after(low, own)
                sums.append(pair_sum(low))
            own_pre, part_sum = [], None
            for part in range(2):
                own_pre.append((back(own, w_down[part]) * hidden_slope[c][part].astype(f32)).astype(bf16))
            for part in range(2):
                term = back(own_pre[part], w_up[part])
                part_sum = term if part_sum is None else part_sum + term
            pre_grad.append(own_pre)
            low = part_sum.astype(bf16)
        sums.append(pair_sum(low))
        whole_pre = [jnp.concatenate([pre_grad[c][p] for c in range(chunks)]) for p in range(2)]
        whole_hidden = [jnp.concatenate([hidden[c][p] for c in range(chunks)]) for p in range(2)]
        whole_branch, whole_two = jnp.concatenate(branch), jnp.concatenate(normed_two)
        ff_members = [
            outer(whole_two, whole_pre[0]), outer(whole_two, whole_pre[1]),
            outer(whole_hidden[0], whole_branch), outer(whole_hidden[1], whole_branch),
        ]
        if layer == 1:
            ff_members.append(jnp.zeros((width, 128), bf16))
        partial = jnp.concatenate(attn_members + ff_members, axis=1)
        if layer == 0:
            sums, (partial, output_rows) = after(sums, (partial, output_rows))
        scattered.append(scatter_rows(partial))
        resid_grad, attn_branch, dq, gain_two_grad = [], [], [], None
        dkv = None
        for c in range(chunks):
            in_part, gain_part = norm_back(resid_two[c], gain_two, sums[c])
            gain_two_grad = gain_part if gain_two_grad is None else gain_two_grad + gain_part
            resid_grad.append(in_part + grad_out[c])
            attn_branch.append(resid_grad[c].astype(bf16))
            attended_grad = back(attn_branch[c], w_out).astype(bf16)
            if layer == 1 and c == 0:
                attended_grad, lows = after(attended_grad, lows)
                output = [member + pair_sum(low) for member, low in zip(resid_two_last, lows)]
                row_block = lax.ppermute(jnp.where(x0, output[0], output[1]), both, across)
                output_rows = jnp.stack(choose(sec0, row_block, swap_section(row_block)))
            own_dq, *dkv = attention_backward(
                packed[c], kv_all, attended_grad, attended[c], lse[c], chunk_segs[c], key_segs, factor,
                None if c == 0 else dkv,
            )
            dq.append(own_dq)
        if layer == 0:
            dkv, scattered[0] = after(dkv, scattered[0])
        else:
            dkv, output = after(dkv, output)
        dkv = jnp.concatenate(dkv, axis=1)
        other_dkv = swap_section(dkv[half_frames:].astype(bf16))
        dkv_own = (dkv[:half_frames] + other_dkv.astype(f32)).astype(bf16)
        packed_grad, sums, low = [], [], None
        for c in range(chunks):
            packed_grad.append(jnp.concatenate([dq[c], dkv_own[c * rows : (c + 1) * rows]], axis=1))
            own = packed_grad[c]
            if low is not None:
                low, own = after(low, own)
                sums.append(pair_sum(low))
            low = back(own, w_qkv).astype(bf16)
        sums.append(pair_sum(low))
        next_grad, gain_one_grad = [], None
        for c in range(chunks):
            in_part, gain_part = norm_back(layer_in[c], gain_one, sums[c])
            gain_one_grad = gain_part if gain_one_grad is None else gain_one_grad + gain_part
            next_grad.append((resid_grad[c] + in_part).astype(bf16))
        whole_one, whole_pg, whole_att, whole_ab = [
            jnp.concatenate(m) for m in (normed_one, packed_grad, attended, attn_branch)
        ]
        grad_out_weight = jnp.transpose(
            outer(whole_att, whole_ab).reshape(-1, in_rows, 2, width // 2), (0, 2, 1, 3)
        ).reshape(-1, width // 2)
        gain_grads = jnp.stack([gain_one_grad, gain_two_grad], axis=1).astype(bf16)
        gain_grads = jnp.pad(gain_grads, ((0, 0), (0, 126)))
        attn_members = [outer(whole_one, whole_pg), gain_grads, grad_out_weight]
        grad_out = [member.astype(f32) for member in next_grad]
    grad_in_low = jnp.concatenate(next_grad)
    scattered.append(scatter_rows(jnp.concatenate(attn_members, axis=1)))

    lig_send = jnp.transpose(grad_in_low.reshape(half_frames, 8, block_width), (1, 0, 2))
    lig_got = lax.all_to_all(lig_send, both, 0, 0, tiled=True).reshape(2, 2, 2, half_frames, block_width)
    lig = jnp.transpose(lig_got[:, :, 0], (1, 0, 2, 3)).reshape(micro_count, row_frames, block_width)
    conv_grad = (lig.astype(f32) * slope.astype(f32)).astype(bf16)
    grad_views = group_view(conv_grad, per_group)
    back = ungroup(conv_back(grad_views, bands), per_group)
    grad_signal = (lig.astype(f32) + back).astype(bf16)
    gs_send = jnp.transpose(
        grad_signal.reshape(micro_count, 4, frames, block_width), (1, 0, 2, 3)
    )
    gs_send = jnp.concatenate([gs_send, gs_send], axis=0)
    taps_grad = conv_taps_grad(sig_views, grad_views, per_group)
    bias_grad = jnp.sum(conv_grad.astype(f32), axis=(0, 1))
    taps_view = jnp.transpose(
        taps_grad.reshape(2, dp_count, 4, rows_here, block_width), (1, 0, 2, 3, 4)
    ).astype(bf16)
    bias_view = jnp.pad(
        jnp.broadcast_to(bias_grad.astype(bf16), (dp_count, 2, 4, 1, block_width)),
        ((0, 0), (0, 0), (0, 0), (0, 15), (0, 0)),
    )
    taps_send = jnp.concatenate([taps_view, bias_view], axis=3)
    gs_got = lax.all_to_all(gs_send, both, 0, 0, tiled=True)
    attn_cols = cut + width // 2

    def over_section(first, second):
        keep, send = choose(sec0, first, second)
        return choose(sec0, keep, swap_section(send))

    def over_x(first, second):
        keep, send = choose(x0, first, second)
        return keep, choose(x0, keep, swap_x(send))

    taps_sum, (_, gs_got) = sum_dp(taps_send, dp, (gs_send, gs_got))
    gs_rows = jnp.transpose(gs_got, (1, 2, 0, 3)).reshape(micro_count, frames, width).astype(f32)
    ends = jnp.where(sec0, gs_rows, output_rows)[None]
    taps_got = lax.all_to_all(
        taps_sum.reshape(8, rows_here + 16, block_width), both, 0, 0, tiled=True
    )
    taps_got, scattered[1] = after(taps_got, scattered[1])
    conv_weight_grad = jnp.transpose(taps_got[:, :rows_here], (1, 0, 2)).reshape(rows_here, width).astype(f32)
    bias_count = conv_bias.shape[0]
    conv_bias_grad = lax.dynamic_slice_in_dim(
        taps_got[:, rows_here].reshape(width),
        ((sec * dp_count + dp) * 4 + seq) * bias_count,
        bias_count,
        0,
    ).astype(f32)

    ff_sets = over_section(scattered[1][:, attn_cols:], scattered[0][:, :-128])
    down_grad = jnp.concatenate(
        [member[:, up_cols + at : up_cols + at + width] for member in ff_sets for at in (0, width)],
        axis=0,
    ).astype(f32)[None]
    _, up_sets = over_x(*(member[:, :up_cols] for member in ff_sets))
    up_grad = jnp.stack(
        [
            jnp.transpose(member.reshape(in_rows, 2, -1, 2, unit), (0, 2, 3, 1, 4))
            for member in up_sets
        ],
        axis=2,
    ).reshape(in_rows, -1).astype(f32)[None]

    attn_sets = over_section(scattered[2], scattered[1][:, :attn_cols])
    out_grad = jnp.concatenate([member[:, cut:attn_cols] for member in attn_sets], axis=1).astype(f32)[None]
    keep, qkv_sets = over_x(*(member[:, :cut] for member in attn_sets))
    norm1_grad = keep[:, qkv_cols].astype(f32)[None]
    norm2_grad = keep[:, qkv_cols + 1].astype(f32)[None]
    qkv_grad = jnp.stack(
        [member[:, :qkv_cols].reshape(in_rows, -1, HEAD_DIM) for member in qkv_sets], axis=2
    ).reshape(in_rows, -1).astype(f32)[None]
    return (ends, conv_weight_grad, conv_bias_grad, norm1_grad, qkv_grad, out_grad, norm2_grad, up_grad, down_grad)


def solution(mesh):
    placed = (
        P("dp", "seq", None),
        P("dp", None),
        P(("section", "dp", "seq"), None),
        P(("section", "dp", "seq")),
        P("section", ("dp", "seq")),
        P("section", ("dp", "seq"), None),
        P("section", ("dp", "seq"), None),
        P("section", ("dp", "seq")),
        P("section", ("dp", "seq"), None),
        P("section", ("dp", "seq"), None),
        P("dp", "seq", None),
    )

    def step(*arrays):
        pairs = mesh.shape["seq"] == 4 and mesh.shape["section"] == 2 and arrays[0].shape[0] == 2
        return (per_device_pairs if pairs else per_device)(*arrays)

    return jax.shard_map(
        step,
        mesh=mesh,
        in_specs=placed,
        out_specs=(
            P("section", "dp", "seq", None),
            P(("section", "dp", "seq"), None),
            P(("section", "dp", "seq")),
            P("section", ("dp", "seq")),
            P("section", ("dp", "seq"), None),
            P("section", ("dp", "seq"), None),
            P("section", ("dp", "seq")),
            P("section", ("dp", "seq"), None),
            P("section", ("dp", "seq"), None),
        ),
        check_vma=False,
    )
```

```python
import functools
import math

import jax
import jax.numpy as jnp
from jax import lax
from jax.experimental import pallas as pl
from jax.experimental.pallas import tpu as pltpu
from jax.sharding import PartitionSpec as P

HEAD_DIM = 64
GROUPS = 16
TAPS = 128


EPS = 1e-05
NEG = -1e30


def padded_2(block, sides, width):
    for axis, dim in sides:
        count = lax.axis_size(axis)
        forward = [(i, i + 1) for i in range(count - 1)]
        backward = [(target, source) for source, target in forward]
        low = lax.ppermute(
            lax.slice_in_dim(block, block.shape[dim] - width, None, axis=dim), axis, forward
        )
        high = lax.ppermute(lax.slice_in_dim(block, 0, width, axis=dim), axis, backward)
        block = jnp.concatenate([low, block, high], axis=dim)
    return block


def from_behind(value, axis, steps):
    count = lax.axis_size(axis)
    first, last = (max(0, -steps), min(count, count - steps))
    return lax.ppermute(value, axis, [(source, source + steps) for source in range(first, last)])


def normalize(values, gain):
    average = jnp.mean(values, axis=-1, keepdims=True)
    centred = values - average
    spread = jnp.mean(centred * centred, axis=-1, keepdims=True)
    return centred * lax.rsqrt(spread + EPS) * gain


def smooth(values):
    return jax.nn.gelu(values, approximate=False)


def conv_taps(padded, kernel, frames):
    width_all = padded.shape[1]
    per_group = width_all // GROUPS
    tap_step = math.gcd(TAPS, 16)
    weight_view = kernel.reshape(TAPS, per_group, GROUPS, per_group)
    running = jnp.zeros((frames, GROUPS, per_group), jnp.float32)
    for first_tap in range(0, TAPS, tap_step):
        windows = jnp.stack(
            [padded[first_tap + offset : first_tap + offset + frames] for offset in range(tap_step)]
        )
        windows = windows.reshape(tap_step, frames, GROUPS, per_group)
        running = running + jnp.einsum(
            "jtgc,jcgo->tgo",
            windows,
            weight_view[first_tap : first_tap + tap_step],
            preferred_element_type=jnp.float32,
        )
    return running.reshape(frames, width_all)


def conv_input_grad(grad_pad, kernel, frames):
    width_all = grad_pad.shape[1]
    per_group = width_all // GROUPS
    tap_step = math.gcd(TAPS, 16)
    weight_view = kernel.reshape(TAPS, per_group, GROUPS, per_group)
    running = jnp.zeros((frames, GROUPS, per_group), jnp.float32)
    for first_tap in range(0, TAPS, tap_step):
        back_windows = jnp.stack(
            [
                grad_pad[TAPS - first_tap - offset : TAPS - first_tap - offset + frames]
                for offset in range(tap_step)
            ]
        )
        back_windows = back_windows.reshape(tap_step, frames, GROUPS, per_group)
        running = running + jnp.einsum(
            "jtgo,jcgo->tgc",
            back_windows,
            weight_view[first_tap : first_tap + tap_step],
            preferred_element_type=jnp.float32,
        )
    return running.reshape(frames, width_all)


def conv_kernel_grad(padded_all, grad_all):
    step_count, frames, width_all = grad_all.shape
    per_group = width_all // GROUPS
    tap_step = math.gcd(TAPS, 16)
    grad_view = grad_all.reshape(step_count * frames, GROUPS, per_group)
    kernel_parts = []
    for first_tap in range(0, TAPS, tap_step):
        windows = jnp.stack(
            [
                padded_all[:, first_tap + offset : first_tap + offset + frames]
                for offset in range(tap_step)
            ]
        )
        windows = windows.reshape(tap_step, step_count * frames, GROUPS, per_group)
        kernel_parts.append(
            jnp.einsum("jtgc,tgo->jcgo", windows, grad_view, preferred_element_type=jnp.float32)
        )
    return jnp.concatenate(kernel_parts, axis=0).reshape(TAPS * per_group, width_all)


def score_block(query_heads, key_block, query_segs, key_segs, factor):
    scores = (
        jnp.einsum("qhd,khd->hqk", query_heads, key_block, preferred_element_type=jnp.float32)
        * factor
    )
    allowed = (query_segs[:, None] == key_segs[None, :])[None]
    return (scores, allowed)


def front(layer_in, weights, kernel, conv_shift, first_section):
    frames, width_all = layer_in.shape
    padded = padded_2(layer_in, (("seq", 0),), TAPS // 2)
    conv_pre = lax.cond(
        first_section,
        lambda: conv_taps(padded, kernel, frames) + conv_shift.astype(jnp.float32),
        lambda: jnp.zeros((frames, width_all), jnp.float32),
    )
    conv_val, conv_pull = jax.vjp(smooth, conv_pre)
    resid_one = layer_in.astype(jnp.float32) + conv_val
    normed_val, norm_pull = jax.vjp(normalize, resid_one, weights[0].astype(jnp.float32))
    normed_one = normed_val.astype(jnp.bfloat16)
    packed = jnp.dot(normed_one, weights[1], preferred_element_type=jnp.float32).astype(
        jnp.bfloat16
    )
    return (padded, conv_pull, resid_one, norm_pull, normed_one, packed)


def tail(resid_one, attn_low, weights):
    resid_two = resid_one + jnp.dot(attn_low, weights[2], preferred_element_type=jnp.float32)
    normed_val, norm_pull = jax.vjp(normalize, resid_two, weights[3].astype(jnp.float32))
    normed_two = normed_val.astype(jnp.bfloat16)
    hidden_pre = jnp.dot(normed_two, weights[4], preferred_element_type=jnp.float32)
    hidden_val, gelu_pull = jax.vjp(smooth, hidden_pre)
    hidden_low = hidden_val.astype(jnp.bfloat16)
    result = resid_two + jnp.dot(hidden_low, weights[5], preferred_element_type=jnp.float32)
    return (result, norm_pull, normed_two, gelu_pull, hidden_low)


def key_loop(keys_all, values_all, segment_row, head_count, visit, initial):
    total_rows = keys_all.shape[0]
    block_rows = math.gcd(total_rows, 512)

    def one_block(block_index, running):
        offset = block_index * block_rows
        key_block = lax.dynamic_slice_in_dim(keys_all, offset, block_rows, 0).reshape(
            block_rows, head_count, HEAD_DIM
        )
        value_block = lax.dynamic_slice_in_dim(values_all, offset, block_rows, 0).reshape(
            block_rows, head_count, HEAD_DIM
        )
        key_segs = lax.dynamic_slice_in_dim(segment_row, offset, block_rows, 0)
        return visit(running, key_block, value_block, key_segs)

    return lax.fori_loop(0, total_rows // block_rows, one_block, initial)


def layer_forward(
    layer_in, segment_row, weights, kernel, conv_shift, first_section, my_start, factor
):
    frames, width_all = layer_in.shape
    head_count = width_all // HEAD_DIM
    padded, conv_pull, resid_one, norm_pull, normed_one, packed = front(
        layer_in, weights, kernel, conv_shift, first_section
    )
    query_heads = packed[:, :width_all].reshape(frames, head_count, HEAD_DIM)
    query_segs = lax.dynamic_slice_in_dim(segment_row, my_start, frames, 0)
    initial = (
        jnp.full((head_count, frames), NEG, jnp.float32),
        jnp.zeros((head_count, frames), jnp.float32),
        jnp.zeros((head_count, frames, HEAD_DIM), jnp.float32),
    )
    key_piece = lax.all_gather(packed[:, width_all : 2 * width_all], "seq", axis=0, tiled=True)
    value_piece = lax.all_gather(packed[:, 2 * width_all :], "seq", axis=0, tiled=True)
    piece_rows = key_piece.shape[0]
    block_rows = math.gcd(piece_rows, 512)

    def one_block(block_index, running):
        run_max, run_sum, run_acc = running
        offset = block_index * block_rows
        key_block = lax.dynamic_slice_in_dim(key_piece, offset, block_rows, 0).reshape(
            block_rows, head_count, HEAD_DIM
        )
        value_block = lax.dynamic_slice_in_dim(value_piece, offset, block_rows, 0).reshape(
            block_rows, head_count, HEAD_DIM
        )
        key_segs = lax.dynamic_slice_in_dim(segment_row, offset, block_rows, 0)
        scores, allowed = score_block(query_heads, key_block, query_segs, key_segs, factor)
        masked = jnp.where(allowed, scores, NEG)
        new_max = jnp.maximum(run_max, jnp.max(masked, axis=-1))
        weights_now = jnp.where(allowed, jnp.exp(masked - new_max[..., None]), 0.0)
        rescale = jnp.exp(run_max - new_max)
        run_sum = run_sum * rescale + jnp.sum(weights_now, axis=-1)
        run_acc = run_acc * rescale[..., None] + jnp.einsum(
            "hqk,khd->hqd",
            weights_now.astype(jnp.bfloat16),
            value_block,
            preferred_element_type=jnp.float32,
        )
        return (new_max, run_sum, run_acc)

    run_max, run_sum, run_acc = lax.fori_loop(0, piece_rows // block_rows, one_block, initial)
    log_total = run_max + jnp.log(run_sum)
    mixture = run_acc / run_sum[..., None]
    attn_low = jnp.transpose(mixture, (1, 0, 2)).reshape(frames, width_all).astype(jnp.bfloat16)
    result, norm_two_pull, normed_two, gelu_pull, hidden_low = tail(resid_one, attn_low, weights)
    kept = (
        padded,
        conv_pull,
        norm_pull,
        normed_one,
        packed,
        log_total,
        mixture,
        attn_low,
        norm_two_pull,
        normed_two,
        gelu_pull,
        hidden_low,
        segment_row,
    )
    return (result, kept)


def layer_backward(kept, grad_out, weights, kernel, first_section, my_start, factor):
    (
        padded,
        conv_pull,
        norm_one_pull,
        normed_one,
        packed,
        log_total,
        mixture,
        attn_low,
        norm_two_pull,
        normed_two,
        gelu_pull,
        hidden_low,
        segment_row,
    ) = kept
    frames, width_all = normed_one.shape
    head_count = width_all // HEAD_DIM
    query_heads = packed[:, :width_all].reshape(frames, head_count, HEAD_DIM)
    key_local = packed[:, width_all : 2 * width_all]
    value_local = packed[:, 2 * width_all :]
    query_segs = lax.dynamic_slice_in_dim(segment_row, my_start, frames, 0)
    keys_all, values_all = (
        lax.all_gather(key_local, "seq", axis=0, tiled=True),
        lax.all_gather(value_local, "seq", axis=0, tiled=True),
    )

    def chances_for(key_block, key_segs):
        scores, allowed = score_block(query_heads, key_block, query_segs, key_segs, factor)
        return jnp.where(
            allowed, jnp.exp(jnp.where(allowed, scores, NEG) - log_total[..., None]), 0.0
        )

    branch_grad = grad_out.astype(jnp.bfloat16)
    hidden_grad = jnp.einsum(
        "to,io->ti", branch_grad, weights[5], preferred_element_type=jnp.float32
    )
    pre_grad = gelu_pull(hidden_grad)[0].astype(jnp.bfloat16)
    normed_two_grad = jnp.einsum(
        "tf,if->ti", pre_grad, weights[4], preferred_element_type=jnp.float32
    )
    resid_two_grad, grad_gain_two = norm_two_pull(normed_two_grad)
    resid_two_grad = resid_two_grad + grad_out
    attn_branch_grad = resid_two_grad.astype(jnp.bfloat16)
    attended_grad = jnp.einsum(
        "to,io->ti", attn_branch_grad, weights[2], preferred_element_type=jnp.float32
    ).astype(jnp.bfloat16)
    dout_heads = attended_grad.reshape(frames, head_count, HEAD_DIM)
    delta_rows = jnp.einsum("qhd,hqd->hq", dout_heads.astype(jnp.float32), mixture)

    def visit_query(running, key_block, value_block, key_segs):
        chances = chances_for(key_block, key_segs)
        prob_grad = jnp.einsum(
            "qhd,khd->hqk", dout_heads, value_block, preferred_element_type=jnp.float32
        )
        score_grad = (chances * (prob_grad - delta_rows[..., None])).astype(jnp.bfloat16)
        return running + jnp.einsum(
            "hqk,khd->qhd", score_grad, key_block, preferred_element_type=jnp.float32
        )

    grad_query = (
        key_loop(
            keys_all,
            values_all,
            segment_row,
            head_count,
            visit_query,
            jnp.zeros((frames, head_count, HEAD_DIM), jnp.float32),
        )
        * factor
    )
    row_stats = (
        lax.all_gather(log_total, "seq", axis=1, tiled=True),
        lax.all_gather(delta_rows, "seq", axis=1, tiled=True),
    )
    key_heads = key_local.reshape(frames, head_count, HEAD_DIM)
    value_heads = value_local.reshape(frames, head_count, HEAD_DIM)
    start_acc = (
        jnp.zeros((frames, head_count, HEAD_DIM), jnp.float32),
        jnp.zeros((frames, head_count, HEAD_DIM), jnp.float32),
    )
    query_piece = lax.all_gather(packed[:, :width_all], "seq", axis=0, tiled=True)
    dout_piece = lax.all_gather(attended_grad, "seq", axis=0, tiled=True)
    piece_rows = query_piece.shape[0]
    block_rows = math.gcd(piece_rows, 512)

    def one_block(block_index, running):
        key_acc, value_acc = running
        offset = block_index * block_rows
        query_block = lax.dynamic_slice_in_dim(query_piece, offset, block_rows, 0).reshape(
            block_rows, head_count, HEAD_DIM
        )
        dout_block = lax.dynamic_slice_in_dim(dout_piece, offset, block_rows, 0).reshape(
            block_rows, head_count, HEAD_DIM
        )
        seg_block = lax.dynamic_slice_in_dim(segment_row, offset, block_rows, 0)
        total_block = lax.dynamic_slice_in_dim(row_stats[0], offset, block_rows, 1)
        delta_block = lax.dynamic_slice_in_dim(row_stats[1], offset, block_rows, 1)
        scores, allowed = score_block(query_block, key_heads, seg_block, query_segs, factor)
        chances = jnp.where(
            allowed, jnp.exp(jnp.where(allowed, scores, NEG) - total_block[..., None]), 0.0
        )
        prob_grad = jnp.einsum(
            "qhd,khd->hqk", dout_block, value_heads, preferred_element_type=jnp.float32
        )
        score_grad = (chances * (prob_grad - delta_block[..., None])).astype(jnp.bfloat16)
        key_acc = (
            key_acc
            + jnp.einsum(
                "hqk,qhd->khd", score_grad, query_block, preferred_element_type=jnp.float32
            )
            * factor
        )
        value_acc = value_acc + jnp.einsum(
            "hqk,qhd->khd",
            chances.astype(jnp.bfloat16),
            dout_block,
            preferred_element_type=jnp.float32,
        )
        return (key_acc, value_acc)

    key_acc, value_acc = lax.fori_loop(0, piece_rows // block_rows, one_block, start_acc)
    grad_key = key_acc.reshape(frames, width_all)
    grad_value = value_acc.reshape(frames, width_all)
    packed_grad = jnp.concatenate(
        [grad_query.reshape(frames, width_all), grad_key, grad_value], axis=1
    ).astype(jnp.bfloat16)
    normed_one_grad = jnp.einsum(
        "tj,ij->ti", packed_grad, weights[1], preferred_element_type=jnp.float32
    )
    resid_one_grad, grad_gain_one = norm_one_pull(normed_one_grad)
    resid_one_grad = resid_one_grad + resid_two_grad
    conv_grad = jnp.where(first_section, conv_pull(resid_one_grad)[0], 0.0).astype(jnp.bfloat16)
    grad_pad = padded_2(conv_grad, (("seq", 0),), TAPS // 2)
    back_sum = lax.cond(
        first_section,
        lambda: conv_input_grad(grad_pad, kernel, frames),
        lambda: jnp.zeros((frames, width_all), jnp.float32),
    )
    grad_in = resid_one_grad + back_sum
    products = (
        normed_one,
        packed_grad,
        attn_low,
        attn_branch_grad,
        normed_two,
        pre_grad,
        hidden_low,
        branch_grad,
        padded,
        conv_grad,
    )
    return (grad_in, (grad_gain_one, grad_gain_two), products)


def per_device(
    signal,
    frame_segment_index,
    conv_weight,
    conv_bias,
    norm1_gain,
    qkv_weight,
    out_weight,
    norm2_gain,
    up_weight,
    down_weight,
    cotangent,
):
    micro_count, frames, width_all = signal.shape
    factor = 1.0 / math.sqrt(HEAD_DIM)
    first_section = lax.axis_index("section") == 0
    my_start = lax.axis_index("seq") * frames
    gathered = (
        lax.all_gather(norm1_gain.astype(jnp.bfloat16), ("dp", "seq"), axis=1, tiled=True),
        lax.all_gather(qkv_weight.astype(jnp.bfloat16), ("dp", "seq"), axis=1, tiled=True),
        lax.all_gather(out_weight.astype(jnp.bfloat16), ("dp", "seq"), axis=1, tiled=True),
        lax.all_gather(norm2_gain.astype(jnp.bfloat16), ("dp", "seq"), axis=1, tiled=True),
        lax.all_gather(up_weight.astype(jnp.bfloat16), ("dp", "seq"), axis=1, tiled=True),
        lax.all_gather(down_weight.astype(jnp.bfloat16), ("dp", "seq"), axis=1, tiled=True),
    )
    weights = tuple((member[0] for member in gathered))
    kernel, conv_shift = (
        lax.all_gather(
            conv_weight.astype(jnp.bfloat16), ("section", "dp", "seq"), axis=0, tiled=True
        ),
        lax.all_gather(
            conv_bias.astype(jnp.bfloat16), ("section", "dp", "seq"), axis=0, tiled=True
        ),
    )
    received = jnp.zeros((frames, width_all), jnp.bfloat16)
    saved = []
    forward_outs = []
    for step_index in range(micro_count + 1):
        own_index = min(step_index, micro_count - 1)
        prior_index = max(step_index - 1, 0)
        layer_in = jnp.where(first_section, signal[own_index], received)
        segment_row = jnp.where(
            first_section, frame_segment_index[own_index], frame_segment_index[prior_index]
        )
        result, kept = layer_forward(
            layer_in, segment_row, weights, kernel, conv_shift, first_section, my_start, factor
        )
        saved.append(kept)
        forward_outs.append(result)
        if step_index < micro_count:
            received = from_behind(result.astype(jnp.bfloat16), "section", 1)
    received_back = jnp.zeros((frames, width_all), jnp.bfloat16)
    input_grads = []
    gain_totals = None
    product_list = []
    for step_index in range(micro_count + 1):
        kept = saved[micro_count - step_index]
        if step_index < micro_count:
            top_grad = cotangent[micro_count - 1 - step_index].astype(jnp.float32)
        else:
            top_grad = jnp.zeros((frames, width_all), jnp.float32)
        incoming = jnp.where(first_section, received_back.astype(jnp.float32), top_grad)
        grad_in, gain_grads, products = layer_backward(
            kept, incoming, weights, kernel, first_section, my_start, factor
        )
        input_grads.append(grad_in)
        product_list.append(products)
        if gain_totals is None:
            gain_totals = gain_grads
        else:
            gain_totals = (gain_totals[0] + gain_grads[0], gain_totals[1] + gain_grads[1])
        if step_index < micro_count:
            received_back = from_behind(grad_in.astype(jnp.bfloat16), "section", -1)

    def joined(position):
        return jnp.concatenate([member[position] for member in product_list], axis=0)

    grad_qkv = jnp.einsum("ti,tj->ij", joined(0), joined(1), preferred_element_type=jnp.float32)
    grad_out_weight = jnp.einsum(
        "ti,to->io", joined(2), joined(3), preferred_element_type=jnp.float32
    )
    grad_up = jnp.einsum("ti,tf->if", joined(4), joined(5), preferred_element_type=jnp.float32)
    grad_down = jnp.einsum("ti,to->io", joined(6), joined(7), preferred_element_type=jnp.float32)
    padded_all = jnp.stack([member[8] for member in product_list])
    conv_grad_all = jnp.stack([member[9] for member in product_list])
    kernel_grad = conv_kernel_grad(padded_all, conv_grad_all)
    bias_grad = jnp.sum(joined(9).astype(jnp.float32), axis=0)
    ends = jnp.stack(
        [
            jnp.where(
                first_section, input_grads[micro_count - mb_index], forward_outs[mb_index + 1]
            )
            for mb_index in range(micro_count)
        ]
    )[None]
    layer_sums = (
        lax.psum_scatter(gain_totals[0][None], ("dp", "seq"), scatter_dimension=1, tiled=True),
        lax.psum_scatter(grad_qkv[None], ("dp", "seq"), scatter_dimension=1, tiled=True),
        lax.psum_scatter(grad_out_weight[None], ("dp", "seq"), scatter_dimension=1, tiled=True),
        lax.psum_scatter(gain_totals[1][None], ("dp", "seq"), scatter_dimension=1, tiled=True),
        lax.psum_scatter(grad_up[None], ("dp", "seq"), scatter_dimension=1, tiled=True),
        lax.psum_scatter(grad_down[None], ("dp", "seq"), scatter_dimension=1, tiled=True),
    )
    conv_sums = (
        lax.psum_scatter(kernel_grad, ("section", "dp", "seq"), scatter_dimension=0, tiled=True),
        lax.psum_scatter(bias_grad, ("section", "dp", "seq"), scatter_dimension=0, tiled=True),
    )
    return (
        ends,
        conv_sums[0],
        conv_sums[1],
        layer_sums[0],
        layer_sums[1],
        layer_sums[2],
        layer_sums[3],
        layer_sums[4],
        layer_sums[5],
    )


def swap_section(value):
    return lax.ppermute(value, "section", [(0, 1), (1, 0)])


def swap_x(value):
    return lax.ppermute(value, "seq", [(q, q ^ 1) for q in range(4)])


def pair_sum(low, behind=None):
    other = swap_x(low)
    if behind is not None:
        other, _ = lax.optimization_barrier((other, behind))
    return low.astype(jnp.float32) + other.astype(jnp.float32)


def after(first, second):
    return lax.optimization_barrier((first, second))


def choose(flag, first, second):
    return jnp.where(flag, first, second), jnp.where(flag, second, first)


def sum_dp(blocks, dp, meanwhile):
    count = lax.axis_size("dp")
    f32, bf16 = jnp.float32, jnp.bfloat16
    meanwhile = list(meanwhile)

    def block(index):
        return lax.dynamic_index_in_dim(blocks, jnp.clip(index, 0, count - 1), 0, keepdims=False)

    running = [None, None]
    for turn, distance in enumerate(range(count - 1, 0, -1)):
        for way, sign in enumerate((1, -1)):
            own = block(dp + sign * distance)
            if running[way] is not None:
                own = (own.astype(f32) + running[way].astype(f32)).astype(bf16)
            live = [(i, i + sign) for i in range(count) if 0 <= i + sign < count and 0 <= i + sign * distance < count]
            running[way] = lax.ppermute(own, "dp", live)
        if turn < len(meanwhile):
            running, meanwhile[turn] = after(running, meanwhile[turn])
            running = list(running)
    total = block(dp).astype(f32) + running[0].astype(f32) + running[1].astype(f32)
    return total.astype(bf16), meanwhile


def line_groups():
    count = lax.axis_size("dp")
    return [
        [(s * count + d) * 4 + 2 * y + x for d in range(count) for y in range(2) for s in range(2)]
        for x in range(2)
    ]


def gather_rows(piece):
    return lax.all_gather(
        piece, ("section", "dp", "seq"), axis=0, tiled=True, axis_index_groups=line_groups()
    )


def scatter_rows(partial):
    return lax.psum_scatter(
        partial, ("section", "dp", "seq"), scatter_dimension=0, tiled=True,
        axis_index_groups=line_groups(),
    )


MESH = pl.DeviceIdType.MESH


def opening_kernel(
    dp_count, parts, conv_ref, signal_ref, keep_ref, send_ref, rest_ref,
    conv_out, signal_out, whole_out, second_out,
    local_sem, a2a_send, a2a_recv, sig_send, sig_recv, line_send, line_recv, own_send, column_recv, rest_recv,
    up_send, up_recv, y_send, y_recv, core_send, core_recv,
):
    sec, dp, seq = (lax.axis_index(name) for name in ("section", "dp", "seq"))
    me = sec * 4 + seq
    x, y = seq % 2, seq // 2
    partner_x = (seq + 1 - 2 * x) % 4
    partner_y = {"seq": (seq + 2) % 4}
    sibling = {"section": 1 - sec}
    has_up, has_down = dp < dp_count - 1, dp > 0
    split = keep_ref.shape[1]
    rows = keep_ref.shape[0] // parts

    barrier = pltpu.get_barrier_semaphore()
    for turn in range(1, 8):
        other = (me + turn) % 8
        pl.semaphore_signal(
            barrier, inc=1, device_id={"section": other // 4, "seq": other % 4}, device_id_type=MESH
        )
    for there, step in ((has_up, 1), (has_down, -1)):

        @pl.when(there)
        def _(step=step):
            pl.semaphore_signal(barrier, inc=1, device_id={"dp": dp + step}, device_id_type=MESH)

    pl.semaphore_wait(barrier, 7 + jnp.where(has_up, 1, 0) + jnp.where(has_down, 1, 0))

    def remote(source, target, send, recv, device):
        return pltpu.make_async_remote_copy(
            src_ref=source, dst_ref=target, send_sem=send, recv_sem=recv,
            device_id=device, device_id_type=MESH,
        )

    def a2a(target, source):
        return remote(
            conv_ref.at[target], conv_out.at[dp, source], a2a_send.at[target], a2a_recv.at[source],
            {"section": target // 4, "seq": target % 4},
        )

    def sig(target, source):
        return remote(
            signal_ref.at[target], signal_out.at[source], sig_send.at[target], sig_recv.at[source],
            {"seq": target},
        )

    for turn in range(1, 8):
        a2a((me + turn) % 8, me).start()
    conv_local = pltpu.make_async_copy(conv_ref.at[me], conv_out.at[dp, me], local_sem.at[0])
    signal_local = pltpu.make_async_copy(signal_ref.at[seq], signal_out.at[seq], local_sem.at[1])
    conv_local.start()
    signal_local.start()

    def columns(layer, half):
        return (second_out if layer else whole_out.at[dp, y, half]).at[:, pl.ds(0, split)]

    def others(layer, half):
        return (second_out if layer else whole_out.at[dp, y, half]).at[:, pl.ds(split, rest_ref.shape[2])]

    class Layer:
        def __init__(self, layer):
            far = {"section": 1 - layer}
            self.mine = sec == layer
            self.even = x == layer
            received = column_recv.at[layer]
            self.keep_local = pltpu.make_async_copy(keep_ref, columns(layer, layer), local_sem.at[2])
            self.rest_local = pltpu.make_async_copy(rest_ref.at[layer], others(layer, layer), local_sem.at[3])
            self.keep_far = remote(keep_ref, columns(layer, 1 - layer), own_send.at[0], received, far)
            self.send_same = remote(
                send_ref, columns(layer, layer), own_send.at[1], received, {"seq": partner_x}
            )
            self.send_cross = remote(
                send_ref, columns(layer, 1 - layer), own_send.at[1], received, {**far, "seq": partner_x}
            )
            self.rest_far = remote(
                rest_ref.at[1 - layer], others(layer, 1 - layer), own_send.at[2], rest_recv.at[layer], far
            )

        def start(self):
            @pl.when(self.mine & self.even)
            def _():
                self.send_same.start()
                self.keep_local.start()

            @pl.when(self.mine & jnp.logical_not(self.even))
            def _():
                self.send_cross.start()
                self.keep_far.start()

            @pl.when(self.mine)
            def _():
                self.rest_far.start()
                self.rest_local.start()

        def wait(self):
            other = jnp.logical_not(self.mine)
            odd = jnp.logical_not(self.even)

            @pl.when(self.mine & self.even)
            def _():
                self.keep_local.wait()

            @pl.when(self.mine & odd)
            def _():
                self.send_same.wait_recv()

            @pl.when(self.mine)
            def _():
                self.rest_local.wait()

            @pl.when(other & self.even)
            def _():
                self.send_cross.wait_recv()

            @pl.when(other & odd)
            def _():
                self.keep_far.wait_recv()

            @pl.when(other)
            def _():
                self.rest_far.wait_recv()

        def finish(self):
            @pl.when(self.mine & self.even)
            def _():
                self.send_same.wait_send()

            @pl.when(self.mine & jnp.logical_not(self.even))
            def _():
                self.send_cross.wait_send()
                self.keep_far.wait_send()

            @pl.when(self.mine)
            def _():
                self.rest_far.wait_send()

    layers = [Layer(0), Layer(1)]
    for layer in layers:
        layer.start()
    for turn in range(1, 4):
        sig((seq + turn) % 4, seq).start()

    def line(slot, direction):
        index = (direction + 1) // 2
        return remote(
            conv_out.at[slot], conv_out.at[slot], line_send.at[index, slot], line_recv.at[slot],
            {"dp": dp + direction},
        )

    def place(slot, row, half, part):
        return whole_out.at[slot, row, half, pl.ds(part * rows, rows)]

    def along(slot, direction, part):
        index = (direction + 1) // 2
        ref = place(slot, y, sec, part)
        return remote(
            ref, ref, up_send.at[index, slot, part], up_recv.at[slot, part], {"dp": dp + direction}
        )

    def across(slot, row, part):
        ref = place(slot, row, sec, part)
        return remote(ref, ref, y_send.at[slot, part], y_recv.at[slot, part], partner_y)

    def to_core(slot, row, half, part):
        ref = place(slot, row, half, part)
        return remote(
            ref, ref, core_send.at[slot, row, part], core_recv.at[slot, row, part], sibling
        )

    for turn in range(1, 8):
        a2a((me + turn) % 8, (me + turn) % 8).wait_recv()
    conv_local.wait()
    for there, direction in ((has_up, 1), (has_down, -1)):

        @pl.when(there)
        def _(direction=direction):
            line(dp, direction).start()

    layers[0].wait()
    for part in range(parts):
        for there, direction in ((has_up, 1), (has_down, -1)):

            @pl.when(there)
            def _(direction=direction, part=part):
                along(dp, direction, part).start()

        across(dp, y, part).start()
        to_core(dp, y, sec, part).start()

    def stage(distance):
        arrivals = []
        for direction in (1, -1):
            slot = dp - direction * distance
            arrives = (slot >= 0) & (slot < dp_count)
            goes_on = arrives & (has_up if direction == 1 else has_down)
            arrivals.append((direction, slot, arrives, goes_on))

            @pl.when(arrives)
            def _(slot=slot, direction=direction):
                line(slot, direction).wait_recv()

            @pl.when(goes_on)
            def _(slot=slot, direction=direction):
                line(slot, direction).start()

        for part in range(parts):
            for direction, slot, arrives, goes_on in arrivals:

                @pl.when(arrives)
                def _(slot=slot, direction=direction, part=part):
                    along(slot, direction, part).wait_recv()

                @pl.when(goes_on)
                def _(slot=slot, direction=direction, part=part):
                    along(slot, direction, part).start()

                @pl.when(arrives)
                def _(slot=slot, part=part):
                    across(slot, y, part).start()
                    to_core(slot, y, sec, part).start()

    def pass_crossed(distance):
        for part in range(parts):
            for sign in (1, -1) if distance else (1,):
                slot = dp - sign * distance

                @pl.when((slot >= 0) & (slot < dp_count))
                def _(slot=slot, part=part):
                    across(slot, 1 - y, part).wait_recv()
                    to_core(slot, 1 - y, sec, part).start()

    for distance in range(1, dp_count):
        stage(distance)
        pass_crossed(distance - 1)
    pass_crossed(dp_count - 1)

    for slot in range(dp_count):
        for part in range(parts):
            for row in range(2):
                to_core(slot, row, 1 - sec, part).wait_recv()
                to_core(slot, row, sec, part).wait_send()
            across(slot, y, part).wait_send()
        for direction in (1, -1):
            sent = (slot <= dp if direction == 1 else slot >= dp) & (has_up if direction == 1 else has_down)

            @pl.when(sent)
            def _(slot=slot, direction=direction):
                line(slot, direction).wait_send()
                for part in range(parts):
                    along(slot, direction, part).wait_send()

    layers[1].wait()
    for layer in layers:
        layer.finish()
    for turn in range(1, 8):
        a2a((me + turn) % 8, me).wait_send()
    for turn in range(1, 4):
        sig((seq + turn) % 4, (seq + turn) % 4).wait_recv()
        sig((seq + turn) % 4, seq).wait_send()
    signal_local.wait()


def opening(conv_send, signal_send, keep, send, rest):
    count = lax.axis_size("dp")
    parts = 2
    rows, columns = keep.shape[0], keep.shape[1] + rest.shape[2]
    anywhere = pl.BlockSpec(memory_space=pl.ANY)
    dma = pltpu.SemaphoreType.DMA
    conv_all, signal_all, whole, second = pl.pallas_call(
        functools.partial(opening_kernel, count, parts),
        in_specs=[anywhere] * 5,
        out_specs=[anywhere] * 4,
        out_shape=[
            jax.ShapeDtypeStruct((count, *conv_send.shape), conv_send.dtype),
            jax.ShapeDtypeStruct(signal_send.shape, signal_send.dtype),
            jax.ShapeDtypeStruct((count, 2, 2, rows, columns), keep.dtype),
            jax.ShapeDtypeStruct((rows, columns), keep.dtype),
        ],
        scratch_shapes=[
            dma((4,)), dma((8,)), dma((8,)), dma((4,)), dma((4,)), dma((2, count)), dma((count,)),
            dma((3,)), dma((2,)), dma((2,)), dma((2, count, parts)), dma((count, parts)), dma((count, parts)),
            dma((count, parts)), dma((count, 2, parts)), dma((count, 2, parts)),
        ],
        compiler_params=pltpu.CompilerParams(
            collective_id=0, has_side_effects=True, vmem_limit_bytes=4 * 1024 * 1024
        ),
        name="opening",
    )(conv_send, signal_send, keep, send, rest)
    return conv_all, signal_all, whole.reshape(-1, columns), second


def slice_exchange_kernel(same_x, send_ref, got_ref, local_sem, send_sem, recv_sem):
    sec, seq = lax.axis_index("section"), lax.axis_index("seq")
    x, y = seq % 2, seq // 2
    if same_x:
        peers = [((sec + a) % 2, 2 * ((y + b) % 2) + x) for a, b in ((0, 1), (1, 0), (1, 1))]
    else:
        peers = [
            ((sec + a) % 2, 2 * ((y + b) % 2) + (x + c) % 2)
            for a in range(2) for b in range(2) for c in range(2) if a + b + c
        ]

    def place(section, seq):
        return section * 2 + seq // 2 if same_x else section * 4 + seq

    barrier = pltpu.get_barrier_semaphore()
    for section, other in peers:
        pl.semaphore_signal(
            barrier, inc=1, device_id={"section": section, "seq": other}, device_id_type=MESH
        )
    pl.semaphore_wait(barrier, len(peers))

    def copy(index, landing):
        section, other = peers[index]
        return pltpu.make_async_remote_copy(
            src_ref=send_ref.at[section * 4 + other], dst_ref=got_ref.at[landing],
            send_sem=send_sem.at[index], recv_sem=recv_sem.at[index],
            device_id={"section": section, "seq": other}, device_id_type=MESH,
        )

    for index in range(len(peers)):
        copy(index, place(sec, seq)).start()
    own = pltpu.make_async_copy(send_ref.at[sec * 4 + seq], got_ref.at[place(sec, seq)], local_sem.at[0])
    own.start()
    for index, peer in enumerate(peers):
        copy(index, place(*peer)).wait_recv()
        copy(index, place(sec, seq)).wait_send()
    own.wait()


def slice_exchange(value, same_x):
    anywhere = pl.BlockSpec(memory_space=pl.ANY)
    dma = pltpu.SemaphoreType.DMA
    count = 4 if same_x else 8
    return pl.pallas_call(
        functools.partial(slice_exchange_kernel, same_x),
        in_specs=[anywhere],
        out_specs=anywhere,
        out_shape=jax.ShapeDtypeStruct((count, *value.shape[1:]), value.dtype),
        scratch_shapes=[dma((1,)), dma((count - 1,)), dma((count - 1,))],
        compiler_params=pltpu.CompilerParams(
            collective_id=2 if same_x else 1, has_side_effects=True, vmem_limit_bytes=4 * 1024 * 1024
        ),
        cost_estimate=pl.CostEstimate(flops=0, bytes_accessed=value.size, transcendentals=0),
        name="slice_exchange",
    )(value)


def norm_stats(values):
    average = jnp.mean(values, axis=-1, keepdims=True)
    centred = values - average
    spread = jnp.mean(centred * centred, axis=-1, keepdims=True)
    return centred, lax.rsqrt(spread + EPS)


def norm_back(values, gain, grad):
    centred, inv = norm_stats(values)
    unit = centred * inv
    gain_grad = jnp.sum(grad * unit, axis=0)
    f = grad * gain
    mean_f = jnp.mean(f, axis=-1, keepdims=True)
    mean_fu = jnp.mean(f * unit, axis=-1, keepdims=True)
    return (f - mean_f - unit * mean_fu) * inv, gain_grad


def gelu_slope(values):
    cdf = 0.5 * (1.0 + lax.erf(values * (1.0 / math.sqrt(2.0))))
    pdf = jnp.exp(-0.5 * values * values) * (1.0 / math.sqrt(2.0 * math.pi))
    return cdf + values * pdf


def attention_forward_kernel(factor, q_ref, k_ref, v_ref, qs_ref, ks_ref, o_ref, lse_ref):
    queries = q_ref[...]
    lane = lax.broadcasted_iota(jnp.int32, queries.shape, 1)
    allowed = qs_ref[...] == ks_ref[...]
    keys = k_ref[...]
    values = v_ref[...]
    outs = []
    for head in range(2):
        mine = (lane < HEAD_DIM) if head == 0 else (lane >= HEAD_DIM)
        own = jnp.where(mine, queries, jnp.zeros_like(queries))
        scores = lax.dot_general(
            own, keys, (((1,), (1,)), ((), ())), preferred_element_type=jnp.float32
        ) * factor
        scores = jnp.where(allowed, scores, NEG)
        top = jnp.max(scores, axis=-1, keepdims=True)
        raised = jnp.exp(scores - top)
        total = jnp.sum(raised, axis=-1, keepdims=True)
        chances = (raised * (1.0 / total)).astype(jnp.bfloat16)
        outs.append(jnp.dot(chances, values, preferred_element_type=jnp.float32))
        lse_ref[0, head] = top + jnp.log(total)
    o_ref[...] = jnp.where(lane < HEAD_DIM, outs[0], outs[1]).astype(o_ref.dtype)


def attention_forward(packed, kv_all, query_segs, key_segs, factor):
    frames = packed.shape[0]
    keys = kv_all.shape[0]
    width = packed.shape[1] // 3
    pairs = width // 128
    rows = math.gcd(frames, 256)
    return pl.pallas_call(
        functools.partial(attention_forward_kernel, factor),
        grid=(pairs, frames // rows),
        in_specs=[
            pl.BlockSpec((rows, 128), lambda h, i: (i, h)),
            pl.BlockSpec((keys, 128), lambda h, i: (0, h)),
            pl.BlockSpec((keys, 128), lambda h, i: (0, pairs + h)),
            pl.BlockSpec((rows, 1), lambda h, i: (i, 0)),
            pl.BlockSpec((1, keys), lambda h, i: (0, 0)),
        ],
        out_specs=[
            pl.BlockSpec((rows, 128), lambda h, i: (i, h)),
            pl.BlockSpec((1, 2, rows, 1), lambda h, i: (h, 0, i, 0)),
        ],
        out_shape=[
            jax.ShapeDtypeStruct((frames, width), jnp.bfloat16),
            jax.ShapeDtypeStruct((pairs, 2, frames, 1), jnp.float32),
        ],
        compiler_params=pltpu.CompilerParams(vmem_limit_bytes=40 * 1024 * 1024),
        cost_estimate=pl.CostEstimate(
            flops=4 * frames * keys * width * 2,
            bytes_accessed=2 * (frames * width * 2 + keys * width * 2),
            transcendentals=frames * keys * (width // HEAD_DIM),
        ),
        name="attention_forward",
    )(packed, kv_all, kv_all, query_segs[:, None], key_segs[None, :])


def attention_backward_kernel(
    factor, q_ref, k_ref, v_ref, g_ref, o_ref, lse_ref, qs_ref, ks_ref, *rest
):
    *begin, dq_ref, dk_ref, dv_ref = rest
    step = pl.program_id(1)

    @pl.when(step == 0)
    def _():
        for index, total_ref in enumerate((dk_ref, dv_ref)):
            total_ref[...] = begin[index][...] if begin else jnp.zeros_like(total_ref)

    queries = q_ref[...]
    grads = g_ref[...]
    keys = k_ref[...]
    values = v_ref[...]
    lane = lax.broadcasted_iota(jnp.int32, queries.shape, 1)
    key_lane = lax.broadcasted_iota(jnp.int32, keys.shape, 1)
    allowed = qs_ref[...] == ks_ref[...]
    product = grads.astype(jnp.float32) * o_ref[...].astype(jnp.float32)
    dq = None
    for head in range(2):
        mine = (lane < HEAD_DIM) if head == 0 else (lane >= HEAD_DIM)
        key_mine = (key_lane < HEAD_DIM) if head == 0 else (key_lane >= HEAD_DIM)
        own_q = jnp.where(mine, queries, jnp.zeros_like(queries))
        own_g = jnp.where(mine, grads, jnp.zeros_like(grads))
        own_k = jnp.where(key_mine, keys, jnp.zeros_like(keys))
        delta = jnp.sum(jnp.where(mine, product, 0.0), axis=-1, keepdims=True)
        scores = lax.dot_general(
            own_q, keys, (((1,), (1,)), ((), ())), preferred_element_type=jnp.float32
        ) * factor
        chances = jnp.exp(jnp.where(allowed, scores, NEG) - lse_ref[0, head])
        prob_grad = lax.dot_general(
            own_g, values, (((1,), (1,)), ((), ())), preferred_element_type=jnp.float32
        )
        score_grad = (chances * (prob_grad - delta)).astype(jnp.bfloat16)
        part = jnp.dot(score_grad, own_k, preferred_element_type=jnp.float32)
        dq = part if dq is None else dq + part
        dk_ref[...] += lax.dot_general(
            score_grad, own_q, (((0,), (0,)), ((), ())), preferred_element_type=jnp.float32
        ) * factor
        dv_ref[...] += lax.dot_general(
            chances.astype(jnp.bfloat16), own_g, (((0,), (0,)), ((), ())),
            preferred_element_type=jnp.float32,
        )
    dq_ref[...] = (dq * factor).astype(dq_ref.dtype)


def attention_backward(packed, kv_all, grads, attended, lse, query_segs, key_segs, factor, begin=None):
    frames = packed.shape[0]
    keys = kv_all.shape[0]
    width = packed.shape[1] // 3
    pairs = width // 128
    rows = math.gcd(frames, 256)
    return pl.pallas_call(
        functools.partial(attention_backward_kernel, factor),
        grid=(pairs, frames // rows),
        in_specs=[
            pl.BlockSpec((rows, 128), lambda h, i: (i, h)),
            pl.BlockSpec((keys, 128), lambda h, i: (0, h)),
            pl.BlockSpec((keys, 128), lambda h, i: (0, pairs + h)),
            pl.BlockSpec((rows, 128), lambda h, i: (i, h)),
            pl.BlockSpec((rows, 128), lambda h, i: (i, h)),
            pl.BlockSpec((1, 2, rows, 1), lambda h, i: (h, 0, i, 0)),
            pl.BlockSpec((rows, 1), lambda h, i: (i, 0)),
            pl.BlockSpec((1, keys), lambda h, i: (0, 0)),
        ]
        + [pl.BlockSpec((keys, 128), lambda h, i: (0, h))] * (2 if begin else 0),
        out_specs=[
            pl.BlockSpec((rows, 128), lambda h, i: (i, h)),
            pl.BlockSpec((keys, 128), lambda h, i: (0, h)),
            pl.BlockSpec((keys, 128), lambda h, i: (0, h)),
        ],
        out_shape=[
            jax.ShapeDtypeStruct((frames, width), jnp.bfloat16),
            jax.ShapeDtypeStruct((keys, width), jnp.float32),
            jax.ShapeDtypeStruct((keys, width), jnp.float32),
        ],
        compiler_params=pltpu.CompilerParams(vmem_limit_bytes=48 * 1024 * 1024),
        cost_estimate=pl.CostEstimate(
            flops=10 * frames * keys * width * 2,
            bytes_accessed=4 * (frames * width * 2 + keys * width * 2),
            transcendentals=frames * keys * (width // HEAD_DIM),
        ),
        name="attention_backward",
    )(packed, kv_all, kv_all, grads, attended, lse, query_segs[:, None], key_segs[None, :], *(begin or ()))


CONV_STEP = 4


def conv_bands(kernel, per_group):
    groups = kernel.shape[1] // per_group
    steps = TAPS // CONV_STEP + 1
    bands = []
    for group in range(groups):
        own = kernel[:, group * per_group : (group + 1) * per_group]
        shifted = [
            jnp.pad(own, ((shift * per_group, (CONV_STEP - shift) * per_group), (0, 0)))
            for shift in range(CONV_STEP)
        ]
        band = jnp.concatenate(shifted, axis=1)
        bands.append(band.reshape(steps, CONV_STEP * per_group, CONV_STEP * per_group))
    return bands


def group_view(values, per_group):
    rows, frames, width = values.shape
    return [
        values[:, :, g * per_group : (g + 1) * per_group].reshape(
            rows, frames // CONV_STEP, CONV_STEP * per_group
        )
        for g in range(width // per_group)
    ]


def ungroup(parts, per_group):
    rows, blocks, _ = parts[0].shape
    return jnp.concatenate(
        [part.reshape(rows, blocks * CONV_STEP, per_group) for part in parts], axis=2
    )


CONV_DIMS = ("NWC", "WIO", "NWC")


def conv_forward(views, bands):
    half = TAPS // 2 // CONV_STEP
    return [
        lax.conv_general_dilated(
            view, band, (1,), [(half, half)], dimension_numbers=CONV_DIMS,
            preferred_element_type=jnp.float32,
        )
        for view, band in zip(views, bands)
    ]


def conv_back(grad_views, bands):
    half = TAPS // 2 // CONV_STEP
    return [
        lax.conv_general_dilated(
            view, jnp.transpose(band[::-1], (0, 2, 1)), (1,), [(half, half)],
            dimension_numbers=CONV_DIMS, preferred_element_type=jnp.float32,
        )
        for view, band in zip(grad_views, bands)
    ]


def conv_taps_grad(views, grad_views, per_group):
    half = TAPS // 2 // CONV_STEP
    results = []
    for view, grad in zip(views, grad_views):
        band = lax.conv_general_dilated(
            view, grad, (1,), [(half, half)],
            dimension_numbers=("CWN", "IWO", "WNC"),
            preferred_element_type=jnp.float32,
        )
        flat = band.reshape(-1, CONV_STEP * per_group)
        total = None
        for shift in range(CONV_STEP):
            part = flat[
                shift * per_group : (shift + TAPS) * per_group,
                shift * per_group : (shift + 1) * per_group,
            ]
            total = part if total is None else total + part
        results.append(total)
    return jnp.concatenate(results, axis=1)


def to_column(vector, width):
    return jnp.pad(vector[:, None], ((0, 0), (0, width - 1)))


def per_device_pairs(
    signal, frame_segment_index, conv_weight, conv_bias, norm1_gain, qkv_weight, out_weight,
    norm2_gain, up_weight, down_weight, cotangent,
):
    micro_count, frames, width = signal.shape
    bf16, f32 = jnp.bfloat16, jnp.float32
    per_group = width // GROUPS
    dp_count = lax.axis_size("dp")
    factor = 1.0 / math.sqrt(HEAD_DIM)
    sec = lax.axis_index("section")
    dp = lax.axis_index("dp")
    seq = lax.axis_index("seq")
    x, y = seq % 2, seq // 2
    sec0, x0 = sec == 0, x == 0
    row_frames = 4 * frames
    half_frames = 2 * frames
    both = ("section", "seq")

    block_width = width // 8
    rows_here = conv_weight.shape[0]
    conv_low = conv_weight.astype(bf16).reshape(rows_here, 8, block_width)
    bias_low = jnp.pad(conv_bias.astype(bf16), (0, block_width - conv_bias.shape[0]))
    bias_rows = jnp.pad(
        jnp.broadcast_to(bias_low[None, None, :], (1, 8, block_width)), ((0, 15), (0, 0), (0, 0))
    )
    conv_send = jnp.transpose(jnp.concatenate([conv_low, bias_rows], axis=0), (1, 0, 2))

    own_half = jnp.where(sec0, signal[:, :, : width // 2], signal[:, :, width // 2 :])
    sig_send = jnp.transpose(own_half.reshape(micro_count, frames, 4, block_width), (2, 0, 1, 3))
    in_rows = qkv_weight.shape[1]
    unit = down_weight.shape[1] // 4
    qkv_view = qkv_weight[0].astype(bf16).reshape(in_rows, -1, 2, HEAD_DIM)
    qkv_parity = [qkv_view[:, :, p].reshape(in_rows, -1) for p in range(2)]
    up_view = up_weight[0].astype(bf16).reshape(in_rows, -1, 2, 2, 2, unit)
    up_parity = [
        jnp.transpose(up_view[:, :, p], (0, 3, 1, 2, 4)).reshape(in_rows, -1) for p in range(2)
    ]
    qkv_cols, up_cols = qkv_parity[0].shape[1], up_parity[0].shape[1]
    col_one = to_column(norm1_gain[0].astype(bf16), 128)
    col_two = to_column(norm2_gain[0].astype(bf16), 128)
    cut = qkv_cols + 128
    keep_cols, send_cols = [
        jnp.concatenate([a, col_one, b, col_two], axis=1)
        for a, b in zip(choose(x0, *qkv_parity), choose(x0, *up_parity))
    ]
    out_low = out_weight[0].astype(bf16)
    down_low = down_weight[0].astype(bf16).reshape(2, 2, unit, width)
    rest = jnp.stack(
        [
            jnp.concatenate(
                [out_low[:, h * width // 2 : (h + 1) * width // 2], down_low[h, 0], down_low[h, 1]], axis=1
            )
            for h in range(2)
        ]
    )
    up_at = cut
    two_at = up_at + up_cols
    out_at = two_at + 128
    down_at = out_at + width // 2
    conv_all, sig_got, whole, second_piece = opening(conv_send, sig_send, keep_cols, send_cols, rest)
    gathered = [whole, gather_rows(second_piece)]
    sig_all = jnp.transpose(sig_got, (1, 0, 2, 3)).reshape(micro_count, row_frames, block_width)
    conv_all = conv_all.reshape(dp_count, 2, 4, rows_here + 16, block_width)
    conv_all = jnp.transpose(conv_all, (1, 0, 2, 3, 4))
    bias_all = conv_all[:, :, :, rows_here, : conv_bias.shape[0]].reshape(width)
    bias_own = lax.dynamic_slice_in_dim(bias_all, (sec * 4 + seq) * block_width, block_width, 0)
    kernel_own = conv_all[:, :, :, :rows_here].reshape(TAPS * per_group, block_width)
    bands = conv_bands(kernel_own, per_group)


    def views(whole):
        w_out = jnp.transpose(
            whole[:, out_at:down_at].reshape(-1, 2, in_rows, width // 2), (0, 2, 1, 3)
        ).reshape(-1, width)
        gain_one = whole[:, qkv_cols].astype(f32)[None, :]
        gain_two = whole[:, two_at].astype(f32)[None, :]
        w_up = [whole[:, up_at + part * width : up_at + (part + 1) * width] for part in range(2)]
        w_down = [whole[:, down_at + part * width : down_at + (part + 1) * width] for part in range(2)]
        return gain_one, whole[:, :qkv_cols], w_out, gain_two, w_up, w_down

    layer_weights = []

    picked = jnp.where(sec0, cotangent[0], cotangent[1])
    across = [(s * 4 + 2 * yy + xx, yy * 4 + 2 * s + xx) for s in range(2) for yy in range(2) for xx in range(2)]
    across = [(a, b) for a, b in across if a != b]

    def over_rows(value):
        return jnp.where(sec == y, value, lax.ppermute(value, both, across))

    cot_own = over_rows(picked)
    cot_other = swap_x(cot_own)
    cot_pair = choose(x0, cot_own, cot_other)
    top_grad = jnp.concatenate(cot_pair, axis=0).astype(f32)

    segment_row = jnp.where(y == 0, frame_segment_index[0], frame_segment_index[1])
    seg_pair = choose(sec0, segment_row[:half_frames], segment_row[half_frames:])
    query_segs = seg_pair[0]
    key_segs = jnp.concatenate(seg_pair)

    sig_views = group_view(sig_all, per_group)
    conv_pre = ungroup(conv_forward(sig_views, bands), per_group) + bias_own.astype(f32)
    stream = (sig_all.astype(f32) + smooth(conv_pre)).astype(bf16)
    slope = gelu_slope(conv_pre).astype(bf16)
    stream_send = stream.reshape(2, 2, half_frames, block_width)
    stream_send = jnp.transpose(stream_send, (1, 0, 2, 3))
    stream_send = jnp.repeat(stream_send.reshape(4, half_frames, block_width), 2, axis=0)
    stream_got = slice_exchange(stream_send, False)
    layer_in = jnp.transpose(stream_got, (1, 0, 2)).reshape(half_frames, width).astype(f32)

    chunks = 2
    rows = half_frames // chunks
    layer_in = [layer_in[c * rows : (c + 1) * rows] for c in range(chunks)]
    chunk_segs = [query_segs[c * rows : (c + 1) * rows] for c in range(chunks)]
    kept = []
    for layer in range(2):
        whole = gathered[layer]
        if layer:
            layer_in = []
            previous_lows[0], whole = after(previous_lows[0], whole)
        layer_weights.append(views(whole))
        gain_one, w_qkv, w_out, gain_two, w_up, w_down = layer_weights[layer]
        normed_one, packed, kv_own, kv_other = [], [], [], []
        for c in range(chunks):
            if layer:
                total = previous[c] + pair_sum(previous_lows[c], packed[-1] if c else None)
                layer_in.append(total.astype(bf16).astype(f32))
            centred, inv = norm_stats(layer_in[c])
            normed_one.append((centred * inv * gain_one).astype(bf16))
            packed.append(jnp.dot(normed_one[c], w_qkv, preferred_element_type=f32).astype(bf16))
            kv_own.append(packed[c][:, width // 2 :])
            kv_other.append(swap_section(kv_own[c]))
        kv_all = jnp.concatenate(kv_own + kv_other, axis=0)
        attended, lse, resid_two, normed_two, hidden, hidden_slope = [], [], [], [], [], []
        attn_lows, lows = [], []
        for c in range(chunks):
            own = packed[c]
            if c:
                attn_lows[-1], own = after(attn_lows[-1], own)
            mixed, log_total = attention_forward(own, kv_all, chunk_segs[c], key_segs, factor)
            attended.append(mixed)
            lse.append(log_total)
            attn_lows.append(jnp.dot(mixed, w_out, preferred_element_type=f32).astype(bf16))
        for c in range(chunks):
            resid_two.append(layer_in[c] + pair_sum(attn_lows[c], lows[-1] if c else None))
            centred, inv = norm_stats(resid_two[c])
            normed_two.append((centred * inv * gain_two).astype(bf16))
            down_sum, own_hidden, own_slope = None, [], []
            for part in range(2):
                hidden_pre = jnp.dot(normed_two[c], w_up[part], preferred_element_type=f32)
                own_hidden.append(smooth(hidden_pre).astype(bf16))
                own_slope.append(gelu_slope(hidden_pre).astype(bf16))
            for part in range(2):
                term = jnp.dot(own_hidden[part], w_down[part], preferred_element_type=f32)
                down_sum = term if down_sum is None else down_sum + term
            hidden.append(own_hidden)
            hidden_slope.append(own_slope)
            lows.append(down_sum.astype(bf16))

        resid_two_last = resid_two
        kept.append((layer_in, normed_one, packed, kv_all, attended, lse, resid_two, normed_two, hidden, hidden_slope))
        previous, previous_lows = resid_two, lows

    def outer(left, right):
        return lax.dot_general(
            left, right, (((0,), (0,)), ((), ())), preferred_element_type=f32
        ).astype(bf16)

    def back(left, right):
        return lax.dot_general(left, right, (((1,), (1,)), ((), ())), preferred_element_type=f32)

    grad_out = [top_grad[c * rows : (c + 1) * rows] for c in range(chunks)]
    attn_members, scattered = [], []
    for layer in (1, 0):
        gain_one, w_qkv, w_out, gain_two, w_up, w_down = layer_weights[layer]
        (layer_in, normed_one, packed, kv_all, attended, lse, resid_two, normed_two, hidden, hidden_slope) = kept[layer]
        branch = [member.astype(bf16) for member in grad_out]
        pre_grad, sums, low = [], [], None
        for c in range(chunks):
            own = branch[c]
            if low is not None:
                low, own = after(low, own)
                sums.append(pair_sum(low))
            own_pre, part_sum = [], None
            for part in range(2):
                own_pre.append((back(own, w_down[part]) * hidden_slope[c][part].astype(f32)).astype(bf16))
            for part in range(2):
                term = back(own_pre[part], w_up[part])
                part_sum = term if part_sum is None else part_sum + term
            pre_grad.append(own_pre)
            low = part_sum.astype(bf16)
        sums.append(pair_sum(low))
        whole_pre = [jnp.concatenate([pre_grad[c][p] for c in range(chunks)]) for p in range(2)]
        whole_hidden = [jnp.concatenate([hidden[c][p] for c in range(chunks)]) for p in range(2)]
        whole_branch, whole_two = jnp.concatenate(branch), jnp.concatenate(normed_two)
        ff_members = [
            outer(whole_two, whole_pre[0]), outer(whole_two, whole_pre[1]),
            outer(whole_hidden[0], whole_branch), outer(whole_hidden[1], whole_branch),
        ]
        if layer == 1:
            ff_members.append(jnp.zeros((width, 128), bf16))
        partial = jnp.concatenate(attn_members + ff_members, axis=1)
        if layer == 0:
            sums, (partial, output_rows) = after(sums, (partial, output_rows))
        scattered.append(scatter_rows(partial))
        resid_grad, attn_branch, dq, gain_two_grad = [], [], [], None
        dkv = None
        for c in range(chunks):
            in_part, gain_part = norm_back(resid_two[c], gain_two, sums[c])
            gain_two_grad = gain_part if gain_two_grad is None else gain_two_grad + gain_part
            resid_grad.append(in_part + grad_out[c])
            attn_branch.append(resid_grad[c].astype(bf16))
            attended_grad = back(attn_branch[c], w_out).astype(bf16)
            if layer == 1 and c == 0:
                attended_grad, lows = after(attended_grad, lows)
                output = [member + pair_sum(low) for member, low in zip(resid_two_last, lows)]
                row_block = over_rows(jnp.where(x0, output[0], output[1]))
                output_rows = jnp.stack(choose(sec0, row_block, swap_section(row_block)))
            own_dq, *dkv = attention_backward(
                packed[c], kv_all, attended_grad, attended[c], lse[c], chunk_segs[c], key_segs, factor,
                None if c == 0 else dkv,
            )
            dq.append(own_dq)
        if layer == 0:
            dkv, scattered[0] = after(dkv, scattered[0])
        else:
            dkv, output = after(dkv, output)
        dkv = jnp.concatenate(dkv, axis=1)
        other_dkv = swap_section(dkv[half_frames:].astype(bf16))
        dkv_own = (dkv[:half_frames] + other_dkv.astype(f32)).astype(bf16)
        packed_grad, sums, low = [], [], None
        for c in range(chunks):
            packed_grad.append(jnp.concatenate([dq[c], dkv_own[c * rows : (c + 1) * rows]], axis=1))
            own = packed_grad[c]
            if low is not None:
                low, own = after(low, own)
                sums.append(pair_sum(low))
            low = back(own, w_qkv).astype(bf16)
        sums.append(pair_sum(low))
        next_grad, gain_one_grad = [], None
        for c in range(chunks):
            in_part, gain_part = norm_back(layer_in[c], gain_one, sums[c])
            gain_one_grad = gain_part if gain_one_grad is None else gain_one_grad + gain_part
            next_grad.append((resid_grad[c] + in_part).astype(bf16))
        whole_one, whole_pg, whole_att, whole_ab = [
            jnp.concatenate(m) for m in (normed_one, packed_grad, attended, attn_branch)
        ]
        grad_out_weight = jnp.transpose(
            outer(whole_att, whole_ab).reshape(-1, in_rows, 2, width // 2), (0, 2, 1, 3)
        ).reshape(-1, width // 2)
        gain_grads = jnp.stack([gain_one_grad, gain_two_grad], axis=1).astype(bf16)
        gain_grads = jnp.pad(gain_grads, ((0, 0), (0, 126)))
        attn_members = [outer(whole_one, whole_pg), gain_grads, grad_out_weight]
        grad_out = [member.astype(f32) for member in next_grad]
    grad_in_low = jnp.concatenate(next_grad)
    scattered.append(scatter_rows(jnp.concatenate(attn_members, axis=1)))

    lig_send = jnp.transpose(grad_in_low.reshape(half_frames, 8, block_width), (1, 0, 2))
    lig_got = lax.all_to_all(lig_send, both, 0, 0, tiled=True).reshape(2, 2, 2, half_frames, block_width)[:, :, 0]
    lig = jnp.transpose(lig_got, (1, 0, 2, 3)).reshape(micro_count, row_frames, block_width)
    conv_grad = (lig.astype(f32) * slope.astype(f32)).astype(bf16)
    grad_views = group_view(conv_grad, per_group)
    back = ungroup(conv_back(grad_views, bands), per_group)
    grad_signal = (lig.astype(f32) + back).astype(bf16)
    gs_send = jnp.transpose(
        grad_signal.reshape(micro_count, 4, frames, block_width), (1, 0, 2, 3)
    )
    gs_send = jnp.concatenate([gs_send, gs_send], axis=0)
    taps_grad = conv_taps_grad(sig_views, grad_views, per_group)
    bias_grad = jnp.sum(conv_grad.astype(f32), axis=(0, 1))
    taps_view = jnp.transpose(
        taps_grad.reshape(2, dp_count, 4, rows_here, block_width), (1, 0, 2, 3, 4)
    ).astype(bf16)
    bias_view = jnp.pad(
        jnp.broadcast_to(bias_grad.astype(bf16), (dp_count, 2, 4, 1, block_width)),
        ((0, 0), (0, 0), (0, 0), (0, 15), (0, 0)),
    )
    taps_send = jnp.concatenate([taps_view, bias_view], axis=3)
    gs_got = lax.all_to_all(gs_send, both, 0, 0, tiled=True)
    attn_cols = cut + width // 2

    def over_section(first, second):
        keep, send = choose(sec0, first, second)
        return choose(sec0, keep, swap_section(send))


    taps_sum, (_, gs_got) = sum_dp(taps_send, dp, (gs_send, gs_got))
    gs_rows = jnp.transpose(gs_got, (1, 2, 0, 3)).reshape(micro_count, frames, width).astype(f32)
    ends = jnp.where(sec0, gs_rows, output_rows)[None]
    taps_got = lax.all_to_all(
        taps_sum.reshape(8, rows_here + 16, block_width), both, 0, 0, tiled=True
    )
    taps_got, scattered[1] = after(taps_got, scattered[1])
    conv_weight_grad = jnp.transpose(taps_got[:, :rows_here], (1, 0, 2)).reshape(rows_here, width).astype(f32)
    bias_count = conv_bias.shape[0]
    conv_bias_grad = lax.dynamic_slice_in_dim(
        taps_got[:, rows_here].reshape(width),
        ((sec * dp_count + dp) * 4 + seq) * bias_count,
        bias_count,
        0,
    ).astype(f32)

    turned = [(t * 4 + 2 * r + c, c * 4 + 2 * r + t) for t in range(2) for r in range(2) for c in range(2) if t != c]
    crossed = [(t * 4 + 2 * r + c, (1 - c) * 4 + 2 * r + t) for t in range(2) for r in range(2) for c in range(2)]

    def home(first, second):
        straight, other = choose(x0, first, second)
        straight = jnp.where(sec == x, straight, lax.ppermute(straight, both, turned))
        other = lax.ppermute(other, both, crossed)
        return choose(sec0, straight, other)

    ff_layers = (scattered[1][:, attn_cols:], scattered[0][:, :-128])
    ff_sets = over_section(*(member[:, up_cols:] for member in ff_layers))
    down_grad = jnp.concatenate(
        [member[:, at : at + width] for member in ff_sets for at in (0, width)], axis=0
    ).astype(f32)[None]
    up_grad = jnp.stack(
        [
            jnp.transpose(member.reshape(in_rows, 2, -1, 2, unit), (0, 2, 3, 1, 4))
            for member in home(*(member[:, :up_cols] for member in ff_layers))
        ],
        axis=2,
    ).reshape(in_rows, -1).astype(f32)[None]
    scattered[2], (up_grad, down_grad) = after(scattered[2], (up_grad, down_grad))
    attn_layers = (scattered[2], scattered[1][:, :attn_cols])
    attn_sets = over_section(*(member[:, cut:] for member in attn_layers))
    out_grad = jnp.concatenate(attn_sets, axis=1).astype(f32)[None]
    qkv_sets = home(*(member[:, :cut] for member in attn_layers))
    norm1_grad = qkv_sets[0][:, qkv_cols].astype(f32)[None]
    norm2_grad = qkv_sets[0][:, qkv_cols + 1].astype(f32)[None]
    qkv_grad = jnp.stack(
        [member[:, :qkv_cols].reshape(in_rows, -1, HEAD_DIM) for member in qkv_sets], axis=2
    ).reshape(in_rows, -1).astype(f32)[None]
    return (ends, conv_weight_grad, conv_bias_grad, norm1_grad, qkv_grad, out_grad, norm2_grad, up_grad, down_grad)


def solution(mesh):
    placed = (
        P("dp", "seq", None),
        P("dp", None),
        P(("section", "dp", "seq"), None),
        P(("section", "dp", "seq")),
        P("section", ("dp", "seq")),
        P("section", ("dp", "seq"), None),
        P("section", ("dp", "seq"), None),
        P("section", ("dp", "seq")),
        P("section", ("dp", "seq"), None),
        P("section", ("dp", "seq"), None),
        P("dp", "seq", None),
    )

    def step(*arrays):
        pairs = mesh.shape["seq"] == 4 and mesh.shape["section"] == 2 and arrays[0].shape[0] == 2
        return (per_device_pairs if pairs else per_device)(*arrays)

    return jax.shard_map(
        step,
        mesh=mesh,
        in_specs=placed,
        out_specs=(
            P("section", "dp", "seq", None),
            P(("section", "dp", "seq"), None),
            P(("section", "dp", "seq")),
            P("section", ("dp", "seq")),
            P("section", ("dp", "seq"), None),
            P("section", ("dp", "seq"), None),
            P("section", ("dp", "seq")),
            P("section", ("dp", "seq"), None),
            P("section", ("dp", "seq"), None),
        ),
        check_vma=False,
    )
```

```python
import functools
import math

import jax
import jax.numpy as jnp
from jax import lax
from jax.experimental import pallas as pl
from jax.experimental.pallas import tpu as pltpu
from jax.sharding import PartitionSpec as P

HEAD_DIM = 64
GROUPS = 16
TAPS = 128


EPS = 1e-05
NEG = -1e30


def padded_2(block, sides, width):
    for axis, dim in sides:
        count = lax.axis_size(axis)
        forward = [(i, i + 1) for i in range(count - 1)]
        backward = [(target, source) for source, target in forward]
        low = lax.ppermute(
            lax.slice_in_dim(block, block.shape[dim] - width, None, axis=dim), axis, forward
        )
        high = lax.ppermute(lax.slice_in_dim(block, 0, width, axis=dim), axis, backward)
        block = jnp.concatenate([low, block, high], axis=dim)
    return block


def from_behind(value, axis, steps):
    count = lax.axis_size(axis)
    first, last = (max(0, -steps), min(count, count - steps))
    return lax.ppermute(value, axis, [(source, source + steps) for source in range(first, last)])


def normalize(values, gain):
    average = jnp.mean(values, axis=-1, keepdims=True)
    centred = values - average
    spread = jnp.mean(centred * centred, axis=-1, keepdims=True)
    return centred * lax.rsqrt(spread + EPS) * gain


def smooth(values):
    return jax.nn.gelu(values, approximate=False)


def conv_taps(padded, kernel, frames):
    width_all = padded.shape[1]
    per_group = width_all // GROUPS
    tap_step = math.gcd(TAPS, 16)
    weight_view = kernel.reshape(TAPS, per_group, GROUPS, per_group)
    running = jnp.zeros((frames, GROUPS, per_group), jnp.float32)
    for first_tap in range(0, TAPS, tap_step):
        windows = jnp.stack(
            [padded[first_tap + offset : first_tap + offset + frames] for offset in range(tap_step)]
        )
        windows = windows.reshape(tap_step, frames, GROUPS, per_group)
        running = running + jnp.einsum(
            "jtgc,jcgo->tgo",
            windows,
            weight_view[first_tap : first_tap + tap_step],
            preferred_element_type=jnp.float32,
        )
    return running.reshape(frames, width_all)


def conv_input_grad(grad_pad, kernel, frames):
    width_all = grad_pad.shape[1]
    per_group = width_all // GROUPS
    tap_step = math.gcd(TAPS, 16)
    weight_view = kernel.reshape(TAPS, per_group, GROUPS, per_group)
    running = jnp.zeros((frames, GROUPS, per_group), jnp.float32)
    for first_tap in range(0, TAPS, tap_step):
        back_windows = jnp.stack(
            [
                grad_pad[TAPS - first_tap - offset : TAPS - first_tap - offset + frames]
                for offset in range(tap_step)
            ]
        )
        back_windows = back_windows.reshape(tap_step, frames, GROUPS, per_group)
        running = running + jnp.einsum(
            "jtgo,jcgo->tgc",
            back_windows,
            weight_view[first_tap : first_tap + tap_step],
            preferred_element_type=jnp.float32,
        )
    return running.reshape(frames, width_all)


def conv_kernel_grad(padded_all, grad_all):
    step_count, frames, width_all = grad_all.shape
    per_group = width_all // GROUPS
    tap_step = math.gcd(TAPS, 16)
    grad_view = grad_all.reshape(step_count * frames, GROUPS, per_group)
    kernel_parts = []
    for first_tap in range(0, TAPS, tap_step):
        windows = jnp.stack(
            [
                padded_all[:, first_tap + offset : first_tap + offset + frames]
                for offset in range(tap_step)
            ]
        )
        windows = windows.reshape(tap_step, step_count * frames, GROUPS, per_group)
        kernel_parts.append(
            jnp.einsum("jtgc,tgo->jcgo", windows, grad_view, preferred_element_type=jnp.float32)
        )
    return jnp.concatenate(kernel_parts, axis=0).reshape(TAPS * per_group, width_all)


def score_block(query_heads, key_block, query_segs, key_segs, factor):
    scores = (
        jnp.einsum("qhd,khd->hqk", query_heads, key_block, preferred_element_type=jnp.float32)
        * factor
    )
    allowed = (query_segs[:, None] == key_segs[None, :])[None]
    return (scores, allowed)


def front(layer_in, weights, kernel, conv_shift, first_section):
    frames, width_all = layer_in.shape
    padded = padded_2(layer_in, (("seq", 0),), TAPS // 2)
    conv_pre = lax.cond(
        first_section,
        lambda: conv_taps(padded, kernel, frames) + conv_shift.astype(jnp.float32),
        lambda: jnp.zeros((frames, width_all), jnp.float32),
    )
    conv_val, conv_pull = jax.vjp(smooth, conv_pre)
    resid_one = layer_in.astype(jnp.float32) + conv_val
    normed_val, norm_pull = jax.vjp(normalize, resid_one, weights[0].astype(jnp.float32))
    normed_one = normed_val.astype(jnp.bfloat16)
    packed = jnp.dot(normed_one, weights[1], preferred_element_type=jnp.float32).astype(
        jnp.bfloat16
    )
    return (padded, conv_pull, resid_one, norm_pull, normed_one, packed)


def tail(resid_one, attn_low, weights):
    resid_two = resid_one + jnp.dot(attn_low, weights[2], preferred_element_type=jnp.float32)
    normed_val, norm_pull = jax.vjp(normalize, resid_two, weights[3].astype(jnp.float32))
    normed_two = normed_val.astype(jnp.bfloat16)
    hidden_pre = jnp.dot(normed_two, weights[4], preferred_element_type=jnp.float32)
    hidden_val, gelu_pull = jax.vjp(smooth, hidden_pre)
    hidden_low = hidden_val.astype(jnp.bfloat16)
    result = resid_two + jnp.dot(hidden_low, weights[5], preferred_element_type=jnp.float32)
    return (result, norm_pull, normed_two, gelu_pull, hidden_low)


def key_loop(keys_all, values_all, segment_row, head_count, visit, initial):
    total_rows = keys_all.shape[0]
    block_rows = math.gcd(total_rows, 512)

    def one_block(block_index, running):
        offset = block_index * block_rows
        key_block = lax.dynamic_slice_in_dim(keys_all, offset, block_rows, 0).reshape(
            block_rows, head_count, HEAD_DIM
        )
        value_block = lax.dynamic_slice_in_dim(values_all, offset, block_rows, 0).reshape(
            block_rows, head_count, HEAD_DIM
        )
        key_segs = lax.dynamic_slice_in_dim(segment_row, offset, block_rows, 0)
        return visit(running, key_block, value_block, key_segs)

    return lax.fori_loop(0, total_rows // block_rows, one_block, initial)


def layer_forward(
    layer_in, segment_row, weights, kernel, conv_shift, first_section, my_start, factor
):
    frames, width_all = layer_in.shape
    head_count = width_all // HEAD_DIM
    padded, conv_pull, resid_one, norm_pull, normed_one, packed = front(
        layer_in, weights, kernel, conv_shift, first_section
    )
    query_heads = packed[:, :width_all].reshape(frames, head_count, HEAD_DIM)
    query_segs = lax.dynamic_slice_in_dim(segment_row, my_start, frames, 0)
    initial = (
        jnp.full((head_count, frames), NEG, jnp.float32),
        jnp.zeros((head_count, frames), jnp.float32),
        jnp.zeros((head_count, frames, HEAD_DIM), jnp.float32),
    )
    key_piece = lax.all_gather(packed[:, width_all : 2 * width_all], "seq", axis=0, tiled=True)
    value_piece = lax.all_gather(packed[:, 2 * width_all :], "seq", axis=0, tiled=True)
    piece_rows = key_piece.shape[0]
    block_rows = math.gcd(piece_rows, 512)

    def one_block(block_index, running):
        run_max, run_sum, run_acc = running
        offset = block_index * block_rows
        key_block = lax.dynamic_slice_in_dim(key_piece, offset, block_rows, 0).reshape(
            block_rows, head_count, HEAD_DIM
        )
        value_block = lax.dynamic_slice_in_dim(value_piece, offset, block_rows, 0).reshape(
            block_rows, head_count, HEAD_DIM
        )
        key_segs = lax.dynamic_slice_in_dim(segment_row, offset, block_rows, 0)
        scores, allowed = score_block(query_heads, key_block, query_segs, key_segs, factor)
        masked = jnp.where(allowed, scores, NEG)
        new_max = jnp.maximum(run_max, jnp.max(masked, axis=-1))
        weights_now = jnp.where(allowed, jnp.exp(masked - new_max[..., None]), 0.0)
        rescale = jnp.exp(run_max - new_max)
        run_sum = run_sum * rescale + jnp.sum(weights_now, axis=-1)
        run_acc = run_acc * rescale[..., None] + jnp.einsum(
            "hqk,khd->hqd",
            weights_now.astype(jnp.bfloat16),
            value_block,
            preferred_element_type=jnp.float32,
        )
        return (new_max, run_sum, run_acc)

    run_max, run_sum, run_acc = lax.fori_loop(0, piece_rows // block_rows, one_block, initial)
    log_total = run_max + jnp.log(run_sum)
    mixture = run_acc / run_sum[..., None]
    attn_low = jnp.transpose(mixture, (1, 0, 2)).reshape(frames, width_all).astype(jnp.bfloat16)
    result, norm_two_pull, normed_two, gelu_pull, hidden_low = tail(resid_one, attn_low, weights)
    kept = (
        padded,
        conv_pull,
        norm_pull,
        normed_one,
        packed,
        log_total,
        mixture,
        attn_low,
        norm_two_pull,
        normed_two,
        gelu_pull,
        hidden_low,
        segment_row,
    )
    return (result, kept)


def layer_backward(kept, grad_out, weights, kernel, first_section, my_start, factor):
    (
        padded,
        conv_pull,
        norm_one_pull,
        normed_one,
        packed,
        log_total,
        mixture,
        attn_low,
        norm_two_pull,
        normed_two,
        gelu_pull,
        hidden_low,
        segment_row,
    ) = kept
    frames, width_all = normed_one.shape
    head_count = width_all // HEAD_DIM
    query_heads = packed[:, :width_all].reshape(frames, head_count, HEAD_DIM)
    key_local = packed[:, width_all : 2 * width_all]
    value_local = packed[:, 2 * width_all :]
    query_segs = lax.dynamic_slice_in_dim(segment_row, my_start, frames, 0)
    keys_all, values_all = (
        lax.all_gather(key_local, "seq", axis=0, tiled=True),
        lax.all_gather(value_local, "seq", axis=0, tiled=True),
    )

    def chances_for(key_block, key_segs):
        scores, allowed = score_block(query_heads, key_block, query_segs, key_segs, factor)
        return jnp.where(
            allowed, jnp.exp(jnp.where(allowed, scores, NEG) - log_total[..., None]), 0.0
        )

    branch_grad = grad_out.astype(jnp.bfloat16)
    hidden_grad = jnp.einsum(
        "to,io->ti", branch_grad, weights[5], preferred_element_type=jnp.float32
    )
    pre_grad = gelu_pull(hidden_grad)[0].astype(jnp.bfloat16)
    normed_two_grad = jnp.einsum(
        "tf,if->ti", pre_grad, weights[4], preferred_element_type=jnp.float32
    )
    resid_two_grad, grad_gain_two = norm_two_pull(normed_two_grad)
    resid_two_grad = resid_two_grad + grad_out
    attn_branch_grad = resid_two_grad.astype(jnp.bfloat16)
    attended_grad = jnp.einsum(
        "to,io->ti", attn_branch_grad, weights[2], preferred_element_type=jnp.float32
    ).astype(jnp.bfloat16)
    dout_heads = attended_grad.reshape(frames, head_count, HEAD_DIM)
    delta_rows = jnp.einsum("qhd,hqd->hq", dout_heads.astype(jnp.float32), mixture)

    def visit_query(running, key_block, value_block, key_segs):
        chances = chances_for(key_block, key_segs)
        prob_grad = jnp.einsum(
            "qhd,khd->hqk", dout_heads, value_block, preferred_element_type=jnp.float32
        )
        score_grad = (chances * (prob_grad - delta_rows[..., None])).astype(jnp.bfloat16)
        return running + jnp.einsum(
            "hqk,khd->qhd", score_grad, key_block, preferred_element_type=jnp.float32
        )

    grad_query = (
        key_loop(
            keys_all,
            values_all,
            segment_row,
            head_count,
            visit_query,
            jnp.zeros((frames, head_count, HEAD_DIM), jnp.float32),
        )
        * factor
    )
    row_stats = (
        lax.all_gather(log_total, "seq", axis=1, tiled=True),
        lax.all_gather(delta_rows, "seq", axis=1, tiled=True),
    )
    key_heads = key_local.reshape(frames, head_count, HEAD_DIM)
    value_heads = value_local.reshape(frames, head_count, HEAD_DIM)
    start_acc = (
        jnp.zeros((frames, head_count, HEAD_DIM), jnp.float32),
        jnp.zeros((frames, head_count, HEAD_DIM), jnp.float32),
    )
    query_piece = lax.all_gather(packed[:, :width_all], "seq", axis=0, tiled=True)
    dout_piece = lax.all_gather(attended_grad, "seq", axis=0, tiled=True)
    piece_rows = query_piece.shape[0]
    block_rows = math.gcd(piece_rows, 512)

    def one_block(block_index, running):
        key_acc, value_acc = running
        offset = block_index * block_rows
        query_block = lax.dynamic_slice_in_dim(query_piece, offset, block_rows, 0).reshape(
            block_rows, head_count, HEAD_DIM
        )
        dout_block = lax.dynamic_slice_in_dim(dout_piece, offset, block_rows, 0).reshape(
            block_rows, head_count, HEAD_DIM
        )
        seg_block = lax.dynamic_slice_in_dim(segment_row, offset, block_rows, 0)
        total_block = lax.dynamic_slice_in_dim(row_stats[0], offset, block_rows, 1)
        delta_block = lax.dynamic_slice_in_dim(row_stats[1], offset, block_rows, 1)
        scores, allowed = score_block(query_block, key_heads, seg_block, query_segs, factor)
        chances = jnp.where(
            allowed, jnp.exp(jnp.where(allowed, scores, NEG) - total_block[..., None]), 0.0
        )
        prob_grad = jnp.einsum(
            "qhd,khd->hqk", dout_block, value_heads, preferred_element_type=jnp.float32
        )
        score_grad = (chances * (prob_grad - delta_block[..., None])).astype(jnp.bfloat16)
        key_acc = (
            key_acc
            + jnp.einsum(
                "hqk,qhd->khd", score_grad, query_block, preferred_element_type=jnp.float32
            )
            * factor
        )
        value_acc = value_acc + jnp.einsum(
            "hqk,qhd->khd",
            chances.astype(jnp.bfloat16),
            dout_block,
            preferred_element_type=jnp.float32,
        )
        return (key_acc, value_acc)

    key_acc, value_acc = lax.fori_loop(0, piece_rows // block_rows, one_block, start_acc)
    grad_key = key_acc.reshape(frames, width_all)
    grad_value = value_acc.reshape(frames, width_all)
    packed_grad = jnp.concatenate(
        [grad_query.reshape(frames, width_all), grad_key, grad_value], axis=1
    ).astype(jnp.bfloat16)
    normed_one_grad = jnp.einsum(
        "tj,ij->ti", packed_grad, weights[1], preferred_element_type=jnp.float32
    )
    resid_one_grad, grad_gain_one = norm_one_pull(normed_one_grad)
    resid_one_grad = resid_one_grad + resid_two_grad
    conv_grad = jnp.where(first_section, conv_pull(resid_one_grad)[0], 0.0).astype(jnp.bfloat16)
    grad_pad = padded_2(conv_grad, (("seq", 0),), TAPS // 2)
    back_sum = lax.cond(
        first_section,
        lambda: conv_input_grad(grad_pad, kernel, frames),
        lambda: jnp.zeros((frames, width_all), jnp.float32),
    )
    grad_in = resid_one_grad + back_sum
    products = (
        normed_one,
        packed_grad,
        attn_low,
        attn_branch_grad,
        normed_two,
        pre_grad,
        hidden_low,
        branch_grad,
        padded,
        conv_grad,
    )
    return (grad_in, (grad_gain_one, grad_gain_two), products)


def per_device(
    signal,
    frame_segment_index,
    conv_weight,
    conv_bias,
    norm1_gain,
    qkv_weight,
    out_weight,
    norm2_gain,
    up_weight,
    down_weight,
    cotangent,
):
    micro_count, frames, width_all = signal.shape
    factor = 1.0 / math.sqrt(HEAD_DIM)
    first_section = lax.axis_index("section") == 0
    my_start = lax.axis_index("seq") * frames
    gathered = (
        lax.all_gather(norm1_gain.astype(jnp.bfloat16), ("dp", "seq"), axis=1, tiled=True),
        lax.all_gather(qkv_weight.astype(jnp.bfloat16), ("dp", "seq"), axis=1, tiled=True),
        lax.all_gather(out_weight.astype(jnp.bfloat16), ("dp", "seq"), axis=1, tiled=True),
        lax.all_gather(norm2_gain.astype(jnp.bfloat16), ("dp", "seq"), axis=1, tiled=True),
        lax.all_gather(up_weight.astype(jnp.bfloat16), ("dp", "seq"), axis=1, tiled=True),
        lax.all_gather(down_weight.astype(jnp.bfloat16), ("dp", "seq"), axis=1, tiled=True),
    )
    weights = tuple((member[0] for member in gathered))
    kernel, conv_shift = (
        lax.all_gather(
            conv_weight.astype(jnp.bfloat16), ("section", "dp", "seq"), axis=0, tiled=True
        ),
        lax.all_gather(
            conv_bias.astype(jnp.bfloat16), ("section", "dp", "seq"), axis=0, tiled=True
        ),
    )
    received = jnp.zeros((frames, width_all), jnp.bfloat16)
    saved = []
    forward_outs = []
    for step_index in range(micro_count + 1):
        own_index = min(step_index, micro_count - 1)
        prior_index = max(step_index - 1, 0)
        layer_in = jnp.where(first_section, signal[own_index], received)
        segment_row = jnp.where(
            first_section, frame_segment_index[own_index], frame_segment_index[prior_index]
        )
        result, kept = layer_forward(
            layer_in, segment_row, weights, kernel, conv_shift, first_section, my_start, factor
        )
        saved.append(kept)
        forward_outs.append(result)
        if step_index < micro_count:
            received = from_behind(result.astype(jnp.bfloat16), "section", 1)
    received_back = jnp.zeros((frames, width_all), jnp.bfloat16)
    input_grads = []
    gain_totals = None
    product_list = []
    for step_index in range(micro_count + 1):
        kept = saved[micro_count - step_index]
        if step_index < micro_count:
            top_grad = cotangent[micro_count - 1 - step_index].astype(jnp.float32)
        else:
            top_grad = jnp.zeros((frames, width_all), jnp.float32)
        incoming = jnp.where(first_section, received_back.astype(jnp.float32), top_grad)
        grad_in, gain_grads, products = layer_backward(
            kept, incoming, weights, kernel, first_section, my_start, factor
        )
        input_grads.append(grad_in)
        product_list.append(products)
        if gain_totals is None:
            gain_totals = gain_grads
        else:
            gain_totals = (gain_totals[0] + gain_grads[0], gain_totals[1] + gain_grads[1])
        if step_index < micro_count:
            received_back = from_behind(grad_in.astype(jnp.bfloat16), "section", -1)

    def joined(position):
        return jnp.concatenate([member[position] for member in product_list], axis=0)

    grad_qkv = jnp.einsum("ti,tj->ij", joined(0), joined(1), preferred_element_type=jnp.float32)
    grad_out_weight = jnp.einsum(
        "ti,to->io", joined(2), joined(3), preferred_element_type=jnp.float32
    )
    grad_up = jnp.einsum("ti,tf->if", joined(4), joined(5), preferred_element_type=jnp.float32)
    grad_down = jnp.einsum("ti,to->io", joined(6), joined(7), preferred_element_type=jnp.float32)
    padded_all = jnp.stack([member[8] for member in product_list])
    conv_grad_all = jnp.stack([member[9] for member in product_list])
    kernel_grad = conv_kernel_grad(padded_all, conv_grad_all)
    bias_grad = jnp.sum(joined(9).astype(jnp.float32), axis=0)
    ends = jnp.stack(
        [
            jnp.where(
                first_section, input_grads[micro_count - mb_index], forward_outs[mb_index + 1]
            )
            for mb_index in range(micro_count)
        ]
    )[None]
    layer_sums = (
        lax.psum_scatter(gain_totals[0][None], ("dp", "seq"), scatter_dimension=1, tiled=True),
        lax.psum_scatter(grad_qkv[None], ("dp", "seq"), scatter_dimension=1, tiled=True),
        lax.psum_scatter(grad_out_weight[None], ("dp", "seq"), scatter_dimension=1, tiled=True),
        lax.psum_scatter(gain_totals[1][None], ("dp", "seq"), scatter_dimension=1, tiled=True),
        lax.psum_scatter(grad_up[None], ("dp", "seq"), scatter_dimension=1, tiled=True),
        lax.psum_scatter(grad_down[None], ("dp", "seq"), scatter_dimension=1, tiled=True),
    )
    conv_sums = (
        lax.psum_scatter(kernel_grad, ("section", "dp", "seq"), scatter_dimension=0, tiled=True),
        lax.psum_scatter(bias_grad, ("section", "dp", "seq"), scatter_dimension=0, tiled=True),
    )
    return (
        ends,
        conv_sums[0],
        conv_sums[1],
        layer_sums[0],
        layer_sums[1],
        layer_sums[2],
        layer_sums[3],
        layer_sums[4],
        layer_sums[5],
    )


def swap_section(value):
    return lax.ppermute(value, "section", [(0, 1), (1, 0)])


def swap_x(value):
    return lax.ppermute(value, "seq", [(q, q ^ 1) for q in range(4)])


def pair_sum(low, behind=None):
    other = swap_x(low)
    if behind is not None:
        other, _ = lax.optimization_barrier((other, behind))
    return low.astype(jnp.float32) + other.astype(jnp.float32)


def after(first, second):
    return lax.optimization_barrier((first, second))


def choose(flag, first, second):
    return jnp.where(flag, first, second), jnp.where(flag, second, first)


def sum_dp(blocks, dp, meanwhile):
    count = lax.axis_size("dp")
    f32, bf16 = jnp.float32, jnp.bfloat16
    meanwhile = list(meanwhile)

    def block(index):
        return lax.dynamic_index_in_dim(blocks, jnp.clip(index, 0, count - 1), 0, keepdims=False)

    running = [None, None]
    for turn, distance in enumerate(range(count - 1, 0, -1)):
        for way, sign in enumerate((1, -1)):
            own = block(dp + sign * distance)
            if running[way] is not None:
                own = (own.astype(f32) + running[way].astype(f32)).astype(bf16)
            live = [(i, i + sign) for i in range(count) if 0 <= i + sign < count and 0 <= i + sign * distance < count]
            running[way] = lax.ppermute(own, "dp", live)
        if turn < len(meanwhile):
            running, meanwhile[turn] = after(running, meanwhile[turn])
            running = list(running)
    total = block(dp).astype(f32) + running[0].astype(f32) + running[1].astype(f32)
    return total.astype(bf16), meanwhile


def line_groups():
    count = lax.axis_size("dp")
    return [
        [(s * count + d) * 4 + 2 * y + x for d in range(count) for y in range(2) for s in range(2)]
        for x in range(2)
    ]


def gather_rows(piece):
    return lax.all_gather(
        piece, ("section", "dp", "seq"), axis=0, tiled=True, axis_index_groups=line_groups()
    )


def scatter_rows(partial):
    return lax.psum_scatter(
        partial, ("section", "dp", "seq"), scatter_dimension=0, tiled=True,
        axis_index_groups=line_groups(),
    )


MESH = pl.DeviceIdType.MESH


def opening_kernel(
    dp_count, parts, conv_ref, signal_ref, keep_ref, send_ref, rest_ref,
    conv_out, signal_out, whole_out, second_out,
    local_sem, a2a_send, a2a_recv, sig_send, sig_recv, line_send, line_recv, own_send, column_recv, rest_recv,
    up_send, up_recv, y_send, y_recv, core_send, core_recv,
):
    sec, dp, seq = (lax.axis_index(name) for name in ("section", "dp", "seq"))
    me = sec * 4 + seq
    x, y = seq % 2, seq // 2
    partner_x = (seq + 1 - 2 * x) % 4
    partner_y = {"seq": (seq + 2) % 4}
    sibling = {"section": 1 - sec}
    has_up, has_down = dp < dp_count - 1, dp > 0
    split = keep_ref.shape[1]
    rows = keep_ref.shape[0] // parts

    barrier = pltpu.get_barrier_semaphore()
    for turn in range(1, 8):
        other = (me + turn) % 8
        pl.semaphore_signal(
            barrier, inc=1, device_id={"section": other // 4, "seq": other % 4}, device_id_type=MESH
        )
    for there, step in ((has_up, 1), (has_down, -1)):

        @pl.when(there)
        def _(step=step):
            pl.semaphore_signal(barrier, inc=1, device_id={"dp": dp + step}, device_id_type=MESH)

    pl.semaphore_wait(barrier, 7 + jnp.where(has_up, 1, 0) + jnp.where(has_down, 1, 0))

    def remote(source, target, send, recv, device):
        return pltpu.make_async_remote_copy(
            src_ref=source, dst_ref=target, send_sem=send, recv_sem=recv,
            device_id=device, device_id_type=MESH,
        )

    def a2a(target, source):
        return remote(
            conv_ref.at[target], conv_out.at[dp, source], a2a_send.at[target], a2a_recv.at[source],
            {"section": target // 4, "seq": target % 4},
        )

    def sig(target, source):
        return remote(
            signal_ref.at[target], signal_out.at[source], sig_send.at[target], sig_recv.at[source],
            {"seq": target},
        )

    for turn in range(1, 8):
        a2a((me + turn) % 8, me).start()
    conv_local = pltpu.make_async_copy(conv_ref.at[me], conv_out.at[dp, me], local_sem.at[0])
    signal_local = pltpu.make_async_copy(signal_ref.at[seq], signal_out.at[seq], local_sem.at[1])
    conv_local.start()
    signal_local.start()

    def columns(layer, half):
        return (second_out if layer else whole_out.at[dp, y, half]).at[:, pl.ds(0, split)]

    def others(layer, half):
        return (second_out if layer else whole_out.at[dp, y, half]).at[:, pl.ds(split, rest_ref.shape[2])]

    class Layer:
        def __init__(self, layer):
            far = {"section": 1 - layer}
            self.mine = sec == layer
            self.even = x == layer
            received = column_recv.at[layer]
            self.keep_local = pltpu.make_async_copy(keep_ref, columns(layer, layer), local_sem.at[2])
            self.rest_local = pltpu.make_async_copy(rest_ref.at[layer], others(layer, layer), local_sem.at[3])
            self.keep_far = remote(keep_ref, columns(layer, 1 - layer), own_send.at[0], received, far)
            self.send_same = remote(
                send_ref, columns(layer, layer), own_send.at[1], received, {"seq": partner_x}
            )
            self.send_cross = remote(
                send_ref, columns(layer, 1 - layer), own_send.at[1], received, {**far, "seq": partner_x}
            )
            self.rest_far = remote(
                rest_ref.at[1 - layer], others(layer, 1 - layer), own_send.at[2], rest_recv.at[layer], far
            )

        def start(self):
            @pl.when(self.mine & self.even)
            def _():
                self.send_same.start()
                self.keep_local.start()

            @pl.when(self.mine & jnp.logical_not(self.even))
            def _():
                self.send_cross.start()
                self.keep_far.start()

            @pl.when(self.mine)
            def _():
                self.rest_far.start()
                self.rest_local.start()

        def wait(self):
            other = jnp.logical_not(self.mine)
            odd = jnp.logical_not(self.even)

            @pl.when(self.mine & self.even)
            def _():
                self.keep_local.wait()

            @pl.when(self.mine & odd)
            def _():
                self.send_same.wait_recv()

            @pl.when(self.mine)
            def _():
                self.rest_local.wait()

            @pl.when(other & self.even)
            def _():
                self.send_cross.wait_recv()

            @pl.when(other & odd)
            def _():
                self.keep_far.wait_recv()

            @pl.when(other)
            def _():
                self.rest_far.wait_recv()

        def finish(self):
            @pl.when(self.mine & self.even)
            def _():
                self.send_same.wait_send()

            @pl.when(self.mine & jnp.logical_not(self.even))
            def _():
                self.send_cross.wait_send()
                self.keep_far.wait_send()

            @pl.when(self.mine)
            def _():
                self.rest_far.wait_send()

    layers = [Layer(0), Layer(1)]
    for layer in layers:
        layer.start()
    for turn in range(1, 4):
        sig((seq + turn) % 4, seq).start()

    def line(slot, direction):
        index = (direction + 1) // 2
        return remote(
            conv_out.at[slot], conv_out.at[slot], line_send.at[index, slot], line_recv.at[slot],
            {"dp": dp + direction},
        )

    def place(slot, row, half, part):
        return whole_out.at[slot, row, half, pl.ds(part * rows, rows)]

    def along(slot, direction, part):
        index = (direction + 1) // 2
        ref = place(slot, y, sec, part)
        return remote(
            ref, ref, up_send.at[index, slot, part], up_recv.at[slot, part], {"dp": dp + direction}
        )

    def across(slot, row, part):
        ref = place(slot, row, sec, part)
        return remote(ref, ref, y_send.at[slot, part], y_recv.at[slot, part], partner_y)

    def to_core(slot, row, half, part):
        ref = place(slot, row, half, part)
        return remote(
            ref, ref, core_send.at[slot, row, part], core_recv.at[slot, row, part], sibling
        )

    for turn in range(1, 8):
        a2a((me + turn) % 8, (me + turn) % 8).wait_recv()
    conv_local.wait()
    for there, direction in ((has_up, 1), (has_down, -1)):

        @pl.when(there)
        def _(direction=direction):
            line(dp, direction).start()

    layers[0].wait()
    for part in range(parts):
        for there, direction in ((has_up, 1), (has_down, -1)):

            @pl.when(there)
            def _(direction=direction, part=part):
                along(dp, direction, part).start()

        across(dp, y, part).start()
        to_core(dp, y, sec, part).start()

    def stage(distance):
        arrivals = []
        for direction in (1, -1):
            slot = dp - direction * distance
            arrives = (slot >= 0) & (slot < dp_count)
            goes_on = arrives & (has_up if direction == 1 else has_down)
            arrivals.append((direction, slot, arrives, goes_on))

            @pl.when(arrives)
            def _(slot=slot, direction=direction):
                line(slot, direction).wait_recv()

            @pl.when(goes_on)
            def _(slot=slot, direction=direction):
                line(slot, direction).start()

        for part in range(parts):
            for direction, slot, arrives, goes_on in arrivals:

                @pl.when(arrives)
                def _(slot=slot, direction=direction, part=part):
                    along(slot, direction, part).wait_recv()

                @pl.when(goes_on)
                def _(slot=slot, direction=direction, part=part):
                    along(slot, direction, part).start()

                @pl.when(arrives)
                def _(slot=slot, part=part):
                    across(slot, y, part).start()
                    to_core(slot, y, sec, part).start()

    def pass_crossed(distance):
        for part in range(parts):
            for sign in (1, -1) if distance else (1,):
                slot = dp - sign * distance

                @pl.when((slot >= 0) & (slot < dp_count))
                def _(slot=slot, part=part):
                    across(slot, 1 - y, part).wait_recv()
                    to_core(slot, 1 - y, sec, part).start()

    for distance in range(1, dp_count):
        stage(distance)
        pass_crossed(distance - 1)
    pass_crossed(dp_count - 1)

    for slot in range(dp_count):
        for part in range(parts):
            for row in range(2):
                to_core(slot, row, 1 - sec, part).wait_recv()
                to_core(slot, row, sec, part).wait_send()
            across(slot, y, part).wait_send()
        for direction in (1, -1):
            sent = (slot <= dp if direction == 1 else slot >= dp) & (has_up if direction == 1 else has_down)

            @pl.when(sent)
            def _(slot=slot, direction=direction):
                line(slot, direction).wait_send()
                for part in range(parts):
                    along(slot, direction, part).wait_send()

    layers[1].wait()
    for layer in layers:
        layer.finish()
    for turn in range(1, 8):
        a2a((me + turn) % 8, me).wait_send()
    for turn in range(1, 4):
        sig((seq + turn) % 4, (seq + turn) % 4).wait_recv()
        sig((seq + turn) % 4, seq).wait_send()
    signal_local.wait()


def opening(conv_send, signal_send, keep, send, rest):
    count = lax.axis_size("dp")
    parts = 2
    rows, columns = keep.shape[0], keep.shape[1] + rest.shape[2]
    anywhere = pl.BlockSpec(memory_space=pl.ANY)
    dma = pltpu.SemaphoreType.DMA
    conv_all, signal_all, whole, second = pl.pallas_call(
        functools.partial(opening_kernel, count, parts),
        in_specs=[anywhere] * 5,
        out_specs=[anywhere] * 4,
        out_shape=[
            jax.ShapeDtypeStruct((count, *conv_send.shape), conv_send.dtype),
            jax.ShapeDtypeStruct(signal_send.shape, signal_send.dtype),
            jax.ShapeDtypeStruct((count, 2, 2, rows, columns), keep.dtype),
            jax.ShapeDtypeStruct((rows, columns), keep.dtype),
        ],
        scratch_shapes=[
            dma((4,)), dma((8,)), dma((8,)), dma((4,)), dma((4,)), dma((2, count)), dma((count,)),
            dma((3,)), dma((2,)), dma((2,)), dma((2, count, parts)), dma((count, parts)), dma((count, parts)),
            dma((count, parts)), dma((count, 2, parts)), dma((count, 2, parts)),
        ],
        compiler_params=pltpu.CompilerParams(
            collective_id=0, has_side_effects=True, vmem_limit_bytes=4 * 1024 * 1024
        ),
        name="opening",
    )(conv_send, signal_send, keep, send, rest)
    return conv_all, signal_all, whole.reshape(-1, columns), second


def norm_stats(values):
    average = jnp.mean(values, axis=-1, keepdims=True)
    centred = values - average
    spread = jnp.mean(centred * centred, axis=-1, keepdims=True)
    return centred, lax.rsqrt(spread + EPS)


def norm_back(values, gain, grad):
    centred, inv = norm_stats(values)
    unit = centred * inv
    gain_grad = jnp.sum(grad * unit, axis=0)
    f = grad * gain
    mean_f = jnp.mean(f, axis=-1, keepdims=True)
    mean_fu = jnp.mean(f * unit, axis=-1, keepdims=True)
    return (f - mean_f - unit * mean_fu) * inv, gain_grad


def gelu_slope(values):
    cdf = 0.5 * (1.0 + lax.erf(values * (1.0 / math.sqrt(2.0))))
    pdf = jnp.exp(-0.5 * values * values) * (1.0 / math.sqrt(2.0 * math.pi))
    return cdf + values * pdf


def attention_forward_kernel(factor, q_ref, k_ref, v_ref, qs_ref, ks_ref, o_ref, lse_ref):
    queries = q_ref[...]
    lane = lax.broadcasted_iota(jnp.int32, queries.shape, 1)
    allowed = qs_ref[...] == ks_ref[...]
    keys = k_ref[...]
    values = v_ref[...]
    outs = []
    for head in range(2):
        mine = (lane < HEAD_DIM) if head == 0 else (lane >= HEAD_DIM)
        own = jnp.where(mine, queries, jnp.zeros_like(queries))
        scores = lax.dot_general(
            own, keys, (((1,), (1,)), ((), ())), preferred_element_type=jnp.float32
        ) * factor
        scores = jnp.where(allowed, scores, NEG)
        top = jnp.max(scores, axis=-1, keepdims=True)
        raised = jnp.exp(scores - top)
        total = jnp.sum(raised, axis=-1, keepdims=True)
        chances = (raised * (1.0 / total)).astype(jnp.bfloat16)
        outs.append(jnp.dot(chances, values, preferred_element_type=jnp.float32))
        lse_ref[0, head] = top + jnp.log(total)
    o_ref[...] = jnp.where(lane < HEAD_DIM, outs[0], outs[1]).astype(o_ref.dtype)


def attention_forward(packed, kv_all, query_segs, key_segs, factor):
    frames = packed.shape[0]
    keys = kv_all.shape[0]
    width = packed.shape[1] // 3
    pairs = width // 128
    rows = math.gcd(frames, 256)
    return pl.pallas_call(
        functools.partial(attention_forward_kernel, factor),
        grid=(pairs, frames // rows),
        in_specs=[
            pl.BlockSpec((rows, 128), lambda h, i: (i, h)),
            pl.BlockSpec((keys, 128), lambda h, i: (0, h)),
            pl.BlockSpec((keys, 128), lambda h, i: (0, pairs + h)),
            pl.BlockSpec((rows, 1), lambda h, i: (i, 0)),
            pl.BlockSpec((1, keys), lambda h, i: (0, 0)),
        ],
        out_specs=[
            pl.BlockSpec((rows, 128), lambda h, i: (i, h)),
            pl.BlockSpec((1, 2, rows, 1), lambda h, i: (h, 0, i, 0)),
        ],
        out_shape=[
            jax.ShapeDtypeStruct((frames, width), jnp.bfloat16),
            jax.ShapeDtypeStruct((pairs, 2, frames, 1), jnp.float32),
        ],
        compiler_params=pltpu.CompilerParams(vmem_limit_bytes=40 * 1024 * 1024),
        cost_estimate=pl.CostEstimate(
            flops=4 * frames * keys * width * 2,
            bytes_accessed=2 * (frames * width * 2 + keys * width * 2),
            transcendentals=frames * keys * (width // HEAD_DIM),
        ),
        name="attention_forward",
    )(packed, kv_all, kv_all, query_segs[:, None], key_segs[None, :])


def attention_backward_kernel(
    factor, q_ref, k_ref, v_ref, g_ref, o_ref, lse_ref, qs_ref, ks_ref, *rest
):
    *begin, dq_ref, dk_ref, dv_ref = rest
    step = pl.program_id(1)

    @pl.when(step == 0)
    def _():
        for index, total_ref in enumerate((dk_ref, dv_ref)):
            total_ref[...] = begin[index][...] if begin else jnp.zeros_like(total_ref)

    queries = q_ref[...]
    grads = g_ref[...]
    keys = k_ref[...]
    values = v_ref[...]
    lane = lax.broadcasted_iota(jnp.int32, queries.shape, 1)
    key_lane = lax.broadcasted_iota(jnp.int32, keys.shape, 1)
    allowed = qs_ref[...] == ks_ref[...]
    product = grads.astype(jnp.float32) * o_ref[...].astype(jnp.float32)
    dq = None
    for head in range(2):
        mine = (lane < HEAD_DIM) if head == 0 else (lane >= HEAD_DIM)
        key_mine = (key_lane < HEAD_DIM) if head == 0 else (key_lane >= HEAD_DIM)
        own_q = jnp.where(mine, queries, jnp.zeros_like(queries))
        own_g = jnp.where(mine, grads, jnp.zeros_like(grads))
        own_k = jnp.where(key_mine, keys, jnp.zeros_like(keys))
        delta = jnp.sum(jnp.where(mine, product, 0.0), axis=-1, keepdims=True)
        scores = lax.dot_general(
            own_q, keys, (((1,), (1,)), ((), ())), preferred_element_type=jnp.float32
        ) * factor
        chances = jnp.exp(jnp.where(allowed, scores, NEG) - lse_ref[0, head])
        prob_grad = lax.dot_general(
            own_g, values, (((1,), (1,)), ((), ())), preferred_element_type=jnp.float32
        )
        score_grad = (chances * (prob_grad - delta)).astype(jnp.bfloat16)
        part = jnp.dot(score_grad, own_k, preferred_element_type=jnp.float32)
        dq = part if dq is None else dq + part
        dk_ref[...] += lax.dot_general(
            score_grad, own_q, (((0,), (0,)), ((), ())), preferred_element_type=jnp.float32
        ) * factor
        dv_ref[...] += lax.dot_general(
            chances.astype(jnp.bfloat16), own_g, (((0,), (0,)), ((), ())),
            preferred_element_type=jnp.float32,
        )
    dq_ref[...] = (dq * factor).astype(dq_ref.dtype)


def attention_backward(packed, kv_all, grads, attended, lse, query_segs, key_segs, factor, begin=None):
    frames = packed.shape[0]
    keys = kv_all.shape[0]
    width = packed.shape[1] // 3
    pairs = width // 128
    rows = math.gcd(frames, 256)
    return pl.pallas_call(
        functools.partial(attention_backward_kernel, factor),
        grid=(pairs, frames // rows),
        in_specs=[
            pl.BlockSpec((rows, 128), lambda h, i: (i, h)),
            pl.BlockSpec((keys, 128), lambda h, i: (0, h)),
            pl.BlockSpec((keys, 128), lambda h, i: (0, pairs + h)),
            pl.BlockSpec((rows, 128), lambda h, i: (i, h)),
            pl.BlockSpec((rows, 128), lambda h, i: (i, h)),
            pl.BlockSpec((1, 2, rows, 1), lambda h, i: (h, 0, i, 0)),
            pl.BlockSpec((rows, 1), lambda h, i: (i, 0)),
            pl.BlockSpec((1, keys), lambda h, i: (0, 0)),
        ]
        + [pl.BlockSpec((keys, 128), lambda h, i: (0, h))] * (2 if begin else 0),
        out_specs=[
            pl.BlockSpec((rows, 128), lambda h, i: (i, h)),
            pl.BlockSpec((keys, 128), lambda h, i: (0, h)),
            pl.BlockSpec((keys, 128), lambda h, i: (0, h)),
        ],
        out_shape=[
            jax.ShapeDtypeStruct((frames, width), jnp.bfloat16),
            jax.ShapeDtypeStruct((keys, width), jnp.float32),
            jax.ShapeDtypeStruct((keys, width), jnp.float32),
        ],
        compiler_params=pltpu.CompilerParams(vmem_limit_bytes=48 * 1024 * 1024),
        cost_estimate=pl.CostEstimate(
            flops=10 * frames * keys * width * 2,
            bytes_accessed=4 * (frames * width * 2 + keys * width * 2),
            transcendentals=frames * keys * (width // HEAD_DIM),
        ),
        name="attention_backward",
    )(packed, kv_all, kv_all, grads, attended, lse, query_segs[:, None], key_segs[None, :], *(begin or ()))


CONV_STEP = 4


def conv_bands(kernel, per_group):
    groups = kernel.shape[1] // per_group
    steps = TAPS // CONV_STEP + 1
    bands = []
    for group in range(groups):
        own = kernel[:, group * per_group : (group + 1) * per_group]
        shifted = [
            jnp.pad(own, ((shift * per_group, (CONV_STEP - shift) * per_group), (0, 0)))
            for shift in range(CONV_STEP)
        ]
        band = jnp.concatenate(shifted, axis=1)
        bands.append(band.reshape(steps, CONV_STEP * per_group, CONV_STEP * per_group))
    return bands


def group_view(values, per_group):
    rows, frames, width = values.shape
    return [
        values[:, :, g * per_group : (g + 1) * per_group].reshape(
            rows, frames // CONV_STEP, CONV_STEP * per_group
        )
        for g in range(width // per_group)
    ]


def ungroup(parts, per_group):
    rows, blocks, _ = parts[0].shape
    return jnp.concatenate(
        [part.reshape(rows, blocks * CONV_STEP, per_group) for part in parts], axis=2
    )


CONV_DIMS = ("NWC", "WIO", "NWC")


def conv_forward(views, bands):
    half = TAPS // 2 // CONV_STEP
    return [
        lax.conv_general_dilated(
            view, band, (1,), [(half, half)], dimension_numbers=CONV_DIMS,
            preferred_element_type=jnp.float32,
        )
        for view, band in zip(views, bands)
    ]


def conv_back(grad_views, bands):
    half = TAPS // 2 // CONV_STEP
    return [
        lax.conv_general_dilated(
            view, jnp.transpose(band[::-1], (0, 2, 1)), (1,), [(half, half)],
            dimension_numbers=CONV_DIMS, preferred_element_type=jnp.float32,
        )
        for view, band in zip(grad_views, bands)
    ]


def conv_taps_grad(views, grad_views, per_group):
    half = TAPS // 2 // CONV_STEP
    results = []
    for view, grad in zip(views, grad_views):
        band = lax.conv_general_dilated(
            view, grad, (1,), [(half, half)],
            dimension_numbers=("CWN", "IWO", "WNC"),
            preferred_element_type=jnp.float32,
        )
        flat = band.reshape(-1, CONV_STEP * per_group)
        total = None
        for shift in range(CONV_STEP):
            part = flat[
                shift * per_group : (shift + TAPS) * per_group,
                shift * per_group : (shift + 1) * per_group,
            ]
            total = part if total is None else total + part
        results.append(total)
    return jnp.concatenate(results, axis=1)


def to_column(vector, width):
    return jnp.pad(vector[:, None], ((0, 0), (0, width - 1)))


def per_device_pairs(
    signal, frame_segment_index, conv_weight, conv_bias, norm1_gain, qkv_weight, out_weight,
    norm2_gain, up_weight, down_weight, cotangent,
):
    micro_count, frames, width = signal.shape
    bf16, f32 = jnp.bfloat16, jnp.float32
    per_group = width // GROUPS
    dp_count = lax.axis_size("dp")
    factor = 1.0 / math.sqrt(HEAD_DIM)
    sec = lax.axis_index("section")
    dp = lax.axis_index("dp")
    seq = lax.axis_index("seq")
    x, y = seq % 2, seq // 2
    sec0, x0 = sec == 0, x == 0
    row_frames = 4 * frames
    half_frames = 2 * frames
    both = ("section", "seq")

    block_width = width // 8
    rows_here = conv_weight.shape[0]
    conv_low = conv_weight.astype(bf16).reshape(rows_here, 8, block_width)
    bias_low = jnp.pad(conv_bias.astype(bf16), (0, block_width - conv_bias.shape[0]))
    bias_rows = jnp.pad(
        jnp.broadcast_to(bias_low[None, None, :], (1, 8, block_width)), ((0, 15), (0, 0), (0, 0))
    )
    conv_send = jnp.transpose(jnp.concatenate([conv_low, bias_rows], axis=0), (1, 0, 2))

    own_half = jnp.where(sec0, signal[:, :, : width // 2], signal[:, :, width // 2 :])
    sig_send = jnp.transpose(own_half.reshape(micro_count, frames, 4, block_width), (2, 0, 1, 3))
    in_rows = qkv_weight.shape[1]
    unit = down_weight.shape[1] // 4
    qkv_view = qkv_weight[0].astype(bf16).reshape(in_rows, -1, 2, HEAD_DIM)
    qkv_parity = [qkv_view[:, :, p].reshape(in_rows, -1) for p in range(2)]
    up_view = up_weight[0].astype(bf16).reshape(in_rows, -1, 2, 2, 2, unit)
    up_parity = [
        jnp.transpose(up_view[:, :, p], (0, 3, 1, 2, 4)).reshape(in_rows, -1) for p in range(2)
    ]
    qkv_cols, up_cols = qkv_parity[0].shape[1], up_parity[0].shape[1]
    col_one = to_column(norm1_gain[0].astype(bf16), 128)
    col_two = to_column(norm2_gain[0].astype(bf16), 128)
    cut = qkv_cols + 128
    keep_cols, send_cols = [
        jnp.concatenate([a, col_one, b, col_two], axis=1)
        for a, b in zip(choose(x0, *qkv_parity), choose(x0, *up_parity))
    ]
    out_low = out_weight[0].astype(bf16)
    down_low = down_weight[0].astype(bf16).reshape(2, 2, unit, width)
    rest = jnp.stack(
        [
            jnp.concatenate(
                [out_low[:, h * width // 2 : (h + 1) * width // 2], down_low[h, 0], down_low[h, 1]], axis=1
            )
            for h in range(2)
        ]
    )
    up_at = cut
    two_at = up_at + up_cols
    out_at = two_at + 128
    down_at = out_at + width // 2
    conv_all, sig_got, whole, second_piece = opening(conv_send, sig_send, keep_cols, send_cols, rest)
    gathered = [whole, gather_rows(second_piece)]
    sig_all = jnp.transpose(sig_got, (1, 0, 2, 3)).reshape(micro_count, row_frames, block_width)
    conv_all = conv_all.reshape(dp_count, 2, 4, rows_here + 16, block_width)
    conv_all = jnp.transpose(conv_all, (1, 0, 2, 3, 4))
    bias_all = conv_all[:, :, :, rows_here, : conv_bias.shape[0]].reshape(width)
    bias_own = lax.dynamic_slice_in_dim(bias_all, (sec * 4 + seq) * block_width, block_width, 0)
    kernel_own = conv_all[:, :, :, :rows_here].reshape(TAPS * per_group, block_width)
    bands = conv_bands(kernel_own, per_group)


    def views(whole):
        w_out = jnp.transpose(
            whole[:, out_at:down_at].reshape(-1, 2, in_rows, width // 2), (0, 2, 1, 3)
        ).reshape(-1, width)
        gain_one = whole[:, qkv_cols].astype(f32)[None, :]
        gain_two = whole[:, two_at].astype(f32)[None, :]
        w_up = [whole[:, up_at + part * width : up_at + (part + 1) * width] for part in range(2)]
        w_down = [whole[:, down_at + part * width : down_at + (part + 1) * width] for part in range(2)]
        return gain_one, whole[:, :qkv_cols], w_out, gain_two, w_up, w_down

    layer_weights = []

    picked = jnp.where(sec0, cotangent[0], cotangent[1])
    across = [(s * 4 + 2 * yy + xx, yy * 4 + 2 * s + xx) for s in range(2) for yy in range(2) for xx in range(2)]
    across = [(a, b) for a, b in across if a != b]

    def over_rows(value):
        return jnp.where(sec == y, value, lax.ppermute(value, both, across))

    cot_own = over_rows(picked)
    cot_other = swap_x(cot_own)
    cot_pair = choose(x0, cot_own, cot_other)
    top_grad = jnp.concatenate(cot_pair, axis=0).astype(f32)

    segment_row = jnp.where(y == 0, frame_segment_index[0], frame_segment_index[1])
    seg_pair = choose(sec0, segment_row[:half_frames], segment_row[half_frames:])
    query_segs = seg_pair[0]
    key_segs = jnp.concatenate(seg_pair)

    sig_views = group_view(sig_all, per_group)
    conv_pre = ungroup(conv_forward(sig_views, bands), per_group) + bias_own.astype(f32)
    stream = (sig_all.astype(f32) + smooth(conv_pre)).astype(bf16)
    slope = gelu_slope(conv_pre).astype(bf16)
    stream_send = stream.reshape(2, 2, half_frames, block_width)
    stream_send = jnp.transpose(stream_send, (1, 0, 2, 3))
    stream_send = jnp.repeat(stream_send.reshape(4, half_frames, block_width), 2, axis=0)
    stream_got = lax.all_to_all(stream_send, both, 0, 0, tiled=True)
    layer_in = jnp.transpose(stream_got, (1, 0, 2)).reshape(half_frames, width).astype(f32)

    chunks = 2
    rows = half_frames // chunks
    layer_in = [layer_in[c * rows : (c + 1) * rows] for c in range(chunks)]
    chunk_segs = [query_segs[c * rows : (c + 1) * rows] for c in range(chunks)]
    kept = []
    for layer in range(2):
        whole = gathered[layer]
        if layer:
            layer_in = []
            previous_lows[0], whole = after(previous_lows[0], whole)
        layer_weights.append(views(whole))
        gain_one, w_qkv, w_out, gain_two, w_up, w_down = layer_weights[layer]
        normed_one, packed, kv_own, kv_other = [], [], [], []
        for c in range(chunks):
            if layer:
                total = previous[c] + pair_sum(previous_lows[c], packed[-1] if c else None)
                layer_in.append(total.astype(bf16).astype(f32))
            centred, inv = norm_stats(layer_in[c])
            normed_one.append((centred * inv * gain_one).astype(bf16))
            packed.append(jnp.dot(normed_one[c], w_qkv, preferred_element_type=f32).astype(bf16))
            kv_own.append(packed[c][:, width // 2 :])
            kv_other.append(swap_section(kv_own[c]))
        kv_all = jnp.concatenate(kv_own + kv_other, axis=0)
        attended, lse, resid_two, normed_two, hidden, hidden_slope = [], [], [], [], [], []
        attn_lows, lows = [], []
        for c in range(chunks):
            own = packed[c]
            if c:
                attn_lows[-1], own = after(attn_lows[-1], own)
            mixed, log_total = attention_forward(own, kv_all, chunk_segs[c], key_segs, factor)
            attended.append(mixed)
            lse.append(log_total)
            attn_lows.append(jnp.dot(mixed, w_out, preferred_element_type=f32).astype(bf16))
        for c in range(chunks):
            resid_two.append(layer_in[c] + pair_sum(attn_lows[c], lows[-1] if c else None))
            centred, inv = norm_stats(resid_two[c])
            normed_two.append((centred * inv * gain_two).astype(bf16))
            down_sum, own_hidden, own_slope = None, [], []
            for part in range(2):
                hidden_pre = jnp.dot(normed_two[c], w_up[part], preferred_element_type=f32)
                own_hidden.append(smooth(hidden_pre).astype(bf16))
                own_slope.append(gelu_slope(hidden_pre).astype(bf16))
            for part in range(2):
                term = jnp.dot(own_hidden[part], w_down[part], preferred_element_type=f32)
                down_sum = term if down_sum is None else down_sum + term
            hidden.append(own_hidden)
            hidden_slope.append(own_slope)
            lows.append(down_sum.astype(bf16))

        resid_two_last = resid_two
        kept.append((layer_in, normed_one, packed, kv_all, attended, lse, resid_two, normed_two, hidden, hidden_slope))
        previous, previous_lows = resid_two, lows

    def outer(left, right):
        return lax.dot_general(
            left, right, (((0,), (0,)), ((), ())), preferred_element_type=f32
        ).astype(bf16)

    def back(left, right):
        return lax.dot_general(left, right, (((1,), (1,)), ((), ())), preferred_element_type=f32)

    grad_out = [top_grad[c * rows : (c + 1) * rows] for c in range(chunks)]
    attn_members, scattered = [], []
    for layer in (1, 0):
        gain_one, w_qkv, w_out, gain_two, w_up, w_down = layer_weights[layer]
        (layer_in, normed_one, packed, kv_all, attended, lse, resid_two, normed_two, hidden, hidden_slope) = kept[layer]
        branch = [member.astype(bf16) for member in grad_out]
        pre_grad, sums, low = [], [], None
        for c in range(chunks):
            own = branch[c]
            if low is not None:
                low, own = after(low, own)
                sums.append(pair_sum(low))
            own_pre, part_sum = [], None
            for part in range(2):
                own_pre.append((back(own, w_down[part]) * hidden_slope[c][part].astype(f32)).astype(bf16))
            for part in range(2):
                term = back(own_pre[part], w_up[part])
                part_sum = term if part_sum is None else part_sum + term
            pre_grad.append(own_pre)
            low = part_sum.astype(bf16)
        sums.append(pair_sum(low))
        whole_pre = [jnp.concatenate([pre_grad[c][p] for c in range(chunks)]) for p in range(2)]
        whole_hidden = [jnp.concatenate([hidden[c][p] for c in range(chunks)]) for p in range(2)]
        whole_branch, whole_two = jnp.concatenate(branch), jnp.concatenate(normed_two)
        ff_members = [
            outer(whole_two, whole_pre[0]), outer(whole_two, whole_pre[1]),
            outer(whole_hidden[0], whole_branch), outer(whole_hidden[1], whole_branch),
        ]
        if layer == 1:
            ff_members.append(jnp.zeros((width, 128), bf16))
        partial = jnp.concatenate(attn_members + ff_members, axis=1)
        if layer == 0:
            sums, partial = after(sums, partial)
        scattered.append(scatter_rows(partial))
        resid_grad, attn_branch, dq, gain_two_grad = [], [], [], None
        dkv = None
        for c in range(chunks):
            in_part, gain_part = norm_back(resid_two[c], gain_two, sums[c])
            gain_two_grad = gain_part if gain_two_grad is None else gain_two_grad + gain_part
            resid_grad.append(in_part + grad_out[c])
            attn_branch.append(resid_grad[c].astype(bf16))
            attended_grad = back(attn_branch[c], w_out).astype(bf16)
            if layer == 1 and c == 0:
                attended_grad, lows = after(attended_grad, lows)
                output = [member + pair_sum(low) for member, low in zip(resid_two_last, lows)]
            own_dq, *dkv = attention_backward(
                packed[c], kv_all, attended_grad, attended[c], lse[c], chunk_segs[c], key_segs, factor,
                None if c == 0 else dkv,
            )
            dq.append(own_dq)
        if layer == 0:
            dkv, scattered[0] = after(dkv, scattered[0])
        else:
            dkv, output = after(dkv, output)
        dkv = jnp.concatenate(dkv, axis=1)
        other_dkv = swap_section(dkv[half_frames:].astype(bf16))
        dkv_own = (dkv[:half_frames] + other_dkv.astype(f32)).astype(bf16)
        packed_grad, sums, low = [], [], None
        for c in range(chunks):
            packed_grad.append(jnp.concatenate([dq[c], dkv_own[c * rows : (c + 1) * rows]], axis=1))
            own = packed_grad[c]
            if low is not None:
                low, own = after(low, own)
                sums.append(pair_sum(low))
            low = back(own, w_qkv).astype(bf16)
        sums.append(pair_sum(low))
        next_grad, gain_one_grad = [], None
        for c in range(chunks):
            in_part, gain_part = norm_back(layer_in[c], gain_one, sums[c])
            gain_one_grad = gain_part if gain_one_grad is None else gain_one_grad + gain_part
            next_grad.append((resid_grad[c] + in_part).astype(bf16))
        whole_one, whole_pg, whole_att, whole_ab = [
            jnp.concatenate(m) for m in (normed_one, packed_grad, attended, attn_branch)
        ]
        grad_out_weight = jnp.transpose(
            outer(whole_att, whole_ab).reshape(-1, in_rows, 2, width // 2), (0, 2, 1, 3)
        ).reshape(-1, width // 2)
        gain_grads = jnp.stack([gain_one_grad, gain_two_grad], axis=1).astype(bf16)
        gain_grads = jnp.pad(gain_grads, ((0, 0), (0, 126)))
        attn_members = [outer(whole_one, whole_pg), gain_grads, grad_out_weight]
        grad_out = [member.astype(f32) for member in next_grad]
    grad_in_low = jnp.concatenate(next_grad)
    scattered.append(scatter_rows(jnp.concatenate(attn_members, axis=1)))

    lig_send = jnp.transpose(grad_in_low.reshape(half_frames, 8, block_width), (1, 0, 2))
    lig_got = lax.all_to_all(lig_send, both, 0, 0, tiled=True).reshape(2, 2, 2, half_frames, block_width)[:, :, 0]
    lig = jnp.transpose(lig_got, (1, 0, 2, 3)).reshape(micro_count, row_frames, block_width)
    conv_grad = (lig.astype(f32) * slope.astype(f32)).astype(bf16)
    grad_views = group_view(conv_grad, per_group)
    back = ungroup(conv_back(grad_views, bands), per_group)
    grad_signal = (lig.astype(f32) + back).astype(bf16)
    gs_send = jnp.transpose(
        grad_signal.reshape(micro_count, 4, frames, block_width), (1, 0, 2, 3)
    )
    gs_send = jnp.concatenate([gs_send, gs_send], axis=0)
    taps_grad = conv_taps_grad(sig_views, grad_views, per_group)
    bias_grad = jnp.sum(conv_grad.astype(f32), axis=(0, 1))
    taps_view = jnp.transpose(
        taps_grad.reshape(2, dp_count, 4, rows_here, block_width), (1, 0, 2, 3, 4)
    ).astype(bf16)
    bias_view = jnp.pad(
        jnp.broadcast_to(bias_grad.astype(bf16), (dp_count, 2, 4, 1, block_width)),
        ((0, 0), (0, 0), (0, 0), (0, 15), (0, 0)),
    )
    taps_send = jnp.concatenate([taps_view, bias_view], axis=3)
    gs_got = lax.all_to_all(gs_send, both, 0, 0, tiled=True)
    attn_cols = cut + width // 2

    def over_section(first, second):
        keep, send = choose(sec0, first, second)
        return choose(sec0, keep, swap_section(send))


    row_block = over_rows(jnp.where(x0, output[0], output[1]).astype(bf16))
    output_rows = jnp.stack(choose(sec0, row_block, swap_section(row_block))).astype(f32)
    taps_sum, (_, gs_got, output_rows) = sum_dp(taps_send, dp, (gs_send, gs_got, output_rows))
    gs_rows = jnp.transpose(gs_got, (1, 2, 0, 3)).reshape(micro_count, frames, width).astype(f32)
    ends = jnp.where(sec0, gs_rows, output_rows)[None]
    taps_got = lax.all_to_all(
        taps_sum.reshape(8, rows_here + 16, block_width), both, 0, 0, tiled=True
    )
    taps_got, scattered[1] = after(taps_got, scattered[1])
    conv_weight_grad = jnp.transpose(taps_got[:, :rows_here], (1, 0, 2)).reshape(rows_here, width).astype(f32)
    bias_count = conv_bias.shape[0]
    conv_bias_grad = lax.dynamic_slice_in_dim(
        taps_got[:, rows_here].reshape(width),
        ((sec * dp_count + dp) * 4 + seq) * bias_count,
        bias_count,
        0,
    ).astype(f32)

    turned = [(t * 4 + 2 * r + c, c * 4 + 2 * r + t) for t in range(2) for r in range(2) for c in range(2) if t != c]
    crossed = [(t * 4 + 2 * r + c, (1 - c) * 4 + 2 * r + t) for t in range(2) for r in range(2) for c in range(2)]

    def home(first, second):
        straight, other = choose(x0, first, second)
        straight = jnp.where(sec == x, straight, lax.ppermute(straight, both, turned))
        other = lax.ppermute(other, both, crossed)
        return choose(sec0, straight, other)

    ff_layers = (scattered[1][:, attn_cols:], scattered[0][:, :-128])
    ff_sets = over_section(*(member[:, up_cols:] for member in ff_layers))
    down_grad = jnp.concatenate(
        [member[:, at : at + width] for member in ff_sets for at in (0, width)], axis=0
    ).astype(f32)[None]
    up_grad = jnp.stack(
        [
            jnp.transpose(member.reshape(in_rows, 2, -1, 2, unit), (0, 2, 3, 1, 4))
            for member in home(*(member[:, :up_cols] for member in ff_layers))
        ],
        axis=2,
    ).reshape(in_rows, -1).astype(f32)[None]
    scattered[2], (up_grad, down_grad) = after(scattered[2], (up_grad, down_grad))
    attn_layers = (scattered[2], scattered[1][:, :attn_cols])
    attn_sets = over_section(*(member[:, cut:] for member in attn_layers))
    out_grad = jnp.concatenate(attn_sets, axis=1).astype(f32)[None]
    qkv_sets = home(*(member[:, :cut] for member in attn_layers))
    norm1_grad = qkv_sets[0][:, qkv_cols].astype(f32)[None]
    norm2_grad = qkv_sets[0][:, qkv_cols + 1].astype(f32)[None]
    qkv_grad = jnp.stack(
        [member[:, :qkv_cols].reshape(in_rows, -1, HEAD_DIM) for member in qkv_sets], axis=2
    ).reshape(in_rows, -1).astype(f32)[None]
    return (ends, conv_weight_grad, conv_bias_grad, norm1_grad, qkv_grad, out_grad, norm2_grad, up_grad, down_grad)


def solution(mesh):
    placed = (
        P("dp", "seq", None),
        P("dp", None),
        P(("section", "dp", "seq"), None),
        P(("section", "dp", "seq")),
        P("section", ("dp", "seq")),
        P("section", ("dp", "seq"), None),
        P("section", ("dp", "seq"), None),
        P("section", ("dp", "seq")),
        P("section", ("dp", "seq"), None),
        P("section", ("dp", "seq"), None),
        P("dp", "seq", None),
    )

    def step(*arrays):
        pairs = mesh.shape["seq"] == 4 and mesh.shape["section"] == 2 and arrays[0].shape[0] == 2
        return (per_device_pairs if pairs else per_device)(*arrays)

    return jax.shard_map(
        step,
        mesh=mesh,
        in_specs=placed,
        out_specs=(
            P("section", "dp", "seq", None),
            P(("section", "dp", "seq"), None),
            P(("section", "dp", "seq")),
            P("section", ("dp", "seq")),
            P("section", ("dp", "seq"), None),
            P("section", ("dp", "seq"), None),
            P("section", ("dp", "seq")),
            P("section", ("dp", "seq"), None),
            P("section", ("dp", "seq"), None),
        ),
        check_vma=False,
    )
```

```python
import functools
import math

import jax
import jax.numpy as jnp
from jax import lax
from jax.experimental import pallas as pl
from jax.experimental.pallas import tpu as pltpu
from jax.sharding import PartitionSpec as P

HEAD_DIM = 64
GROUPS = 16
TAPS = 128


EPS = 1e-05
NEG = -1e30


def padded_2(block, sides, width):
    for axis, dim in sides:
        count = lax.axis_size(axis)
        forward = [(i, i + 1) for i in range(count - 1)]
        backward = [(target, source) for source, target in forward]
        low = lax.ppermute(
            lax.slice_in_dim(block, block.shape[dim] - width, None, axis=dim), axis, forward
        )
        high = lax.ppermute(lax.slice_in_dim(block, 0, width, axis=dim), axis, backward)
        block = jnp.concatenate([low, block, high], axis=dim)
    return block


def from_behind(value, axis, steps):
    count = lax.axis_size(axis)
    first, last = (max(0, -steps), min(count, count - steps))
    return lax.ppermute(value, axis, [(source, source + steps) for source in range(first, last)])


def normalize(values, gain):
    average = jnp.mean(values, axis=-1, keepdims=True)
    centred = values - average
    spread = jnp.mean(centred * centred, axis=-1, keepdims=True)
    return centred * lax.rsqrt(spread + EPS) * gain


def smooth(values):
    return jax.nn.gelu(values, approximate=False)


def conv_taps(padded, kernel, frames):
    width_all = padded.shape[1]
    per_group = width_all // GROUPS
    tap_step = math.gcd(TAPS, 16)
    weight_view = kernel.reshape(TAPS, per_group, GROUPS, per_group)
    running = jnp.zeros((frames, GROUPS, per_group), jnp.float32)
    for first_tap in range(0, TAPS, tap_step):
        windows = jnp.stack(
            [padded[first_tap + offset : first_tap + offset + frames] for offset in range(tap_step)]
        )
        windows = windows.reshape(tap_step, frames, GROUPS, per_group)
        running = running + jnp.einsum(
            "jtgc,jcgo->tgo",
            windows,
            weight_view[first_tap : first_tap + tap_step],
            preferred_element_type=jnp.float32,
        )
    return running.reshape(frames, width_all)


def conv_input_grad(grad_pad, kernel, frames):
    width_all = grad_pad.shape[1]
    per_group = width_all // GROUPS
    tap_step = math.gcd(TAPS, 16)
    weight_view = kernel.reshape(TAPS, per_group, GROUPS, per_group)
    running = jnp.zeros((frames, GROUPS, per_group), jnp.float32)
    for first_tap in range(0, TAPS, tap_step):
        back_windows = jnp.stack(
            [
                grad_pad[TAPS - first_tap - offset : TAPS - first_tap - offset + frames]
                for offset in range(tap_step)
            ]
        )
        back_windows = back_windows.reshape(tap_step, frames, GROUPS, per_group)
        running = running + jnp.einsum(
            "jtgo,jcgo->tgc",
            back_windows,
            weight_view[first_tap : first_tap + tap_step],
            preferred_element_type=jnp.float32,
        )
    return running.reshape(frames, width_all)


def conv_kernel_grad(padded_all, grad_all):
    step_count, frames, width_all = grad_all.shape
    per_group = width_all // GROUPS
    tap_step = math.gcd(TAPS, 16)
    grad_view = grad_all.reshape(step_count * frames, GROUPS, per_group)
    kernel_parts = []
    for first_tap in range(0, TAPS, tap_step):
        windows = jnp.stack(
            [
                padded_all[:, first_tap + offset : first_tap + offset + frames]
                for offset in range(tap_step)
            ]
        )
        windows = windows.reshape(tap_step, step_count * frames, GROUPS, per_group)
        kernel_parts.append(
            jnp.einsum("jtgc,tgo->jcgo", windows, grad_view, preferred_element_type=jnp.float32)
        )
    return jnp.concatenate(kernel_parts, axis=0).reshape(TAPS * per_group, width_all)


def score_block(query_heads, key_block, query_segs, key_segs, factor):
    scores = (
        jnp.einsum("qhd,khd->hqk", query_heads, key_block, preferred_element_type=jnp.float32)
        * factor
    )
    allowed = (query_segs[:, None] == key_segs[None, :])[None]
    return (scores, allowed)


def front(layer_in, weights, kernel, conv_shift, first_section):
    frames, width_all = layer_in.shape
    padded = padded_2(layer_in, (("seq", 0),), TAPS // 2)
    conv_pre = lax.cond(
        first_section,
        lambda: conv_taps(padded, kernel, frames) + conv_shift.astype(jnp.float32),
        lambda: jnp.zeros((frames, width_all), jnp.float32),
    )
    conv_val, conv_pull = jax.vjp(smooth, conv_pre)
    resid_one = layer_in.astype(jnp.float32) + conv_val
    normed_val, norm_pull = jax.vjp(normalize, resid_one, weights[0].astype(jnp.float32))
    normed_one = normed_val.astype(jnp.bfloat16)
    packed = jnp.dot(normed_one, weights[1], preferred_element_type=jnp.float32).astype(
        jnp.bfloat16
    )
    return (padded, conv_pull, resid_one, norm_pull, normed_one, packed)


def tail(resid_one, attn_low, weights):
    resid_two = resid_one + jnp.dot(attn_low, weights[2], preferred_element_type=jnp.float32)
    normed_val, norm_pull = jax.vjp(normalize, resid_two, weights[3].astype(jnp.float32))
    normed_two = normed_val.astype(jnp.bfloat16)
    hidden_pre = jnp.dot(normed_two, weights[4], preferred_element_type=jnp.float32)
    hidden_val, gelu_pull = jax.vjp(smooth, hidden_pre)
    hidden_low = hidden_val.astype(jnp.bfloat16)
    result = resid_two + jnp.dot(hidden_low, weights[5], preferred_element_type=jnp.float32)
    return (result, norm_pull, normed_two, gelu_pull, hidden_low)


def key_loop(keys_all, values_all, segment_row, head_count, visit, initial):
    total_rows = keys_all.shape[0]
    block_rows = math.gcd(total_rows, 512)

    def one_block(block_index, running):
        offset = block_index * block_rows
        key_block = lax.dynamic_slice_in_dim(keys_all, offset, block_rows, 0).reshape(
            block_rows, head_count, HEAD_DIM
        )
        value_block = lax.dynamic_slice_in_dim(values_all, offset, block_rows, 0).reshape(
            block_rows, head_count, HEAD_DIM
        )
        key_segs = lax.dynamic_slice_in_dim(segment_row, offset, block_rows, 0)
        return visit(running, key_block, value_block, key_segs)

    return lax.fori_loop(0, total_rows // block_rows, one_block, initial)


def layer_forward(
    layer_in, segment_row, weights, kernel, conv_shift, first_section, my_start, factor
):
    frames, width_all = layer_in.shape
    head_count = width_all // HEAD_DIM
    padded, conv_pull, resid_one, norm_pull, normed_one, packed = front(
        layer_in, weights, kernel, conv_shift, first_section
    )
    query_heads = packed[:, :width_all].reshape(frames, head_count, HEAD_DIM)
    query_segs = lax.dynamic_slice_in_dim(segment_row, my_start, frames, 0)
    initial = (
        jnp.full((head_count, frames), NEG, jnp.float32),
        jnp.zeros((head_count, frames), jnp.float32),
        jnp.zeros((head_count, frames, HEAD_DIM), jnp.float32),
    )
    key_piece = lax.all_gather(packed[:, width_all : 2 * width_all], "seq", axis=0, tiled=True)
    value_piece = lax.all_gather(packed[:, 2 * width_all :], "seq", axis=0, tiled=True)
    piece_rows = key_piece.shape[0]
    block_rows = math.gcd(piece_rows, 512)

    def one_block(block_index, running):
        run_max, run_sum, run_acc = running
        offset = block_index * block_rows
        key_block = lax.dynamic_slice_in_dim(key_piece, offset, block_rows, 0).reshape(
            block_rows, head_count, HEAD_DIM
        )
        value_block = lax.dynamic_slice_in_dim(value_piece, offset, block_rows, 0).reshape(
            block_rows, head_count, HEAD_DIM
        )
        key_segs = lax.dynamic_slice_in_dim(segment_row, offset, block_rows, 0)
        scores, allowed = score_block(query_heads, key_block, query_segs, key_segs, factor)
        masked = jnp.where(allowed, scores, NEG)
        new_max = jnp.maximum(run_max, jnp.max(masked, axis=-1))
        weights_now = jnp.where(allowed, jnp.exp(masked - new_max[..., None]), 0.0)
        rescale = jnp.exp(run_max - new_max)
        run_sum = run_sum * rescale + jnp.sum(weights_now, axis=-1)
        run_acc = run_acc * rescale[..., None] + jnp.einsum(
            "hqk,khd->hqd",
            weights_now.astype(jnp.bfloat16),
            value_block,
            preferred_element_type=jnp.float32,
        )
        return (new_max, run_sum, run_acc)

    run_max, run_sum, run_acc = lax.fori_loop(0, piece_rows // block_rows, one_block, initial)
    log_total = run_max + jnp.log(run_sum)
    mixture = run_acc / run_sum[..., None]
    attn_low = jnp.transpose(mixture, (1, 0, 2)).reshape(frames, width_all).astype(jnp.bfloat16)
    result, norm_two_pull, normed_two, gelu_pull, hidden_low = tail(resid_one, attn_low, weights)
    kept = (
        padded,
        conv_pull,
        norm_pull,
        normed_one,
        packed,
        log_total,
        mixture,
        attn_low,
        norm_two_pull,
        normed_two,
        gelu_pull,
        hidden_low,
        segment_row,
    )
    return (result, kept)


def layer_backward(kept, grad_out, weights, kernel, first_section, my_start, factor):
    (
        padded,
        conv_pull,
        norm_one_pull,
        normed_one,
        packed,
        log_total,
        mixture,
        attn_low,
        norm_two_pull,
        normed_two,
        gelu_pull,
        hidden_low,
        segment_row,
    ) = kept
    frames, width_all = normed_one.shape
    head_count = width_all // HEAD_DIM
    query_heads = packed[:, :width_all].reshape(frames, head_count, HEAD_DIM)
    key_local = packed[:, width_all : 2 * width_all]
    value_local = packed[:, 2 * width_all :]
    query_segs = lax.dynamic_slice_in_dim(segment_row, my_start, frames, 0)
    keys_all, values_all = (
        lax.all_gather(key_local, "seq", axis=0, tiled=True),
        lax.all_gather(value_local, "seq", axis=0, tiled=True),
    )

    def chances_for(key_block, key_segs):
        scores, allowed = score_block(query_heads, key_block, query_segs, key_segs, factor)
        return jnp.where(
            allowed, jnp.exp(jnp.where(allowed, scores, NEG) - log_total[..., None]), 0.0
        )

    branch_grad = grad_out.astype(jnp.bfloat16)
    hidden_grad = jnp.einsum(
        "to,io->ti", branch_grad, weights[5], preferred_element_type=jnp.float32
    )
    pre_grad = gelu_pull(hidden_grad)[0].astype(jnp.bfloat16)
    normed_two_grad = jnp.einsum(
        "tf,if->ti", pre_grad, weights[4], preferred_element_type=jnp.float32
    )
    resid_two_grad, grad_gain_two = norm_two_pull(normed_two_grad)
    resid_two_grad = resid_two_grad + grad_out
    attn_branch_grad = resid_two_grad.astype(jnp.bfloat16)
    attended_grad = jnp.einsum(
        "to,io->ti", attn_branch_grad, weights[2], preferred_element_type=jnp.float32
    ).astype(jnp.bfloat16)
    dout_heads = attended_grad.reshape(frames, head_count, HEAD_DIM)
    delta_rows = jnp.einsum("qhd,hqd->hq", dout_heads.astype(jnp.float32), mixture)

    def visit_query(running, key_block, value_block, key_segs):
        chances = chances_for(key_block, key_segs)
        prob_grad = jnp.einsum(
            "qhd,khd->hqk", dout_heads, value_block, preferred_element_type=jnp.float32
        )
        score_grad = (chances * (prob_grad - delta_rows[..., None])).astype(jnp.bfloat16)
        return running + jnp.einsum(
            "hqk,khd->qhd", score_grad, key_block, preferred_element_type=jnp.float32
        )

    grad_query = (
        key_loop(
            keys_all,
            values_all,
            segment_row,
            head_count,
            visit_query,
            jnp.zeros((frames, head_count, HEAD_DIM), jnp.float32),
        )
        * factor
    )
    row_stats = (
        lax.all_gather(log_total, "seq", axis=1, tiled=True),
        lax.all_gather(delta_rows, "seq", axis=1, tiled=True),
    )
    key_heads = key_local.reshape(frames, head_count, HEAD_DIM)
    value_heads = value_local.reshape(frames, head_count, HEAD_DIM)
    start_acc = (
        jnp.zeros((frames, head_count, HEAD_DIM), jnp.float32),
        jnp.zeros((frames, head_count, HEAD_DIM), jnp.float32),
    )
    query_piece = lax.all_gather(packed[:, :width_all], "seq", axis=0, tiled=True)
    dout_piece = lax.all_gather(attended_grad, "seq", axis=0, tiled=True)
    piece_rows = query_piece.shape[0]
    block_rows = math.gcd(piece_rows, 512)

    def one_block(block_index, running):
        key_acc, value_acc = running
        offset = block_index * block_rows
        query_block = lax.dynamic_slice_in_dim(query_piece, offset, block_rows, 0).reshape(
            block_rows, head_count, HEAD_DIM
        )
        dout_block = lax.dynamic_slice_in_dim(dout_piece, offset, block_rows, 0).reshape(
            block_rows, head_count, HEAD_DIM
        )
        seg_block = lax.dynamic_slice_in_dim(segment_row, offset, block_rows, 0)
        total_block = lax.dynamic_slice_in_dim(row_stats[0], offset, block_rows, 1)
        delta_block = lax.dynamic_slice_in_dim(row_stats[1], offset, block_rows, 1)
        scores, allowed = score_block(query_block, key_heads, seg_block, query_segs, factor)
        chances = jnp.where(
            allowed, jnp.exp(jnp.where(allowed, scores, NEG) - total_block[..., None]), 0.0
        )
        prob_grad = jnp.einsum(
            "qhd,khd->hqk", dout_block, value_heads, preferred_element_type=jnp.float32
        )
        score_grad = (chances * (prob_grad - delta_block[..., None])).astype(jnp.bfloat16)
        key_acc = (
            key_acc
            + jnp.einsum(
                "hqk,qhd->khd", score_grad, query_block, preferred_element_type=jnp.float32
            )
            * factor
        )
        value_acc = value_acc + jnp.einsum(
            "hqk,qhd->khd",
            chances.astype(jnp.bfloat16),
            dout_block,
            preferred_element_type=jnp.float32,
        )
        return (key_acc, value_acc)

    key_acc, value_acc = lax.fori_loop(0, piece_rows // block_rows, one_block, start_acc)
    grad_key = key_acc.reshape(frames, width_all)
    grad_value = value_acc.reshape(frames, width_all)
    packed_grad = jnp.concatenate(
        [grad_query.reshape(frames, width_all), grad_key, grad_value], axis=1
    ).astype(jnp.bfloat16)
    normed_one_grad = jnp.einsum(
        "tj,ij->ti", packed_grad, weights[1], preferred_element_type=jnp.float32
    )
    resid_one_grad, grad_gain_one = norm_one_pull(normed_one_grad)
    resid_one_grad = resid_one_grad + resid_two_grad
    conv_grad = jnp.where(first_section, conv_pull(resid_one_grad)[0], 0.0).astype(jnp.bfloat16)
    grad_pad = padded_2(conv_grad, (("seq", 0),), TAPS // 2)
    back_sum = lax.cond(
        first_section,
        lambda: conv_input_grad(grad_pad, kernel, frames),
        lambda: jnp.zeros((frames, width_all), jnp.float32),
    )
    grad_in = resid_one_grad + back_sum
    products = (
        normed_one,
        packed_grad,
        attn_low,
        attn_branch_grad,
        normed_two,
        pre_grad,
        hidden_low,
        branch_grad,
        padded,
        conv_grad,
    )
    return (grad_in, (grad_gain_one, grad_gain_two), products)


def per_device(
    signal,
    frame_segment_index,
    conv_weight,
    conv_bias,
    norm1_gain,
    qkv_weight,
    out_weight,
    norm2_gain,
    up_weight,
    down_weight,
    cotangent,
):
    micro_count, frames, width_all = signal.shape
    factor = 1.0 / math.sqrt(HEAD_DIM)
    first_section = lax.axis_index("section") == 0
    my_start = lax.axis_index("seq") * frames
    gathered = (
        lax.all_gather(norm1_gain.astype(jnp.bfloat16), ("dp", "seq"), axis=1, tiled=True),
        lax.all_gather(qkv_weight.astype(jnp.bfloat16), ("dp", "seq"), axis=1, tiled=True),
        lax.all_gather(out_weight.astype(jnp.bfloat16), ("dp", "seq"), axis=1, tiled=True),
        lax.all_gather(norm2_gain.astype(jnp.bfloat16), ("dp", "seq"), axis=1, tiled=True),
        lax.all_gather(up_weight.astype(jnp.bfloat16), ("dp", "seq"), axis=1, tiled=True),
        lax.all_gather(down_weight.astype(jnp.bfloat16), ("dp", "seq"), axis=1, tiled=True),
    )
    weights = tuple((member[0] for member in gathered))
    kernel, conv_shift = (
        lax.all_gather(
            conv_weight.astype(jnp.bfloat16), ("section", "dp", "seq"), axis=0, tiled=True
        ),
        lax.all_gather(
            conv_bias.astype(jnp.bfloat16), ("section", "dp", "seq"), axis=0, tiled=True
        ),
    )
    received = jnp.zeros((frames, width_all), jnp.bfloat16)
    saved = []
    forward_outs = []
    for step_index in range(micro_count + 1):
        own_index = min(step_index, micro_count - 1)
        prior_index = max(step_index - 1, 0)
        layer_in = jnp.where(first_section, signal[own_index], received)
        segment_row = jnp.where(
            first_section, frame_segment_index[own_index], frame_segment_index[prior_index]
        )
        result, kept = layer_forward(
            layer_in, segment_row, weights, kernel, conv_shift, first_section, my_start, factor
        )
        saved.append(kept)
        forward_outs.append(result)
        if step_index < micro_count:
            received = from_behind(result.astype(jnp.bfloat16), "section", 1)
    received_back = jnp.zeros((frames, width_all), jnp.bfloat16)
    input_grads = []
    gain_totals = None
    product_list = []
    for step_index in range(micro_count + 1):
        kept = saved[micro_count - step_index]
        if step_index < micro_count:
            top_grad = cotangent[micro_count - 1 - step_index].astype(jnp.float32)
        else:
            top_grad = jnp.zeros((frames, width_all), jnp.float32)
        incoming = jnp.where(first_section, received_back.astype(jnp.float32), top_grad)
        grad_in, gain_grads, products = layer_backward(
            kept, incoming, weights, kernel, first_section, my_start, factor
        )
        input_grads.append(grad_in)
        product_list.append(products)
        if gain_totals is None:
            gain_totals = gain_grads
        else:
            gain_totals = (gain_totals[0] + gain_grads[0], gain_totals[1] + gain_grads[1])
        if step_index < micro_count:
            received_back = from_behind(grad_in.astype(jnp.bfloat16), "section", -1)

    def joined(position):
        return jnp.concatenate([member[position] for member in product_list], axis=0)

    grad_qkv = jnp.einsum("ti,tj->ij", joined(0), joined(1), preferred_element_type=jnp.float32)
    grad_out_weight = jnp.einsum(
        "ti,to->io", joined(2), joined(3), preferred_element_type=jnp.float32
    )
    grad_up = jnp.einsum("ti,tf->if", joined(4), joined(5), preferred_element_type=jnp.float32)
    grad_down = jnp.einsum("ti,to->io", joined(6), joined(7), preferred_element_type=jnp.float32)
    padded_all = jnp.stack([member[8] for member in product_list])
    conv_grad_all = jnp.stack([member[9] for member in product_list])
    kernel_grad = conv_kernel_grad(padded_all, conv_grad_all)
    bias_grad = jnp.sum(joined(9).astype(jnp.float32), axis=0)
    ends = jnp.stack(
        [
            jnp.where(
                first_section, input_grads[micro_count - mb_index], forward_outs[mb_index + 1]
            )
            for mb_index in range(micro_count)
        ]
    )[None]
    layer_sums = (
        lax.psum_scatter(gain_totals[0][None], ("dp", "seq"), scatter_dimension=1, tiled=True),
        lax.psum_scatter(grad_qkv[None], ("dp", "seq"), scatter_dimension=1, tiled=True),
        lax.psum_scatter(grad_out_weight[None], ("dp", "seq"), scatter_dimension=1, tiled=True),
        lax.psum_scatter(gain_totals[1][None], ("dp", "seq"), scatter_dimension=1, tiled=True),
        lax.psum_scatter(grad_up[None], ("dp", "seq"), scatter_dimension=1, tiled=True),
        lax.psum_scatter(grad_down[None], ("dp", "seq"), scatter_dimension=1, tiled=True),
    )
    conv_sums = (
        lax.psum_scatter(kernel_grad, ("section", "dp", "seq"), scatter_dimension=0, tiled=True),
        lax.psum_scatter(bias_grad, ("section", "dp", "seq"), scatter_dimension=0, tiled=True),
    )
    return (
        ends,
        conv_sums[0],
        conv_sums[1],
        layer_sums[0],
        layer_sums[1],
        layer_sums[2],
        layer_sums[3],
        layer_sums[4],
        layer_sums[5],
    )


def swap_section(value):
    return lax.ppermute(value, "section", [(0, 1), (1, 0)])


def swap_x(value):
    return lax.ppermute(value, "seq", [(q, q ^ 1) for q in range(4)])


def pair_sum(low, behind=None):
    other = swap_x(low)
    if behind is not None:
        other, _ = lax.optimization_barrier((other, behind))
    return low.astype(jnp.float32) + other.astype(jnp.float32)


def after(first, second):
    return lax.optimization_barrier((first, second))


def choose(flag, first, second):
    return jnp.where(flag, first, second), jnp.where(flag, second, first)


def sum_dp(blocks, dp, meanwhile):
    count = lax.axis_size("dp")
    f32, bf16 = jnp.float32, jnp.bfloat16
    meanwhile = list(meanwhile)

    def block(index):
        return lax.dynamic_index_in_dim(blocks, jnp.clip(index, 0, count - 1), 0, keepdims=False)

    running = [None, None]
    for turn, distance in enumerate(range(count - 1, 0, -1)):
        for way, sign in enumerate((1, -1)):
            own = block(dp + sign * distance)
            if running[way] is not None:
                own = (own.astype(f32) + running[way].astype(f32)).astype(bf16)
            live = [(i, i + sign) for i in range(count) if 0 <= i + sign < count and 0 <= i + sign * distance < count]
            running[way] = lax.ppermute(own, "dp", live)
        if turn < len(meanwhile):
            running, meanwhile[turn] = after(running, meanwhile[turn])
            running = list(running)
    total = block(dp).astype(f32) + running[0].astype(f32) + running[1].astype(f32)
    return total.astype(bf16), meanwhile


def line_groups():
    count = lax.axis_size("dp")
    return [
        [(s * count + d) * 4 + 2 * y + x for d in range(count) for y in range(2) for s in range(2)]
        for x in range(2)
    ]


def gather_rows(piece):
    return lax.all_gather(
        piece, ("section", "dp", "seq"), axis=0, tiled=True, axis_index_groups=line_groups()
    )


def scatter_rows(partial):
    return lax.psum_scatter(
        partial, ("section", "dp", "seq"), scatter_dimension=0, tiled=True,
        axis_index_groups=line_groups(),
    )


MESH = pl.DeviceIdType.MESH


def opening_kernel(
    dp_count, parts, conv_ref, signal_ref, keep_ref, send_ref, rest_ref,
    conv_out, signal_out, whole_out, second_out,
    local_sem, a2a_send, a2a_recv, sig_send, sig_recv, line_send, line_recv, own_send, column_recv, rest_recv,
    up_send, up_recv, y_send, y_recv, core_send, core_recv,
):
    sec, dp, seq = (lax.axis_index(name) for name in ("section", "dp", "seq"))
    me = sec * 4 + seq
    x, y = seq % 2, seq // 2
    partner_x = (seq + 1 - 2 * x) % 4
    partner_y = {"seq": (seq + 2) % 4}
    sibling = {"section": 1 - sec}
    has_up, has_down = dp < dp_count - 1, dp > 0
    split = keep_ref.shape[1]
    rows = keep_ref.shape[0] // parts

    barrier = pltpu.get_barrier_semaphore()
    for turn in range(1, 8):
        other = (me + turn) % 8
        pl.semaphore_signal(
            barrier, inc=1, device_id={"section": other // 4, "seq": other % 4}, device_id_type=MESH
        )
    for there, step in ((has_up, 1), (has_down, -1)):

        @pl.when(there)
        def _(step=step):
            pl.semaphore_signal(barrier, inc=1, device_id={"dp": dp + step}, device_id_type=MESH)

    pl.semaphore_wait(barrier, 7 + jnp.where(has_up, 1, 0) + jnp.where(has_down, 1, 0))

    def remote(source, target, send, recv, device):
        return pltpu.make_async_remote_copy(
            src_ref=source, dst_ref=target, send_sem=send, recv_sem=recv,
            device_id=device, device_id_type=MESH,
        )

    def a2a(target, source):
        return remote(
            conv_ref.at[target], conv_out.at[dp, source], a2a_send.at[target], a2a_recv.at[source],
            {"section": target // 4, "seq": target % 4},
        )

    def sig(target, source):
        return remote(
            signal_ref.at[target], signal_out.at[source], sig_send.at[target], sig_recv.at[source],
            {"seq": target},
        )

    for turn in range(1, 8):
        a2a((me + turn) % 8, me).start()
    conv_local = pltpu.make_async_copy(conv_ref.at[me], conv_out.at[dp, me], local_sem.at[0])
    signal_local = pltpu.make_async_copy(signal_ref.at[seq], signal_out.at[seq], local_sem.at[1])
    conv_local.start()
    signal_local.start()

    def columns(layer, half):
        return (second_out if layer else whole_out.at[dp, y, half]).at[:, pl.ds(0, split)]

    def others(layer, half):
        return (second_out if layer else whole_out.at[dp, y, half]).at[:, pl.ds(split, rest_ref.shape[2])]

    class Layer:
        def __init__(self, layer):
            far = {"section": 1 - layer}
            self.mine = sec == layer
            self.even = x == layer
            received = column_recv.at[layer]
            self.keep_local = pltpu.make_async_copy(keep_ref, columns(layer, layer), local_sem.at[2])
            self.rest_local = pltpu.make_async_copy(rest_ref.at[layer], others(layer, layer), local_sem.at[3])
            self.keep_far = remote(keep_ref, columns(layer, 1 - layer), own_send.at[0], received, far)
            self.send_same = remote(
                send_ref, columns(layer, layer), own_send.at[1], received, {"seq": partner_x}
            )
            self.send_cross = remote(
                send_ref, columns(layer, 1 - layer), own_send.at[1], received, {**far, "seq": partner_x}
            )
            self.rest_far = remote(
                rest_ref.at[1 - layer], others(layer, 1 - layer), own_send.at[2], rest_recv.at[layer], far
            )

        def start(self):
            @pl.when(self.mine & self.even)
            def _():
                self.send_same.start()
                self.keep_local.start()

            @pl.when(self.mine & jnp.logical_not(self.even))
            def _():
                self.send_cross.start()
                self.keep_far.start()

            @pl.when(self.mine)
            def _():
                self.rest_far.start()
                self.rest_local.start()

        def wait(self):
            other = jnp.logical_not(self.mine)
            odd = jnp.logical_not(self.even)

            @pl.when(self.mine & self.even)
            def _():
                self.keep_local.wait()

            @pl.when(self.mine & odd)
            def _():
                self.send_same.wait_recv()

            @pl.when(self.mine)
            def _():
                self.rest_local.wait()

            @pl.when(other & self.even)
            def _():
                self.send_cross.wait_recv()

            @pl.when(other & odd)
            def _():
                self.keep_far.wait_recv()

            @pl.when(other)
            def _():
                self.rest_far.wait_recv()

        def finish(self):
            @pl.when(self.mine & self.even)
            def _():
                self.send_same.wait_send()

            @pl.when(self.mine & jnp.logical_not(self.even))
            def _():
                self.send_cross.wait_send()
                self.keep_far.wait_send()

            @pl.when(self.mine)
            def _():
                self.rest_far.wait_send()

    layers = [Layer(0), Layer(1)]
    for layer in layers:
        layer.start()
    for turn in range(1, 4):
        sig((seq + turn) % 4, seq).start()

    def line(slot, direction):
        index = (direction + 1) // 2
        return remote(
            conv_out.at[slot], conv_out.at[slot], line_send.at[index, slot], line_recv.at[slot],
            {"dp": dp + direction},
        )

    def place(slot, row, half, part):
        return whole_out.at[slot, row, half, pl.ds(part * rows, rows)]

    def along(slot, direction, part):
        index = (direction + 1) // 2
        ref = place(slot, y, sec, part)
        return remote(
            ref, ref, up_send.at[index, slot, part], up_recv.at[slot, part], {"dp": dp + direction}
        )

    def across(slot, row, part):
        ref = place(slot, row, sec, part)
        return remote(ref, ref, y_send.at[slot, part], y_recv.at[slot, part], partner_y)

    def to_core(slot, row, half, part):
        ref = place(slot, row, half, part)
        return remote(
            ref, ref, core_send.at[slot, row, part], core_recv.at[slot, row, part], sibling
        )

    for turn in range(1, 8):
        a2a((me + turn) % 8, (me + turn) % 8).wait_recv()
    conv_local.wait()
    for there, direction in ((has_up, 1), (has_down, -1)):

        @pl.when(there)
        def _(direction=direction):
            line(dp, direction).start()

    layers[0].wait()
    for part in range(parts):
        for there, direction in ((has_up, 1), (has_down, -1)):

            @pl.when(there)
            def _(direction=direction, part=part):
                along(dp, direction, part).start()

        across(dp, y, part).start()
        to_core(dp, y, sec, part).start()

    def stage(distance):
        arrivals = []
        for direction in (1, -1):
            slot = dp - direction * distance
            arrives = (slot >= 0) & (slot < dp_count)
            goes_on = arrives & (has_up if direction == 1 else has_down)
            arrivals.append((direction, slot, arrives, goes_on))

            @pl.when(arrives)
            def _(slot=slot, direction=direction):
                line(slot, direction).wait_recv()

            @pl.when(goes_on)
            def _(slot=slot, direction=direction):
                line(slot, direction).start()

        for part in range(parts):
            for direction, slot, arrives, goes_on in arrivals:

                @pl.when(arrives)
                def _(slot=slot, direction=direction, part=part):
                    along(slot, direction, part).wait_recv()

                @pl.when(goes_on)
                def _(slot=slot, direction=direction, part=part):
                    along(slot, direction, part).start()

                @pl.when(arrives)
                def _(slot=slot, part=part):
                    across(slot, y, part).start()
                    to_core(slot, y, sec, part).start()

    def pass_crossed(distance):
        for part in range(parts):
            for sign in (1, -1) if distance else (1,):
                slot = dp - sign * distance

                @pl.when((slot >= 0) & (slot < dp_count))
                def _(slot=slot, part=part):
                    across(slot, 1 - y, part).wait_recv()
                    to_core(slot, 1 - y, sec, part).start()

    for distance in range(1, dp_count):
        stage(distance)
        pass_crossed(distance - 1)
    pass_crossed(dp_count - 1)

    for slot in range(dp_count):
        for part in range(parts):
            for row in range(2):
                to_core(slot, row, 1 - sec, part).wait_recv()
                to_core(slot, row, sec, part).wait_send()
            across(slot, y, part).wait_send()
        for direction in (1, -1):
            sent = (slot <= dp if direction == 1 else slot >= dp) & (has_up if direction == 1 else has_down)

            @pl.when(sent)
            def _(slot=slot, direction=direction):
                line(slot, direction).wait_send()
                for part in range(parts):
                    along(slot, direction, part).wait_send()

    layers[1].wait()
    for layer in layers:
        layer.finish()
    for turn in range(1, 8):
        a2a((me + turn) % 8, me).wait_send()
    for turn in range(1, 4):
        sig((seq + turn) % 4, (seq + turn) % 4).wait_recv()
        sig((seq + turn) % 4, seq).wait_send()
    signal_local.wait()


def opening(conv_send, signal_send, keep, send, rest):
    count = lax.axis_size("dp")
    parts = 2
    rows, columns = keep.shape[0], keep.shape[1] + rest.shape[2]
    anywhere = pl.BlockSpec(memory_space=pl.ANY)
    dma = pltpu.SemaphoreType.DMA
    conv_all, signal_all, whole, second = pl.pallas_call(
        functools.partial(opening_kernel, count, parts),
        in_specs=[anywhere] * 5,
        out_specs=[anywhere] * 4,
        out_shape=[
            jax.ShapeDtypeStruct((count, *conv_send.shape), conv_send.dtype),
            jax.ShapeDtypeStruct(signal_send.shape, signal_send.dtype),
            jax.ShapeDtypeStruct((count, 2, 2, rows, columns), keep.dtype),
            jax.ShapeDtypeStruct((rows, columns), keep.dtype),
        ],
        scratch_shapes=[
            dma((4,)), dma((8,)), dma((8,)), dma((4,)), dma((4,)), dma((2, count)), dma((count,)),
            dma((3,)), dma((2,)), dma((2,)), dma((2, count, parts)), dma((count, parts)), dma((count, parts)),
            dma((count, parts)), dma((count, 2, parts)), dma((count, 2, parts)),
        ],
        compiler_params=pltpu.CompilerParams(
            collective_id=0, has_side_effects=True, vmem_limit_bytes=4 * 1024 * 1024
        ),
        name="opening",
    )(conv_send, signal_send, keep, send, rest)
    return conv_all, signal_all, whole.reshape(-1, columns), second


def norm_stats(values):
    average = jnp.mean(values, axis=-1, keepdims=True)
    centred = values - average
    spread = jnp.mean(centred * centred, axis=-1, keepdims=True)
    return centred, lax.rsqrt(spread + EPS)


def norm_back(values, gain, grad):
    centred, inv = norm_stats(values)
    unit = centred * inv
    gain_grad = jnp.sum(grad * unit, axis=0)
    f = grad * gain
    mean_f = jnp.mean(f, axis=-1, keepdims=True)
    mean_fu = jnp.mean(f * unit, axis=-1, keepdims=True)
    return (f - mean_f - unit * mean_fu) * inv, gain_grad


def gelu_slope(values):
    cdf = 0.5 * (1.0 + lax.erf(values * (1.0 / math.sqrt(2.0))))
    pdf = jnp.exp(-0.5 * values * values) * (1.0 / math.sqrt(2.0 * math.pi))
    return cdf + values * pdf


def attention_forward_kernel(factor, q_ref, k_ref, v_ref, qs_ref, ks_ref, o_ref, lse_ref):
    queries = q_ref[...]
    lane = lax.broadcasted_iota(jnp.int32, queries.shape, 1)
    allowed = qs_ref[...] == ks_ref[...]
    keys = k_ref[...]
    values = v_ref[...]
    outs = []
    for head in range(2):
        mine = (lane < HEAD_DIM) if head == 0 else (lane >= HEAD_DIM)
        own = jnp.where(mine, queries, jnp.zeros_like(queries))
        scores = lax.dot_general(
            own, keys, (((1,), (1,)), ((), ())), preferred_element_type=jnp.float32
        ) * factor
        scores = jnp.where(allowed, scores, NEG)
        top = jnp.max(scores, axis=-1, keepdims=True)
        raised = jnp.exp(scores - top)
        total = jnp.sum(raised, axis=-1, keepdims=True)
        chances = (raised * (1.0 / total)).astype(jnp.bfloat16)
        outs.append(jnp.dot(chances, values, preferred_element_type=jnp.float32))
        lse_ref[0, head] = top + jnp.log(total)
    o_ref[...] = jnp.where(lane < HEAD_DIM, outs[0], outs[1]).astype(o_ref.dtype)


def attention_forward(packed, kv_all, query_segs, key_segs, factor):
    frames = packed.shape[0]
    keys = kv_all.shape[0]
    width = packed.shape[1] // 3
    pairs = width // 128
    rows = math.gcd(frames, 256)
    return pl.pallas_call(
        functools.partial(attention_forward_kernel, factor),
        grid=(pairs, frames // rows),
        in_specs=[
            pl.BlockSpec((rows, 128), lambda h, i: (i, h)),
            pl.BlockSpec((keys, 128), lambda h, i: (0, h)),
            pl.BlockSpec((keys, 128), lambda h, i: (0, pairs + h)),
            pl.BlockSpec((rows, 1), lambda h, i: (i, 0)),
            pl.BlockSpec((1, keys), lambda h, i: (0, 0)),
        ],
        out_specs=[
            pl.BlockSpec((rows, 128), lambda h, i: (i, h)),
            pl.BlockSpec((1, 2, rows, 1), lambda h, i: (h, 0, i, 0)),
        ],
        out_shape=[
            jax.ShapeDtypeStruct((frames, width), jnp.bfloat16),
            jax.ShapeDtypeStruct((pairs, 2, frames, 1), jnp.float32),
        ],
        compiler_params=pltpu.CompilerParams(vmem_limit_bytes=40 * 1024 * 1024),
        cost_estimate=pl.CostEstimate(
            flops=4 * frames * keys * width * 2,
            bytes_accessed=2 * (frames * width * 2 + keys * width * 2),
            transcendentals=frames * keys * (width // HEAD_DIM),
        ),
        name="attention_forward",
    )(packed, kv_all, kv_all, query_segs[:, None], key_segs[None, :])


def attention_backward_kernel(
    factor, q_ref, k_ref, v_ref, g_ref, o_ref, lse_ref, qs_ref, ks_ref, *rest
):
    *begin, dq_ref, dk_ref, dv_ref = rest
    step = pl.program_id(1)

    @pl.when(step == 0)
    def _():
        for index, total_ref in enumerate((dk_ref, dv_ref)):
            total_ref[...] = begin[index][...] if begin else jnp.zeros_like(total_ref)

    queries = q_ref[...]
    grads = g_ref[...]
    keys = k_ref[...]
    values = v_ref[...]
    lane = lax.broadcasted_iota(jnp.int32, queries.shape, 1)
    key_lane = lax.broadcasted_iota(jnp.int32, keys.shape, 1)
    allowed = qs_ref[...] == ks_ref[...]
    product = grads.astype(jnp.float32) * o_ref[...].astype(jnp.float32)
    dq = None
    for head in range(2):
        mine = (lane < HEAD_DIM) if head == 0 else (lane >= HEAD_DIM)
        key_mine = (key_lane < HEAD_DIM) if head == 0 else (key_lane >= HEAD_DIM)
        own_q = jnp.where(mine, queries, jnp.zeros_like(queries))
        own_g = jnp.where(mine, grads, jnp.zeros_like(grads))
        own_k = jnp.where(key_mine, keys, jnp.zeros_like(keys))
        delta = jnp.sum(jnp.where(mine, product, 0.0), axis=-1, keepdims=True)
        scores = lax.dot_general(
            own_q, keys, (((1,), (1,)), ((), ())), preferred_element_type=jnp.float32
        ) * factor
        chances = jnp.exp(jnp.where(allowed, scores, NEG) - lse_ref[0, head])
        prob_grad = lax.dot_general(
            own_g, values, (((1,), (1,)), ((), ())), preferred_element_type=jnp.float32
        )
        score_grad = (chances * (prob_grad - delta)).astype(jnp.bfloat16)
        part = jnp.dot(score_grad, own_k, preferred_element_type=jnp.float32)
        dq = part if dq is None else dq + part
        dk_ref[...] += lax.dot_general(
            score_grad, own_q, (((0,), (0,)), ((), ())), preferred_element_type=jnp.float32
        ) * factor
        dv_ref[...] += lax.dot_general(
            chances.astype(jnp.bfloat16), own_g, (((0,), (0,)), ((), ())),
            preferred_element_type=jnp.float32,
        )
    dq_ref[...] = (dq * factor).astype(dq_ref.dtype)


def attention_backward(packed, kv_all, grads, attended, lse, query_segs, key_segs, factor, begin=None):
    frames = packed.shape[0]
    keys = kv_all.shape[0]
    width = packed.shape[1] // 3
    pairs = width // 128
    rows = math.gcd(frames, 256)
    return pl.pallas_call(
        functools.partial(attention_backward_kernel, factor),
        grid=(pairs, frames // rows),
        in_specs=[
            pl.BlockSpec((rows, 128), lambda h, i: (i, h)),
            pl.BlockSpec((keys, 128), lambda h, i: (0, h)),
            pl.BlockSpec((keys, 128), lambda h, i: (0, pairs + h)),
            pl.BlockSpec((rows, 128), lambda h, i: (i, h)),
            pl.BlockSpec((rows, 128), lambda h, i: (i, h)),
            pl.BlockSpec((1, 2, rows, 1), lambda h, i: (h, 0, i, 0)),
            pl.BlockSpec((rows, 1), lambda h, i: (i, 0)),
            pl.BlockSpec((1, keys), lambda h, i: (0, 0)),
        ]
        + [pl.BlockSpec((keys, 128), lambda h, i: (0, h))] * (2 if begin else 0),
        out_specs=[
            pl.BlockSpec((rows, 128), lambda h, i: (i, h)),
            pl.BlockSpec((keys, 128), lambda h, i: (0, h)),
            pl.BlockSpec((keys, 128), lambda h, i: (0, h)),
        ],
        out_shape=[
            jax.ShapeDtypeStruct((frames, width), jnp.bfloat16),
            jax.ShapeDtypeStruct((keys, width), jnp.float32),
            jax.ShapeDtypeStruct((keys, width), jnp.float32),
        ],
        compiler_params=pltpu.CompilerParams(vmem_limit_bytes=48 * 1024 * 1024),
        cost_estimate=pl.CostEstimate(
            flops=10 * frames * keys * width * 2,
            bytes_accessed=4 * (frames * width * 2 + keys * width * 2),
            transcendentals=frames * keys * (width // HEAD_DIM),
        ),
        name="attention_backward",
    )(packed, kv_all, kv_all, grads, attended, lse, query_segs[:, None], key_segs[None, :], *(begin or ()))


CONV_STEP = 4


def conv_bands(kernel, per_group):
    groups = kernel.shape[1] // per_group
    steps = TAPS // CONV_STEP + 1
    bands = []
    for group in range(groups):
        own = kernel[:, group * per_group : (group + 1) * per_group]
        shifted = [
            jnp.pad(own, ((shift * per_group, (CONV_STEP - shift) * per_group), (0, 0)))
            for shift in range(CONV_STEP)
        ]
        band = jnp.concatenate(shifted, axis=1)
        bands.append(band.reshape(steps, CONV_STEP * per_group, CONV_STEP * per_group))
    return bands


def group_view(values, per_group):
    rows, frames, width = values.shape
    return [
        values[:, :, g * per_group : (g + 1) * per_group].reshape(
            rows, frames // CONV_STEP, CONV_STEP * per_group
        )
        for g in range(width // per_group)
    ]


def ungroup(parts, per_group):
    rows, blocks, _ = parts[0].shape
    return jnp.concatenate(
        [part.reshape(rows, blocks * CONV_STEP, per_group) for part in parts], axis=2
    )


CONV_DIMS = ("NWC", "WIO", "NWC")


def conv_forward(views, bands):
    half = TAPS // 2 // CONV_STEP
    return [
        lax.conv_general_dilated(
            view, band, (1,), [(half, half)], dimension_numbers=CONV_DIMS,
            preferred_element_type=jnp.float32,
        )
        for view, band in zip(views, bands)
    ]


def conv_back(grad_views, bands):
    half = TAPS // 2 // CONV_STEP
    return [
        lax.conv_general_dilated(
            view, jnp.transpose(band[::-1], (0, 2, 1)), (1,), [(half, half)],
            dimension_numbers=CONV_DIMS, preferred_element_type=jnp.float32,
        )
        for view, band in zip(grad_views, bands)
    ]


def conv_taps_grad(views, grad_views, per_group):
    half = TAPS // 2 // CONV_STEP
    results = []
    for view, grad in zip(views, grad_views):
        band = lax.conv_general_dilated(
            view, grad, (1,), [(half, half)],
            dimension_numbers=("CWN", "IWO", "WNC"),
            preferred_element_type=jnp.float32,
        )
        flat = band.reshape(-1, CONV_STEP * per_group)
        total = None
        for shift in range(CONV_STEP):
            part = flat[
                shift * per_group : (shift + TAPS) * per_group,
                shift * per_group : (shift + 1) * per_group,
            ]
            total = part if total is None else total + part
        results.append(total)
    return jnp.concatenate(results, axis=1)


def to_column(vector, width):
    return jnp.pad(vector[:, None], ((0, 0), (0, width - 1)))


def per_device_pairs(
    signal, frame_segment_index, conv_weight, conv_bias, norm1_gain, qkv_weight, out_weight,
    norm2_gain, up_weight, down_weight, cotangent,
):
    micro_count, frames, width = signal.shape
    bf16, f32 = jnp.bfloat16, jnp.float32
    per_group = width // GROUPS
    dp_count = lax.axis_size("dp")
    factor = 1.0 / math.sqrt(HEAD_DIM)
    sec = lax.axis_index("section")
    dp = lax.axis_index("dp")
    seq = lax.axis_index("seq")
    x, y = seq % 2, seq // 2
    sec0, x0 = sec == 0, x == 0
    row_frames = 4 * frames
    half_frames = 2 * frames
    both = ("section", "seq")

    block_width = width // 8
    rows_here = conv_weight.shape[0]
    conv_low = conv_weight.astype(bf16).reshape(rows_here, 8, block_width)
    bias_low = jnp.pad(conv_bias.astype(bf16), (0, block_width - conv_bias.shape[0]))
    bias_rows = jnp.pad(
        jnp.broadcast_to(bias_low[None, None, :], (1, 8, block_width)), ((0, 15), (0, 0), (0, 0))
    )
    conv_send = jnp.transpose(jnp.concatenate([conv_low, bias_rows], axis=0), (1, 0, 2))

    own_half = jnp.where(sec0, signal[:, :, : width // 2], signal[:, :, width // 2 :])
    sig_send = jnp.transpose(own_half.reshape(micro_count, frames, 4, block_width), (2, 0, 1, 3))
    in_rows = qkv_weight.shape[1]
    unit = down_weight.shape[1] // 4
    qkv_view = qkv_weight[0].astype(bf16).reshape(in_rows, -1, 2, HEAD_DIM)
    qkv_parity = [qkv_view[:, :, p].reshape(in_rows, -1) for p in range(2)]
    up_view = up_weight[0].astype(bf16).reshape(in_rows, -1, 2, 2, 2, unit)
    up_parity = [
        jnp.transpose(up_view[:, :, p], (0, 3, 1, 2, 4)).reshape(in_rows, -1) for p in range(2)
    ]
    qkv_cols, up_cols = qkv_parity[0].shape[1], up_parity[0].shape[1]
    col_one = to_column(norm1_gain[0].astype(bf16), 128)
    col_two = to_column(norm2_gain[0].astype(bf16), 128)
    cut = qkv_cols + 128
    keep_cols, send_cols = [
        jnp.concatenate([a, col_one, b, col_two], axis=1)
        for a, b in zip(choose(x0, *qkv_parity), choose(x0, *up_parity))
    ]
    out_low = out_weight[0].astype(bf16)
    down_low = down_weight[0].astype(bf16).reshape(2, 2, unit, width)
    rest = jnp.stack(
        [
            jnp.concatenate(
                [out_low[:, h * width // 2 : (h + 1) * width // 2], down_low[h, 0], down_low[h, 1]], axis=1
            )
            for h in range(2)
        ]
    )
    up_at = cut
    two_at = up_at + up_cols
    out_at = two_at + 128
    down_at = out_at + width // 2
    conv_all, sig_got, whole, second_piece = opening(conv_send, sig_send, keep_cols, send_cols, rest)
    gathered = [whole, gather_rows(second_piece)]
    sig_all = jnp.transpose(sig_got, (1, 0, 2, 3)).reshape(micro_count, row_frames, block_width)
    conv_all = conv_all.reshape(dp_count, 2, 4, rows_here + 16, block_width)
    conv_all = jnp.transpose(conv_all, (1, 0, 2, 3, 4))
    bias_all = conv_all[:, :, :, rows_here, : conv_bias.shape[0]].reshape(width)
    bias_own = lax.dynamic_slice_in_dim(bias_all, (sec * 4 + seq) * block_width, block_width, 0)
    kernel_own = conv_all[:, :, :, :rows_here].reshape(TAPS * per_group, block_width)
    bands = conv_bands(kernel_own, per_group)


    def views(whole):
        w_out = jnp.transpose(
            whole[:, out_at:down_at].reshape(-1, 2, in_rows, width // 2), (0, 2, 1, 3)
        ).reshape(-1, width)
        gain_one = whole[:, qkv_cols].astype(f32)[None, :]
        gain_two = whole[:, two_at].astype(f32)[None, :]
        w_up = [whole[:, up_at + part * width : up_at + (part + 1) * width] for part in range(2)]
        w_down = [whole[:, down_at + part * width : down_at + (part + 1) * width] for part in range(2)]
        return gain_one, whole[:, :qkv_cols], w_out, gain_two, w_up, w_down

    layer_weights = []

    picked = jnp.where(sec0, cotangent[0], cotangent[1])
    across = [(s * 4 + 2 * yy + xx, yy * 4 + 2 * s + xx) for s in range(2) for yy in range(2) for xx in range(2)]
    cot_own = lax.ppermute(picked, both, across)
    cot_other = swap_x(cot_own)
    cot_pair = choose(x0, cot_own, cot_other)
    top_grad = jnp.concatenate(cot_pair, axis=0).astype(f32)

    segment_row = jnp.where(y == 0, frame_segment_index[0], frame_segment_index[1])
    seg_pair = choose(sec0, segment_row[:half_frames], segment_row[half_frames:])
    query_segs = seg_pair[0]
    key_segs = jnp.concatenate(seg_pair)

    sig_views = group_view(sig_all, per_group)
    conv_pre = ungroup(conv_forward(sig_views, bands), per_group) + bias_own.astype(f32)
    stream = (sig_all.astype(f32) + smooth(conv_pre)).astype(bf16)
    slope = gelu_slope(conv_pre).astype(bf16)
    stream_send = stream.reshape(2, 2, half_frames, block_width)
    stream_send = jnp.transpose(stream_send, (1, 0, 2, 3))
    stream_send = jnp.repeat(stream_send.reshape(4, half_frames, block_width), 2, axis=0)
    stream_got = lax.all_to_all(stream_send, both, 0, 0, tiled=True)
    layer_in = jnp.transpose(stream_got, (1, 0, 2)).reshape(half_frames, width).astype(f32)

    chunks = 2
    rows = half_frames // chunks
    layer_in = [layer_in[c * rows : (c + 1) * rows] for c in range(chunks)]
    chunk_segs = [query_segs[c * rows : (c + 1) * rows] for c in range(chunks)]
    kept = []
    for layer in range(2):
        whole = gathered[layer]
        if layer:
            layer_in = []
            previous_lows[0], whole = after(previous_lows[0], whole)
        layer_weights.append(views(whole))
        gain_one, w_qkv, w_out, gain_two, w_up, w_down = layer_weights[layer]
        normed_one, packed, kv_own, kv_other = [], [], [], []
        for c in range(chunks):
            if layer:
                total = previous[c] + pair_sum(previous_lows[c], packed[-1] if c else None)
                layer_in.append(total.astype(bf16).astype(f32))
            centred, inv = norm_stats(layer_in[c])
            normed_one.append((centred * inv * gain_one).astype(bf16))
            packed.append(jnp.dot(normed_one[c], w_qkv, preferred_element_type=f32).astype(bf16))
            kv_own.append(packed[c][:, width // 2 :])
            kv_other.append(swap_section(kv_own[c]))
        kv_all = jnp.concatenate(kv_own + kv_other, axis=0)
        attended, lse, resid_two, normed_two, hidden, hidden_slope = [], [], [], [], [], []
        attn_lows, lows = [], []
        for c in range(chunks):
            own = packed[c]
            if c:
                attn_lows[-1], own = after(attn_lows[-1], own)
            mixed, log_total = attention_forward(own, kv_all, chunk_segs[c], key_segs, factor)
            attended.append(mixed)
            lse.append(log_total)
            attn_lows.append(jnp.dot(mixed, w_out, preferred_element_type=f32).astype(bf16))
        for c in range(chunks):
            resid_two.append(layer_in[c] + pair_sum(attn_lows[c], lows[-1] if c else None))
            centred, inv = norm_stats(resid_two[c])
            normed_two.append((centred * inv * gain_two).astype(bf16))
            down_sum, own_hidden, own_slope = None, [], []
            for part in range(2):
                hidden_pre = jnp.dot(normed_two[c], w_up[part], preferred_element_type=f32)
                own_hidden.append(smooth(hidden_pre).astype(bf16))
                own_slope.append(gelu_slope(hidden_pre).astype(bf16))
            for part in range(2):
                term = jnp.dot(own_hidden[part], w_down[part], preferred_element_type=f32)
                down_sum = term if down_sum is None else down_sum + term
            hidden.append(own_hidden)
            hidden_slope.append(own_slope)
            lows.append(down_sum.astype(bf16))

        resid_two_last = resid_two
        kept.append((layer_in, normed_one, packed, kv_all, attended, lse, resid_two, normed_two, hidden, hidden_slope))
        previous, previous_lows = resid_two, lows

    def outer(left, right):
        return lax.dot_general(
            left, right, (((0,), (0,)), ((), ())), preferred_element_type=f32
        ).astype(bf16)

    def back(left, right):
        return lax.dot_general(left, right, (((1,), (1,)), ((), ())), preferred_element_type=f32)

    grad_out = [top_grad[c * rows : (c + 1) * rows] for c in range(chunks)]
    attn_members, scattered = [], []
    for layer in (1, 0):
        gain_one, w_qkv, w_out, gain_two, w_up, w_down = layer_weights[layer]
        (layer_in, normed_one, packed, kv_all, attended, lse, resid_two, normed_two, hidden, hidden_slope) = kept[layer]
        branch = [member.astype(bf16) for member in grad_out]
        pre_grad, sums, low = [], [], None
        for c in range(chunks):
            own = branch[c]
            if low is not None:
                low, own = after(low, own)
                sums.append(pair_sum(low))
            own_pre, part_sum = [], None
            for part in range(2):
                own_pre.append((back(own, w_down[part]) * hidden_slope[c][part].astype(f32)).astype(bf16))
            for part in range(2):
                term = back(own_pre[part], w_up[part])
                part_sum = term if part_sum is None else part_sum + term
            pre_grad.append(own_pre)
            low = part_sum.astype(bf16)
        sums.append(pair_sum(low))
        whole_pre = [jnp.concatenate([pre_grad[c][p] for c in range(chunks)]) for p in range(2)]
        whole_hidden = [jnp.concatenate([hidden[c][p] for c in range(chunks)]) for p in range(2)]
        whole_branch, whole_two = jnp.concatenate(branch), jnp.concatenate(normed_two)
        ff_members = [
            outer(whole_two, whole_pre[0]), outer(whole_two, whole_pre[1]),
            outer(whole_hidden[0], whole_branch), outer(whole_hidden[1], whole_branch),
        ]
        if layer == 1:
            ff_members.append(jnp.zeros((width, 128), bf16))
        partial = jnp.concatenate(attn_members + ff_members, axis=1)
        if layer == 0:
            sums, (partial, output_rows) = after(sums, (partial, output_rows))
        scattered.append(scatter_rows(partial))
        resid_grad, attn_branch, dq, gain_two_grad = [], [], [], None
        dkv = None
        for c in range(chunks):
            in_part, gain_part = norm_back(resid_two[c], gain_two, sums[c])
            gain_two_grad = gain_part if gain_two_grad is None else gain_two_grad + gain_part
            resid_grad.append(in_part + grad_out[c])
            attn_branch.append(resid_grad[c].astype(bf16))
            attended_grad = back(attn_branch[c], w_out).astype(bf16)
            if layer == 1 and c == 0:
                attended_grad, lows = after(attended_grad, lows)
                output = [member + pair_sum(low) for member, low in zip(resid_two_last, lows)]
                row_block = lax.ppermute(jnp.where(x0, output[0], output[1]), both, across)
                output_rows = jnp.stack(choose(sec0, row_block, swap_section(row_block)))
            own_dq, *dkv = attention_backward(
                packed[c], kv_all, attended_grad, attended[c], lse[c], chunk_segs[c], key_segs, factor,
                None if c == 0 else dkv,
            )
            dq.append(own_dq)
        if layer == 0:
            dkv, scattered[0] = after(dkv, scattered[0])
        else:
            dkv, output = after(dkv, output)
        dkv = jnp.concatenate(dkv, axis=1)
        other_dkv = swap_section(dkv[half_frames:].astype(bf16))
        dkv_own = (dkv[:half_frames] + other_dkv.astype(f32)).astype(bf16)
        packed_grad, sums, low = [], [], None
        for c in range(chunks):
            packed_grad.append(jnp.concatenate([dq[c], dkv_own[c * rows : (c + 1) * rows]], axis=1))
            own = packed_grad[c]
            if low is not None:
                low, own = after(low, own)
                sums.append(pair_sum(low))
            low = back(own, w_qkv).astype(bf16)
        sums.append(pair_sum(low))
        next_grad, gain_one_grad = [], None
        for c in range(chunks):
            in_part, gain_part = norm_back(layer_in[c], gain_one, sums[c])
            gain_one_grad = gain_part if gain_one_grad is None else gain_one_grad + gain_part
            next_grad.append((resid_grad[c] + in_part).astype(bf16))
        whole_one, whole_pg, whole_att, whole_ab = [
            jnp.concatenate(m) for m in (normed_one, packed_grad, attended, attn_branch)
        ]
        grad_out_weight = jnp.transpose(
            outer(whole_att, whole_ab).reshape(-1, in_rows, 2, width // 2), (0, 2, 1, 3)
        ).reshape(-1, width // 2)
        gain_grads = jnp.stack([gain_one_grad, gain_two_grad], axis=1).astype(bf16)
        gain_grads = jnp.pad(gain_grads, ((0, 0), (0, 126)))
        attn_members = [outer(whole_one, whole_pg), gain_grads, grad_out_weight]
        grad_out = [member.astype(f32) for member in next_grad]
    grad_in_low = jnp.concatenate(next_grad)
    scattered.append(scatter_rows(jnp.concatenate(attn_members, axis=1)))

    lig_send = jnp.transpose(grad_in_low.reshape(half_frames, 8, block_width), (1, 0, 2))
    lig_got = lax.all_to_all(lig_send, both, 0, 0, tiled=True).reshape(2, 2, 2, half_frames, block_width)
    lig = jnp.transpose(lig_got[:, :, 0], (1, 0, 2, 3)).reshape(micro_count, row_frames, block_width)
    conv_grad = (lig.astype(f32) * slope.astype(f32)).astype(bf16)
    grad_views = group_view(conv_grad, per_group)
    back = ungroup(conv_back(grad_views, bands), per_group)
    grad_signal = (lig.astype(f32) + back).astype(bf16)
    gs_send = jnp.transpose(
        grad_signal.reshape(micro_count, 4, frames, block_width), (1, 0, 2, 3)
    )
    gs_send = jnp.concatenate([gs_send, gs_send], axis=0)
    taps_grad = conv_taps_grad(sig_views, grad_views, per_group)
    bias_grad = jnp.sum(conv_grad.astype(f32), axis=(0, 1))
    taps_view = jnp.transpose(
        taps_grad.reshape(2, dp_count, 4, rows_here, block_width), (1, 0, 2, 3, 4)
    ).astype(bf16)
    bias_view = jnp.pad(
        jnp.broadcast_to(bias_grad.astype(bf16), (dp_count, 2, 4, 1, block_width)),
        ((0, 0), (0, 0), (0, 0), (0, 15), (0, 0)),
    )
    taps_send = jnp.concatenate([taps_view, bias_view], axis=3)
    gs_got = lax.all_to_all(gs_send, both, 0, 0, tiled=True)
    attn_cols = cut + width // 2

    def over_section(first, second):
        keep, send = choose(sec0, first, second)
        return choose(sec0, keep, swap_section(send))


    taps_sum, (_, gs_got) = sum_dp(taps_send, dp, (gs_send, gs_got))
    gs_rows = jnp.transpose(gs_got, (1, 2, 0, 3)).reshape(micro_count, frames, width).astype(f32)
    ends = jnp.where(sec0, gs_rows, output_rows)[None]
    taps_got = lax.all_to_all(
        taps_sum.reshape(8, rows_here + 16, block_width), both, 0, 0, tiled=True
    )
    taps_got, scattered[1] = after(taps_got, scattered[1])
    conv_weight_grad = jnp.transpose(taps_got[:, :rows_here], (1, 0, 2)).reshape(rows_here, width).astype(f32)
    bias_count = conv_bias.shape[0]
    conv_bias_grad = lax.dynamic_slice_in_dim(
        taps_got[:, rows_here].reshape(width),
        ((sec * dp_count + dp) * 4 + seq) * bias_count,
        bias_count,
        0,
    ).astype(f32)

    turned = [(t * 4 + 2 * r + c, c * 4 + 2 * r + t) for t in range(2) for r in range(2) for c in range(2) if t != c]
    crossed = [(t * 4 + 2 * r + c, (1 - c) * 4 + 2 * r + t) for t in range(2) for r in range(2) for c in range(2)]

    def home(first, second):
        straight, other = choose(x0, first, second)
        straight = jnp.where(sec == x, straight, lax.ppermute(straight, both, turned))
        other = lax.ppermute(other, both, crossed)
        return choose(sec0, straight, other)

    ff_layers = (scattered[1][:, attn_cols:], scattered[0][:, :-128])
    ff_sets = over_section(*(member[:, up_cols:] for member in ff_layers))
    down_grad = jnp.concatenate(
        [member[:, at : at + width] for member in ff_sets for at in (0, width)], axis=0
    ).astype(f32)[None]
    up_grad = jnp.stack(
        [
            jnp.transpose(member.reshape(in_rows, 2, -1, 2, unit), (0, 2, 3, 1, 4))
            for member in home(*(member[:, :up_cols] for member in ff_layers))
        ],
        axis=2,
    ).reshape(in_rows, -1).astype(f32)[None]
    scattered[2], (up_grad, down_grad) = after(scattered[2], (up_grad, down_grad))
    attn_layers = (scattered[2], scattered[1][:, :attn_cols])
    attn_sets = over_section(*(member[:, cut:] for member in attn_layers))
    out_grad = jnp.concatenate(attn_sets, axis=1).astype(f32)[None]
    qkv_sets = home(*(member[:, :cut] for member in attn_layers))
    norm1_grad = qkv_sets[0][:, qkv_cols].astype(f32)[None]
    norm2_grad = qkv_sets[0][:, qkv_cols + 1].astype(f32)[None]
    qkv_grad = jnp.stack(
        [member[:, :qkv_cols].reshape(in_rows, -1, HEAD_DIM) for member in qkv_sets], axis=2
    ).reshape(in_rows, -1).astype(f32)[None]
    return (ends, conv_weight_grad, conv_bias_grad, norm1_grad, qkv_grad, out_grad, norm2_grad, up_grad, down_grad)


def solution(mesh):
    placed = (
        P("dp", "seq", None),
        P("dp", None),
        P(("section", "dp", "seq"), None),
        P(("section", "dp", "seq")),
        P("section", ("dp", "seq")),
        P("section", ("dp", "seq"), None),
        P("section", ("dp", "seq"), None),
        P("section", ("dp", "seq")),
        P("section", ("dp", "seq"), None),
        P("section", ("dp", "seq"), None),
        P("dp", "seq", None),
    )

    def step(*arrays):
        pairs = mesh.shape["seq"] == 4 and mesh.shape["section"] == 2 and arrays[0].shape[0] == 2
        return (per_device_pairs if pairs else per_device)(*arrays)

    return jax.shard_map(
        step,
        mesh=mesh,
        in_specs=placed,
        out_specs=(
            P("section", "dp", "seq", None),
            P(("section", "dp", "seq"), None),
            P(("section", "dp", "seq")),
            P("section", ("dp", "seq")),
            P("section", ("dp", "seq"), None),
            P("section", ("dp", "seq"), None),
            P("section", ("dp", "seq")),
            P("section", ("dp", "seq"), None),
            P("section", ("dp", "seq"), None),
        ),
        check_vma=False,
    )
```

```python
import functools
import math

import jax
import jax.numpy as jnp
from jax import lax
from jax.experimental import pallas as pl
from jax.experimental.pallas import tpu as pltpu
from jax.sharding import PartitionSpec as P

HEAD_DIM = 64
GROUPS = 16
TAPS = 128


EPS = 1e-05
NEG = -1e30


def padded_2(block, sides, width):
    for axis, dim in sides:
        count = lax.axis_size(axis)
        forward = [(i, i + 1) for i in range(count - 1)]
        backward = [(target, source) for source, target in forward]
        low = lax.ppermute(
            lax.slice_in_dim(block, block.shape[dim] - width, None, axis=dim), axis, forward
        )
        high = lax.ppermute(lax.slice_in_dim(block, 0, width, axis=dim), axis, backward)
        block = jnp.concatenate([low, block, high], axis=dim)
    return block


def from_behind(value, axis, steps):
    count = lax.axis_size(axis)
    first, last = (max(0, -steps), min(count, count - steps))
    return lax.ppermute(value, axis, [(source, source + steps) for source in range(first, last)])


def normalize(values, gain):
    average = jnp.mean(values, axis=-1, keepdims=True)
    centred = values - average
    spread = jnp.mean(centred * centred, axis=-1, keepdims=True)
    return centred * lax.rsqrt(spread + EPS) * gain


def smooth(values):
    return jax.nn.gelu(values, approximate=False)


def conv_taps(padded, kernel, frames):
    width_all = padded.shape[1]
    per_group = width_all // GROUPS
    tap_step = math.gcd(TAPS, 16)
    weight_view = kernel.reshape(TAPS, per_group, GROUPS, per_group)
    running = jnp.zeros((frames, GROUPS, per_group), jnp.float32)
    for first_tap in range(0, TAPS, tap_step):
        windows = jnp.stack(
            [padded[first_tap + offset : first_tap + offset + frames] for offset in range(tap_step)]
        )
        windows = windows.reshape(tap_step, frames, GROUPS, per_group)
        running = running + jnp.einsum(
            "jtgc,jcgo->tgo",
            windows,
            weight_view[first_tap : first_tap + tap_step],
            preferred_element_type=jnp.float32,
        )
    return running.reshape(frames, width_all)


def conv_input_grad(grad_pad, kernel, frames):
    width_all = grad_pad.shape[1]
    per_group = width_all // GROUPS
    tap_step = math.gcd(TAPS, 16)
    weight_view = kernel.reshape(TAPS, per_group, GROUPS, per_group)
    running = jnp.zeros((frames, GROUPS, per_group), jnp.float32)
    for first_tap in range(0, TAPS, tap_step):
        back_windows = jnp.stack(
            [
                grad_pad[TAPS - first_tap - offset : TAPS - first_tap - offset + frames]
                for offset in range(tap_step)
            ]
        )
        back_windows = back_windows.reshape(tap_step, frames, GROUPS, per_group)
        running = running + jnp.einsum(
            "jtgo,jcgo->tgc",
            back_windows,
            weight_view[first_tap : first_tap + tap_step],
            preferred_element_type=jnp.float32,
        )
    return running.reshape(frames, width_all)


def conv_kernel_grad(padded_all, grad_all):
    step_count, frames, width_all = grad_all.shape
    per_group = width_all // GROUPS
    tap_step = math.gcd(TAPS, 16)
    grad_view = grad_all.reshape(step_count * frames, GROUPS, per_group)
    kernel_parts = []
    for first_tap in range(0, TAPS, tap_step):
        windows = jnp.stack(
            [
                padded_all[:, first_tap + offset : first_tap + offset + frames]
                for offset in range(tap_step)
            ]
        )
        windows = windows.reshape(tap_step, step_count * frames, GROUPS, per_group)
        kernel_parts.append(
            jnp.einsum("jtgc,tgo->jcgo", windows, grad_view, preferred_element_type=jnp.float32)
        )
    return jnp.concatenate(kernel_parts, axis=0).reshape(TAPS * per_group, width_all)


def score_block(query_heads, key_block, query_segs, key_segs, factor):
    scores = (
        jnp.einsum("qhd,khd->hqk", query_heads, key_block, preferred_element_type=jnp.float32)
        * factor
    )
    allowed = (query_segs[:, None] == key_segs[None, :])[None]
    return (scores, allowed)


def front(layer_in, weights, kernel, conv_shift, first_section):
    frames, width_all = layer_in.shape
    padded = padded_2(layer_in, (("seq", 0),), TAPS // 2)
    conv_pre = lax.cond(
        first_section,
        lambda: conv_taps(padded, kernel, frames) + conv_shift.astype(jnp.float32),
        lambda: jnp.zeros((frames, width_all), jnp.float32),
    )
    conv_val, conv_pull = jax.vjp(smooth, conv_pre)
    resid_one = layer_in.astype(jnp.float32) + conv_val
    normed_val, norm_pull = jax.vjp(normalize, resid_one, weights[0].astype(jnp.float32))
    normed_one = normed_val.astype(jnp.bfloat16)
    packed = jnp.dot(normed_one, weights[1], preferred_element_type=jnp.float32).astype(
        jnp.bfloat16
    )
    return (padded, conv_pull, resid_one, norm_pull, normed_one, packed)


def tail(resid_one, attn_low, weights):
    resid_two = resid_one + jnp.dot(attn_low, weights[2], preferred_element_type=jnp.float32)
    normed_val, norm_pull = jax.vjp(normalize, resid_two, weights[3].astype(jnp.float32))
    normed_two = normed_val.astype(jnp.bfloat16)
    hidden_pre = jnp.dot(normed_two, weights[4], preferred_element_type=jnp.float32)
    hidden_val, gelu_pull = jax.vjp(smooth, hidden_pre)
    hidden_low = hidden_val.astype(jnp.bfloat16)
    result = resid_two + jnp.dot(hidden_low, weights[5], preferred_element_type=jnp.float32)
    return (result, norm_pull, normed_two, gelu_pull, hidden_low)


def key_loop(keys_all, values_all, segment_row, head_count, visit, initial):
    total_rows = keys_all.shape[0]
    block_rows = math.gcd(total_rows, 512)

    def one_block(block_index, running):
        offset = block_index * block_rows
        key_block = lax.dynamic_slice_in_dim(keys_all, offset, block_rows, 0).reshape(
            block_rows, head_count, HEAD_DIM
        )
        value_block = lax.dynamic_slice_in_dim(values_all, offset, block_rows, 0).reshape(
            block_rows, head_count, HEAD_DIM
        )
        key_segs = lax.dynamic_slice_in_dim(segment_row, offset, block_rows, 0)
        return visit(running, key_block, value_block, key_segs)

    return lax.fori_loop(0, total_rows // block_rows, one_block, initial)


def layer_forward(
    layer_in, segment_row, weights, kernel, conv_shift, first_section, my_start, factor
):
    frames, width_all = layer_in.shape
    head_count = width_all // HEAD_DIM
    padded, conv_pull, resid_one, norm_pull, normed_one, packed = front(
        layer_in, weights, kernel, conv_shift, first_section
    )
    query_heads = packed[:, :width_all].reshape(frames, head_count, HEAD_DIM)
    query_segs = lax.dynamic_slice_in_dim(segment_row, my_start, frames, 0)
    initial = (
        jnp.full((head_count, frames), NEG, jnp.float32),
        jnp.zeros((head_count, frames), jnp.float32),
        jnp.zeros((head_count, frames, HEAD_DIM), jnp.float32),
    )
    key_piece = lax.all_gather(packed[:, width_all : 2 * width_all], "seq", axis=0, tiled=True)
    value_piece = lax.all_gather(packed[:, 2 * width_all :], "seq", axis=0, tiled=True)
    piece_rows = key_piece.shape[0]
    block_rows = math.gcd(piece_rows, 512)

    def one_block(block_index, running):
        run_max, run_sum, run_acc = running
        offset = block_index * block_rows
        key_block = lax.dynamic_slice_in_dim(key_piece, offset, block_rows, 0).reshape(
            block_rows, head_count, HEAD_DIM
        )
        value_block = lax.dynamic_slice_in_dim(value_piece, offset, block_rows, 0).reshape(
            block_rows, head_count, HEAD_DIM
        )
        key_segs = lax.dynamic_slice_in_dim(segment_row, offset, block_rows, 0)
        scores, allowed = score_block(query_heads, key_block, query_segs, key_segs, factor)
        masked = jnp.where(allowed, scores, NEG)
        new_max = jnp.maximum(run_max, jnp.max(masked, axis=-1))
        weights_now = jnp.where(allowed, jnp.exp(masked - new_max[..., None]), 0.0)
        rescale = jnp.exp(run_max - new_max)
        run_sum = run_sum * rescale + jnp.sum(weights_now, axis=-1)
        run_acc = run_acc * rescale[..., None] + jnp.einsum(
            "hqk,khd->hqd",
            weights_now.astype(jnp.bfloat16),
            value_block,
            preferred_element_type=jnp.float32,
        )
        return (new_max, run_sum, run_acc)

    run_max, run_sum, run_acc = lax.fori_loop(0, piece_rows // block_rows, one_block, initial)
    log_total = run_max + jnp.log(run_sum)
    mixture = run_acc / run_sum[..., None]
    attn_low = jnp.transpose(mixture, (1, 0, 2)).reshape(frames, width_all).astype(jnp.bfloat16)
    result, norm_two_pull, normed_two, gelu_pull, hidden_low = tail(resid_one, attn_low, weights)
    kept = (
        padded,
        conv_pull,
        norm_pull,
        normed_one,
        packed,
        log_total,
        mixture,
        attn_low,
        norm_two_pull,
        normed_two,
        gelu_pull,
        hidden_low,
        segment_row,
    )
    return (result, kept)


def layer_backward(kept, grad_out, weights, kernel, first_section, my_start, factor):
    (
        padded,
        conv_pull,
        norm_one_pull,
        normed_one,
        packed,
        log_total,
        mixture,
        attn_low,
        norm_two_pull,
        normed_two,
        gelu_pull,
        hidden_low,
        segment_row,
    ) = kept
    frames, width_all = normed_one.shape
    head_count = width_all // HEAD_DIM
    query_heads = packed[:, :width_all].reshape(frames, head_count, HEAD_DIM)
    key_local = packed[:, width_all : 2 * width_all]
    value_local = packed[:, 2 * width_all :]
    query_segs = lax.dynamic_slice_in_dim(segment_row, my_start, frames, 0)
    keys_all, values_all = (
        lax.all_gather(key_local, "seq", axis=0, tiled=True),
        lax.all_gather(value_local, "seq", axis=0, tiled=True),
    )

    def chances_for(key_block, key_segs):
        scores, allowed = score_block(query_heads, key_block, query_segs, key_segs, factor)
        return jnp.where(
            allowed, jnp.exp(jnp.where(allowed, scores, NEG) - log_total[..., None]), 0.0
        )

    branch_grad = grad_out.astype(jnp.bfloat16)
    hidden_grad = jnp.einsum(
        "to,io->ti", branch_grad, weights[5], preferred_element_type=jnp.float32
    )
    pre_grad = gelu_pull(hidden_grad)[0].astype(jnp.bfloat16)
    normed_two_grad = jnp.einsum(
        "tf,if->ti", pre_grad, weights[4], preferred_element_type=jnp.float32
    )
    resid_two_grad, grad_gain_two = norm_two_pull(normed_two_grad)
    resid_two_grad = resid_two_grad + grad_out
    attn_branch_grad = resid_two_grad.astype(jnp.bfloat16)
    attended_grad = jnp.einsum(
        "to,io->ti", attn_branch_grad, weights[2], preferred_element_type=jnp.float32
    ).astype(jnp.bfloat16)
    dout_heads = attended_grad.reshape(frames, head_count, HEAD_DIM)
    delta_rows = jnp.einsum("qhd,hqd->hq", dout_heads.astype(jnp.float32), mixture)

    def visit_query(running, key_block, value_block, key_segs):
        chances = chances_for(key_block, key_segs)
        prob_grad = jnp.einsum(
            "qhd,khd->hqk", dout_heads, value_block, preferred_element_type=jnp.float32
        )
        score_grad = (chances * (prob_grad - delta_rows[..., None])).astype(jnp.bfloat16)
        return running + jnp.einsum(
            "hqk,khd->qhd", score_grad, key_block, preferred_element_type=jnp.float32
        )

    grad_query = (
        key_loop(
            keys_all,
            values_all,
            segment_row,
            head_count,
            visit_query,
            jnp.zeros((frames, head_count, HEAD_DIM), jnp.float32),
        )
        * factor
    )
    row_stats = (
        lax.all_gather(log_total, "seq", axis=1, tiled=True),
        lax.all_gather(delta_rows, "seq", axis=1, tiled=True),
    )
    key_heads = key_local.reshape(frames, head_count, HEAD_DIM)
    value_heads = value_local.reshape(frames, head_count, HEAD_DIM)
    start_acc = (
        jnp.zeros((frames, head_count, HEAD_DIM), jnp.float32),
        jnp.zeros((frames, head_count, HEAD_DIM), jnp.float32),
    )
    query_piece = lax.all_gather(packed[:, :width_all], "seq", axis=0, tiled=True)
    dout_piece = lax.all_gather(attended_grad, "seq", axis=0, tiled=True)
    piece_rows = query_piece.shape[0]
    block_rows = math.gcd(piece_rows, 512)

    def one_block(block_index, running):
        key_acc, value_acc = running
        offset = block_index * block_rows
        query_block = lax.dynamic_slice_in_dim(query_piece, offset, block_rows, 0).reshape(
            block_rows, head_count, HEAD_DIM
        )
        dout_block = lax.dynamic_slice_in_dim(dout_piece, offset, block_rows, 0).reshape(
            block_rows, head_count, HEAD_DIM
        )
        seg_block = lax.dynamic_slice_in_dim(segment_row, offset, block_rows, 0)
        total_block = lax.dynamic_slice_in_dim(row_stats[0], offset, block_rows, 1)
        delta_block = lax.dynamic_slice_in_dim(row_stats[1], offset, block_rows, 1)
        scores, allowed = score_block(query_block, key_heads, seg_block, query_segs, factor)
        chances = jnp.where(
            allowed, jnp.exp(jnp.where(allowed, scores, NEG) - total_block[..., None]), 0.0
        )
        prob_grad = jnp.einsum(
            "qhd,khd->hqk", dout_block, value_heads, preferred_element_type=jnp.float32
        )
        score_grad = (chances * (prob_grad - delta_block[..., None])).astype(jnp.bfloat16)
        key_acc = (
            key_acc
            + jnp.einsum(
                "hqk,qhd->khd", score_grad, query_block, preferred_element_type=jnp.float32
            )
            * factor
        )
        value_acc = value_acc + jnp.einsum(
            "hqk,qhd->khd",
            chances.astype(jnp.bfloat16),
            dout_block,
            preferred_element_type=jnp.float32,
        )
        return (key_acc, value_acc)

    key_acc, value_acc = lax.fori_loop(0, piece_rows // block_rows, one_block, start_acc)
    grad_key = key_acc.reshape(frames, width_all)
    grad_value = value_acc.reshape(frames, width_all)
    packed_grad = jnp.concatenate(
        [grad_query.reshape(frames, width_all), grad_key, grad_value], axis=1
    ).astype(jnp.bfloat16)
    normed_one_grad = jnp.einsum(
        "tj,ij->ti", packed_grad, weights[1], preferred_element_type=jnp.float32
    )
    resid_one_grad, grad_gain_one = norm_one_pull(normed_one_grad)
    resid_one_grad = resid_one_grad + resid_two_grad
    conv_grad = jnp.where(first_section, conv_pull(resid_one_grad)[0], 0.0).astype(jnp.bfloat16)
    grad_pad = padded_2(conv_grad, (("seq", 0),), TAPS // 2)
    back_sum = lax.cond(
        first_section,
        lambda: conv_input_grad(grad_pad, kernel, frames),
        lambda: jnp.zeros((frames, width_all), jnp.float32),
    )
    grad_in = resid_one_grad + back_sum
    products = (
        normed_one,
        packed_grad,
        attn_low,
        attn_branch_grad,
        normed_two,
        pre_grad,
        hidden_low,
        branch_grad,
        padded,
        conv_grad,
    )
    return (grad_in, (grad_gain_one, grad_gain_two), products)


def per_device(
    signal,
    frame_segment_index,
    conv_weight,
    conv_bias,
    norm1_gain,
    qkv_weight,
    out_weight,
    norm2_gain,
    up_weight,
    down_weight,
    cotangent,
):
    micro_count, frames, width_all = signal.shape
    factor = 1.0 / math.sqrt(HEAD_DIM)
    first_section = lax.axis_index("section") == 0
    my_start = lax.axis_index("seq") * frames
    gathered = (
        lax.all_gather(norm1_gain.astype(jnp.bfloat16), ("dp", "seq"), axis=1, tiled=True),
        lax.all_gather(qkv_weight.astype(jnp.bfloat16), ("dp", "seq"), axis=1, tiled=True),
        lax.all_gather(out_weight.astype(jnp.bfloat16), ("dp", "seq"), axis=1, tiled=True),
        lax.all_gather(norm2_gain.astype(jnp.bfloat16), ("dp", "seq"), axis=1, tiled=True),
        lax.all_gather(up_weight.astype(jnp.bfloat16), ("dp", "seq"), axis=1, tiled=True),
        lax.all_gather(down_weight.astype(jnp.bfloat16), ("dp", "seq"), axis=1, tiled=True),
    )
    weights = tuple((member[0] for member in gathered))
    kernel, conv_shift = (
        lax.all_gather(
            conv_weight.astype(jnp.bfloat16), ("section", "dp", "seq"), axis=0, tiled=True
        ),
        lax.all_gather(
            conv_bias.astype(jnp.bfloat16), ("section", "dp", "seq"), axis=0, tiled=True
        ),
    )
    received = jnp.zeros((frames, width_all), jnp.bfloat16)
    saved = []
    forward_outs = []
    for step_index in range(micro_count + 1):
        own_index = min(step_index, micro_count - 1)
        prior_index = max(step_index - 1, 0)
        layer_in = jnp.where(first_section, signal[own_index], received)
        segment_row = jnp.where(
            first_section, frame_segment_index[own_index], frame_segment_index[prior_index]
        )
        result, kept = layer_forward(
            layer_in, segment_row, weights, kernel, conv_shift, first_section, my_start, factor
        )
        saved.append(kept)
        forward_outs.append(result)
        if step_index < micro_count:
            received = from_behind(result.astype(jnp.bfloat16), "section", 1)
    received_back = jnp.zeros((frames, width_all), jnp.bfloat16)
    input_grads = []
    gain_totals = None
    product_list = []
    for step_index in range(micro_count + 1):
        kept = saved[micro_count - step_index]
        if step_index < micro_count:
            top_grad = cotangent[micro_count - 1 - step_index].astype(jnp.float32)
        else:
            top_grad = jnp.zeros((frames, width_all), jnp.float32)
        incoming = jnp.where(first_section, received_back.astype(jnp.float32), top_grad)
        grad_in, gain_grads, products = layer_backward(
            kept, incoming, weights, kernel, first_section, my_start, factor
        )
        input_grads.append(grad_in)
        product_list.append(products)
        if gain_totals is None:
            gain_totals = gain_grads
        else:
            gain_totals = (gain_totals[0] + gain_grads[0], gain_totals[1] + gain_grads[1])
        if step_index < micro_count:
            received_back = from_behind(grad_in.astype(jnp.bfloat16), "section", -1)

    def joined(position):
        return jnp.concatenate([member[position] for member in product_list], axis=0)

    grad_qkv = jnp.einsum("ti,tj->ij", joined(0), joined(1), preferred_element_type=jnp.float32)
    grad_out_weight = jnp.einsum(
        "ti,to->io", joined(2), joined(3), preferred_element_type=jnp.float32
    )
    grad_up = jnp.einsum("ti,tf->if", joined(4), joined(5), preferred_element_type=jnp.float32)
    grad_down = jnp.einsum("ti,to->io", joined(6), joined(7), preferred_element_type=jnp.float32)
    padded_all = jnp.stack([member[8] for member in product_list])
    conv_grad_all = jnp.stack([member[9] for member in product_list])
    kernel_grad = conv_kernel_grad(padded_all, conv_grad_all)
    bias_grad = jnp.sum(joined(9).astype(jnp.float32), axis=0)
    ends = jnp.stack(
        [
            jnp.where(
                first_section, input_grads[micro_count - mb_index], forward_outs[mb_index + 1]
            )
            for mb_index in range(micro_count)
        ]
    )[None]
    layer_sums = (
        lax.psum_scatter(gain_totals[0][None], ("dp", "seq"), scatter_dimension=1, tiled=True),
        lax.psum_scatter(grad_qkv[None], ("dp", "seq"), scatter_dimension=1, tiled=True),
        lax.psum_scatter(grad_out_weight[None], ("dp", "seq"), scatter_dimension=1, tiled=True),
        lax.psum_scatter(gain_totals[1][None], ("dp", "seq"), scatter_dimension=1, tiled=True),
        lax.psum_scatter(grad_up[None], ("dp", "seq"), scatter_dimension=1, tiled=True),
        lax.psum_scatter(grad_down[None], ("dp", "seq"), scatter_dimension=1, tiled=True),
    )
    conv_sums = (
        lax.psum_scatter(kernel_grad, ("section", "dp", "seq"), scatter_dimension=0, tiled=True),
        lax.psum_scatter(bias_grad, ("section", "dp", "seq"), scatter_dimension=0, tiled=True),
    )
    return (
        ends,
        conv_sums[0],
        conv_sums[1],
        layer_sums[0],
        layer_sums[1],
        layer_sums[2],
        layer_sums[3],
        layer_sums[4],
        layer_sums[5],
    )


def swap_section(value):
    return lax.ppermute(value, "section", [(0, 1), (1, 0)])


def swap_x(value):
    return lax.ppermute(value, "seq", [(q, q ^ 1) for q in range(4)])


def pair_sum(low, behind=None):
    other = swap_x(low)
    if behind is not None:
        other, _ = lax.optimization_barrier((other, behind))
    return low.astype(jnp.float32) + other.astype(jnp.float32)


def after(first, second):
    return lax.optimization_barrier((first, second))


def choose(flag, first, second):
    return jnp.where(flag, first, second), jnp.where(flag, second, first)


def sum_dp(blocks, dp, meanwhile):
    count = lax.axis_size("dp")
    f32, bf16 = jnp.float32, jnp.bfloat16
    meanwhile = list(meanwhile)

    def block(index):
        return lax.dynamic_index_in_dim(blocks, jnp.clip(index, 0, count - 1), 0, keepdims=False)

    running = [None, None]
    for turn, distance in enumerate(range(count - 1, 0, -1)):
        for way, sign in enumerate((1, -1)):
            own = block(dp + sign * distance)
            if running[way] is not None:
                own = (own.astype(f32) + running[way].astype(f32)).astype(bf16)
            live = [(i, i + sign) for i in range(count) if 0 <= i + sign < count and 0 <= i + sign * distance < count]
            running[way] = lax.ppermute(own, "dp", live)
        if turn < len(meanwhile):
            running, meanwhile[turn] = after(running, meanwhile[turn])
            running = list(running)
    total = block(dp).astype(f32) + running[0].astype(f32) + running[1].astype(f32)
    return total.astype(bf16), meanwhile


def line_groups():
    count = lax.axis_size("dp")
    return [
        [(s * count + d) * 4 + 2 * y + x for d in range(count) for y in range(2) for s in range(2)]
        for x in range(2)
    ]


def gather_rows(piece):
    return lax.all_gather(
        piece, ("section", "dp", "seq"), axis=0, tiled=True, axis_index_groups=line_groups()
    )


def scatter_rows(partial):
    return lax.psum_scatter(
        partial, ("section", "dp", "seq"), scatter_dimension=0, tiled=True,
        axis_index_groups=line_groups(),
    )


MESH = pl.DeviceIdType.MESH


def opening_kernel(
    dp_count, parts, conv_ref, signal_ref, keep_ref, send_ref, rest_ref,
    conv_out, signal_out, whole_out, second_out,
    local_sem, a2a_send, a2a_recv, sig_send, sig_recv, line_send, line_recv, own_send, column_recv, rest_recv,
    up_send, up_recv, y_send, y_recv, core_send, core_recv,
):
    sec, dp, seq = (lax.axis_index(name) for name in ("section", "dp", "seq"))
    me = sec * 4 + seq
    x, y = seq % 2, seq // 2
    partner_x = (seq + 1 - 2 * x) % 4
    partner_y = {"seq": (seq + 2) % 4}
    sibling = {"section": 1 - sec}
    has_up, has_down = dp < dp_count - 1, dp > 0
    split = keep_ref.shape[1]
    rows = keep_ref.shape[0] // parts

    barrier = pltpu.get_barrier_semaphore()
    for turn in range(1, 8):
        other = (me + turn) % 8
        pl.semaphore_signal(
            barrier, inc=1, device_id={"section": other // 4, "seq": other % 4}, device_id_type=MESH
        )
    for there, step in ((has_up, 1), (has_down, -1)):

        @pl.when(there)
        def _(step=step):
            pl.semaphore_signal(barrier, inc=1, device_id={"dp": dp + step}, device_id_type=MESH)

    pl.semaphore_wait(barrier, 7 + jnp.where(has_up, 1, 0) + jnp.where(has_down, 1, 0))

    def remote(source, target, send, recv, device):
        return pltpu.make_async_remote_copy(
            src_ref=source, dst_ref=target, send_sem=send, recv_sem=recv,
            device_id=device, device_id_type=MESH,
        )

    def a2a(target, source):
        return remote(
            conv_ref.at[target], conv_out.at[dp, source], a2a_send.at[target], a2a_recv.at[source],
            {"section": target // 4, "seq": target % 4},
        )

    def sig(target, source):
        return remote(
            signal_ref.at[target], signal_out.at[source], sig_send.at[target], sig_recv.at[source],
            {"seq": target},
        )

    for turn in range(1, 8):
        a2a((me + turn) % 8, me).start()
    conv_local = pltpu.make_async_copy(conv_ref.at[me], conv_out.at[dp, me], local_sem.at[0])
    signal_local = pltpu.make_async_copy(signal_ref.at[seq], signal_out.at[seq], local_sem.at[1])
    conv_local.start()
    signal_local.start()

    def columns(layer, half):
        return (second_out if layer else whole_out.at[dp, y, half]).at[:, pl.ds(0, split)]

    def others(layer, half):
        return (second_out if layer else whole_out.at[dp, y, half]).at[:, pl.ds(split, rest_ref.shape[2])]

    class Layer:
        def __init__(self, layer):
            far = {"section": 1 - layer}
            self.mine = sec == layer
            self.even = x == layer
            received = column_recv.at[layer]
            self.keep_local = pltpu.make_async_copy(keep_ref, columns(layer, layer), local_sem.at[2])
            self.rest_local = pltpu.make_async_copy(rest_ref.at[layer], others(layer, layer), local_sem.at[3])
            self.keep_far = remote(keep_ref, columns(layer, 1 - layer), own_send.at[0], received, far)
            self.send_same = remote(
                send_ref, columns(layer, layer), own_send.at[1], received, {"seq": partner_x}
            )
            self.send_cross = remote(
                send_ref, columns(layer, 1 - layer), own_send.at[1], received, {**far, "seq": partner_x}
            )
            self.rest_far = remote(
                rest_ref.at[1 - layer], others(layer, 1 - layer), own_send.at[2], rest_recv.at[layer], far
            )

        def start(self):
            @pl.when(self.mine & self.even)
            def _():
                self.send_same.start()
                self.keep_local.start()

            @pl.when(self.mine & jnp.logical_not(self.even))
            def _():
                self.send_cross.start()
                self.keep_far.start()

            @pl.when(self.mine)
            def _():
                self.rest_far.start()
                self.rest_local.start()

        def wait(self):
            other = jnp.logical_not(self.mine)
            odd = jnp.logical_not(self.even)

            @pl.when(self.mine & self.even)
            def _():
                self.keep_local.wait()

            @pl.when(self.mine & odd)
            def _():
                self.send_same.wait_recv()

            @pl.when(self.mine)
            def _():
                self.rest_local.wait()

            @pl.when(other & self.even)
            def _():
                self.send_cross.wait_recv()

            @pl.when(other & odd)
            def _():
                self.keep_far.wait_recv()

            @pl.when(other)
            def _():
                self.rest_far.wait_recv()

        def finish(self):
            @pl.when(self.mine & self.even)
            def _():
                self.send_same.wait_send()

            @pl.when(self.mine & jnp.logical_not(self.even))
            def _():
                self.send_cross.wait_send()
                self.keep_far.wait_send()

            @pl.when(self.mine)
            def _():
                self.rest_far.wait_send()

    layers = [Layer(0), Layer(1)]
    for layer in layers:
        layer.start()
    for turn in range(1, 4):
        sig((seq + turn) % 4, seq).start()

    def line(slot, direction):
        index = (direction + 1) // 2
        return remote(
            conv_out.at[slot], conv_out.at[slot], line_send.at[index, slot], line_recv.at[slot],
            {"dp": dp + direction},
        )

    def place(slot, row, half, part):
        return whole_out.at[slot, row, half, pl.ds(part * rows, rows)]

    def along(slot, direction, part):
        index = (direction + 1) // 2
        ref = place(slot, y, sec, part)
        return remote(
            ref, ref, up_send.at[index, slot, part], up_recv.at[slot, part], {"dp": dp + direction}
        )

    def across(slot, row, part):
        ref = place(slot, row, sec, part)
        return remote(ref, ref, y_send.at[slot, part], y_recv.at[slot, part], partner_y)

    def to_core(slot, row, half, part):
        ref = place(slot, row, half, part)
        return remote(
            ref, ref, core_send.at[slot, row, part], core_recv.at[slot, row, part], sibling
        )

    for turn in range(1, 8):
        a2a((me + turn) % 8, (me + turn) % 8).wait_recv()
    conv_local.wait()
    for there, direction in ((has_up, 1), (has_down, -1)):

        @pl.when(there)
        def _(direction=direction):
            line(dp, direction).start()

    layers[0].wait()
    for part in range(parts):
        for there, direction in ((has_up, 1), (has_down, -1)):

            @pl.when(there)
            def _(direction=direction, part=part):
                along(dp, direction, part).start()

        across(dp, y, part).start()
        to_core(dp, y, sec, part).start()

    def stage(distance):
        arrivals = []
        for direction in (1, -1):
            slot = dp - direction * distance
            arrives = (slot >= 0) & (slot < dp_count)
            goes_on = arrives & (has_up if direction == 1 else has_down)
            arrivals.append((direction, slot, arrives, goes_on))

            @pl.when(arrives)
            def _(slot=slot, direction=direction):
                line(slot, direction).wait_recv()

            @pl.when(goes_on)
            def _(slot=slot, direction=direction):
                line(slot, direction).start()

        for part in range(parts):
            for direction, slot, arrives, goes_on in arrivals:

                @pl.when(arrives)
                def _(slot=slot, direction=direction, part=part):
                    along(slot, direction, part).wait_recv()

                @pl.when(goes_on)
                def _(slot=slot, direction=direction, part=part):
                    along(slot, direction, part).start()

                @pl.when(arrives)
                def _(slot=slot, part=part):
                    across(slot, y, part).start()
                    to_core(slot, y, sec, part).start()

    def pass_crossed(distance):
        for part in range(parts):
            for sign in (1, -1) if distance else (1,):
                slot = dp - sign * distance

                @pl.when((slot >= 0) & (slot < dp_count))
                def _(slot=slot, part=part):
                    across(slot, 1 - y, part).wait_recv()
                    to_core(slot, 1 - y, sec, part).start()

    for distance in range(1, dp_count):
        stage(distance)
        pass_crossed(distance - 1)
    pass_crossed(dp_count - 1)

    for slot in range(dp_count):
        for part in range(parts):
            for row in range(2):
                to_core(slot, row, 1 - sec, part).wait_recv()
                to_core(slot, row, sec, part).wait_send()
            across(slot, y, part).wait_send()
        for direction in (1, -1):
            sent = (slot <= dp if direction == 1 else slot >= dp) & (has_up if direction == 1 else has_down)

            @pl.when(sent)
            def _(slot=slot, direction=direction):
                line(slot, direction).wait_send()
                for part in range(parts):
                    along(slot, direction, part).wait_send()

    layers[1].wait()
    for layer in layers:
        layer.finish()
    for turn in range(1, 8):
        a2a((me + turn) % 8, me).wait_send()
    for turn in range(1, 4):
        sig((seq + turn) % 4, (seq + turn) % 4).wait_recv()
        sig((seq + turn) % 4, seq).wait_send()
    signal_local.wait()


def opening(conv_send, signal_send, keep, send, rest):
    count = lax.axis_size("dp")
    parts = 2
    rows, columns = keep.shape[0], keep.shape[1] + rest.shape[2]
    anywhere = pl.BlockSpec(memory_space=pl.ANY)
    dma = pltpu.SemaphoreType.DMA
    conv_all, signal_all, whole, second = pl.pallas_call(
        functools.partial(opening_kernel, count, parts),
        in_specs=[anywhere] * 5,
        out_specs=[anywhere] * 4,
        out_shape=[
            jax.ShapeDtypeStruct((count, *conv_send.shape), conv_send.dtype),
            jax.ShapeDtypeStruct(signal_send.shape, signal_send.dtype),
            jax.ShapeDtypeStruct((count, 2, 2, rows, columns), keep.dtype),
            jax.ShapeDtypeStruct((rows, columns), keep.dtype),
        ],
        scratch_shapes=[
            dma((4,)), dma((8,)), dma((8,)), dma((4,)), dma((4,)), dma((2, count)), dma((count,)),
            dma((3,)), dma((2,)), dma((2,)), dma((2, count, parts)), dma((count, parts)), dma((count, parts)),
            dma((count, parts)), dma((count, 2, parts)), dma((count, 2, parts)),
        ],
        compiler_params=pltpu.CompilerParams(
            collective_id=0, has_side_effects=True, vmem_limit_bytes=4 * 1024 * 1024
        ),
        name="opening",
    )(conv_send, signal_send, keep, send, rest)
    return conv_all, signal_all, whole.reshape(-1, columns), second


def norm_stats(values):
    average = jnp.mean(values, axis=-1, keepdims=True)
    centred = values - average
    spread = jnp.mean(centred * centred, axis=-1, keepdims=True)
    return centred, lax.rsqrt(spread + EPS)


def norm_back(values, gain, grad):
    centred, inv = norm_stats(values)
    unit = centred * inv
    gain_grad = jnp.sum(grad * unit, axis=0)
    f = grad * gain
    mean_f = jnp.mean(f, axis=-1, keepdims=True)
    mean_fu = jnp.mean(f * unit, axis=-1, keepdims=True)
    return (f - mean_f - unit * mean_fu) * inv, gain_grad


def gelu_slope(values):
    cdf = 0.5 * (1.0 + lax.erf(values * (1.0 / math.sqrt(2.0))))
    pdf = jnp.exp(-0.5 * values * values) * (1.0 / math.sqrt(2.0 * math.pi))
    return cdf + values * pdf


def attention_forward_kernel(factor, q_ref, k_ref, v_ref, qs_ref, ks_ref, o_ref, lse_ref):
    queries = q_ref[...]
    lane = lax.broadcasted_iota(jnp.int32, queries.shape, 1)
    allowed = qs_ref[...] == ks_ref[...]
    keys = k_ref[...]
    values = v_ref[...]
    outs = []
    for head in range(2):
        mine = (lane < HEAD_DIM) if head == 0 else (lane >= HEAD_DIM)
        own = jnp.where(mine, queries, jnp.zeros_like(queries))
        scores = lax.dot_general(
            own, keys, (((1,), (1,)), ((), ())), preferred_element_type=jnp.float32
        ) * factor
        scores = jnp.where(allowed, scores, NEG)
        top = jnp.max(scores, axis=-1, keepdims=True)
        raised = jnp.exp(scores - top)
        total = jnp.sum(raised, axis=-1, keepdims=True)
        chances = (raised * (1.0 / total)).astype(jnp.bfloat16)
        outs.append(jnp.dot(chances, values, preferred_element_type=jnp.float32))
        lse_ref[0, head] = top + jnp.log(total)
    o_ref[...] = jnp.where(lane < HEAD_DIM, outs[0], outs[1]).astype(o_ref.dtype)


def attention_forward(packed, kv_all, query_segs, key_segs, factor):
    frames = packed.shape[0]
    keys = kv_all.shape[0]
    width = packed.shape[1] // 3
    pairs = width // 128
    rows = math.gcd(frames, 256)
    return pl.pallas_call(
        functools.partial(attention_forward_kernel, factor),
        grid=(pairs, frames // rows),
        in_specs=[
            pl.BlockSpec((rows, 128), lambda h, i: (i, h)),
            pl.BlockSpec((keys, 128), lambda h, i: (0, h)),
            pl.BlockSpec((keys, 128), lambda h, i: (0, pairs + h)),
            pl.BlockSpec((rows, 1), lambda h, i: (i, 0)),
            pl.BlockSpec((1, keys), lambda h, i: (0, 0)),
        ],
        out_specs=[
            pl.BlockSpec((rows, 128), lambda h, i: (i, h)),
            pl.BlockSpec((1, 2, rows, 1), lambda h, i: (h, 0, i, 0)),
        ],
        out_shape=[
            jax.ShapeDtypeStruct((frames, width), jnp.bfloat16),
            jax.ShapeDtypeStruct((pairs, 2, frames, 1), jnp.float32),
        ],
        compiler_params=pltpu.CompilerParams(vmem_limit_bytes=40 * 1024 * 1024),
        cost_estimate=pl.CostEstimate(
            flops=4 * frames * keys * width * 2,
            bytes_accessed=2 * (frames * width * 2 + keys * width * 2),
            transcendentals=frames * keys * (width // HEAD_DIM),
        ),
        name="attention_forward",
    )(packed, kv_all, kv_all, query_segs[:, None], key_segs[None, :])


def attention_backward_kernel(
    factor, q_ref, k_ref, v_ref, g_ref, o_ref, lse_ref, qs_ref, ks_ref, *rest
):
    *begin, dq_ref, dk_ref, dv_ref = rest
    step = pl.program_id(1)

    @pl.when(step == 0)
    def _():
        for index, total_ref in enumerate((dk_ref, dv_ref)):
            total_ref[...] = begin[index][...] if begin else jnp.zeros_like(total_ref)

    queries = q_ref[...]
    grads = g_ref[...]
    keys = k_ref[...]
    values = v_ref[...]
    lane = lax.broadcasted_iota(jnp.int32, queries.shape, 1)
    key_lane = lax.broadcasted_iota(jnp.int32, keys.shape, 1)
    allowed = qs_ref[...] == ks_ref[...]
    product = grads.astype(jnp.float32) * o_ref[...].astype(jnp.float32)
    dq = None
    for head in range(2):
        mine = (lane < HEAD_DIM) if head == 0 else (lane >= HEAD_DIM)
        key_mine = (key_lane < HEAD_DIM) if head == 0 else (key_lane >= HEAD_DIM)
        own_q = jnp.where(mine, queries, jnp.zeros_like(queries))
        own_g = jnp.where(mine, grads, jnp.zeros_like(grads))
        own_k = jnp.where(key_mine, keys, jnp.zeros_like(keys))
        delta = jnp.sum(jnp.where(mine, product, 0.0), axis=-1, keepdims=True)
        scores = lax.dot_general(
            own_q, keys, (((1,), (1,)), ((), ())), preferred_element_type=jnp.float32
        ) * factor
        chances = jnp.exp(jnp.where(allowed, scores, NEG) - lse_ref[0, head])
        prob_grad = lax.dot_general(
            own_g, values, (((1,), (1,)), ((), ())), preferred_element_type=jnp.float32
        )
        score_grad = (chances * (prob_grad - delta)).astype(jnp.bfloat16)
        part = jnp.dot(score_grad, own_k, preferred_element_type=jnp.float32)
        dq = part if dq is None else dq + part
        dk_ref[...] += lax.dot_general(
            score_grad, own_q, (((0,), (0,)), ((), ())), preferred_element_type=jnp.float32
        ) * factor
        dv_ref[...] += lax.dot_general(
            chances.astype(jnp.bfloat16), own_g, (((0,), (0,)), ((), ())),
            preferred_element_type=jnp.float32,
        )
    dq_ref[...] = (dq * factor).astype(dq_ref.dtype)


def attention_backward(packed, kv_all, grads, attended, lse, query_segs, key_segs, factor, begin=None):
    frames = packed.shape[0]
    keys = kv_all.shape[0]
    width = packed.shape[1] // 3
    pairs = width // 128
    rows = math.gcd(frames, 256)
    return pl.pallas_call(
        functools.partial(attention_backward_kernel, factor),
        grid=(pairs, frames // rows),
        in_specs=[
            pl.BlockSpec((rows, 128), lambda h, i: (i, h)),
            pl.BlockSpec((keys, 128), lambda h, i: (0, h)),
            pl.BlockSpec((keys, 128), lambda h, i: (0, pairs + h)),
            pl.BlockSpec((rows, 128), lambda h, i: (i, h)),
            pl.BlockSpec((rows, 128), lambda h, i: (i, h)),
            pl.BlockSpec((1, 2, rows, 1), lambda h, i: (h, 0, i, 0)),
            pl.BlockSpec((rows, 1), lambda h, i: (i, 0)),
            pl.BlockSpec((1, keys), lambda h, i: (0, 0)),
        ]
        + [pl.BlockSpec((keys, 128), lambda h, i: (0, h))] * (2 if begin else 0),
        out_specs=[
            pl.BlockSpec((rows, 128), lambda h, i: (i, h)),
            pl.BlockSpec((keys, 128), lambda h, i: (0, h)),
            pl.BlockSpec((keys, 128), lambda h, i: (0, h)),
        ],
        out_shape=[
            jax.ShapeDtypeStruct((frames, width), jnp.bfloat16),
            jax.ShapeDtypeStruct((keys, width), jnp.float32),
            jax.ShapeDtypeStruct((keys, width), jnp.float32),
        ],
        compiler_params=pltpu.CompilerParams(vmem_limit_bytes=48 * 1024 * 1024),
        cost_estimate=pl.CostEstimate(
            flops=10 * frames * keys * width * 2,
            bytes_accessed=4 * (frames * width * 2 + keys * width * 2),
            transcendentals=frames * keys * (width // HEAD_DIM),
        ),
        name="attention_backward",
    )(packed, kv_all, kv_all, grads, attended, lse, query_segs[:, None], key_segs[None, :], *(begin or ()))


CONV_STEP = 4


def conv_bands(kernel, per_group):
    groups = kernel.shape[1] // per_group
    steps = TAPS // CONV_STEP + 1
    bands = []
    for group in range(groups):
        own = kernel[:, group * per_group : (group + 1) * per_group]
        shifted = [
            jnp.pad(own, ((shift * per_group, (CONV_STEP - shift) * per_group), (0, 0)))
            for shift in range(CONV_STEP)
        ]
        band = jnp.concatenate(shifted, axis=1)
        bands.append(band.reshape(steps, CONV_STEP * per_group, CONV_STEP * per_group))
    return bands


def group_view(values, per_group):
    rows, frames, width = values.shape
    return [
        values[:, :, g * per_group : (g + 1) * per_group].reshape(
            rows, frames // CONV_STEP, CONV_STEP * per_group
        )
        for g in range(width // per_group)
    ]


def ungroup(parts, per_group):
    rows, blocks, _ = parts[0].shape
    return jnp.concatenate(
        [part.reshape(rows, blocks * CONV_STEP, per_group) for part in parts], axis=2
    )


CONV_DIMS = ("NWC", "WIO", "NWC")


def conv_forward(views, bands):
    half = TAPS // 2 // CONV_STEP
    return [
        lax.conv_general_dilated(
            view, band, (1,), [(half, half)], dimension_numbers=CONV_DIMS,
            preferred_element_type=jnp.float32,
        )
        for view, band in zip(views, bands)
    ]


def conv_back(grad_views, bands):
    half = TAPS // 2 // CONV_STEP
    return [
        lax.conv_general_dilated(
            view, jnp.transpose(band[::-1], (0, 2, 1)), (1,), [(half, half)],
            dimension_numbers=CONV_DIMS, preferred_element_type=jnp.float32,
        )
        for view, band in zip(grad_views, bands)
    ]


def conv_taps_grad(views, grad_views, per_group):
    half = TAPS // 2 // CONV_STEP
    results = []
    for view, grad in zip(views, grad_views):
        band = lax.conv_general_dilated(
            view, grad, (1,), [(half, half)],
            dimension_numbers=("CWN", "IWO", "WNC"),
            preferred_element_type=jnp.float32,
        )
        flat = band.reshape(-1, CONV_STEP * per_group)
        total = None
        for shift in range(CONV_STEP):
            part = flat[
                shift * per_group : (shift + TAPS) * per_group,
                shift * per_group : (shift + 1) * per_group,
            ]
            total = part if total is None else total + part
        results.append(total)
    return jnp.concatenate(results, axis=1)


def to_column(vector, width):
    return jnp.pad(vector[:, None], ((0, 0), (0, width - 1)))


def per_device_pairs(
    signal, frame_segment_index, conv_weight, conv_bias, norm1_gain, qkv_weight, out_weight,
    norm2_gain, up_weight, down_weight, cotangent,
):
    micro_count, frames, width = signal.shape
    bf16, f32 = jnp.bfloat16, jnp.float32
    per_group = width // GROUPS
    dp_count = lax.axis_size("dp")
    factor = 1.0 / math.sqrt(HEAD_DIM)
    sec = lax.axis_index("section")
    dp = lax.axis_index("dp")
    seq = lax.axis_index("seq")
    x, y = seq % 2, seq // 2
    sec0, x0 = sec == 0, x == 0
    row_frames = 4 * frames
    half_frames = 2 * frames
    both = ("section", "seq")

    block_width = width // 8
    rows_here = conv_weight.shape[0]
    conv_low = conv_weight.astype(bf16).reshape(rows_here, 8, block_width)
    bias_low = jnp.pad(conv_bias.astype(bf16), (0, block_width - conv_bias.shape[0]))
    bias_rows = jnp.pad(
        jnp.broadcast_to(bias_low[None, None, :], (1, 8, block_width)), ((0, 15), (0, 0), (0, 0))
    )
    conv_send = jnp.transpose(jnp.concatenate([conv_low, bias_rows], axis=0), (1, 0, 2))

    own_half = jnp.where(sec0, signal[:, :, : width // 2], signal[:, :, width // 2 :])
    sig_send = jnp.transpose(own_half.reshape(micro_count, frames, 4, block_width), (2, 0, 1, 3))
    in_rows = qkv_weight.shape[1]
    unit = down_weight.shape[1] // 4
    qkv_view = qkv_weight[0].astype(bf16).reshape(in_rows, -1, 2, HEAD_DIM)
    qkv_parity = [qkv_view[:, :, p].reshape(in_rows, -1) for p in range(2)]
    up_view = up_weight[0].astype(bf16).reshape(in_rows, -1, 2, 2, 2, unit)
    up_parity = [
        jnp.transpose(up_view[:, :, p], (0, 3, 1, 2, 4)).reshape(in_rows, -1) for p in range(2)
    ]
    qkv_cols, up_cols = qkv_parity[0].shape[1], up_parity[0].shape[1]
    col_one = to_column(norm1_gain[0].astype(bf16), 128)
    col_two = to_column(norm2_gain[0].astype(bf16), 128)
    cut = qkv_cols + 128
    keep_cols, send_cols = [
        jnp.concatenate([a, col_one, b, col_two], axis=1)
        for a, b in zip(choose(x0, *qkv_parity), choose(x0, *up_parity))
    ]
    out_low = out_weight[0].astype(bf16)
    down_low = down_weight[0].astype(bf16).reshape(2, 2, unit, width)
    rest = jnp.stack(
        [
            jnp.concatenate(
                [out_low[:, h * width // 2 : (h + 1) * width // 2], down_low[h, 0], down_low[h, 1]], axis=1
            )
            for h in range(2)
        ]
    )
    up_at = cut
    two_at = up_at + up_cols
    out_at = two_at + 128
    down_at = out_at + width // 2
    conv_all, sig_got, whole, second_piece = opening(conv_send, sig_send, keep_cols, send_cols, rest)
    gathered = [whole, gather_rows(second_piece)]
    sig_all = jnp.transpose(sig_got, (1, 0, 2, 3)).reshape(micro_count, row_frames, block_width)
    conv_all = conv_all.reshape(dp_count, 2, 4, rows_here + 16, block_width)
    conv_all = jnp.transpose(conv_all, (1, 0, 2, 3, 4))
    bias_all = conv_all[:, :, :, rows_here, : conv_bias.shape[0]].reshape(width)
    bias_own = lax.dynamic_slice_in_dim(bias_all, (sec * 4 + seq) * block_width, block_width, 0)
    kernel_own = conv_all[:, :, :, :rows_here].reshape(TAPS * per_group, block_width)
    bands = conv_bands(kernel_own, per_group)


    def views(whole):
        w_out = jnp.transpose(
            whole[:, out_at:down_at].reshape(-1, 2, in_rows, width // 2), (0, 2, 1, 3)
        ).reshape(-1, width)
        gain_one = whole[:, qkv_cols].astype(f32)[None, :]
        gain_two = whole[:, two_at].astype(f32)[None, :]
        w_up = [whole[:, up_at + part * width : up_at + (part + 1) * width] for part in range(2)]
        w_down = [whole[:, down_at + part * width : down_at + (part + 1) * width] for part in range(2)]
        return gain_one, whole[:, :qkv_cols], w_out, gain_two, w_up, w_down

    layer_weights = []

    picked = jnp.where(sec0, cotangent[0], cotangent[1])
    across = [(s * 4 + 2 * yy + xx, yy * 4 + 2 * s + xx) for s in range(2) for yy in range(2) for xx in range(2)]
    cot_own = lax.ppermute(picked, both, across)
    cot_other = swap_x(cot_own)
    cot_pair = choose(x0, cot_own, cot_other)
    top_grad = jnp.concatenate(cot_pair, axis=0).astype(f32)

    segment_row = jnp.where(y == 0, frame_segment_index[0], frame_segment_index[1])
    seg_pair = choose(sec0, segment_row[:half_frames], segment_row[half_frames:])
    query_segs = seg_pair[0]
    key_segs = jnp.concatenate(seg_pair)

    sig_views = group_view(sig_all, per_group)
    conv_pre = ungroup(conv_forward(sig_views, bands), per_group) + bias_own.astype(f32)
    stream = (sig_all.astype(f32) + smooth(conv_pre)).astype(bf16)
    slope = gelu_slope(conv_pre).astype(bf16)
    stream_send = stream.reshape(2, 2, half_frames, block_width)
    stream_send = jnp.transpose(stream_send, (1, 0, 2, 3))
    stream_send = jnp.repeat(stream_send.reshape(4, half_frames, block_width), 2, axis=0)
    stream_got = lax.all_to_all(stream_send, both, 0, 0, tiled=True)
    layer_in = jnp.transpose(stream_got, (1, 0, 2)).reshape(half_frames, width).astype(f32)

    chunks = 2
    rows = half_frames // chunks
    layer_in = [layer_in[c * rows : (c + 1) * rows] for c in range(chunks)]
    chunk_segs = [query_segs[c * rows : (c + 1) * rows] for c in range(chunks)]
    kept = []
    for layer in range(2):
        whole = gathered[layer]
        if layer:
            layer_in = []
            previous_lows[0], whole = after(previous_lows[0], whole)
        layer_weights.append(views(whole))
        gain_one, w_qkv, w_out, gain_two, w_up, w_down = layer_weights[layer]
        normed_one, packed, kv_own, kv_other = [], [], [], []
        for c in range(chunks):
            if layer:
                total = previous[c] + pair_sum(previous_lows[c], packed[-1] if c else None)
                layer_in.append(total.astype(bf16).astype(f32))
            centred, inv = norm_stats(layer_in[c])
            normed_one.append((centred * inv * gain_one).astype(bf16))
            packed.append(jnp.dot(normed_one[c], w_qkv, preferred_element_type=f32).astype(bf16))
            kv_own.append(packed[c][:, width // 2 :])
            kv_other.append(swap_section(kv_own[c]))
        kv_all = jnp.concatenate(kv_own + kv_other, axis=0)
        attended, lse, resid_two, normed_two, hidden, hidden_slope = [], [], [], [], [], []
        attn_lows, lows = [], []
        for c in range(chunks):
            own = packed[c]
            if c:
                attn_lows[-1], own = after(attn_lows[-1], own)
            mixed, log_total = attention_forward(own, kv_all, chunk_segs[c], key_segs, factor)
            attended.append(mixed)
            lse.append(log_total)
            attn_lows.append(jnp.dot(mixed, w_out, preferred_element_type=f32).astype(bf16))
        for c in range(chunks):
            resid_two.append(layer_in[c] + pair_sum(attn_lows[c], lows[-1] if c else None))
            centred, inv = norm_stats(resid_two[c])
            normed_two.append((centred * inv * gain_two).astype(bf16))
            down_sum, own_hidden, own_slope = None, [], []
            for part in range(2):
                hidden_pre = jnp.dot(normed_two[c], w_up[part], preferred_element_type=f32)
                own_hidden.append(smooth(hidden_pre).astype(bf16))
                own_slope.append(gelu_slope(hidden_pre).astype(bf16))
            for part in range(2):
                term = jnp.dot(own_hidden[part], w_down[part], preferred_element_type=f32)
                down_sum = term if down_sum is None else down_sum + term
            hidden.append(own_hidden)
            hidden_slope.append(own_slope)
            lows.append(down_sum.astype(bf16))

        resid_two_last = resid_two
        kept.append((layer_in, normed_one, packed, kv_all, attended, lse, resid_two, normed_two, hidden, hidden_slope))
        previous, previous_lows = resid_two, lows

    def outer(left, right):
        return lax.dot_general(
            left, right, (((0,), (0,)), ((), ())), preferred_element_type=f32
        ).astype(bf16)

    def back(left, right):
        return lax.dot_general(left, right, (((1,), (1,)), ((), ())), preferred_element_type=f32)

    grad_out = [top_grad[c * rows : (c + 1) * rows] for c in range(chunks)]
    attn_members, scattered = [], []
    for layer in (1, 0):
        gain_one, w_qkv, w_out, gain_two, w_up, w_down = layer_weights[layer]
        (layer_in, normed_one, packed, kv_all, attended, lse, resid_two, normed_two, hidden, hidden_slope) = kept[layer]
        branch = [member.astype(bf16) for member in grad_out]
        pre_grad, sums, low = [], [], None
        for c in range(chunks):
            own = branch[c]
            if low is not None:
                low, own = after(low, own)
                sums.append(pair_sum(low))
            own_pre, part_sum = [], None
            for part in range(2):
                own_pre.append((back(own, w_down[part]) * hidden_slope[c][part].astype(f32)).astype(bf16))
            for part in range(2):
                term = back(own_pre[part], w_up[part])
                part_sum = term if part_sum is None else part_sum + term
            pre_grad.append(own_pre)
            low = part_sum.astype(bf16)
        sums.append(pair_sum(low))
        whole_pre = [jnp.concatenate([pre_grad[c][p] for c in range(chunks)]) for p in range(2)]
        whole_hidden = [jnp.concatenate([hidden[c][p] for c in range(chunks)]) for p in range(2)]
        whole_branch, whole_two = jnp.concatenate(branch), jnp.concatenate(normed_two)
        ff_members = [
            outer(whole_two, whole_pre[0]), outer(whole_two, whole_pre[1]),
            outer(whole_hidden[0], whole_branch), outer(whole_hidden[1], whole_branch),
        ]
        if layer == 1:
            ff_members.append(jnp.zeros((width, 128), bf16))
        partial = jnp.concatenate(attn_members + ff_members, axis=1)
        if layer == 0:
            sums, (partial, output_rows) = after(sums, (partial, output_rows))
        scattered.append(scatter_rows(partial))
        resid_grad, attn_branch, dq, gain_two_grad = [], [], [], None
        dkv = None
        for c in range(chunks):
            in_part, gain_part = norm_back(resid_two[c], gain_two, sums[c])
            gain_two_grad = gain_part if gain_two_grad is None else gain_two_grad + gain_part
            resid_grad.append(in_part + grad_out[c])
            attn_branch.append(resid_grad[c].astype(bf16))
            attended_grad = back(attn_branch[c], w_out).astype(bf16)
            if layer == 1 and c == 0:
                attended_grad, lows = after(attended_grad, lows)
                output = [member + pair_sum(low) for member, low in zip(resid_two_last, lows)]
                row_block = lax.ppermute(jnp.where(x0, output[0], output[1]), both, across)
                output_rows = jnp.stack(choose(sec0, row_block, swap_section(row_block)))
            own_dq, *dkv = attention_backward(
                packed[c], kv_all, attended_grad, attended[c], lse[c], chunk_segs[c], key_segs, factor,
                None if c == 0 else dkv,
            )
            dq.append(own_dq)
        if layer == 0:
            dkv, scattered[0] = after(dkv, scattered[0])
        else:
            dkv, output = after(dkv, output)
        dkv = jnp.concatenate(dkv, axis=1)
        other_dkv = swap_section(dkv[half_frames:].astype(bf16))
        dkv_own = (dkv[:half_frames] + other_dkv.astype(f32)).astype(bf16)
        packed_grad, sums, low = [], [], None
        for c in range(chunks):
            packed_grad.append(jnp.concatenate([dq[c], dkv_own[c * rows : (c + 1) * rows]], axis=1))
            own = packed_grad[c]
            if low is not None:
                low, own = after(low, own)
                sums.append(pair_sum(low))
            low = back(own, w_qkv).astype(bf16)
        sums.append(pair_sum(low))
        next_grad, gain_one_grad = [], None
        for c in range(chunks):
            in_part, gain_part = norm_back(layer_in[c], gain_one, sums[c])
            gain_one_grad = gain_part if gain_one_grad is None else gain_one_grad + gain_part
            next_grad.append((resid_grad[c] + in_part).astype(bf16))
        whole_one, whole_pg, whole_att, whole_ab = [
            jnp.concatenate(m) for m in (normed_one, packed_grad, attended, attn_branch)
        ]
        grad_out_weight = jnp.transpose(
            outer(whole_att, whole_ab).reshape(-1, in_rows, 2, width // 2), (0, 2, 1, 3)
        ).reshape(-1, width // 2)
        gain_grads = jnp.stack([gain_one_grad, gain_two_grad], axis=1).astype(bf16)
        gain_grads = jnp.pad(gain_grads, ((0, 0), (0, 126)))
        attn_members = [outer(whole_one, whole_pg), gain_grads, grad_out_weight]
        grad_out = [member.astype(f32) for member in next_grad]
    grad_in_low = jnp.concatenate(next_grad)
    scattered.append(scatter_rows(jnp.concatenate(attn_members, axis=1)))

    lig_send = jnp.transpose(grad_in_low.reshape(half_frames, 8, block_width), (1, 0, 2))
    def gradient_block(section, place):
        return lax.dynamic_index_in_dim(lig_send, section * 4 + place, 0, keepdims=False)

    beyond = (seq + 2) % 4
    corner = [(t * 4 + q, (1 - t) * 4 + (q ^ 2)) for t in range(2) for q in range(4)]
    near = choose(sec0, gradient_block(sec, seq), swap_section(gradient_block(1 - sec, seq)))
    far = choose(
        sec0,
        lax.ppermute(gradient_block(sec, beyond), "seq", [(q, q ^ 2) for q in range(4)]),
        lax.ppermute(gradient_block(1 - sec, beyond), both, corner),
    )
    lig = jnp.stack(choose(y == 0, jnp.concatenate(near), jnp.concatenate(far)))
    conv_grad = (lig.astype(f32) * slope.astype(f32)).astype(bf16)
    grad_views = group_view(conv_grad, per_group)
    back = ungroup(conv_back(grad_views, bands), per_group)
    grad_signal = (lig.astype(f32) + back).astype(bf16)
    gs_send = jnp.transpose(
        grad_signal.reshape(micro_count, 4, frames, block_width), (1, 0, 2, 3)
    )
    gs_send = jnp.concatenate([gs_send, gs_send], axis=0)
    taps_grad = conv_taps_grad(sig_views, grad_views, per_group)
    bias_grad = jnp.sum(conv_grad.astype(f32), axis=(0, 1))
    taps_view = jnp.transpose(
        taps_grad.reshape(2, dp_count, 4, rows_here, block_width), (1, 0, 2, 3, 4)
    ).astype(bf16)
    bias_view = jnp.pad(
        jnp.broadcast_to(bias_grad.astype(bf16), (dp_count, 2, 4, 1, block_width)),
        ((0, 0), (0, 0), (0, 0), (0, 15), (0, 0)),
    )
    taps_send = jnp.concatenate([taps_view, bias_view], axis=3)
    gs_got = lax.all_to_all(gs_send, both, 0, 0, tiled=True)
    attn_cols = cut + width // 2

    def over_section(first, second):
        keep, send = choose(sec0, first, second)
        return choose(sec0, keep, swap_section(send))


    taps_sum, (_, gs_got) = sum_dp(taps_send, dp, (gs_send, gs_got))
    gs_rows = jnp.transpose(gs_got, (1, 2, 0, 3)).reshape(micro_count, frames, width).astype(f32)
    ends = jnp.where(sec0, gs_rows, output_rows)[None]
    taps_got = lax.all_to_all(
        taps_sum.reshape(8, rows_here + 16, block_width), both, 0, 0, tiled=True
    )
    taps_got, scattered[1] = after(taps_got, scattered[1])
    conv_weight_grad = jnp.transpose(taps_got[:, :rows_here], (1, 0, 2)).reshape(rows_here, width).astype(f32)
    bias_count = conv_bias.shape[0]
    conv_bias_grad = lax.dynamic_slice_in_dim(
        taps_got[:, rows_here].reshape(width),
        ((sec * dp_count + dp) * 4 + seq) * bias_count,
        bias_count,
        0,
    ).astype(f32)

    turned = [(t * 4 + 2 * r + c, c * 4 + 2 * r + t) for t in range(2) for r in range(2) for c in range(2) if t != c]
    crossed = [(t * 4 + 2 * r + c, (1 - c) * 4 + 2 * r + t) for t in range(2) for r in range(2) for c in range(2)]

    def home(first, second):
        straight, other = choose(x0, first, second)
        straight = jnp.where(sec == x, straight, lax.ppermute(straight, both, turned))
        other = lax.ppermute(other, both, crossed)
        return choose(sec0, straight, other)

    ff_layers = (scattered[1][:, attn_cols:], scattered[0][:, :-128])
    ff_sets = over_section(*(member[:, up_cols:] for member in ff_layers))
    down_grad = jnp.concatenate(
        [member[:, at : at + width] for member in ff_sets for at in (0, width)], axis=0
    ).astype(f32)[None]
    up_grad = jnp.stack(
        [
            jnp.transpose(member.reshape(in_rows, 2, -1, 2, unit), (0, 2, 3, 1, 4))
            for member in home(*(member[:, :up_cols] for member in ff_layers))
        ],
        axis=2,
    ).reshape(in_rows, -1).astype(f32)[None]
    scattered[2], (up_grad, down_grad) = after(scattered[2], (up_grad, down_grad))
    attn_layers = (scattered[2], scattered[1][:, :attn_cols])
    attn_sets = over_section(*(member[:, cut:] for member in attn_layers))
    out_grad = jnp.concatenate(attn_sets, axis=1).astype(f32)[None]
    qkv_sets = home(*(member[:, :cut] for member in attn_layers))
    norm1_grad = qkv_sets[0][:, qkv_cols].astype(f32)[None]
    norm2_grad = qkv_sets[0][:, qkv_cols + 1].astype(f32)[None]
    qkv_grad = jnp.stack(
        [member[:, :qkv_cols].reshape(in_rows, -1, HEAD_DIM) for member in qkv_sets], axis=2
    ).reshape(in_rows, -1).astype(f32)[None]
    return (ends, conv_weight_grad, conv_bias_grad, norm1_grad, qkv_grad, out_grad, norm2_grad, up_grad, down_grad)


def solution(mesh):
    placed = (
        P("dp", "seq", None),
        P("dp", None),
        P(("section", "dp", "seq"), None),
        P(("section", "dp", "seq")),
        P("section", ("dp", "seq")),
        P("section", ("dp", "seq"), None),
        P("section", ("dp", "seq"), None),
        P("section", ("dp", "seq")),
        P("section", ("dp", "seq"), None),
        P("section", ("dp", "seq"), None),
        P("dp", "seq", None),
    )

    def step(*arrays):
        pairs = mesh.shape["seq"] == 4 and mesh.shape["section"] == 2 and arrays[0].shape[0] == 2
        return (per_device_pairs if pairs else per_device)(*arrays)

    return jax.shard_map(
        step,
        mesh=mesh,
        in_specs=placed,
        out_specs=(
            P("section", "dp", "seq", None),
            P(("section", "dp", "seq"), None),
            P(("section", "dp", "seq")),
            P("section", ("dp", "seq")),
            P("section", ("dp", "seq"), None),
            P("section", ("dp", "seq"), None),
            P("section", ("dp", "seq")),
            P("section", ("dp", "seq"), None),
            P("section", ("dp", "seq"), None),
        ),
        check_vma=False,
    )
```

```python
import functools
import math

import jax
import jax.numpy as jnp
from jax import lax
from jax.experimental import pallas as pl
from jax.experimental.pallas import tpu as pltpu
from jax.sharding import PartitionSpec as P

HEAD_DIM = 64
GROUPS = 16
TAPS = 128


EPS = 1e-05
NEG = -1e30


def padded_2(block, sides, width):
    for axis, dim in sides:
        count = lax.axis_size(axis)
        forward = [(i, i + 1) for i in range(count - 1)]
        backward = [(target, source) for source, target in forward]
        low = lax.ppermute(
            lax.slice_in_dim(block, block.shape[dim] - width, None, axis=dim), axis, forward
        )
        high = lax.ppermute(lax.slice_in_dim(block, 0, width, axis=dim), axis, backward)
        block = jnp.concatenate([low, block, high], axis=dim)
    return block


def from_behind(value, axis, steps):
    count = lax.axis_size(axis)
    first, last = (max(0, -steps), min(count, count - steps))
    return lax.ppermute(value, axis, [(source, source + steps) for source in range(first, last)])


def normalize(values, gain):
    average = jnp.mean(values, axis=-1, keepdims=True)
    centred = values - average
    spread = jnp.mean(centred * centred, axis=-1, keepdims=True)
    return centred * lax.rsqrt(spread + EPS) * gain


def smooth(values):
    return jax.nn.gelu(values, approximate=False)


def conv_taps(padded, kernel, frames):
    width_all = padded.shape[1]
    per_group = width_all // GROUPS
    tap_step = math.gcd(TAPS, 16)
    weight_view = kernel.reshape(TAPS, per_group, GROUPS, per_group)
    running = jnp.zeros((frames, GROUPS, per_group), jnp.float32)
    for first_tap in range(0, TAPS, tap_step):
        windows = jnp.stack(
            [padded[first_tap + offset : first_tap + offset + frames] for offset in range(tap_step)]
        )
        windows = windows.reshape(tap_step, frames, GROUPS, per_group)
        running = running + jnp.einsum(
            "jtgc,jcgo->tgo",
            windows,
            weight_view[first_tap : first_tap + tap_step],
            preferred_element_type=jnp.float32,
        )
    return running.reshape(frames, width_all)


def conv_input_grad(grad_pad, kernel, frames):
    width_all = grad_pad.shape[1]
    per_group = width_all // GROUPS
    tap_step = math.gcd(TAPS, 16)
    weight_view = kernel.reshape(TAPS, per_group, GROUPS, per_group)
    running = jnp.zeros((frames, GROUPS, per_group), jnp.float32)
    for first_tap in range(0, TAPS, tap_step):
        back_windows = jnp.stack(
            [
                grad_pad[TAPS - first_tap - offset : TAPS - first_tap - offset + frames]
                for offset in range(tap_step)
            ]
        )
        back_windows = back_windows.reshape(tap_step, frames, GROUPS, per_group)
        running = running + jnp.einsum(
            "jtgo,jcgo->tgc",
            back_windows,
            weight_view[first_tap : first_tap + tap_step],
            preferred_element_type=jnp.float32,
        )
    return running.reshape(frames, width_all)


def conv_kernel_grad(padded_all, grad_all):
    step_count, frames, width_all = grad_all.shape
    per_group = width_all // GROUPS
    tap_step = math.gcd(TAPS, 16)
    grad_view = grad_all.reshape(step_count * frames, GROUPS, per_group)
    kernel_parts = []
    for first_tap in range(0, TAPS, tap_step):
        windows = jnp.stack(
            [
                padded_all[:, first_tap + offset : first_tap + offset + frames]
                for offset in range(tap_step)
            ]
        )
        windows = windows.reshape(tap_step, step_count * frames, GROUPS, per_group)
        kernel_parts.append(
            jnp.einsum("jtgc,tgo->jcgo", windows, grad_view, preferred_element_type=jnp.float32)
        )
    return jnp.concatenate(kernel_parts, axis=0).reshape(TAPS * per_group, width_all)


def score_block(query_heads, key_block, query_segs, key_segs, factor):
    scores = (
        jnp.einsum("qhd,khd->hqk", query_heads, key_block, preferred_element_type=jnp.float32)
        * factor
    )
    allowed = (query_segs[:, None] == key_segs[None, :])[None]
    return (scores, allowed)


def front(layer_in, weights, kernel, conv_shift, first_section):
    frames, width_all = layer_in.shape
    padded = padded_2(layer_in, (("seq", 0),), TAPS // 2)
    conv_pre = lax.cond(
        first_section,
        lambda: conv_taps(padded, kernel, frames) + conv_shift.astype(jnp.float32),
        lambda: jnp.zeros((frames, width_all), jnp.float32),
    )
    conv_val, conv_pull = jax.vjp(smooth, conv_pre)
    resid_one = layer_in.astype(jnp.float32) + conv_val
    normed_val, norm_pull = jax.vjp(normalize, resid_one, weights[0].astype(jnp.float32))
    normed_one = normed_val.astype(jnp.bfloat16)
    packed = jnp.dot(normed_one, weights[1], preferred_element_type=jnp.float32).astype(
        jnp.bfloat16
    )
    return (padded, conv_pull, resid_one, norm_pull, normed_one, packed)


def tail(resid_one, attn_low, weights):
    resid_two = resid_one + jnp.dot(attn_low, weights[2], preferred_element_type=jnp.float32)
    normed_val, norm_pull = jax.vjp(normalize, resid_two, weights[3].astype(jnp.float32))
    normed_two = normed_val.astype(jnp.bfloat16)
    hidden_pre = jnp.dot(normed_two, weights[4], preferred_element_type=jnp.float32)
    hidden_val, gelu_pull = jax.vjp(smooth, hidden_pre)
    hidden_low = hidden_val.astype(jnp.bfloat16)
    result = resid_two + jnp.dot(hidden_low, weights[5], preferred_element_type=jnp.float32)
    return (result, norm_pull, normed_two, gelu_pull, hidden_low)


def key_loop(keys_all, values_all, segment_row, head_count, visit, initial):
    total_rows = keys_all.shape[0]
    block_rows = math.gcd(total_rows, 512)

    def one_block(block_index, running):
        offset = block_index * block_rows
        key_block = lax.dynamic_slice_in_dim(keys_all, offset, block_rows, 0).reshape(
            block_rows, head_count, HEAD_DIM
        )
        value_block = lax.dynamic_slice_in_dim(values_all, offset, block_rows, 0).reshape(
            block_rows, head_count, HEAD_DIM
        )
        key_segs = lax.dynamic_slice_in_dim(segment_row, offset, block_rows, 0)
        return visit(running, key_block, value_block, key_segs)

    return lax.fori_loop(0, total_rows // block_rows, one_block, initial)


def layer_forward(
    layer_in, segment_row, weights, kernel, conv_shift, first_section, my_start, factor
):
    frames, width_all = layer_in.shape
    head_count = width_all // HEAD_DIM
    padded, conv_pull, resid_one, norm_pull, normed_one, packed = front(
        layer_in, weights, kernel, conv_shift, first_section
    )
    query_heads = packed[:, :width_all].reshape(frames, head_count, HEAD_DIM)
    query_segs = lax.dynamic_slice_in_dim(segment_row, my_start, frames, 0)
    initial = (
        jnp.full((head_count, frames), NEG, jnp.float32),
        jnp.zeros((head_count, frames), jnp.float32),
        jnp.zeros((head_count, frames, HEAD_DIM), jnp.float32),
    )
    key_piece = lax.all_gather(packed[:, width_all : 2 * width_all], "seq", axis=0, tiled=True)
    value_piece = lax.all_gather(packed[:, 2 * width_all :], "seq", axis=0, tiled=True)
    piece_rows = key_piece.shape[0]
    block_rows = math.gcd(piece_rows, 512)

    def one_block(block_index, running):
        run_max, run_sum, run_acc = running
        offset = block_index * block_rows
        key_block = lax.dynamic_slice_in_dim(key_piece, offset, block_rows, 0).reshape(
            block_rows, head_count, HEAD_DIM
        )
        value_block = lax.dynamic_slice_in_dim(value_piece, offset, block_rows, 0).reshape(
            block_rows, head_count, HEAD_DIM
        )
        key_segs = lax.dynamic_slice_in_dim(segment_row, offset, block_rows, 0)
        scores, allowed = score_block(query_heads, key_block, query_segs, key_segs, factor)
        masked = jnp.where(allowed, scores, NEG)
        new_max = jnp.maximum(run_max, jnp.max(masked, axis=-1))
        weights_now = jnp.where(allowed, jnp.exp(masked - new_max[..., None]), 0.0)
        rescale = jnp.exp(run_max - new_max)
        run_sum = run_sum * rescale + jnp.sum(weights_now, axis=-1)
        run_acc = run_acc * rescale[..., None] + jnp.einsum(
            "hqk,khd->hqd",
            weights_now.astype(jnp.bfloat16),
            value_block,
            preferred_element_type=jnp.float32,
        )
        return (new_max, run_sum, run_acc)

    run_max, run_sum, run_acc = lax.fori_loop(0, piece_rows // block_rows, one_block, initial)
    log_total = run_max + jnp.log(run_sum)
    mixture = run_acc / run_sum[..., None]
    attn_low = jnp.transpose(mixture, (1, 0, 2)).reshape(frames, width_all).astype(jnp.bfloat16)
    result, norm_two_pull, normed_two, gelu_pull, hidden_low = tail(resid_one, attn_low, weights)
    kept = (
        padded,
        conv_pull,
        norm_pull,
        normed_one,
        packed,
        log_total,
        mixture,
        attn_low,
        norm_two_pull,
        normed_two,
        gelu_pull,
        hidden_low,
        segment_row,
    )
    return (result, kept)


def layer_backward(kept, grad_out, weights, kernel, first_section, my_start, factor):
    (
        padded,
        conv_pull,
        norm_one_pull,
        normed_one,
        packed,
        log_total,
        mixture,
        attn_low,
        norm_two_pull,
        normed_two,
        gelu_pull,
        hidden_low,
        segment_row,
    ) = kept
    frames, width_all = normed_one.shape
    head_count = width_all // HEAD_DIM
    query_heads = packed[:, :width_all].reshape(frames, head_count, HEAD_DIM)
    key_local = packed[:, width_all : 2 * width_all]
    value_local = packed[:, 2 * width_all :]
    query_segs = lax.dynamic_slice_in_dim(segment_row, my_start, frames, 0)
    keys_all, values_all = (
        lax.all_gather(key_local, "seq", axis=0, tiled=True),
        lax.all_gather(value_local, "seq", axis=0, tiled=True),
    )

    def chances_for(key_block, key_segs):
        scores, allowed = score_block(query_heads, key_block, query_segs, key_segs, factor)
        return jnp.where(
            allowed, jnp.exp(jnp.where(allowed, scores, NEG) - log_total[..., None]), 0.0
        )

    branch_grad = grad_out.astype(jnp.bfloat16)
    hidden_grad = jnp.einsum(
        "to,io->ti", branch_grad, weights[5], preferred_element_type=jnp.float32
    )
    pre_grad = gelu_pull(hidden_grad)[0].astype(jnp.bfloat16)
    normed_two_grad = jnp.einsum(
        "tf,if->ti", pre_grad, weights[4], preferred_element_type=jnp.float32
    )
    resid_two_grad, grad_gain_two = norm_two_pull(normed_two_grad)
    resid_two_grad = resid_two_grad + grad_out
    attn_branch_grad = resid_two_grad.astype(jnp.bfloat16)
    attended_grad = jnp.einsum(
        "to,io->ti", attn_branch_grad, weights[2], preferred_element_type=jnp.float32
    ).astype(jnp.bfloat16)
    dout_heads = attended_grad.reshape(frames, head_count, HEAD_DIM)
    delta_rows = jnp.einsum("qhd,hqd->hq", dout_heads.astype(jnp.float32), mixture)

    def visit_query(running, key_block, value_block, key_segs):
        chances = chances_for(key_block, key_segs)
        prob_grad = jnp.einsum(
            "qhd,khd->hqk", dout_heads, value_block, preferred_element_type=jnp.float32
        )
        score_grad = (chances * (prob_grad - delta_rows[..., None])).astype(jnp.bfloat16)
        return running + jnp.einsum(
            "hqk,khd->qhd", score_grad, key_block, preferred_element_type=jnp.float32
        )

    grad_query = (
        key_loop(
            keys_all,
            values_all,
            segment_row,
            head_count,
            visit_query,
            jnp.zeros((frames, head_count, HEAD_DIM), jnp.float32),
        )
        * factor
    )
    row_stats = (
        lax.all_gather(log_total, "seq", axis=1, tiled=True),
        lax.all_gather(delta_rows, "seq", axis=1, tiled=True),
    )
    key_heads = key_local.reshape(frames, head_count, HEAD_DIM)
    value_heads = value_local.reshape(frames, head_count, HEAD_DIM)
    start_acc = (
        jnp.zeros((frames, head_count, HEAD_DIM), jnp.float32),
        jnp.zeros((frames, head_count, HEAD_DIM), jnp.float32),
    )
    query_piece = lax.all_gather(packed[:, :width_all], "seq", axis=0, tiled=True)
    dout_piece = lax.all_gather(attended_grad, "seq", axis=0, tiled=True)
    piece_rows = query_piece.shape[0]
    block_rows = math.gcd(piece_rows, 512)

    def one_block(block_index, running):
        key_acc, value_acc = running
        offset = block_index * block_rows
        query_block = lax.dynamic_slice_in_dim(query_piece, offset, block_rows, 0).reshape(
            block_rows, head_count, HEAD_DIM
        )
        dout_block = lax.dynamic_slice_in_dim(dout_piece, offset, block_rows, 0).reshape(
            block_rows, head_count, HEAD_DIM
        )
        seg_block = lax.dynamic_slice_in_dim(segment_row, offset, block_rows, 0)
        total_block = lax.dynamic_slice_in_dim(row_stats[0], offset, block_rows, 1)
        delta_block = lax.dynamic_slice_in_dim(row_stats[1], offset, block_rows, 1)
        scores, allowed = score_block(query_block, key_heads, seg_block, query_segs, factor)
        chances = jnp.where(
            allowed, jnp.exp(jnp.where(allowed, scores, NEG) - total_block[..., None]), 0.0
        )
        prob_grad = jnp.einsum(
            "qhd,khd->hqk", dout_block, value_heads, preferred_element_type=jnp.float32
        )
        score_grad = (chances * (prob_grad - delta_block[..., None])).astype(jnp.bfloat16)
        key_acc = (
            key_acc
            + jnp.einsum(
                "hqk,qhd->khd", score_grad, query_block, preferred_element_type=jnp.float32
            )
            * factor
        )
        value_acc = value_acc + jnp.einsum(
            "hqk,qhd->khd",
            chances.astype(jnp.bfloat16),
            dout_block,
            preferred_element_type=jnp.float32,
        )
        return (key_acc, value_acc)

    key_acc, value_acc = lax.fori_loop(0, piece_rows // block_rows, one_block, start_acc)
    grad_key = key_acc.reshape(frames, width_all)
    grad_value = value_acc.reshape(frames, width_all)
    packed_grad = jnp.concatenate(
        [grad_query.reshape(frames, width_all), grad_key, grad_value], axis=1
    ).astype(jnp.bfloat16)
    normed_one_grad = jnp.einsum(
        "tj,ij->ti", packed_grad, weights[1], preferred_element_type=jnp.float32
    )
    resid_one_grad, grad_gain_one = norm_one_pull(normed_one_grad)
    resid_one_grad = resid_one_grad + resid_two_grad
    conv_grad = jnp.where(first_section, conv_pull(resid_one_grad)[0], 0.0).astype(jnp.bfloat16)
    grad_pad = padded_2(conv_grad, (("seq", 0),), TAPS // 2)
    back_sum = lax.cond(
        first_section,
        lambda: conv_input_grad(grad_pad, kernel, frames),
        lambda: jnp.zeros((frames, width_all), jnp.float32),
    )
    grad_in = resid_one_grad + back_sum
    products = (
        normed_one,
        packed_grad,
        attn_low,
        attn_branch_grad,
        normed_two,
        pre_grad,
        hidden_low,
        branch_grad,
        padded,
        conv_grad,
    )
    return (grad_in, (grad_gain_one, grad_gain_two), products)


def per_device(
    signal,
    frame_segment_index,
    conv_weight,
    conv_bias,
    norm1_gain,
    qkv_weight,
    out_weight,
    norm2_gain,
    up_weight,
    down_weight,
    cotangent,
):
    micro_count, frames, width_all = signal.shape
    factor = 1.0 / math.sqrt(HEAD_DIM)
    first_section = lax.axis_index("section") == 0
    my_start = lax.axis_index("seq") * frames
    gathered = (
        lax.all_gather(norm1_gain.astype(jnp.bfloat16), ("dp", "seq"), axis=1, tiled=True),
        lax.all_gather(qkv_weight.astype(jnp.bfloat16), ("dp", "seq"), axis=1, tiled=True),
        lax.all_gather(out_weight.astype(jnp.bfloat16), ("dp", "seq"), axis=1, tiled=True),
        lax.all_gather(norm2_gain.astype(jnp.bfloat16), ("dp", "seq"), axis=1, tiled=True),
        lax.all_gather(up_weight.astype(jnp.bfloat16), ("dp", "seq"), axis=1, tiled=True),
        lax.all_gather(down_weight.astype(jnp.bfloat16), ("dp", "seq"), axis=1, tiled=True),
    )
    weights = tuple((member[0] for member in gathered))
    kernel, conv_shift = (
        lax.all_gather(
            conv_weight.astype(jnp.bfloat16), ("section", "dp", "seq"), axis=0, tiled=True
        ),
        lax.all_gather(
            conv_bias.astype(jnp.bfloat16), ("section", "dp", "seq"), axis=0, tiled=True
        ),
    )
    received = jnp.zeros((frames, width_all), jnp.bfloat16)
    saved = []
    forward_outs = []
    for step_index in range(micro_count + 1):
        own_index = min(step_index, micro_count - 1)
        prior_index = max(step_index - 1, 0)
        layer_in = jnp.where(first_section, signal[own_index], received)
        segment_row = jnp.where(
            first_section, frame_segment_index[own_index], frame_segment_index[prior_index]
        )
        result, kept = layer_forward(
            layer_in, segment_row, weights, kernel, conv_shift, first_section, my_start, factor
        )
        saved.append(kept)
        forward_outs.append(result)
        if step_index < micro_count:
            received = from_behind(result.astype(jnp.bfloat16), "section", 1)
    received_back = jnp.zeros((frames, width_all), jnp.bfloat16)
    input_grads = []
    gain_totals = None
    product_list = []
    for step_index in range(micro_count + 1):
        kept = saved[micro_count - step_index]
        if step_index < micro_count:
            top_grad = cotangent[micro_count - 1 - step_index].astype(jnp.float32)
        else:
            top_grad = jnp.zeros((frames, width_all), jnp.float32)
        incoming = jnp.where(first_section, received_back.astype(jnp.float32), top_grad)
        grad_in, gain_grads, products = layer_backward(
            kept, incoming, weights, kernel, first_section, my_start, factor
        )
        input_grads.append(grad_in)
        product_list.append(products)
        if gain_totals is None:
            gain_totals = gain_grads
        else:
            gain_totals = (gain_totals[0] + gain_grads[0], gain_totals[1] + gain_grads[1])
        if step_index < micro_count:
            received_back = from_behind(grad_in.astype(jnp.bfloat16), "section", -1)

    def joined(position):
        return jnp.concatenate([member[position] for member in product_list], axis=0)

    grad_qkv = jnp.einsum("ti,tj->ij", joined(0), joined(1), preferred_element_type=jnp.float32)
    grad_out_weight = jnp.einsum(
        "ti,to->io", joined(2), joined(3), preferred_element_type=jnp.float32
    )
    grad_up = jnp.einsum("ti,tf->if", joined(4), joined(5), preferred_element_type=jnp.float32)
    grad_down = jnp.einsum("ti,to->io", joined(6), joined(7), preferred_element_type=jnp.float32)
    padded_all = jnp.stack([member[8] for member in product_list])
    conv_grad_all = jnp.stack([member[9] for member in product_list])
    kernel_grad = conv_kernel_grad(padded_all, conv_grad_all)
    bias_grad = jnp.sum(joined(9).astype(jnp.float32), axis=0)
    ends = jnp.stack(
        [
            jnp.where(
                first_section, input_grads[micro_count - mb_index], forward_outs[mb_index + 1]
            )
            for mb_index in range(micro_count)
        ]
    )[None]
    layer_sums = (
        lax.psum_scatter(gain_totals[0][None], ("dp", "seq"), scatter_dimension=1, tiled=True),
        lax.psum_scatter(grad_qkv[None], ("dp", "seq"), scatter_dimension=1, tiled=True),
        lax.psum_scatter(grad_out_weight[None], ("dp", "seq"), scatter_dimension=1, tiled=True),
        lax.psum_scatter(gain_totals[1][None], ("dp", "seq"), scatter_dimension=1, tiled=True),
        lax.psum_scatter(grad_up[None], ("dp", "seq"), scatter_dimension=1, tiled=True),
        lax.psum_scatter(grad_down[None], ("dp", "seq"), scatter_dimension=1, tiled=True),
    )
    conv_sums = (
        lax.psum_scatter(kernel_grad, ("section", "dp", "seq"), scatter_dimension=0, tiled=True),
        lax.psum_scatter(bias_grad, ("section", "dp", "seq"), scatter_dimension=0, tiled=True),
    )
    return (
        ends,
        conv_sums[0],
        conv_sums[1],
        layer_sums[0],
        layer_sums[1],
        layer_sums[2],
        layer_sums[3],
        layer_sums[4],
        layer_sums[5],
    )


def swap_section(value):
    return lax.ppermute(value, "section", [(0, 1), (1, 0)])


def swap_x(value):
    return lax.ppermute(value, "seq", [(q, q ^ 1) for q in range(4)])


def pair_sum(low, behind=None):
    other = swap_x(low)
    if behind is not None:
        other, _ = lax.optimization_barrier((other, behind))
    return low.astype(jnp.float32) + other.astype(jnp.float32)


def after(first, second):
    return lax.optimization_barrier((first, second))


def choose(flag, first, second):
    return jnp.where(flag, first, second), jnp.where(flag, second, first)


def sum_dp(blocks, dp, meanwhile):
    count = lax.axis_size("dp")
    f32, bf16 = jnp.float32, jnp.bfloat16
    meanwhile = list(meanwhile)

    def block(index):
        return lax.dynamic_index_in_dim(blocks, jnp.clip(index, 0, count - 1), 0, keepdims=False)

    running = [None, None]
    for turn, distance in enumerate(range(count - 1, 0, -1)):
        for way, sign in enumerate((1, -1)):
            own = block(dp + sign * distance)
            if running[way] is not None:
                own = (own.astype(f32) + running[way].astype(f32)).astype(bf16)
            live = [(i, i + sign) for i in range(count) if 0 <= i + sign < count and 0 <= i + sign * distance < count]
            running[way] = lax.ppermute(own, "dp", live)
        if turn < len(meanwhile):
            running, meanwhile[turn] = after(running, meanwhile[turn])
            running = list(running)
    total = block(dp).astype(f32) + running[0].astype(f32) + running[1].astype(f32)
    return total.astype(bf16), meanwhile


def line_groups():
    count = lax.axis_size("dp")
    return [
        [(s * count + d) * 4 + 2 * y + x for d in range(count) for y in range(2) for s in range(2)]
        for x in range(2)
    ]


def gather_rows(piece):
    return lax.all_gather(
        piece, ("section", "dp", "seq"), axis=0, tiled=True, axis_index_groups=line_groups()
    )


def scatter_rows(partial):
    return lax.psum_scatter(
        partial, ("section", "dp", "seq"), scatter_dimension=0, tiled=True,
        axis_index_groups=line_groups(),
    )


MESH = pl.DeviceIdType.MESH


def opening_kernel(
    dp_count, parts, conv_ref, signal_ref, keep_ref, send_ref, rest_ref,
    conv_out, signal_out, whole_out, second_out,
    local_sem, a2a_send, a2a_recv, sig_send, sig_recv, line_send, line_recv, own_send, column_recv, rest_recv,
    up_send, up_recv, y_send, y_recv, core_send, core_recv,
):
    sec, dp, seq = (lax.axis_index(name) for name in ("section", "dp", "seq"))
    me = sec * 4 + seq
    x, y = seq % 2, seq // 2
    partner_x = (seq + 1 - 2 * x) % 4
    partner_y = {"seq": (seq + 2) % 4}
    sibling = {"section": 1 - sec}
    has_up, has_down = dp < dp_count - 1, dp > 0
    split = keep_ref.shape[1]
    rows = keep_ref.shape[0] // parts

    barrier = pltpu.get_barrier_semaphore()
    for turn in range(1, 8):
        other = (me + turn) % 8
        pl.semaphore_signal(
            barrier, inc=1, device_id={"section": other // 4, "seq": other % 4}, device_id_type=MESH
        )
    for there, step in ((has_up, 1), (has_down, -1)):

        @pl.when(there)
        def _(step=step):
            pl.semaphore_signal(barrier, inc=1, device_id={"dp": dp + step}, device_id_type=MESH)

    pl.semaphore_wait(barrier, 7 + jnp.where(has_up, 1, 0) + jnp.where(has_down, 1, 0))

    def remote(source, target, send, recv, device):
        return pltpu.make_async_remote_copy(
            src_ref=source, dst_ref=target, send_sem=send, recv_sem=recv,
            device_id=device, device_id_type=MESH,
        )

    def a2a(target, source):
        return remote(
            conv_ref.at[target], conv_out.at[dp, source], a2a_send.at[target], a2a_recv.at[source],
            {"section": target // 4, "seq": target % 4},
        )

    def sig(target, source):
        return remote(
            signal_ref.at[target], signal_out.at[source], sig_send.at[target], sig_recv.at[source],
            {"seq": target},
        )

    for turn in range(1, 8):
        a2a((me + turn) % 8, me).start()
    conv_local = pltpu.make_async_copy(conv_ref.at[me], conv_out.at[dp, me], local_sem.at[0])
    signal_local = pltpu.make_async_copy(signal_ref.at[seq], signal_out.at[seq], local_sem.at[1])
    conv_local.start()
    signal_local.start()

    def columns(layer, half):
        return (second_out if layer else whole_out.at[dp, y, half]).at[:, pl.ds(0, split)]

    def others(layer, half):
        return (second_out if layer else whole_out.at[dp, y, half]).at[:, pl.ds(split, rest_ref.shape[2])]

    class Layer:
        def __init__(self, layer):
            far = {"section": 1 - layer}
            self.mine = sec == layer
            self.even = x == layer
            received = column_recv.at[layer]
            self.keep_local = pltpu.make_async_copy(keep_ref, columns(layer, layer), local_sem.at[2])
            self.rest_local = pltpu.make_async_copy(rest_ref.at[layer], others(layer, layer), local_sem.at[3])
            self.keep_far = remote(keep_ref, columns(layer, 1 - layer), own_send.at[0], received, far)
            self.send_same = remote(
                send_ref, columns(layer, layer), own_send.at[1], received, {"seq": partner_x}
            )
            self.send_cross = remote(
                send_ref, columns(layer, 1 - layer), own_send.at[1], received, {**far, "seq": partner_x}
            )
            self.rest_far = remote(
                rest_ref.at[1 - layer], others(layer, 1 - layer), own_send.at[2], rest_recv.at[layer], far
            )

        def start(self):
            @pl.when(self.mine & self.even)
            def _():
                self.send_same.start()
                self.keep_local.start()

            @pl.when(self.mine & jnp.logical_not(self.even))
            def _():
                self.send_cross.start()
                self.keep_far.start()

            @pl.when(self.mine)
            def _():
                self.rest_far.start()
                self.rest_local.start()

        def wait(self):
            other = jnp.logical_not(self.mine)
            odd = jnp.logical_not(self.even)

            @pl.when(self.mine & self.even)
            def _():
                self.keep_local.wait()

            @pl.when(self.mine & odd)
            def _():
                self.send_same.wait_recv()

            @pl.when(self.mine)
            def _():
                self.rest_local.wait()

            @pl.when(other & self.even)
            def _():
                self.send_cross.wait_recv()

            @pl.when(other & odd)
            def _():
                self.keep_far.wait_recv()

            @pl.when(other)
            def _():
                self.rest_far.wait_recv()

        def finish(self):
            @pl.when(self.mine & self.even)
            def _():
                self.send_same.wait_send()

            @pl.when(self.mine & jnp.logical_not(self.even))
            def _():
                self.send_cross.wait_send()
                self.keep_far.wait_send()

            @pl.when(self.mine)
            def _():
                self.rest_far.wait_send()

    layers = [Layer(0), Layer(1)]
    for layer in layers:
        layer.start()
    for turn in range(1, 4):
        sig((seq + turn) % 4, seq).start()

    def line(slot, direction):
        index = (direction + 1) // 2
        return remote(
            conv_out.at[slot], conv_out.at[slot], line_send.at[index, slot], line_recv.at[slot],
            {"dp": dp + direction},
        )

    def place(slot, row, half, part):
        return whole_out.at[slot, row, half, pl.ds(part * rows, rows)]

    def along(slot, direction, part):
        index = (direction + 1) // 2
        ref = place(slot, y, sec, part)
        return remote(
            ref, ref, up_send.at[index, slot, part], up_recv.at[slot, part], {"dp": dp + direction}
        )

    def across(slot, row, part):
        ref = place(slot, row, sec, part)
        return remote(ref, ref, y_send.at[slot, part], y_recv.at[slot, part], partner_y)

    def to_core(slot, row, half, part):
        ref = place(slot, row, half, part)
        return remote(
            ref, ref, core_send.at[slot, row, part], core_recv.at[slot, row, part], sibling
        )

    for turn in range(1, 8):
        a2a((me + turn) % 8, (me + turn) % 8).wait_recv()
    conv_local.wait()
    for there, direction in ((has_up, 1), (has_down, -1)):

        @pl.when(there)
        def _(direction=direction):
            line(dp, direction).start()

    layers[0].wait()
    for part in range(parts):
        for there, direction in ((has_up, 1), (has_down, -1)):

            @pl.when(there)
            def _(direction=direction, part=part):
                along(dp, direction, part).start()

        across(dp, y, part).start()
        to_core(dp, y, sec, part).start()

    def stage(distance):
        arrivals = []
        for direction in (1, -1):
            slot = dp - direction * distance
            arrives = (slot >= 0) & (slot < dp_count)
            goes_on = arrives & (has_up if direction == 1 else has_down)
            arrivals.append((direction, slot, arrives, goes_on))

            @pl.when(arrives)
            def _(slot=slot, direction=direction):
                line(slot, direction).wait_recv()

            @pl.when(goes_on)
            def _(slot=slot, direction=direction):
                line(slot, direction).start()

        for part in range(parts):
            for direction, slot, arrives, goes_on in arrivals:

                @pl.when(arrives)
                def _(slot=slot, direction=direction, part=part):
                    along(slot, direction, part).wait_recv()

                @pl.when(goes_on)
                def _(slot=slot, direction=direction, part=part):
                    along(slot, direction, part).start()

                @pl.when(arrives)
                def _(slot=slot, part=part):
                    across(slot, y, part).start()
                    to_core(slot, y, sec, part).start()

    def pass_crossed(distance):
        for part in range(parts):
            for sign in (1, -1) if distance else (1,):
                slot = dp - sign * distance

                @pl.when((slot >= 0) & (slot < dp_count))
                def _(slot=slot, part=part):
                    across(slot, 1 - y, part).wait_recv()
                    to_core(slot, 1 - y, sec, part).start()

    for distance in range(1, dp_count):
        stage(distance)
        pass_crossed(distance - 1)
    pass_crossed(dp_count - 1)

    for slot in range(dp_count):
        for part in range(parts):
            for row in range(2):
                to_core(slot, row, 1 - sec, part).wait_recv()
                to_core(slot, row, sec, part).wait_send()
            across(slot, y, part).wait_send()
        for direction in (1, -1):
            sent = (slot <= dp if direction == 1 else slot >= dp) & (has_up if direction == 1 else has_down)

            @pl.when(sent)
            def _(slot=slot, direction=direction):
                line(slot, direction).wait_send()
                for part in range(parts):
                    along(slot, direction, part).wait_send()

    layers[1].wait()
    for layer in layers:
        layer.finish()
    for turn in range(1, 8):
        a2a((me + turn) % 8, me).wait_send()
    for turn in range(1, 4):
        sig((seq + turn) % 4, (seq + turn) % 4).wait_recv()
        sig((seq + turn) % 4, seq).wait_send()
    signal_local.wait()


def opening(conv_send, signal_send, keep, send, rest):
    count = lax.axis_size("dp")
    parts = 2
    rows, columns = keep.shape[0], keep.shape[1] + rest.shape[2]
    anywhere = pl.BlockSpec(memory_space=pl.ANY)
    dma = pltpu.SemaphoreType.DMA
    conv_all, signal_all, whole, second = pl.pallas_call(
        functools.partial(opening_kernel, count, parts),
        in_specs=[anywhere] * 5,
        out_specs=[anywhere] * 4,
        out_shape=[
            jax.ShapeDtypeStruct((count, *conv_send.shape), conv_send.dtype),
            jax.ShapeDtypeStruct(signal_send.shape, signal_send.dtype),
            jax.ShapeDtypeStruct((count, 2, 2, rows, columns), keep.dtype),
            jax.ShapeDtypeStruct((rows, columns), keep.dtype),
        ],
        scratch_shapes=[
            dma((4,)), dma((8,)), dma((8,)), dma((4,)), dma((4,)), dma((2, count)), dma((count,)),
            dma((3,)), dma((2,)), dma((2,)), dma((2, count, parts)), dma((count, parts)), dma((count, parts)),
            dma((count, parts)), dma((count, 2, parts)), dma((count, 2, parts)),
        ],
        compiler_params=pltpu.CompilerParams(
            collective_id=0, has_side_effects=True, vmem_limit_bytes=4 * 1024 * 1024
        ),
        name="opening",
    )(conv_send, signal_send, keep, send, rest)
    return conv_all, signal_all, whole.reshape(-1, columns), second


def norm_stats(values):
    average = jnp.mean(values, axis=-1, keepdims=True)
    centred = values - average
    spread = jnp.mean(centred * centred, axis=-1, keepdims=True)
    return centred, lax.rsqrt(spread + EPS)


def norm_back(values, gain, grad):
    centred, inv = norm_stats(values)
    unit = centred * inv
    gain_grad = jnp.sum(grad * unit, axis=0)
    f = grad * gain
    mean_f = jnp.mean(f, axis=-1, keepdims=True)
    mean_fu = jnp.mean(f * unit, axis=-1, keepdims=True)
    return (f - mean_f - unit * mean_fu) * inv, gain_grad


def gelu_slope(values):
    cdf = 0.5 * (1.0 + lax.erf(values * (1.0 / math.sqrt(2.0))))
    pdf = jnp.exp(-0.5 * values * values) * (1.0 / math.sqrt(2.0 * math.pi))
    return cdf + values * pdf


def attention_forward_kernel(factor, q_ref, k_ref, v_ref, qs_ref, ks_ref, o_ref, lse_ref):
    queries = q_ref[...]
    lane = lax.broadcasted_iota(jnp.int32, queries.shape, 1)
    allowed = qs_ref[...] == ks_ref[...]
    keys = k_ref[...]
    values = v_ref[...]
    outs = []
    for head in range(2):
        mine = (lane < HEAD_DIM) if head == 0 else (lane >= HEAD_DIM)
        own = jnp.where(mine, queries, jnp.zeros_like(queries))
        scores = lax.dot_general(
            own, keys, (((1,), (1,)), ((), ())), preferred_element_type=jnp.float32
        ) * factor
        scores = jnp.where(allowed, scores, NEG)
        top = jnp.max(scores, axis=-1, keepdims=True)
        raised = jnp.exp(scores - top)
        total = jnp.sum(raised, axis=-1, keepdims=True)
        chances = (raised * (1.0 / total)).astype(jnp.bfloat16)
        outs.append(jnp.dot(chances, values, preferred_element_type=jnp.float32))
        lse_ref[0, head] = top + jnp.log(total)
    o_ref[...] = jnp.where(lane < HEAD_DIM, outs[0], outs[1]).astype(o_ref.dtype)


def attention_forward(packed, kv_all, query_segs, key_segs, factor):
    frames = packed.shape[0]
    keys = kv_all.shape[0]
    width = packed.shape[1] // 3
    pairs = width // 128
    rows = math.gcd(frames, 256)
    return pl.pallas_call(
        functools.partial(attention_forward_kernel, factor),
        grid=(pairs, frames // rows),
        in_specs=[
            pl.BlockSpec((rows, 128), lambda h, i: (i, h)),
            pl.BlockSpec((keys, 128), lambda h, i: (0, h)),
            pl.BlockSpec((keys, 128), lambda h, i: (0, pairs + h)),
            pl.BlockSpec((rows, 1), lambda h, i: (i, 0)),
            pl.BlockSpec((1, keys), lambda h, i: (0, 0)),
        ],
        out_specs=[
            pl.BlockSpec((rows, 128), lambda h, i: (i, h)),
            pl.BlockSpec((1, 2, rows, 1), lambda h, i: (h, 0, i, 0)),
        ],
        out_shape=[
            jax.ShapeDtypeStruct((frames, width), jnp.bfloat16),
            jax.ShapeDtypeStruct((pairs, 2, frames, 1), jnp.float32),
        ],
        compiler_params=pltpu.CompilerParams(vmem_limit_bytes=40 * 1024 * 1024),
        cost_estimate=pl.CostEstimate(
            flops=4 * frames * keys * width * 2,
            bytes_accessed=2 * (frames * width * 2 + keys * width * 2),
            transcendentals=frames * keys * (width // HEAD_DIM),
        ),
        name="attention_forward",
    )(packed, kv_all, kv_all, query_segs[:, None], key_segs[None, :])


def attention_backward_kernel(
    factor, q_ref, k_ref, v_ref, g_ref, o_ref, lse_ref, qs_ref, ks_ref, *rest
):
    *begin, dq_ref, dk_ref, dv_ref = rest
    step = pl.program_id(1)

    @pl.when(step == 0)
    def _():
        for index, total_ref in enumerate((dk_ref, dv_ref)):
            total_ref[...] = begin[index][...] if begin else jnp.zeros_like(total_ref)

    queries = q_ref[...]
    grads = g_ref[...]
    keys = k_ref[...]
    values = v_ref[...]
    lane = lax.broadcasted_iota(jnp.int32, queries.shape, 1)
    key_lane = lax.broadcasted_iota(jnp.int32, keys.shape, 1)
    allowed = qs_ref[...] == ks_ref[...]
    product = grads.astype(jnp.float32) * o_ref[...].astype(jnp.float32)
    dq = None
    for head in range(2):
        mine = (lane < HEAD_DIM) if head == 0 else (lane >= HEAD_DIM)
        key_mine = (key_lane < HEAD_DIM) if head == 0 else (key_lane >= HEAD_DIM)
        own_q = jnp.where(mine, queries, jnp.zeros_like(queries))
        own_g = jnp.where(mine, grads, jnp.zeros_like(grads))
        own_k = jnp.where(key_mine, keys, jnp.zeros_like(keys))
        delta = jnp.sum(jnp.where(mine, product, 0.0), axis=-1, keepdims=True)
        scores = lax.dot_general(
            own_q, keys, (((1,), (1,)), ((), ())), preferred_element_type=jnp.float32
        ) * factor
        chances = jnp.exp(jnp.where(allowed, scores, NEG) - lse_ref[0, head])
        prob_grad = lax.dot_general(
            own_g, values, (((1,), (1,)), ((), ())), preferred_element_type=jnp.float32
        )
        score_grad = (chances * (prob_grad - delta)).astype(jnp.bfloat16)
        part = jnp.dot(score_grad, own_k, preferred_element_type=jnp.float32)
        dq = part if dq is None else dq + part
        dk_ref[...] += lax.dot_general(
            score_grad, own_q, (((0,), (0,)), ((), ())), preferred_element_type=jnp.float32
        ) * factor
        dv_ref[...] += lax.dot_general(
            chances.astype(jnp.bfloat16), own_g, (((0,), (0,)), ((), ())),
            preferred_element_type=jnp.float32,
        )
    dq_ref[...] = (dq * factor).astype(dq_ref.dtype)


def attention_backward(packed, kv_all, grads, attended, lse, query_segs, key_segs, factor, begin=None):
    frames = packed.shape[0]
    keys = kv_all.shape[0]
    width = packed.shape[1] // 3
    pairs = width // 128
    rows = math.gcd(frames, 256)
    return pl.pallas_call(
        functools.partial(attention_backward_kernel, factor),
        grid=(pairs, frames // rows),
        in_specs=[
            pl.BlockSpec((rows, 128), lambda h, i: (i, h)),
            pl.BlockSpec((keys, 128), lambda h, i: (0, h)),
            pl.BlockSpec((keys, 128), lambda h, i: (0, pairs + h)),
            pl.BlockSpec((rows, 128), lambda h, i: (i, h)),
            pl.BlockSpec((rows, 128), lambda h, i: (i, h)),
            pl.BlockSpec((1, 2, rows, 1), lambda h, i: (h, 0, i, 0)),
            pl.BlockSpec((rows, 1), lambda h, i: (i, 0)),
            pl.BlockSpec((1, keys), lambda h, i: (0, 0)),
        ]
        + [pl.BlockSpec((keys, 128), lambda h, i: (0, h))] * (2 if begin else 0),
        out_specs=[
            pl.BlockSpec((rows, 128), lambda h, i: (i, h)),
            pl.BlockSpec((keys, 128), lambda h, i: (0, h)),
            pl.BlockSpec((keys, 128), lambda h, i: (0, h)),
        ],
        out_shape=[
            jax.ShapeDtypeStruct((frames, width), jnp.bfloat16),
            jax.ShapeDtypeStruct((keys, width), jnp.float32),
            jax.ShapeDtypeStruct((keys, width), jnp.float32),
        ],
        compiler_params=pltpu.CompilerParams(vmem_limit_bytes=48 * 1024 * 1024),
        cost_estimate=pl.CostEstimate(
            flops=10 * frames * keys * width * 2,
            bytes_accessed=4 * (frames * width * 2 + keys * width * 2),
            transcendentals=frames * keys * (width // HEAD_DIM),
        ),
        name="attention_backward",
    )(packed, kv_all, kv_all, grads, attended, lse, query_segs[:, None], key_segs[None, :], *(begin or ()))


CONV_STEP = 4


def conv_bands(kernel, per_group):
    groups = kernel.shape[1] // per_group
    steps = TAPS // CONV_STEP + 1
    bands = []
    for group in range(groups):
        own = kernel[:, group * per_group : (group + 1) * per_group]
        shifted = [
            jnp.pad(own, ((shift * per_group, (CONV_STEP - shift) * per_group), (0, 0)))
            for shift in range(CONV_STEP)
        ]
        band = jnp.concatenate(shifted, axis=1)
        bands.append(band.reshape(steps, CONV_STEP * per_group, CONV_STEP * per_group))
    return bands


def group_view(values, per_group):
    rows, frames, width = values.shape
    return [
        values[:, :, g * per_group : (g + 1) * per_group].reshape(
            rows, frames // CONV_STEP, CONV_STEP * per_group
        )
        for g in range(width // per_group)
    ]


def ungroup(parts, per_group):
    rows, blocks, _ = parts[0].shape
    return jnp.concatenate(
        [part.reshape(rows, blocks * CONV_STEP, per_group) for part in parts], axis=2
    )


CONV_DIMS = ("NWC", "WIO", "NWC")


def conv_forward(views, bands):
    half = TAPS // 2 // CONV_STEP
    return [
        lax.conv_general_dilated(
            view, band, (1,), [(half, half)], dimension_numbers=CONV_DIMS,
            preferred_element_type=jnp.float32,
        )
        for view, band in zip(views, bands)
    ]


def conv_back(grad_views, bands):
    half = TAPS // 2 // CONV_STEP
    return [
        lax.conv_general_dilated(
            view, jnp.transpose(band[::-1], (0, 2, 1)), (1,), [(half, half)],
            dimension_numbers=CONV_DIMS, preferred_element_type=jnp.float32,
        )
        for view, band in zip(grad_views, bands)
    ]


def conv_taps_grad(views, grad_views, per_group):
    half = TAPS // 2 // CONV_STEP
    results = []
    for view, grad in zip(views, grad_views):
        band = lax.conv_general_dilated(
            view, grad, (1,), [(half, half)],
            dimension_numbers=("CWN", "IWO", "WNC"),
            preferred_element_type=jnp.float32,
        )
        flat = band.reshape(-1, CONV_STEP * per_group)
        total = None
        for shift in range(CONV_STEP):
            part = flat[
                shift * per_group : (shift + TAPS) * per_group,
                shift * per_group : (shift + 1) * per_group,
            ]
            total = part if total is None else total + part
        results.append(total)
    return jnp.concatenate(results, axis=1)


def to_column(vector, width):
    return jnp.pad(vector[:, None], ((0, 0), (0, width - 1)))


def per_device_pairs(
    signal, frame_segment_index, conv_weight, conv_bias, norm1_gain, qkv_weight, out_weight,
    norm2_gain, up_weight, down_weight, cotangent,
):
    micro_count, frames, width = signal.shape
    bf16, f32 = jnp.bfloat16, jnp.float32
    per_group = width // GROUPS
    dp_count = lax.axis_size("dp")
    factor = 1.0 / math.sqrt(HEAD_DIM)
    sec = lax.axis_index("section")
    dp = lax.axis_index("dp")
    seq = lax.axis_index("seq")
    x, y = seq % 2, seq // 2
    sec0, x0 = sec == 0, x == 0
    row_frames = 4 * frames
    half_frames = 2 * frames
    both = ("section", "seq")

    block_width = width // 8
    rows_here = conv_weight.shape[0]
    conv_low = conv_weight.astype(bf16).reshape(rows_here, 8, block_width)
    bias_low = jnp.pad(conv_bias.astype(bf16), (0, block_width - conv_bias.shape[0]))
    bias_rows = jnp.pad(
        jnp.broadcast_to(bias_low[None, None, :], (1, 8, block_width)), ((0, 15), (0, 0), (0, 0))
    )
    conv_send = jnp.transpose(jnp.concatenate([conv_low, bias_rows], axis=0), (1, 0, 2))

    own_half = jnp.where(sec0, signal[:, :, : width // 2], signal[:, :, width // 2 :])
    sig_send = jnp.transpose(own_half.reshape(micro_count, frames, 4, block_width), (2, 0, 1, 3))
    in_rows = qkv_weight.shape[1]
    unit = down_weight.shape[1] // 4
    qkv_view = qkv_weight[0].astype(bf16).reshape(in_rows, -1, 2, HEAD_DIM)
    qkv_parity = [qkv_view[:, :, p].reshape(in_rows, -1) for p in range(2)]
    up_view = up_weight[0].astype(bf16).reshape(in_rows, -1, 2, 2, 2, unit)
    up_parity = [
        jnp.transpose(up_view[:, :, p], (0, 3, 1, 2, 4)).reshape(in_rows, -1) for p in range(2)
    ]
    qkv_cols, up_cols = qkv_parity[0].shape[1], up_parity[0].shape[1]
    col_one = to_column(norm1_gain[0].astype(bf16), 128)
    col_two = to_column(norm2_gain[0].astype(bf16), 128)
    cut = qkv_cols + 128
    keep_cols, send_cols = [
        jnp.concatenate([a, col_one, b, col_two], axis=1)
        for a, b in zip(choose(x0, *qkv_parity), choose(x0, *up_parity))
    ]
    out_low = out_weight[0].astype(bf16)
    down_low = down_weight[0].astype(bf16).reshape(2, 2, unit, width)
    rest = jnp.stack(
        [
            jnp.concatenate(
                [out_low[:, h * width // 2 : (h + 1) * width // 2], down_low[h, 0], down_low[h, 1]], axis=1
            )
            for h in range(2)
        ]
    )
    up_at = cut
    two_at = up_at + up_cols
    out_at = two_at + 128
    down_at = out_at + width // 2
    conv_all, sig_got, whole, second_piece = opening(conv_send, sig_send, keep_cols, send_cols, rest)
    gathered = [whole, gather_rows(second_piece)]
    sig_all = jnp.transpose(sig_got, (1, 0, 2, 3)).reshape(micro_count, row_frames, block_width)
    conv_all = conv_all.reshape(dp_count, 2, 4, rows_here + 16, block_width)
    conv_all = jnp.transpose(conv_all, (1, 0, 2, 3, 4))
    bias_all = conv_all[:, :, :, rows_here, : conv_bias.shape[0]].reshape(width)
    bias_own = lax.dynamic_slice_in_dim(bias_all, (sec * 4 + seq) * block_width, block_width, 0)
    kernel_own = conv_all[:, :, :, :rows_here].reshape(TAPS * per_group, block_width)
    bands = conv_bands(kernel_own, per_group)


    def views(whole):
        w_out = jnp.transpose(
            whole[:, out_at:down_at].reshape(-1, 2, in_rows, width // 2), (0, 2, 1, 3)
        ).reshape(-1, width)
        gain_one = whole[:, qkv_cols].astype(f32)[None, :]
        gain_two = whole[:, two_at].astype(f32)[None, :]
        w_up = [whole[:, up_at + part * width : up_at + (part + 1) * width] for part in range(2)]
        w_down = [whole[:, down_at + part * width : down_at + (part + 1) * width] for part in range(2)]
        return gain_one, whole[:, :qkv_cols], w_out, gain_two, w_up, w_down

    layer_weights = []

    picked = jnp.where(sec0, cotangent[0], cotangent[1])
    across = [(s * 4 + 2 * yy + xx, yy * 4 + 2 * s + xx) for s in range(2) for yy in range(2) for xx in range(2)]
    cot_own = lax.ppermute(picked, both, across)
    cot_other = swap_x(cot_own)
    cot_pair = choose(x0, cot_own, cot_other)
    top_grad = jnp.concatenate(cot_pair, axis=0).astype(f32)

    segment_row = jnp.where(y == 0, frame_segment_index[0], frame_segment_index[1])
    seg_pair = choose(sec0, segment_row[:half_frames], segment_row[half_frames:])
    query_segs = seg_pair[0]
    key_segs = jnp.concatenate(seg_pair)

    sig_views = group_view(sig_all, per_group)
    conv_pre = ungroup(conv_forward(sig_views, bands), per_group) + bias_own.astype(f32)
    stream = (sig_all.astype(f32) + smooth(conv_pre)).astype(bf16)
    slope = gelu_slope(conv_pre).astype(bf16)
    stream_send = stream.reshape(2, 2, half_frames, block_width)
    stream_send = jnp.transpose(stream_send, (1, 0, 2, 3))
    stream_send = jnp.repeat(stream_send.reshape(4, half_frames, block_width), 2, axis=0)
    stream_got = lax.all_to_all(stream_send, both, 0, 0, tiled=True)
    layer_in = jnp.transpose(stream_got, (1, 0, 2)).reshape(half_frames, width).astype(f32)

    chunks = 2
    rows = half_frames // chunks
    layer_in = [layer_in[c * rows : (c + 1) * rows] for c in range(chunks)]
    chunk_segs = [query_segs[c * rows : (c + 1) * rows] for c in range(chunks)]
    kept = []
    for layer in range(2):
        whole = gathered[layer]
        if layer:
            layer_in = []
            previous_lows[0], whole = after(previous_lows[0], whole)
        layer_weights.append(views(whole))
        gain_one, w_qkv, w_out, gain_two, w_up, w_down = layer_weights[layer]
        normed_one, packed, kv_own, kv_other = [], [], [], []
        for c in range(chunks):
            if layer:
                total = previous[c] + pair_sum(previous_lows[c], packed[-1] if c else None)
                layer_in.append(total.astype(bf16).astype(f32))
            centred, inv = norm_stats(layer_in[c])
            normed_one.append((centred * inv * gain_one).astype(bf16))
            packed.append(jnp.dot(normed_one[c], w_qkv, preferred_element_type=f32).astype(bf16))
            kv_own.append(packed[c][:, width // 2 :])
            kv_other.append(swap_section(kv_own[c]))
        kv_all = jnp.concatenate(kv_own + kv_other, axis=0)
        attended, lse, resid_two, normed_two, hidden, hidden_slope = [], [], [], [], [], []
        attn_lows, lows = [], []
        for c in range(chunks):
            own = packed[c]
            if c:
                attn_lows[-1], own = after(attn_lows[-1], own)
            mixed, log_total = attention_forward(own, kv_all, chunk_segs[c], key_segs, factor)
            attended.append(mixed)
            lse.append(log_total)
            attn_lows.append(jnp.dot(mixed, w_out, preferred_element_type=f32).astype(bf16))
        for c in range(chunks):
            resid_two.append(layer_in[c] + pair_sum(attn_lows[c], lows[-1] if c else None))
            centred, inv = norm_stats(resid_two[c])
            normed_two.append((centred * inv * gain_two).astype(bf16))
            down_sum, own_hidden, own_slope = None, [], []
            for part in range(2):
                hidden_pre = jnp.dot(normed_two[c], w_up[part], preferred_element_type=f32)
                own_hidden.append(smooth(hidden_pre).astype(bf16))
                own_slope.append(gelu_slope(hidden_pre).astype(bf16))
            for part in range(2):
                term = jnp.dot(own_hidden[part], w_down[part], preferred_element_type=f32)
                down_sum = term if down_sum is None else down_sum + term
            hidden.append(own_hidden)
            hidden_slope.append(own_slope)
            lows.append(down_sum.astype(bf16))

        resid_two_last = resid_two
        kept.append((layer_in, normed_one, packed, kv_all, attended, lse, resid_two, normed_two, hidden, hidden_slope))
        previous, previous_lows = resid_two, lows

    def outer(left, right):
        return lax.dot_general(
            left, right, (((0,), (0,)), ((), ())), preferred_element_type=f32
        ).astype(bf16)

    def back(left, right):
        return lax.dot_general(left, right, (((1,), (1,)), ((), ())), preferred_element_type=f32)

    grad_out = [top_grad[c * rows : (c + 1) * rows] for c in range(chunks)]
    attn_members, scattered = [], []
    for layer in (1, 0):
        gain_one, w_qkv, w_out, gain_two, w_up, w_down = layer_weights[layer]
        (layer_in, normed_one, packed, kv_all, attended, lse, resid_two, normed_two, hidden, hidden_slope) = kept[layer]
        branch = [member.astype(bf16) for member in grad_out]
        pre_grad, sums, low = [], [], None
        for c in range(chunks):
            own = branch[c]
            if low is not None:
                low, own = after(low, own)
                sums.append(pair_sum(low))
            own_pre, part_sum = [], None
            for part in range(2):
                own_pre.append((back(own, w_down[part]) * hidden_slope[c][part].astype(f32)).astype(bf16))
            for part in range(2):
                term = back(own_pre[part], w_up[part])
                part_sum = term if part_sum is None else part_sum + term
            pre_grad.append(own_pre)
            low = part_sum.astype(bf16)
        sums.append(pair_sum(low))
        whole_pre = [jnp.concatenate([pre_grad[c][p] for c in range(chunks)]) for p in range(2)]
        whole_hidden = [jnp.concatenate([hidden[c][p] for c in range(chunks)]) for p in range(2)]
        whole_branch, whole_two = jnp.concatenate(branch), jnp.concatenate(normed_two)
        ff_members = [
            outer(whole_two, whole_pre[0]), outer(whole_two, whole_pre[1]),
            outer(whole_hidden[0], whole_branch), outer(whole_hidden[1], whole_branch),
        ]
        if layer == 1:
            ff_members.append(jnp.zeros((width, 128), bf16))
        partial = jnp.concatenate(attn_members + ff_members, axis=1)
        if layer == 0:
            sums, (partial, output_rows) = after(sums, (partial, output_rows))
        scattered.append(scatter_rows(partial))
        resid_grad, attn_branch, dq, gain_two_grad = [], [], [], None
        dkv = None
        for c in range(chunks):
            in_part, gain_part = norm_back(resid_two[c], gain_two, sums[c])
            gain_two_grad = gain_part if gain_two_grad is None else gain_two_grad + gain_part
            resid_grad.append(in_part + grad_out[c])
            attn_branch.append(resid_grad[c].astype(bf16))
            attended_grad = back(attn_branch[c], w_out).astype(bf16)
            if layer == 1 and c == 0:
                attended_grad, lows = after(attended_grad, lows)
                output = [member + pair_sum(low) for member, low in zip(resid_two_last, lows)]
                row_block = lax.ppermute(jnp.where(x0, output[0], output[1]), both, across)
                output_rows = jnp.stack(choose(sec0, row_block, swap_section(row_block)))
            own_dq, *dkv = attention_backward(
                packed[c], kv_all, attended_grad, attended[c], lse[c], chunk_segs[c], key_segs, factor,
                None if c == 0 else dkv,
            )
            dq.append(own_dq)
        if layer == 0:
            dkv, scattered[0] = after(dkv, scattered[0])
        else:
            dkv, output = after(dkv, output)
        dkv = jnp.concatenate(dkv, axis=1)
        other_dkv = swap_section(dkv[half_frames:].astype(bf16))
        dkv_own = (dkv[:half_frames] + other_dkv.astype(f32)).astype(bf16)
        packed_grad, sums, low = [], [], None
        for c in range(chunks):
            packed_grad.append(jnp.concatenate([dq[c], dkv_own[c * rows : (c + 1) * rows]], axis=1))
            own = packed_grad[c]
            if low is not None:
                low, own = after(low, own)
                sums.append(pair_sum(low))
            low = back(own, w_qkv).astype(bf16)
        sums.append(pair_sum(low))
        next_grad, gain_one_grad = [], None
        for c in range(chunks):
            in_part, gain_part = norm_back(layer_in[c], gain_one, sums[c])
            gain_one_grad = gain_part if gain_one_grad is None else gain_one_grad + gain_part
            next_grad.append((resid_grad[c] + in_part).astype(bf16))
        whole_one, whole_pg, whole_att, whole_ab = [
            jnp.concatenate(m) for m in (normed_one, packed_grad, attended, attn_branch)
        ]
        grad_out_weight = jnp.transpose(
            outer(whole_att, whole_ab).reshape(-1, in_rows, 2, width // 2), (0, 2, 1, 3)
        ).reshape(-1, width // 2)
        gain_grads = jnp.stack([gain_one_grad, gain_two_grad], axis=1).astype(bf16)
        gain_grads = jnp.pad(gain_grads, ((0, 0), (0, 126)))
        attn_members = [outer(whole_one, whole_pg), gain_grads, grad_out_weight]
        grad_out = [member.astype(f32) for member in next_grad]
    grad_in_low = jnp.concatenate(next_grad)
    scattered.append(scatter_rows(jnp.concatenate(attn_members, axis=1)))

    lig_send = jnp.transpose(grad_in_low.reshape(half_frames, 8, block_width), (1, 0, 2))
    def gradient_block(section, place):
        return lax.dynamic_index_in_dim(lig_send, section * 4 + place, 0, keepdims=False)

    beyond = (seq + 2) % 4
    corner = [(t * 4 + q, (1 - t) * 4 + (q ^ 2)) for t in range(2) for q in range(4)]
    near = choose(sec0, gradient_block(sec, seq), swap_section(gradient_block(1 - sec, seq)))
    far = choose(
        sec0,
        lax.ppermute(gradient_block(sec, beyond), "seq", [(q, q ^ 2) for q in range(4)]),
        lax.ppermute(gradient_block(1 - sec, beyond), both, corner),
    )
    lig = jnp.stack(choose(y == 0, jnp.concatenate(near), jnp.concatenate(far)))
    conv_grad = (lig.astype(f32) * slope.astype(f32)).astype(bf16)
    grad_views = group_view(conv_grad, per_group)
    back = ungroup(conv_back(grad_views, bands), per_group)
    grad_signal = (lig.astype(f32) + back).astype(bf16)
    gs_send = jnp.transpose(
        grad_signal.reshape(micro_count, 4, frames, block_width), (1, 0, 2, 3)
    )
    gs_send = jnp.concatenate([gs_send, gs_send], axis=0)
    taps_grad = conv_taps_grad(sig_views, grad_views, per_group)
    bias_grad = jnp.sum(conv_grad.astype(f32), axis=(0, 1))
    taps_view = jnp.transpose(
        taps_grad.reshape(2, dp_count, 4, rows_here, block_width), (1, 0, 2, 3, 4)
    ).astype(bf16)
    bias_view = jnp.pad(
        jnp.broadcast_to(bias_grad.astype(bf16), (dp_count, 2, 4, 1, block_width)),
        ((0, 0), (0, 0), (0, 0), (0, 15), (0, 0)),
    )
    taps_send = jnp.concatenate([taps_view, bias_view], axis=3)
    gs_got = lax.all_to_all(gs_send, both, 0, 0, tiled=True)
    attn_cols = cut + width // 2

    def over_section(first, second):
        keep, send = choose(sec0, first, second)
        return choose(sec0, keep, swap_section(send))


    taps_sum, (_, _, gs_got) = sum_dp(taps_send, dp, (gs_send, (), gs_got))
    gs_rows = jnp.transpose(gs_got, (1, 2, 0, 3)).reshape(micro_count, frames, width).astype(f32)
    ends = jnp.where(sec0, gs_rows, output_rows)[None]
    taps_got = lax.all_to_all(
        taps_sum.reshape(8, rows_here + 16, block_width), both, 0, 0, tiled=True
    )
    taps_got, scattered[1] = after(taps_got, scattered[1])
    conv_weight_grad = jnp.transpose(taps_got[:, :rows_here], (1, 0, 2)).reshape(rows_here, width).astype(f32)
    bias_count = conv_bias.shape[0]
    conv_bias_grad = lax.dynamic_slice_in_dim(
        taps_got[:, rows_here].reshape(width),
        ((sec * dp_count + dp) * 4 + seq) * bias_count,
        bias_count,
        0,
    ).astype(f32)

    turned = [(t * 4 + 2 * r + c, c * 4 + 2 * r + t) for t in range(2) for r in range(2) for c in range(2) if t != c]
    crossed = [(t * 4 + 2 * r + c, (1 - c) * 4 + 2 * r + t) for t in range(2) for r in range(2) for c in range(2)]

    def home(first, second):
        straight, other = choose(x0, first, second)
        straight = jnp.where(sec == x, straight, lax.ppermute(straight, both, turned))
        other = lax.ppermute(other, both, crossed)
        return choose(sec0, straight, other)

    ff_layers = (scattered[1][:, attn_cols:], scattered[0][:, :-128])
    ff_sets = over_section(*(member[:, up_cols:] for member in ff_layers))
    down_grad = jnp.concatenate(
        [member[:, at : at + width] for member in ff_sets for at in (0, width)], axis=0
    ).astype(f32)[None]
    up_grad = jnp.stack(
        [
            jnp.transpose(member.reshape(in_rows, 2, -1, 2, unit), (0, 2, 3, 1, 4))
            for member in home(*(member[:, :up_cols] for member in ff_layers))
        ],
        axis=2,
    ).reshape(in_rows, -1).astype(f32)[None]
    scattered[2], (up_grad, down_grad) = after(scattered[2], (up_grad, down_grad))
    attn_layers = (scattered[2], scattered[1][:, :attn_cols])
    attn_sets = over_section(*(member[:, cut:] for member in attn_layers))
    out_grad = jnp.concatenate(attn_sets, axis=1).astype(f32)[None]
    qkv_sets = home(*(member[:, :cut] for member in attn_layers))
    norm1_grad = qkv_sets[0][:, qkv_cols].astype(f32)[None]
    norm2_grad = qkv_sets[0][:, qkv_cols + 1].astype(f32)[None]
    qkv_grad = jnp.stack(
        [member[:, :qkv_cols].reshape(in_rows, -1, HEAD_DIM) for member in qkv_sets], axis=2
    ).reshape(in_rows, -1).astype(f32)[None]
    return (ends, conv_weight_grad, conv_bias_grad, norm1_grad, qkv_grad, out_grad, norm2_grad, up_grad, down_grad)


def solution(mesh):
    placed = (
        P("dp", "seq", None),
        P("dp", None),
        P(("section", "dp", "seq"), None),
        P(("section", "dp", "seq")),
        P("section", ("dp", "seq")),
        P("section", ("dp", "seq"), None),
        P("section", ("dp", "seq"), None),
        P("section", ("dp", "seq")),
        P("section", ("dp", "seq"), None),
        P("section", ("dp", "seq"), None),
        P("dp", "seq", None),
    )

    def step(*arrays):
        pairs = mesh.shape["seq"] == 4 and mesh.shape["section"] == 2 and arrays[0].shape[0] == 2
        return (per_device_pairs if pairs else per_device)(*arrays)

    return jax.shard_map(
        step,
        mesh=mesh,
        in_specs=placed,
        out_specs=(
            P("section", "dp", "seq", None),
            P(("section", "dp", "seq"), None),
            P(("section", "dp", "seq")),
            P("section", ("dp", "seq")),
            P("section", ("dp", "seq"), None),
            P("section", ("dp", "seq"), None),
            P("section", ("dp", "seq")),
            P("section", ("dp", "seq"), None),
            P("section", ("dp", "seq"), None),
        ),
        check_vma=False,
    )
```
